32 devices in a mesh: dp: 4 (over y, x), expert: 8 (over z, core).
Axes of the slice: x: 2, y: 2, z: 4, core: 2. Of those that a mesh axis runs over, the one named last changes fastest.
Arguments:
- images: float32 [128, 197, 512], P(('dp', 'expert')), may hold values from -6 to 6
- cotangent: float32 [128, 197, 512], P(('dp', 'expert')), may hold values from -6 to 6
- routes: int32 [2, 128, 197, 2], P(None, ('dp', 'expert')), may hold values from 0 to 15, all different within a row
- query_weight: float32 [2, 512, 512], P(None, 'dp'), may hold values from -0.25 to 0.25
- key_weight: float32 [2, 512, 512], P(None, 'dp'), may hold values from -0.25 to 0.25
- value_weight: float32 [2, 512, 512], P(None, 'dp'), may hold values from -0.25 to 0.25
- output_weight: float32 [2, 512, 512], P(None, 'dp'), may hold values from -2 to 2
- router_weight: float32 [2, 512, 16], P(None, 'dp'), may hold values from -0.1875 to 0.1875
- query_bias: float32 [2, 512], P(None, 'dp'), may hold values from -1.2 to 1.2
- value_bias: float32 [2, 512], P(None, 'dp'), may hold values from -1.2 to 1.2
- output_bias: float32 [2, 512], P(None, 'dp'), may hold values from -1.2 to 1.2
- attend_gain: float32 [2, 512], P(None, 'dp'), may hold values from 0.5 to 1.5
- attend_shift: float32 [2, 512], P(None, 'dp'), may hold values from -0.6 to 0.6
- expert_gain: float32 [2, 512], P(None, 'dp'), may hold values from 0.5 to 1.5
- expert_shift: float32 [2, 512], P(None, 'dp'), may hold values from -0.6 to 0.6
- inner_weight: float32 [2, 16, 512, 2048], P(None, 'expert', 'dp'), may hold values from -0.25 to 0.25
- inner_bias: float32 [2, 16, 2048], P(None, 'expert', 'dp'), may hold values from -0.6 to 0.6
- outer_weight: float32 [2, 16, 2048, 512], P(None, 'expert', 'dp'), may hold values from -0.1875 to 0.1875
- outer_bias: float32 [2, 16, 512], P(None, 'expert', 'dp'), may hold values from -0.6 to 0.6
Outputs:
- layer_output: float32 [128, 197, 512], P(('dp', 'expert'))
- images_gradient: float32 [128, 197, 512], P(('dp', 'expert'))
- query_weight_gradient: float32 [2, 512, 512], P(None, 'dp')
- key_weight_gradient: float32 [2, 512, 512], P(None, 'dp')
- value_weight_gradient: float32 [2, 512, 512], P(None, 'dp')
- output_weight_gradient: float32 [2, 512, 512], P(None, 'dp')
- router_weight_gradient: float32 [2, 512, 16], P(None, 'dp')
- query_bias_gradient: float32 [2, 512], P(None, 'dp')
- value_bias_gradient: float32 [2, 512], P(None, 'dp')
- output_bias_gradient: float32 [2, 512], P(None, 'dp')
- attend_gain_gradient: float32 [2, 512], P(None, 'dp')
- attend_shift_gradient: float32 [2, 512], P(None, 'dp')
- expert_gain_gradient: float32 [2, 512], P(None, 'dp')
- expert_shift_gradient: float32 [2, 512], P(None, 'dp')
- inner_weight_gradient: float32 [2, 16, 512, 2048], P(None, 'expert', 'dp')
- inner_bias_gradient: float32 [2, 16, 2048], P(None, 'expert', 'dp')
- outer_weight_gradient: float32 [2, 16, 2048, 512], P(None, 'expert', 'dp')
- outer_bias_gradient: float32 [2, 16, 512], P(None, 'expert', 'dp')
The draws below stay inside these ranges and needn't reach their ends.
All inputs are finite; a program needn't handle non-finite values.
Results may differ from the reference program's by a relative error of at most 0.015.
Values may be sent and summed in bfloat16 or wider, within the bound.
A program may use at most 320 MiB of HBM per device.

```python
import jax
import jax.numpy as jnp
from jax import lax

D = 512
HEADS = 8
HEAD_DIM = 64
FF = 2048
SEQ = 197
LAYERS = 2
IMG_DEV = 4
EXPERTS = 16
IMAGES = 128
CAP = 128
N_DP = 4
N_EXPERT = 8


def spiked(values, own_key, source, target, parts, factor):
    owner, partner = [(jnp.arange(values.shape[position]) // (values.shape[position] // parts)).reshape([-1 if axis == position else 1 for axis in range(values.ndim)]) for position in (source, target)]
    chosen = jax.random.permutation(own_key, parts)[partner]
    strong = (owner == chosen) | (owner == (partner + parts // 2) % parts)
    return jnp.where(strong, factor * values, values)


def level_of(own_key, shape, pieces, low, top_value):
    level, own = 1.0, jax.random.fold_in(own_key, 6)
    for position, parts in pieces:
        draws = jnp.exp(jax.random.uniform(jax.random.fold_in(own, position), (parts,), jnp.float32, low / len(pieces), top_value / len(pieces)))
        level = level * jnp.repeat(draws, shape[position] // parts).reshape([-1 if axis == position else 1 for axis in range(len(shape))])
    return level


def choose_distinct(key, rows, amount, top, lift):
    sequence = jax.random.permutation(jax.random.fold_in(key, 1), amount)
    favour = sequence
    for power in range(3):
        favour = favour * favour // amount
    favour = favour * lift // amount
    chance = jax.random.randint(jax.random.fold_in(key, 2), (rows, amount), 0, 4096) + favour
    holders = jax.random.permutation(jax.random.fold_in(key, 3), rows)[jnp.arange(amount) % rows]
    chance = jnp.where(jnp.arange(rows)[:, None] == holders[None, :], 1 << 14, chance)
    merit = chance * amount + jnp.arange(amount)
    return lax.top_k(merit.astype(jnp.int32), top)[1].astype(jnp.int32)


def bell_draw(stream_key, dims, spread, limit, split=(), kind=jnp.bfloat16):
    array = jax.random.normal(stream_key, dims, jnp.float32) * spread
    if len(split) > 0:
        array = level_of(stream_key, dims, split, -0.22, 0.18) * array
    return jnp.clip(array, min=-limit, max=limit).astype(kind)


def noise_with(own_key, extent, spread, bound, split, heavy, held_as=jnp.bfloat16):
    drawn = spread * jax.random.normal(own_key, extent, jnp.float32)
    if split:
        drawn = drawn * level_of(own_key, extent, split, -0.22, 0.18)
    return jnp.clip(spiked(drawn, jax.random.fold_in(own_key, 3), *heavy), -bound, bound).astype(held_as)


def setup_inputs(seed: int = 0) -> dict:
    streams_of = jax.random.split(jax.random.key(seed), 20)
    images = noise_with(streams_of[0], (IMAGES, SEQ, D), 1.0, 6.0, ((0, 32),), (0, 2, 32, 2.75), jnp.float32)
    cotangent = bell_draw(streams_of[1], (IMAGES, SEQ, D), 1.0, 6.0, ((0, 32),), jnp.float32)
    routes = choose_distinct(streams_of[2], LAYERS * IMAGES * SEQ, EXPERTS, 2, 1024).reshape((LAYERS, IMAGES, SEQ, 2))
    query_weight = bell_draw(streams_of[3], (LAYERS, D, D), D ** -0.5, 0.25, ((1, 4),), jnp.float32)
    key_weight = bell_draw(streams_of[4], (LAYERS, D, D), D ** -0.5, 0.25, ((1, 4),), jnp.float32)
    value_weight = bell_draw(streams_of[5], (LAYERS, D, D), D ** -0.5, 0.25, ((1, 4),), jnp.float32)
    output_weight = bell_draw(streams_of[6], (LAYERS, D, D), (max(1, 4 * D // SEQ)) ** -0.5, 2.0, ((1, 4),), jnp.float32)
    router_weight = bell_draw(streams_of[7], (LAYERS, D, EXPERTS), (2 * D) ** -0.5, 0.1875, ((1, 4),), jnp.float32)
    query_bias = bell_draw(streams_of[8], (LAYERS, D), 0.2, 1.2, ((1, 4),), jnp.float32)
    value_bias = bell_draw(streams_of[9], (LAYERS, D), 0.2, 1.2, ((1, 4),), jnp.float32)
    output_bias = bell_draw(streams_of[10], (LAYERS, D), 0.2, 1.2, ((1, 4),), jnp.float32)
    attend_gain = jnp.clip(1.0 + 0.1 * jax.random.normal(streams_of[11], (LAYERS, D), jnp.float32), 0.5, 1.5)
    attend_shift = bell_draw(streams_of[12], (LAYERS, D), 0.1, 0.6, ((1, 4),), jnp.float32)
    expert_gain = jnp.clip(1.0 + 0.1 * jax.random.normal(streams_of[13], (LAYERS, D), jnp.float32), 0.5, 1.5)
    expert_shift = bell_draw(streams_of[14], (LAYERS, D), 0.1, 0.6, ((1, 4),), jnp.float32)
    inner_weight = bell_draw(streams_of[15], (LAYERS, EXPERTS, D, FF), D ** -0.5, 0.25, ((1, 8), (2, 4)), jnp.float32)
    inner_bias = bell_draw(streams_of[16], (LAYERS, EXPERTS, FF), 0.1, 0.6, ((1, 8), (2, 4)), jnp.float32)
    outer_weight = bell_draw(streams_of[17], (LAYERS, EXPERTS, FF, D), (FF // 2) ** -0.5, 0.1875, ((1, 8), (2, 4)), jnp.float32)
    outer_bias = bell_draw(streams_of[18], (LAYERS, EXPERTS, D), 0.1, 0.6, ((1, 8), (2, 4)), jnp.float32)
    return dict(images=images, cotangent=cotangent, routes=routes, query_weight=query_weight, key_weight=key_weight, value_weight=value_weight, output_weight=output_weight, router_weight=router_weight, query_bias=query_bias, value_bias=value_bias, output_bias=output_bias, attend_gain=attend_gain, attend_shift=attend_shift, expert_gain=expert_gain, expert_shift=expert_shift, inner_weight=inner_weight, inner_bias=inner_bias, outer_weight=outer_weight, outer_bias=outer_bias)


@jax.custom_vjp
def low(v):
    return lax.optimization_barrier(v.astype(jnp.bfloat16)).astype(jnp.float32)

@jax.custom_vjp
def low_back(v):
    return v

def low_keep(v):
    return (low(v), None)

def low_pass(kept, grad):
    return (grad,)

def back_keep(v):
    return (v, None)

def back_low(kept, grad):
    return (low(grad),)
low.defvjp(low_keep, low_pass)
low_back.defvjp(back_keep, back_low)
EPSILON = 1e-06
HIGHEST = lax.Precision.HIGHEST

def norm_rows(rows, gain, shift):
    mean_value = lax.optimization_barrier(jnp.mean(rows, axis=-1, keepdims=True))
    centered = rows - mean_value
    variance = lax.optimization_barrier(jnp.mean(centered * centered, axis=-1, keepdims=True))
    return centered * lax.rsqrt(variance + EPSILON) * gain + shift

def attend_plain(block, query_weight, key_weight, value_weight, query_bias, value_bias):
    shape4 = (IMG_DEV, SEQ, HEADS, HEAD_DIM)
    queries = low(low_back(jnp.dot(block, query_weight, precision=HIGHEST) + query_bias)).reshape(shape4)
    keys = low(low_back(jnp.dot(block, key_weight, precision=HIGHEST))).reshape(shape4)
    values = low(low_back(jnp.dot(block, value_weight, precision=HIGHEST) + value_bias)).reshape(shape4)
    scores = low_back(jnp.einsum('iqhe,ikhe->ihqk', queries, keys, precision=HIGHEST) * HEAD_DIM ** (-0.5))
    attention = low(jax.nn.softmax(scores, axis=-1))
    mixed = jnp.einsum('ihqk,ikhe->iqhe', attention, values, precision=HIGHEST)
    return low(low_back(mixed.reshape(IMG_DEV * SEQ, D)))

def expert_plain(rows, inner_weight, inner_bias, outer_weight, outer_bias):
    inner = low_back(jnp.dot(rows, inner_weight, precision=HIGHEST) + inner_bias)
    activated = low(jax.nn.gelu(inner, approximate=False))
    return low(low_back(jnp.dot(activated, outer_weight, precision=HIGHEST) + outer_bias))

def layer_forward(rows, routes_here, params):
    query_weight, key_weight, value_weight, output_weight, router_weight, query_bias, value_bias, output_bias, attend_gain, attend_shift, expert_gain, expert_shift, inner_weight, inner_bias, outer_weight, outer_bias = [low(item) for item in params]
    devices = N_DP * N_EXPERT
    tokens_all = IMAGES * SEQ
    normed = low(norm_rows(rows, attend_gain, attend_shift))
    blocks = normed.reshape(devices, IMG_DEV * SEQ, D)
    attend_saved = jax.checkpoint(attend_plain)
    context = lax.map(lambda block: attend_saved(block, query_weight, key_weight, value_weight, query_bias, value_bias), blocks)
    context = context.reshape(tokens_all, D)
    branch = low_back(jnp.dot(context, output_weight, precision=HIGHEST) + output_bias)
    middle = rows + branch
    hidden = low(norm_rows(middle, expert_gain, expert_shift))
    logits = low_back(jnp.dot(hidden, router_weight, precision=HIGHEST))
    pairs = routes_here.reshape(tokens_all, 2).astype(jnp.int32)
    chosen = jnp.take_along_axis(logits, pairs, axis=1)
    gates = jax.nn.softmax(chosen, axis=1)
    pair_experts = pairs.reshape(devices, IMG_DEV * SEQ * 2)
    table = (pair_experts[:, :, None] == jnp.arange(EXPERTS, dtype=jnp.int32)[None, None, :]).astype(jnp.int32)
    before = jnp.cumsum(table, axis=1) - table
    slot = lax.optimization_barrier(jnp.sum(before * table, axis=2))
    valid = slot < CAP
    dest = jnp.where(valid, pair_experts * CAP + slot, EXPERTS * CAP)
    stride = EXPERTS * CAP + 1
    global_index = (jnp.arange(devices, dtype=jnp.int32)[:, None] * stride + dest).reshape(-1).astype(jnp.int32)
    pair_rows = jnp.repeat(hidden, 2, axis=0)
    buffer = jnp.zeros((devices * stride, D), jnp.float32).at[global_index].add(pair_rows)
    buffer = buffer.reshape(devices, stride, D)[:, :EXPERTS * CAP].reshape(devices, EXPERTS, CAP, D)
    buffer = low_back(buffer)
    per_expert = jnp.transpose(buffer, (1, 0, 2, 3)).reshape(EXPERTS, devices * CAP, D)
    expert_saved = jax.checkpoint(expert_plain)
    produced = lax.map(lambda items: expert_saved(items[0], items[1], items[2], items[3], items[4]), (per_expert, inner_weight, inner_bias, outer_weight, outer_bias))
    produced = jnp.transpose(produced.reshape(EXPERTS, devices, CAP, D), (1, 0, 2, 3)).reshape(devices, EXPERTS * CAP, D)
    produced = jnp.concatenate([produced, jnp.zeros((devices, 1, D), jnp.float32)], axis=1).reshape(devices * stride, D)
    picked = jnp.take(produced, global_index, axis=0)
    weight = gates.reshape(-1) * valid.reshape(-1).astype(jnp.float32)
    mixture = lax.optimization_barrier(jnp.sum((picked * weight[:, None]).reshape(tokens_all, 2, D), axis=1))
    return middle + mixture

def reference(images, cotangent, routes, query_weight, key_weight, value_weight, output_weight, router_weight, query_bias, value_bias, output_bias, attend_gain, attend_shift, expert_gain, expert_shift, inner_weight, inner_bias, outer_weight, outer_bias):
    params = (query_weight, key_weight, value_weight, output_weight, router_weight, query_bias, value_bias, output_bias, attend_gain, attend_shift, expert_gain, expert_shift, inner_weight, inner_bias, outer_weight, outer_bias)

    def forward(rows, weights):
        for layer in range(LAYERS):
            rows = layer_forward(rows, routes[layer], tuple((item[layer] for item in weights)))
        return rows
    start = images.reshape(IMAGES * SEQ, D)
    result, pull = jax.vjp(forward, start, params)
    start_grad, grads = pull(cotangent.reshape(IMAGES * SEQ, D))
    return (result.reshape(IMAGES, SEQ, D), start_grad.reshape(IMAGES, SEQ, D), grads[0], grads[1], grads[2], grads[3], grads[4], grads[5], grads[6], grads[7], grads[8], grads[9], grads[10], grads[11], grads[12], grads[13], grads[14], grads[15])
```

```python
import functools

import jax
import jax.numpy as jnp
from jax import lax
from jax.experimental import pallas as pl
from jax.experimental.pallas import tpu as pltpu
from jax.sharding import PartitionSpec as P

HEADS = 8
HEAD_DIM = 64
LAYERS = 2
EPSILON = 1e-06
FACTOR = HEAD_DIM**-0.5
VEC_AT = 64
BIAS_AT = 72
MISC = 128
FF_BLOCK = 512
VMEM = 56 * 1024 * 1024

F32 = jnp.float32
BF16 = jnp.bfloat16


def dot(a, b):
    return jnp.dot(a, b, preferred_element_type=F32)


def dot_nt(a, b):
    return lax.dot_general(a, b, (((1,), (1,)), ((), ())), preferred_element_type=F32)


def dot_tn(a, b):
    return lax.dot_general(a, b, (((0,), (0,)), ((), ())), preferred_element_type=F32)


def standardize(rows):
    mean_value = jnp.mean(rows, axis=-1, keepdims=True)
    centered = rows - mean_value
    variance = jnp.mean(centered * centered, axis=-1, keepdims=True)
    scale = lax.rsqrt(variance + EPSILON)
    return centered * scale, scale


def standardize_back(upstream, unit, scale, gain):
    along = upstream * gain
    inner = (
        along
        - jnp.mean(along, axis=-1, keepdims=True)
        - unit * jnp.mean(along * unit, axis=-1, keepdims=True)
    )
    return inner * scale


def vectors_of(misc_ref):
    turned = misc_ref[...].astype(F32).T
    return [turned[VEC_AT + n : VEC_AT + n + 1, :] for n in range(7)]


def pick(dest, buffers):
    total = None
    for number, buffer in enumerate(buffers):
        count = buffer.shape[0]
        lanes = lax.broadcasted_iota(jnp.int32, (dest.shape[0], count), 1)
        chosen = (dest - number * count == lanes).astype(F32).astype(BF16)
        part = dot(chosen, buffer[...])
        total = part if total is None else total + part
    return total


def spread(dest_rows, sources, outs, first):
    half = outs[0].shape[0]
    step = 256
    length = dest_rows[0].shape[1]
    for number, out in enumerate(outs):
        for start in range(0, half, step):
            slots = lax.broadcasted_iota(jnp.int32, (step, length), 0) + (number * half + start)
            if len(sources) == 1:
                hit = (slots == dest_rows[0]) | (slots == dest_rows[1])
                block = dot(hit.astype(F32).astype(BF16), sources[0])
            else:
                block = dot((slots == dest_rows[0]).astype(F32).astype(BF16), sources[0])
                block = block + dot((slots == dest_rows[1]).astype(F32).astype(BF16), sources[1])
            block = block.astype(BF16)

            @pl.when(first)
            def _(out=out, start=start, block=block):
                out[start : start + step, :] = block

            @pl.when(jnp.logical_not(first))
            def _(out=out, start=start, block=block):
                out[start : start + step, :] += block


def lane_masks(length):
    lanes = lax.broadcasted_iota(jnp.int32, (length, 2 * HEAD_DIM), 1)
    return (lanes < HEAD_DIM).astype(F32).astype(BF16), (lanes >= HEAD_DIM).astype(F32).astype(BF16)


def attend_body(
    rows, routes_ref, drow_ref, wq, wk, wv, wo, misc,
    t_ref, q_ref, k_ref, v_ref, o_ref, lse_ref, gates_ref, outs,
):
    length = rows.shape[0]
    qb, vb, ob, again, ashift, egain, eshift = vectors_of(misc)
    unit, _ = standardize(rows)
    low = (unit * again + ashift).astype(BF16)
    queries = (dot(low, wq[...]) + qb).astype(BF16)
    keys = dot(low, wk[...]).astype(BF16)
    values = (dot(low, wv[...]) + vb).astype(BF16)
    q_ref[0] = queries
    k_ref[0] = keys
    v_ref[0] = values
    masks = lane_masks(length)
    lanes = lax.broadcasted_iota(jnp.int32, (length, MISC), 1)
    first_half = lax.broadcasted_iota(jnp.int32, (length, 2 * HEAD_DIM), 1) < HEAD_DIM
    sums = jnp.zeros((length, MISC), F32)
    for pair in range(HEADS // 2):
        cols = slice(pair * 2 * HEAD_DIM, (pair + 1) * 2 * HEAD_DIM)
        mixed = []
        for side in range(2):
            scores = dot_nt(queries[:, cols] * (masks[side] * FACTOR), keys[:, cols])
            highest = jnp.max(scores, axis=-1, keepdims=True)
            expo = jnp.exp(scores - highest)
            total = jnp.sum(expo, axis=-1, keepdims=True)
            attention = (expo * (1.0 / total)).astype(BF16)
            sums = jnp.where(lanes == 2 * pair + side, highest + jnp.log(total), sums)
            mixed.append(dot(attention, values[:, cols]))
        o_ref[0, :, cols] = jnp.where(first_half, mixed[0], mixed[1]).astype(BF16)
    lse_ref[0] = sums
    middle = rows + (dot(o_ref[0], wo[...]) + ob)
    t_ref[0] = middle
    unit_two, _ = standardize(middle)
    hidden = (unit_two * egain + eshift).astype(BF16)
    logits = dot(hidden, misc[...])
    pair_experts = routes_ref[0]
    zero = jnp.sum(jnp.where(lanes == pair_experts[:, 0:1], logits, 0.0), axis=-1, keepdims=True)
    one = jnp.sum(jnp.where(lanes == pair_experts[:, 1:2], logits, 0.0), axis=-1, keepdims=True)
    gate_zero = 1.0 / (1.0 + jnp.exp(one - zero))
    gate_one = 1.0 / (1.0 + jnp.exp(zero - one))
    gates_ref[0, :, 0:1] = gate_zero
    gates_ref[0, :, 1:2] = gate_one
    drow = drow_ref[0]
    spread([drow[0:1, :], drow[1:2, :]], [hidden], outs, pl.program_id(0) == 0)


def combine_body(middle, gates_ref, dcol_ref, back, yzero_ref, yone_ref):
    dest = dcol_ref[0]
    gates = gates_ref[0]
    zero = pick(dest[:, 0:1], back)
    one = pick(dest[:, 1:2], back)
    if yzero_ref is not None:
        yzero_ref[0] = zero.astype(BF16)
        yone_ref[0] = one.astype(BF16)
    return middle + (gates[:, 0:1] * zero + gates[:, 1:2] * one), zero, one


def grads_body(upstream, zero, one, gates_ref, routes_ref, drow_ref, dz_ref, outs):
    length = upstream.shape[0]
    gates = gates_ref[0]
    gate_zero, gate_one = gates[:, 0:1], gates[:, 1:2]
    grad_zero = jnp.sum(zero * upstream, axis=-1, keepdims=True)
    grad_one = jnp.sum(one * upstream, axis=-1, keepdims=True)
    along = gate_zero * grad_zero + gate_one * grad_one
    lanes = lax.broadcasted_iota(jnp.int32, (length, MISC), 1)
    pair_experts = routes_ref[0]
    dz = jnp.where(lanes == pair_experts[:, 0:1], gate_zero * (grad_zero - along), 0.0)
    dz = dz + jnp.where(lanes == pair_experts[:, 1:2], gate_one * (grad_one - along), 0.0)
    dz_ref[0] = dz.astype(BF16)
    drow = drow_ref[0]
    spread(
        [drow[0:1, :], drow[1:2, :]],
        [(gate_zero * upstream).astype(BF16), (gate_one * upstream).astype(BF16)],
        outs,
        pl.program_id(0) == 0,
    )


def first_kernel(rows, routes, drow, wq, wk, wv, wo, misc, *outs):
    attend_body(rows[0], routes, drow, wq, wk, wv, wo, misc, *outs[:7], outs[7:])


def next_kernel(
    middle, gates, dcol, back_a, back_b, routes, drow, wq, wk, wv, wo, misc, rows_ref, yzero, yone, *outs
):
    rows, _, _ = combine_body(middle[0], gates, dcol, (back_a, back_b), yzero, yone)
    rows_ref[0] = rows
    attend_body(rows, routes, drow, wq, wk, wv, wo, misc, *outs[:7], outs[7:])


def turn_kernel(middle, gates, dcol, back_a, back_b, cotangent, routes, drow, result, dz, out_a, out_b):
    rows, zero, one = combine_body(middle[0], gates, dcol, (back_a, back_b), None, None)
    result[0] = rows
    grads_body(cotangent[0], zero, one, gates, routes, drow, dz, (out_a, out_b))


def back_kernel(
    upstream, rows, middle, q_ref, k_ref, v_ref, o_ref, lse_ref, dz_ref, dcol, came_a, came_b,
    wq, wk, wv, wo, misc, *rest,
):
    if len(rest) > 3:
        yzero, yone, gates_below, routes_below, drow_below, grad_ref, wgrad, dz_below, out_a, out_b, vgrad = rest
    else:
        grad_ref, wgrad, vgrad = rest
    first = pl.program_id(0) == 0
    length = rows.shape[1]
    width = rows.shape[2]
    qb, vb, ob, again, ashift, egain, eshift = vectors_of(misc)

    @pl.when(first)
    def _():
        wgrad[...] = jnp.zeros_like(wgrad)
        vgrad[...] = jnp.zeros_like(vgrad)

    def add_vector(number, value):
        vgrad[VEC_AT + number : VEC_AT + number + 1, :] += jnp.sum(value, axis=0, keepdims=True)

    unit_two, scale_two = standardize(middle[0])
    hidden = (unit_two * egain + eshift).astype(BF16)
    dz = dz_ref[0]
    dest = dcol[0]
    dhidden = dot_nt(dz, misc[...])
    for number, came in enumerate((came_a, came_b)):
        count = came.shape[0]
        lanes = lax.broadcasted_iota(jnp.int32, (length, count), 1) + number * count
        hit = (dest[:, 0:1] == lanes) | (dest[:, 1:2] == lanes)
        dhidden = dhidden + dot(hit.astype(F32).astype(BF16), came[...])
    wgrad[:, 4 * width :] += dot_tn(hidden, dz)
    add_vector(5, dhidden * unit_two)
    add_vector(6, dhidden)
    dmiddle = upstream[0] + standardize_back(dhidden, unit_two, scale_two, egain)
    dbranch = dmiddle.astype(BF16)
    wgrad[:, 3 * width : 4 * width] += dot_tn(o_ref[0], dbranch)
    add_vector(2, dbranch.astype(F32))
    dcontext = dot_nt(dbranch, wo[...]).astype(BF16)
    masks = lane_masks(length)
    first_half = lax.broadcasted_iota(jnp.int32, (length, 2 * HEAD_DIM), 1) < HEAD_DIM
    dqs, dks, dvs = [], [], []
    for pair in range(HEADS // 2):
        cols = slice(pair * 2 * HEAD_DIM, (pair + 1) * 2 * HEAD_DIM)
        keys = k_ref[0, :, cols]
        values = v_ref[0, :, cols]
        queries = q_ref[0, :, cols]
        dvalues, dqueries, dkeys = None, [], None
        for side in range(2):
            own_queries = queries * (masks[side] * FACTOR)
            own_context = dcontext[:, cols] * masks[side]
            scores = dot_nt(own_queries, keys)
            number = 2 * pair + side
            attention = jnp.exp(scores - lse_ref[0, :, number : number + 1])
            prob = dot_nt(own_context, values)
            weighed = attention * prob
            delta = jnp.sum(weighed, axis=-1, keepdims=True)
            dscores = (weighed - attention * delta).astype(BF16)
            dvalue = dot_tn(attention.astype(BF16), own_context)
            dkey = dot_tn(dscores, own_queries)
            dvalues = dvalue if dvalues is None else dvalues + dvalue
            dkeys = dkey if dkeys is None else dkeys + dkey
            dqueries.append(dot(dscores, keys))
        dqs.append((jnp.where(first_half, dqueries[0], dqueries[1]) * FACTOR).astype(BF16))
        dks.append(dkeys.astype(BF16))
        dvs.append(dvalues.astype(BF16))
    dq = jnp.concatenate(dqs, axis=1)
    dk = jnp.concatenate(dks, axis=1)
    dv = jnp.concatenate(dvs, axis=1)
    unit, scale = standardize(rows[0])
    low = (unit * again + ashift).astype(BF16)
    wgrad[:, 0:width] += dot_tn(low, dq)
    wgrad[:, width : 2 * width] += dot_tn(low, dk)
    wgrad[:, 2 * width : 3 * width] += dot_tn(low, dv)
    add_vector(0, dq.astype(F32))
    add_vector(1, dv.astype(F32))
    dlow = dot_nt(dq, wq[...]) + dot_nt(dk, wk[...]) + dot_nt(dv, wv[...])
    add_vector(3, dlow * unit)
    add_vector(4, dlow)
    grad = dmiddle + standardize_back(dlow, unit, scale, again)
    grad_ref[0] = grad
    if len(rest) > 3:
        grads_body(
            grad, yzero[0].astype(F32), yone[0].astype(F32), gates_below, routes_below, drow_below, dz_below,
            (out_a, out_b),
        )

    @pl.when(pl.program_id(0) == pl.num_programs(0) - 1)
    def _():
        wgrad[:, 4 * width :] += vgrad[...].T


def per_image(array):
    return pl.BlockSpec((1,) + array.shape[1:], lambda i: (i,) + (0,) * (len(array.shape) - 1))


def whole(array):
    return pl.BlockSpec(array.shape, lambda i: (0,) * len(array.shape))


def packed_specs(packed):
    width = packed.shape[0]
    specs = [pl.BlockSpec((width, width), lambda i, n=n: (0, n)) for n in range(4)]
    return specs + [pl.BlockSpec((width, MISC), lambda i: (0, 4 * width // MISC))]


def call(body, grid, inputs, outputs, scratch=(), flops=0, aliases=None):
    moved = sum(a.size * a.dtype.itemsize for a, _ in inputs)
    shapes = [jax.ShapeDtypeStruct(s, t) for s, t, _ in outputs]
    moved += sum(s.size * s.dtype.itemsize for s in shapes)
    return pl.pallas_call(
        body,
        grid=grid,
        in_specs=[s for _, s in inputs],
        out_specs=[s for _, _, s in outputs],
        out_shape=shapes,
        scratch_shapes=list(scratch),
        compiler_params=pltpu.CompilerParams(vmem_limit_bytes=VMEM),
        cost_estimate=pl.CostEstimate(flops=flops, bytes_accessed=moved, transcendentals=0),
    )(*[a for a, _ in inputs])


def images_out(images, length, columns, kind):
    shape = (images, length, columns)
    return (shape, kind, pl.BlockSpec((1, length, columns), lambda i: (i, 0, 0)))


def slots_out(half, width):
    return [((half, width), BF16, pl.BlockSpec((half, width), lambda i: (0, 0)))] * 2


def attend_outputs(images, length, width, half):
    return [
        images_out(images, length, width, F32),
        images_out(images, length, width, BF16),
        images_out(images, length, width, BF16),
        images_out(images, length, width, BF16),
        images_out(images, length, width, BF16),
        images_out(images, length, MISC, F32),
        images_out(images, length, 2, F32),
    ] + slots_out(half, width)


def gelu(value):
    return 0.5 * value * (1.0 + lax.erf(value * 0.7071067811865476))


def expert_kernel(x_ref, w1_ref, b1_ref, w2_ref, b2_ref, y_ref, acc):
    step = pl.program_id(0)
    rows = x_ref.shape[0]
    chunk = 256
    for start in range(0, rows, chunk):
        part = slice(start, start + chunk)
        inner = dot(x_ref[part, :], w1_ref[0]) + b1_ref[0]
        term = dot(gelu(inner).astype(BF16), w2_ref[0])

        @pl.when(step == 0)
        def _(part=part, term=term):
            acc[part, :] = term + b2_ref[0]

        @pl.when(step > 0)
        def _(part=part, term=term):
            acc[part, :] += term

    @pl.when(step == pl.num_programs(0) - 1)
    def _():
        y_ref[...] = acc[...].astype(BF16)


def slope_kernel(x_ref, w1_ref, b1_ref, g_ref, s_ref):
    rows = x_ref.shape[0]
    chunk = 256
    for start in range(0, rows, chunk):
        part = slice(start, start + chunk)
        inner = dot(x_ref[part, :], w1_ref[0]) + b1_ref[0]
        normal = 0.5 * (1.0 + lax.erf(inner * 0.7071067811865476))
        g_ref[part, :] = (inner * normal).astype(BF16)
        s_ref[part, :] = (normal + inner * (jnp.exp(-0.5 * inner * inner) * 0.3989422804014327)).astype(BF16)


def expert_back_kernel(dy_ref, s_ref, w1_ref, w2_ref, du_ref, dx_ref, acc):
    step = pl.program_id(0)
    rows = dy_ref.shape[0]
    chunk = 256
    for start in range(0, rows, chunk):
        part = slice(start, start + chunk)
        dg = dot_nt(dy_ref[part, :], w2_ref[0])
        du = (dg * s_ref[part, :].astype(F32)).astype(BF16)
        du_ref[part, :] = du
        term = dot_nt(du, w1_ref[0])

        @pl.when(step == 0)
        def _(part=part, term=term):
            acc[part, :] = term

        @pl.when(step > 0)
        def _(part=part, term=term):
            acc[part, :] += term

    @pl.when(step == pl.num_programs(0) - 1)
    def _():
        dx_ref[...] = acc[...].astype(BF16)


def expert_weight_kernel(x_ref, g_ref, du_ref, dy_ref, dw1_ref, dw2_ref, db1_ref, db2_ref):
    dw1_ref[...] = dot_tn(x_ref[...], du_ref[...]).astype(BF16)
    dw2_ref[...] = dot_tn(g_ref[...], dy_ref[...]).astype(BF16)
    db1_ref[...] = jnp.sum(du_ref[...].astype(F32), axis=0, keepdims=True)

    @pl.when(pl.program_id(0) == 0)
    def _():
        db2_ref[...] = jnp.sum(dy_ref[...].astype(F32), axis=0, keepdims=True)


def inner_specs(j, width, ff):
    return (
        pl.BlockSpec((1, width, FF_BLOCK), lambda f: (j, 0, f)),
        pl.BlockSpec((1, 1, FF_BLOCK), lambda f: (j, 0, f)),
        pl.BlockSpec((1, FF_BLOCK, width), lambda f: (j, f, 0)),
        pl.BlockSpec((1, 1, width), lambda f: (j, 0, 0)),
    )


def columns_of(rows, ff):
    return ((rows, ff), BF16, pl.BlockSpec((rows, FF_BLOCK), lambda f: (0, f)))


def expert_forward(x, expert, j):
    w1, b1, w2, b2 = expert
    rows, width = x.shape
    ff = w1.shape[2]
    i1, i2, i3, i4 = inner_specs(j, width, ff)
    return call(
        expert_kernel, (ff // FF_BLOCK,),
        [(x, whole(x)), (w1, i1), (b1, i2), (w2, i3), (b2, i4)],
        [((rows, width), BF16, pl.BlockSpec((rows, width), lambda f: (0, 0)))],
        [pltpu.VMEM((rows, width), F32)],
        flops=4 * rows * width * ff,
    )[0]


def expert_slopes(x, expert, j):
    w1, b1, w2, b2 = expert
    rows, width = x.shape
    ff = w1.shape[2]
    i1, i2, _, _ = inner_specs(j, width, ff)
    return call(
        slope_kernel, (ff // FF_BLOCK,), [(x, whole(x)), (w1, i1), (b1, i2)],
        [columns_of(rows, ff), columns_of(rows, ff)],
        flops=2 * rows * width * ff,
    )


def expert_backward(dy, slopes, expert, j):
    w1, b1, w2, b2 = expert
    rows, width = dy.shape
    ff = w1.shape[2]
    i1, _, i3, _ = inner_specs(j, width, ff)
    by_columns = pl.BlockSpec((rows, FF_BLOCK), lambda f: (0, f))
    return call(
        expert_back_kernel, (ff // FF_BLOCK,),
        [(dy, whole(dy)), (slopes, by_columns), (w1, i1), (w2, i3)],
        [columns_of(rows, ff), ((rows, width), BF16, pl.BlockSpec((rows, width), lambda f: (0, 0)))],
        [pltpu.VMEM((rows, width), F32)],
        flops=4 * rows * width * ff,
    )


def expert_weight_grads(x, g, du, dy):
    rows, width = x.shape
    ff = g.shape[1]
    by_columns = pl.BlockSpec((rows, FF_BLOCK), lambda f: (0, f))
    return call(
        expert_weight_kernel, (ff // FF_BLOCK,),
        [(x, whole(x)), (g, by_columns), (du, by_columns), (dy, whole(dy))],
        [
            ((width, ff), BF16, pl.BlockSpec((width, FF_BLOCK), lambda f: (0, f))),
            ((ff, width), BF16, pl.BlockSpec((FF_BLOCK, width), lambda f: (f, 0))),
            ((1, ff), F32, pl.BlockSpec((1, FF_BLOCK), lambda f: (0, f))),
            ((1, width), F32, pl.BlockSpec((1, width), lambda f: (0, 0))),
        ],
        flops=4 * rows * width * ff,
    )


def destinations(routes, experts_all, owners):
    layers, images, length, _ = routes.shape
    tokens = images * length
    pairs = routes.reshape(layers, tokens, 2)
    hot = (pairs[..., None] == jnp.arange(experts_all, dtype=jnp.int32)).astype(F32)
    counts = (hot[:, :, 0] + hot[:, :, 1]).astype(BF16)
    earlier = (jnp.arange(tokens)[:, None] > jnp.arange(tokens)[None, :]).astype(BF16)
    before = jnp.einsum("ts,lse->lte", earlier, counts, preferred_element_type=F32)
    slot = jnp.sum(before[:, :, None, :] * hot, axis=-1).astype(jnp.int32)
    capacity = (10 * tokens // (4 * experts_all) + 7) // 8 * 8
    local = experts_all // owners
    row = ((pairs % local) * owners + pairs // local) * capacity + slot
    dest = jnp.where(slot < capacity, row, -1)
    return dest.reshape(layers, images, length, 2), capacity


def exchange(array):
    owners = lax.axis_size("expert")
    rows, width = array.shape
    swapped = lax.all_to_all(
        array.reshape(owners, rows // owners, width), "expert", split_axis=0, concat_axis=0, tiled=True
    )
    return swapped.reshape(rows, width)


def shards(
    images, cotangent, routes, query_weight, key_weight, value_weight, output_weight, router_weight, query_bias,
    value_bias, output_bias, attend_gain, attend_shift, expert_gain, expert_shift, inner_weight, inner_bias,
    outer_weight, outer_bias,
):
    count, length, width = images.shape
    parts = lax.axis_size("dp")
    owners = lax.axis_size("expert")
    experts_all = router_weight.shape[2]
    local = inner_weight.shape[1]
    ff = inner_weight.shape[3]
    share = width // parts
    tokens = count * length
    squares = (query_weight, key_weight, value_weight, output_weight)
    vectors = (query_bias, value_bias, output_bias, attend_gain, attend_shift, expert_gain, expert_shift)
    bias_columns = ff // width + 1

    biases = jnp.concatenate(
        [inner_bias.reshape(LAYERS, local, ff // width, share), outer_bias.reshape(LAYERS, local, 1, share)], axis=2
    )
    biases = biases.reshape(LAYERS * local * bias_columns, share).T

    packed = []
    for layer in range(LAYERS):
        misc = [router_weight[layer], jnp.zeros((share, VEC_AT - experts_all), F32)]
        misc += [jnp.stack([v[layer] for v in vectors], axis=1), jnp.zeros((share, BIAS_AT - VEC_AT - 7), F32)]
        if layer == 0:
            misc += [biases, jnp.zeros((share, MISC - BIAS_AT - biases.shape[1]), F32)]
        else:
            misc += [jnp.zeros((share, MISC - BIAS_AT), F32)]
        mine = jnp.concatenate([s[layer] for s in squares] + misc, axis=1).astype(BF16)
        packed.append(lax.all_gather(mine, "dp", axis=0, tiled=True))
    spare = packed[0][:, 4 * width + BIAS_AT : 4 * width + BIAS_AT + biases.shape[1]].astype(F32)
    spare = spare.reshape(parts, share, LAYERS, local, bias_columns)
    inner_biases = jnp.transpose(spare[..., :-1], (2, 3, 0, 4, 1)).reshape(LAYERS, local, 1, ff)
    outer_biases = jnp.transpose(spare[..., -1:], (2, 3, 4, 0, 1)).reshape(LAYERS, local, 1, width)
    experts = []
    for layer in range(LAYERS):
        experts.append((
            lax.all_gather(inner_weight[layer].astype(BF16), "dp", axis=1, tiled=True),
            inner_biases[layer],
            lax.all_gather(outer_weight[layer].astype(BF16), "dp", axis=1, tiled=True),
            outer_biases[layer],
        ))

    dcol, capacity = destinations(routes, experts_all, owners)
    drow = jnp.transpose(dcol, (0, 1, 3, 2))
    half = owners * capacity
    dense_flops = 8 * tokens * width * width + 4 * tokens * half * width

    saved = []
    back = None
    rows = images
    for layer in range(LAYERS):
        weights = [(packed[layer], s) for s in packed_specs(packed[layer])]
        routing = [(routes[layer], per_image(routes[layer])), (drow[layer], per_image(drow[layer]))]
        outputs = attend_outputs(count, length, width, half)
        if layer == 0:
            done = call(
                first_kernel, (count,), [(rows, per_image(rows))] + routing + weights, outputs, flops=dense_flops
            )
            picked = None
        else:
            before = saved[-1]
            done = call(
                next_kernel, (count,),
                [
                    (before["middle"], per_image(before["middle"])),
                    (before["gates"], per_image(before["gates"])),
                    (dcol[layer - 1], per_image(dcol[layer - 1])),
                    (back[0], whole(back[0])),
                    (back[1], whole(back[1])),
                ] + routing + weights,
                [
                    images_out(count, length, width, F32),
                    images_out(count, length, width, BF16),
                    images_out(count, length, width, BF16),
                ] + outputs,
                flops=dense_flops,
            )
            rows, *picked = done[:3]
            done = done[3:]
            before["picked"] = picked
        middle, queries, keys, values, context, sums, gates = done[:7]
        arrived = [exchange(item) for item in done[7:]]
        produced = [expert_forward(arrived[j], experts[layer], j) for j in range(local)]
        back = [exchange(item) for item in produced]
        slopes = [expert_slopes(arrived[j], experts[layer], j) for j in range(local)]
        saved.append({
            "rows": rows, "middle": middle, "attend": (queries, keys, values, context, sums), "gates": gates,
            "arrived": arrived, "slopes": slopes,
        })

    last = saved[-1]
    result, dz, *sent = call(
        turn_kernel, (count,),
        [(last["middle"], per_image(last["middle"])), (last["gates"], per_image(last["gates"]))]
        + [(dcol[-1], per_image(dcol[-1])), (back[0], whole(back[0])), (back[1], whole(back[1]))]
        + [(cotangent, per_image(cotangent)), (routes[-1], per_image(routes[-1])), (drow[-1], per_image(drow[-1]))],
        [images_out(count, length, width, F32), images_out(count, length, MISC, BF16)] + slots_out(half, width),
        flops=dense_flops,
    )
    upstream = cotangent
    dense_grads = [None] * LAYERS
    bias_grads = [None] * LAYERS
    inner_grads = [None] * LAYERS
    outer_grads = [None] * LAYERS
    for layer in reversed(range(LAYERS)):
        kept = saved[layer]
        dys = [exchange(item) for item in sent]
        dus, dxs = [], []
        for j in range(local):
            du, dx = expert_backward(dys[j], kept["slopes"][j][1], experts[layer], j)
            dus.append(du)
            dxs.append(dx)
        came = [exchange(item) for item in dxs]
        grads = [
            expert_weight_grads(kept["arrived"][j], kept["slopes"][j][0], dus[j], dys[j]) for j in range(local)
        ]
        inner_grads[layer] = [lax.psum_scatter(g[0], "dp", scatter_dimension=0, tiled=True) for g in grads]
        outer_grads[layer] = [lax.psum_scatter(g[1], "dp", scatter_dimension=0, tiled=True) for g in grads]
        bias_grads[layer] = [
            jnp.concatenate([g[2].reshape(parts, ff // parts), g[3].reshape(parts, share)], axis=1) for g in grads
        ]
        weights = [(packed[layer], s) for s in packed_specs(packed[layer])]
        inputs = [upstream, kept["rows"], kept["middle"], *kept["attend"], dz, dcol[layer]]
        inputs = [(a, per_image(a)) for a in inputs] + [(a, whole(a)) for a in came] + weights
        outputs = [
            images_out(count, length, width, F32),
            (
                (width, 4 * width + MISC), F32,
                pl.BlockSpec((width, 4 * width + MISC), lambda i: (0, 0)),
            ),
        ]
        if layer > 0:
            below = saved[layer - 1]
            extra = [*below["picked"], below["gates"], routes[layer - 1], drow[layer - 1]]
            inputs += [(a, per_image(a)) for a in extra]
            outputs += [images_out(count, length, MISC, BF16)] + slots_out(half, width)
        done = call(
            back_kernel, (count,), inputs, outputs, [pltpu.VMEM((MISC, width), F32)], flops=3 * dense_flops
        )
        upstream, wgrad = done[:2]
        if layer > 0:
            dz, *sent = done[2:]
        mine = lax.psum_scatter(wgrad, "dp", scatter_dimension=0, tiled=True)
        dense_grads[layer] = lax.psum(mine, "expert")

    small = jnp.stack([jnp.stack(b, axis=1) for b in bias_grads], axis=1)
    small = lax.psum_scatter(small, "dp", scatter_dimension=0, tiled=False)
    inner_bias_grad = small[:, :, : ff // parts]
    outer_bias_grad = small[:, :, ff // parts :]
    both = jnp.stack(dense_grads)
    square_grads = [both[:, :, n * width : (n + 1) * width] for n in range(4)]
    tail = both[:, :, 4 * width :]
    return (
        rows_out(result, images),
        upstream,
        *square_grads,
        tail[:, :, :experts_all],
        *[tail[:, :, VEC_AT + n] for n in range(7)],
        jnp.stack([jnp.stack(g) for g in inner_grads]).astype(F32),
        inner_bias_grad,
        jnp.stack([jnp.stack(g) for g in outer_grads]).astype(F32),
        outer_bias_grad,
    )


def rows_out(result, images):
    return result.reshape(images.shape)


def solution(mesh):
    both = P(("dp", "expert"), None, None)
    square = P(None, "dp", None)
    vector = P(None, "dp")
    matrix = P(None, "expert", "dp", None)
    bias = P(None, "expert", "dp")
    grads = (square,) * 5 + (vector,) * 7 + (matrix, bias, matrix, bias)
    return jax.shard_map(
        shards,
        mesh=mesh,
        in_specs=(both, both, P(None, ("dp", "expert"), None, None)) + grads,
        out_specs=(both, both) + grads,
        check_vma=False,
    )
```

```python
import functools

import jax
import jax.numpy as jnp
from jax import lax
from jax.experimental import pallas as pl
from jax.experimental.pallas import tpu as pltpu
from jax.sharding import PartitionSpec as P

HEADS = 8
HEAD_DIM = 64
LAYERS = 2
EPSILON = 1e-06
FACTOR = HEAD_DIM**-0.5
VEC_AT = 64
BIAS_AT = 72
MISC = 128
FF_BLOCK = 512
VMEM = 56 * 1024 * 1024

F32 = jnp.float32
BF16 = jnp.bfloat16


def dot(a, b):
    return jnp.dot(a, b, preferred_element_type=F32)


def dot_nt(a, b):
    return lax.dot_general(a, b, (((1,), (1,)), ((), ())), preferred_element_type=F32)


def dot_tn(a, b):
    return lax.dot_general(a, b, (((0,), (0,)), ((), ())), preferred_element_type=F32)


def standardize(rows):
    mean_value = jnp.mean(rows, axis=-1, keepdims=True)
    centered = rows - mean_value
    variance = jnp.mean(centered * centered, axis=-1, keepdims=True)
    scale = lax.rsqrt(variance + EPSILON)
    return centered * scale, scale


def standardize_back(upstream, unit, scale, gain):
    along = upstream * gain
    inner = (
        along
        - jnp.mean(along, axis=-1, keepdims=True)
        - unit * jnp.mean(along * unit, axis=-1, keepdims=True)
    )
    return inner * scale


def vectors_of(misc_ref):
    turned = misc_ref[...].astype(F32).T
    return [turned[VEC_AT + n : VEC_AT + n + 1, :] for n in range(7)]


def pick(dest, buffers):
    total = None
    for number, buffer in enumerate(buffers):
        count = buffer.shape[0]
        lanes = lax.broadcasted_iota(jnp.int32, (dest.shape[0], count), 1)
        chosen = (dest - number * count == lanes).astype(F32).astype(BF16)
        part = dot(chosen, buffer[...])
        total = part if total is None else total + part
    return total


def spread(dest_rows, sources, outs, first):
    half = outs[0].shape[0]
    step = 256
    length = dest_rows[0].shape[1]
    for number, out in enumerate(outs):
        for start in range(0, half, step):
            slots = lax.broadcasted_iota(jnp.int32, (step, length), 0) + (number * half + start)
            if len(sources) == 1:
                hit = (slots == dest_rows[0]) | (slots == dest_rows[1])
                block = dot(hit.astype(F32).astype(BF16), sources[0])
            else:
                block = dot((slots == dest_rows[0]).astype(F32).astype(BF16), sources[0])
                block = block + dot((slots == dest_rows[1]).astype(F32).astype(BF16), sources[1])
            block = block.astype(BF16)

            @pl.when(first)
            def _(out=out, start=start, block=block):
                out[start : start + step, :] = block

            @pl.when(jnp.logical_not(first))
            def _(out=out, start=start, block=block):
                out[start : start + step, :] += block


def lane_masks(length):
    lanes = lax.broadcasted_iota(jnp.int32, (length, 2 * HEAD_DIM), 1)
    return (lanes < HEAD_DIM).astype(F32).astype(BF16), (lanes >= HEAD_DIM).astype(F32).astype(BF16)


def attend_body(
    rows, routes_ref, drow_ref, wq, wk, wv, wo, misc,
    t_ref, q_ref, k_ref, v_ref, o_ref, lse_ref, gates_ref, outs,
):
    length = rows.shape[0]
    qb, vb, ob, again, ashift, egain, eshift = vectors_of(misc)
    unit, _ = standardize(rows)
    low = (unit * again + ashift).astype(BF16)
    queries = (dot(low, wq[...]) + qb).astype(BF16)
    keys = dot(low, wk[...]).astype(BF16)
    values = (dot(low, wv[...]) + vb).astype(BF16)
    q_ref[0] = queries
    k_ref[0] = keys
    v_ref[0] = values
    masks = lane_masks(length)
    lanes = lax.broadcasted_iota(jnp.int32, (length, MISC), 1)
    first_half = lax.broadcasted_iota(jnp.int32, (length, 2 * HEAD_DIM), 1) < HEAD_DIM
    sums = jnp.zeros((length, MISC), F32)
    for pair in range(HEADS // 2):
        cols = slice(pair * 2 * HEAD_DIM, (pair + 1) * 2 * HEAD_DIM)
        mixed = []
        for side in range(2):
            scores = dot_nt(queries[:, cols] * (masks[side] * FACTOR), keys[:, cols])
            highest = jnp.max(scores, axis=-1, keepdims=True)
            expo = jnp.exp(scores - highest)
            total = jnp.sum(expo, axis=-1, keepdims=True)
            attention = (expo * (1.0 / total)).astype(BF16)
            sums = jnp.where(lanes == 2 * pair + side, highest + jnp.log(total), sums)
            mixed.append(dot(attention, values[:, cols]))
        o_ref[0, :, cols] = jnp.where(first_half, mixed[0], mixed[1]).astype(BF16)
    lse_ref[0] = sums
    middle = rows + (dot(o_ref[0], wo[...]) + ob)
    t_ref[0] = middle
    unit_two, _ = standardize(middle)
    hidden = (unit_two * egain + eshift).astype(BF16)
    logits = dot(hidden, misc[...])
    pair_experts = routes_ref[0]
    zero = jnp.sum(jnp.where(lanes == pair_experts[:, 0:1], logits, 0.0), axis=-1, keepdims=True)
    one = jnp.sum(jnp.where(lanes == pair_experts[:, 1:2], logits, 0.0), axis=-1, keepdims=True)
    gate_zero = 1.0 / (1.0 + jnp.exp(one - zero))
    gate_one = 1.0 / (1.0 + jnp.exp(zero - one))
    gates_ref[0, :, 0:1] = gate_zero
    gates_ref[0, :, 1:2] = gate_one
    drow = drow_ref[0]
    spread([drow[0:1, :], drow[1:2, :]], [hidden], outs, pl.program_id(0) == 0)


def combine_body(middle, gates_ref, dcol_ref, back, yzero_ref, yone_ref):
    dest = dcol_ref[0]
    gates = gates_ref[0]
    zero = pick(dest[:, 0:1], back)
    one = pick(dest[:, 1:2], back)
    if yzero_ref is not None:
        yzero_ref[0] = zero.astype(BF16)
        yone_ref[0] = one.astype(BF16)
    return middle + (gates[:, 0:1] * zero + gates[:, 1:2] * one), zero, one


def grads_body(upstream, zero, one, gates_ref, routes_ref, drow_ref, dz_ref, outs):
    length = upstream.shape[0]
    gates = gates_ref[0]
    gate_zero, gate_one = gates[:, 0:1], gates[:, 1:2]
    grad_zero = jnp.sum(zero * upstream, axis=-1, keepdims=True)
    grad_one = jnp.sum(one * upstream, axis=-1, keepdims=True)
    along = gate_zero * grad_zero + gate_one * grad_one
    lanes = lax.broadcasted_iota(jnp.int32, (length, MISC), 1)
    pair_experts = routes_ref[0]
    dz = jnp.where(lanes == pair_experts[:, 0:1], gate_zero * (grad_zero - along), 0.0)
    dz = dz + jnp.where(lanes == pair_experts[:, 1:2], gate_one * (grad_one - along), 0.0)
    dz_ref[0] = dz.astype(BF16)
    drow = drow_ref[0]
    spread(
        [drow[0:1, :], drow[1:2, :]],
        [(gate_zero * upstream).astype(BF16), (gate_one * upstream).astype(BF16)],
        outs,
        pl.program_id(0) == 0,
    )


def first_kernel(rows, routes, drow, wq, wk, wv, wo, misc, *outs):
    attend_body(rows[0], routes, drow, wq, wk, wv, wo, misc, *outs[:7], outs[7:])


def next_kernel(
    middle, gates, dcol, back_a, back_b, routes, drow, wq, wk, wv, wo, misc, rows_ref, yzero, yone, *outs
):
    rows, _, _ = combine_body(middle[0], gates, dcol, (back_a, back_b), yzero, yone)
    rows_ref[0] = rows
    attend_body(rows, routes, drow, wq, wk, wv, wo, misc, *outs[:7], outs[7:])


def turn_kernel(middle, gates, dcol, back_a, back_b, cotangent, routes, drow, result, dz, out_a, out_b):
    rows, zero, one = combine_body(middle[0], gates, dcol, (back_a, back_b), None, None)
    result[0] = rows
    grads_body(cotangent[0], zero, one, gates, routes, drow, dz, (out_a, out_b))


def back_kernel(
    upstream, rows, middle, q_ref, k_ref, v_ref, o_ref, lse_ref, dz_ref, dcol, came_a, came_b,
    wq, wk, wv, wo, misc, *rest,
):
    bias, *rest = rest
    if len(rest) > 4:
        yzero, yone, gates_below, routes_below, drow_below, grad_ref, sent, dz_below, out_a, out_b, wgrad, vgrad = rest
    else:
        grad_ref, sent, wgrad, vgrad = rest
    first = pl.program_id(0) == 0
    length = rows.shape[1]
    width = rows.shape[2]
    qb, vb, ob, again, ashift, egain, eshift = vectors_of(misc)

    @pl.when(first)
    def _():
        wgrad[...] = jnp.zeros_like(wgrad)
        vgrad[...] = jnp.zeros_like(vgrad)

    def add_vector(number, value):
        vgrad[VEC_AT + number : VEC_AT + number + 1, :] += jnp.sum(value, axis=0, keepdims=True)

    unit_two, scale_two = standardize(middle[0])
    hidden = (unit_two * egain + eshift).astype(BF16)
    dz = dz_ref[0]
    dest = dcol[0]
    dhidden = dot_nt(dz, misc[...])
    for number, came in enumerate((came_a, came_b)):
        count = came.shape[0]
        lanes = lax.broadcasted_iota(jnp.int32, (length, count), 1) + number * count
        hit = (dest[:, 0:1] == lanes) | (dest[:, 1:2] == lanes)
        dhidden = dhidden + dot(hit.astype(F32).astype(BF16), came[...])
    wgrad[:, 4 * width :] += dot_tn(hidden, dz)
    add_vector(5, dhidden * unit_two)
    add_vector(6, dhidden)
    dmiddle = upstream[0] + standardize_back(dhidden, unit_two, scale_two, egain)
    dbranch = dmiddle.astype(BF16)
    wgrad[:, 3 * width : 4 * width] += dot_tn(o_ref[0], dbranch)
    add_vector(2, dbranch.astype(F32))
    dcontext = dot_nt(dbranch, wo[...]).astype(BF16)
    masks = lane_masks(length)
    first_half = lax.broadcasted_iota(jnp.int32, (length, 2 * HEAD_DIM), 1) < HEAD_DIM
    dqs, dks, dvs = [], [], []
    for pair in range(HEADS // 2):
        cols = slice(pair * 2 * HEAD_DIM, (pair + 1) * 2 * HEAD_DIM)
        keys = k_ref[0, :, cols]
        values = v_ref[0, :, cols]
        queries = q_ref[0, :, cols]
        dvalues, dqueries, dkeys = None, [], None
        for side in range(2):
            own_queries = queries * (masks[side] * FACTOR)
            own_context = dcontext[:, cols] * masks[side]
            scores = dot_nt(own_queries, keys)
            number = 2 * pair + side
            attention = jnp.exp(scores - lse_ref[0, :, number : number + 1])
            prob = dot_nt(own_context, values)
            weighed = attention * prob
            delta = jnp.sum(weighed, axis=-1, keepdims=True)
            dscores = (weighed - attention * delta).astype(BF16)
            dvalue = dot_tn(attention.astype(BF16), own_context)
            dkey = dot_tn(dscores, own_queries)
            dvalues = dvalue if dvalues is None else dvalues + dvalue
            dkeys = dkey if dkeys is None else dkeys + dkey
            dqueries.append(dot(dscores, keys))
        dqs.append((jnp.where(first_half, dqueries[0], dqueries[1]) * FACTOR).astype(BF16))
        dks.append(dkeys.astype(BF16))
        dvs.append(dvalues.astype(BF16))
    dq = jnp.concatenate(dqs, axis=1)
    dk = jnp.concatenate(dks, axis=1)
    dv = jnp.concatenate(dvs, axis=1)
    unit, scale = standardize(rows[0])
    low = (unit * again + ashift).astype(BF16)
    wgrad[:, 0:width] += dot_tn(low, dq)
    wgrad[:, width : 2 * width] += dot_tn(low, dk)
    wgrad[:, 2 * width : 3 * width] += dot_tn(low, dv)
    add_vector(0, dq.astype(F32))
    add_vector(1, dv.astype(F32))
    dlow = dot_nt(dq, wq[...]) + dot_nt(dk, wk[...]) + dot_nt(dv, wv[...])
    add_vector(3, dlow * unit)
    add_vector(4, dlow)
    grad = dmiddle + standardize_back(dlow, unit, scale, again)
    grad_ref[0] = grad
    if len(rest) > 4:
        grads_body(
            grad, yzero[0].astype(F32), yone[0].astype(F32), gates_below, routes_below, drow_below, dz_below,
            (out_a, out_b),
        )

    @pl.when(pl.program_id(0) == pl.num_programs(0) - 1)
    def _():
        wgrad[:, 4 * width :] += vgrad[...].T
        sent[:, : 4 * width + MISC] = wgrad[...].astype(BF16)
        sent[:, 4 * width + MISC :] = bias[...]


def per_image(array):
    return pl.BlockSpec((1,) + array.shape[1:], lambda i: (i,) + (0,) * (len(array.shape) - 1))


def whole(array):
    return pl.BlockSpec(array.shape, lambda i: (0,) * len(array.shape))


def packed_specs(packed):
    width = packed.shape[0]
    specs = [pl.BlockSpec((width, width), lambda i, n=n: (0, n)) for n in range(4)]
    return specs + [pl.BlockSpec((width, MISC), lambda i: (0, 4 * width // MISC))]


def call(body, grid, inputs, outputs, scratch=(), flops=0, aliases=None):
    moved = sum(a.size * a.dtype.itemsize for a, _ in inputs)
    shapes = [jax.ShapeDtypeStruct(s, t) for s, t, _ in outputs]
    moved += sum(s.size * s.dtype.itemsize for s in shapes)
    return pl.pallas_call(
        body,
        grid=grid,
        in_specs=[s for _, s in inputs],
        out_specs=[s for _, _, s in outputs],
        out_shape=shapes,
        scratch_shapes=list(scratch),
        compiler_params=pltpu.CompilerParams(vmem_limit_bytes=VMEM),
        cost_estimate=pl.CostEstimate(flops=flops, bytes_accessed=moved, transcendentals=0),
    )(*[a for a, _ in inputs])


def images_out(images, length, columns, kind):
    shape = (images, length, columns)
    return (shape, kind, pl.BlockSpec((1, length, columns), lambda i: (i, 0, 0)))


def slots_out(half, width):
    return [((half, width), BF16, pl.BlockSpec((half, width), lambda i: (0, 0)))] * 2


def attend_outputs(images, length, width, half):
    return [
        images_out(images, length, width, F32),
        images_out(images, length, width, BF16),
        images_out(images, length, width, BF16),
        images_out(images, length, width, BF16),
        images_out(images, length, width, BF16),
        images_out(images, length, MISC, F32),
        images_out(images, length, 2, F32),
    ] + slots_out(half, width)


def gelu(value):
    return 0.5 * value * (1.0 + lax.erf(value * 0.7071067811865476))


def block_of(ref):
    return ref[...].reshape(-1, ref.shape[-1])


def expert_kernel(x_ref, w1_ref, b1_ref, w2_ref, b2_ref, y_ref, acc):
    step = pl.program_id(0)
    w1, w2 = block_of(w1_ref), block_of(w2_ref)
    rows = x_ref.shape[0]
    chunk = 256
    for start in range(0, rows, chunk):
        part = slice(start, start + chunk)
        inner = dot(x_ref[part, :], w1) + b1_ref[0]
        term = dot(gelu(inner).astype(BF16), w2)

        @pl.when(step == 0)
        def _(part=part, term=term):
            acc[part, :] = term + b2_ref[0]

        @pl.when(step > 0)
        def _(part=part, term=term):
            acc[part, :] += term

    @pl.when(step == pl.num_programs(0) - 1)
    def _():
        y_ref[...] = acc[...].astype(BF16)


def slope_kernel(x_ref, w1_ref, b1_ref, g_ref, s_ref):
    rows = x_ref.shape[0]
    w1 = block_of(w1_ref)
    chunk = 256
    for start in range(0, rows, chunk):
        part = slice(start, start + chunk)
        inner = dot(x_ref[part, :], w1) + b1_ref[0]
        normal = 0.5 * (1.0 + lax.erf(inner * 0.7071067811865476))
        g_ref[part, :] = (inner * normal).astype(BF16)
        s_ref[part, :] = (normal + inner * (jnp.exp(-0.5 * inner * inner) * 0.3989422804014327)).astype(BF16)


def expert_back_kernel(dy_ref, s_ref, w1_ref, w2_ref, du_ref, dx_ref, acc):
    step = pl.program_id(0)
    w1, w2 = block_of(w1_ref), block_of(w2_ref)
    rows = dy_ref.shape[0]
    chunk = 256
    for start in range(0, rows, chunk):
        part = slice(start, start + chunk)
        dg = dot_nt(dy_ref[part, :], w2)
        du = (dg * s_ref[part, :].astype(F32)).astype(BF16)
        du_ref[part, :] = du
        term = dot_nt(du, w1)

        @pl.when(step == 0)
        def _(part=part, term=term):
            acc[part, :] = term

        @pl.when(step > 0)
        def _(part=part, term=term):
            acc[part, :] += term

    @pl.when(step == pl.num_programs(0) - 1)
    def _():
        dx_ref[...] = acc[...].astype(BF16)


def expert_weight_kernel(x_ref, g_ref, du_ref, dy_ref, out_ref, db1_ref, db2_ref):
    step = pl.program_id(0)
    parts, rows, _ = out_ref.shape
    width = x_ref.shape[1]
    share = width // parts
    dw1 = dot_tn(x_ref[...], du_ref[...]).astype(BF16)
    place = pl.ds(pl.multiple_of(step * share, share), share)
    for part in range(parts):
        out_ref[part, place, :] = dw1[part * share : (part + 1) * share, :]
    dw2 = dot_tn(g_ref[...], dy_ref[...]).astype(BF16)
    take = rows // 2
    each = FF_BLOCK // take
    for part in range(each):
        out_ref[step * each + part, take:, :] = dw2[part * take : (part + 1) * take, :]
    db1_ref[...] = jnp.sum(du_ref[...].astype(F32), axis=0, keepdims=True)

    @pl.when(step == 0)
    def _():
        db2_ref[...] = jnp.sum(dy_ref[...].astype(F32), axis=0, keepdims=True)


def inner_specs(packed, j):
    parts, _, rows, width = packed.shape
    share, take = width // parts, rows // 2
    return (
        pl.BlockSpec((parts, 1, share, width), lambda f: (0, j, f, 0)),
        pl.BlockSpec((1, 1, FF_BLOCK), lambda f: (j, 0, f)),
        pl.BlockSpec((FF_BLOCK // take, 1, take, width), lambda f: (f, j, 1, 0)),
        pl.BlockSpec((1, 1, width), lambda f: (j, 0, 0)),
    )


def columns_of(rows, ff):
    return ((rows, ff), BF16, pl.BlockSpec((rows, FF_BLOCK), lambda f: (0, f)))


def expert_forward(x, expert, j):
    packed, b1, b2 = expert
    rows, width = x.shape
    ff = b1.shape[2]
    i1, i2, i3, i4 = inner_specs(packed, j)
    return call(
        expert_kernel, (ff // FF_BLOCK,),
        [(x, whole(x)), (packed, i1), (b1, i2), (packed, i3), (b2, i4)],
        [((rows, width), BF16, pl.BlockSpec((rows, width), lambda f: (0, 0)))],
        [pltpu.VMEM((rows, width), F32)],
        flops=4 * rows * width * ff,
    )[0]


def expert_slopes(x, expert, j):
    packed, b1, b2 = expert
    rows, width = x.shape
    ff = b1.shape[2]
    i1, i2, _, _ = inner_specs(packed, j)
    return call(
        slope_kernel, (ff // FF_BLOCK,), [(x, whole(x)), (packed, i1), (b1, i2)],
        [columns_of(rows, ff), columns_of(rows, ff)],
        flops=2 * rows * width * ff,
    )


def expert_backward(dy, slopes, expert, j):
    packed, b1, b2 = expert
    rows, width = dy.shape
    ff = b1.shape[2]
    i1, _, i3, _ = inner_specs(packed, j)
    by_columns = pl.BlockSpec((rows, FF_BLOCK), lambda f: (0, f))
    return call(
        expert_back_kernel, (ff // FF_BLOCK,),
        [(dy, whole(dy)), (slopes, by_columns), (packed, i1), (packed, i3)],
        [columns_of(rows, ff), ((rows, width), BF16, pl.BlockSpec((rows, width), lambda f: (0, 0)))],
        [pltpu.VMEM((rows, width), F32)],
        flops=4 * rows * width * ff,
    )


def expert_weight_grads(x, g, du, dy, parts):
    rows, width = x.shape
    ff = g.shape[1]
    by_columns = pl.BlockSpec((rows, FF_BLOCK), lambda f: (0, f))
    packed = (parts, 2 * ff // parts, width)
    return call(
        expert_weight_kernel, (ff // FF_BLOCK,),
        [(x, whole(x)), (g, by_columns), (du, by_columns), (dy, whole(dy))],
        [
            (packed, BF16, pl.BlockSpec(packed, lambda f: (0, 0, 0))),
            ((1, ff), F32, pl.BlockSpec((1, FF_BLOCK), lambda f: (0, f))),
            ((1, width), F32, pl.BlockSpec((1, width), lambda f: (0, 0))),
        ],
        flops=4 * rows * width * ff,
    )


def destinations(routes, experts_all, owners):
    layers, images, length, _ = routes.shape
    tokens = images * length
    pairs = routes.reshape(layers, tokens, 2)
    hot = (pairs[..., None] == jnp.arange(experts_all, dtype=jnp.int32)).astype(F32)
    counts = (hot[:, :, 0] + hot[:, :, 1]).astype(BF16)
    earlier = (jnp.arange(tokens)[:, None] > jnp.arange(tokens)[None, :]).astype(BF16)
    before = jnp.einsum("ts,lse->lte", earlier, counts, preferred_element_type=F32)
    slot = jnp.sum(before[:, :, None, :] * hot, axis=-1).astype(jnp.int32)
    capacity = (10 * tokens // (4 * experts_all) + 7) // 8 * 8
    local = experts_all // owners
    row = ((pairs % local) * owners + pairs // local) * capacity + slot
    dest = jnp.where(slot < capacity, row, -1)
    return dest.reshape(layers, images, length, 2), capacity


def exchange(array):
    owners = lax.axis_size("expert")
    rows, width = array.shape
    swapped = lax.all_to_all(
        array.reshape(owners, rows // owners, width), "expert", split_axis=0, concat_axis=0, tiled=True
    )
    return swapped.reshape(rows, width)


def shards(
    images, cotangent, routes, query_weight, key_weight, value_weight, output_weight, router_weight, query_bias,
    value_bias, output_bias, attend_gain, attend_shift, expert_gain, expert_shift, inner_weight, inner_bias,
    outer_weight, outer_bias,
):
    count, length, width = images.shape
    parts = lax.axis_size("dp")
    owners = lax.axis_size("expert")
    experts_all = router_weight.shape[2]
    local = inner_weight.shape[1]
    ff = inner_weight.shape[3]
    share = width // parts
    tokens = count * length
    squares = (query_weight, key_weight, value_weight, output_weight)
    vectors = (query_bias, value_bias, output_bias, attend_gain, attend_shift, expert_gain, expert_shift)
    bias_columns = ff // width + 1
    bias_room = -(-experts_all * bias_columns // MISC) * MISC

    biases = jnp.concatenate(
        [inner_bias.reshape(LAYERS, local, share, ff // width), outer_bias.reshape(LAYERS, local, share, 1)], axis=3
    )
    biases = jnp.transpose(biases, (2, 0, 1, 3)).reshape(share, LAYERS * local * bias_columns)

    packed = []
    experts = []
    for layer in range(LAYERS):
        misc = [router_weight[layer], jnp.zeros((share, VEC_AT - experts_all), F32)]
        misc += [jnp.stack([v[layer] for v in vectors], axis=1), jnp.zeros((share, BIAS_AT - VEC_AT - 7), F32)]
        if layer == 0:
            misc += [biases, jnp.zeros((share, MISC - BIAS_AT - biases.shape[1]), F32)]
        else:
            misc += [jnp.zeros((share, MISC - BIAS_AT), F32)]
        mine = jnp.concatenate([s[layer] for s in squares] + misc, axis=1).astype(BF16)
        packed.append(lax.all_gather(mine, "dp", axis=0, tiled=True))
        mine = jnp.transpose(inner_weight[layer].reshape(local, share, ff // FF_BLOCK, FF_BLOCK), (0, 2, 1, 3))
        mine = jnp.concatenate([mine.reshape(local, ff // parts, width), outer_weight[layer]], axis=1).astype(BF16)
        experts.append(lax.all_gather(mine, "dp", axis=0, tiled=False))
    spare = packed[0][:, 4 * width + BIAS_AT : 4 * width + BIAS_AT + biases.shape[1]].astype(F32)
    spare = jnp.transpose(spare.reshape(width, LAYERS, local, bias_columns), (1, 2, 0, 3))
    inner_biases = spare[..., :-1].reshape(LAYERS, local, 1, ff)
    outer_biases = spare[..., -1].reshape(LAYERS, local, 1, width)
    experts = [(experts[n], inner_biases[n], outer_biases[n]) for n in range(LAYERS)]

    dcol, capacity = destinations(routes, experts_all, owners)
    drow = jnp.transpose(dcol, (0, 1, 3, 2))
    half = owners * capacity
    dense_flops = 8 * tokens * width * width + 4 * tokens * half * width

    saved = []
    back = None
    rows = images
    for layer in range(LAYERS):
        weights = [(packed[layer], s) for s in packed_specs(packed[layer])]
        routing = [(routes[layer], per_image(routes[layer])), (drow[layer], per_image(drow[layer]))]
        outputs = attend_outputs(count, length, width, half)
        if layer == 0:
            done = call(
                first_kernel, (count,), [(rows, per_image(rows))] + routing + weights, outputs, flops=dense_flops
            )
            picked = None
        else:
            before = saved[-1]
            done = call(
                next_kernel, (count,),
                [
                    (before["middle"], per_image(before["middle"])),
                    (before["gates"], per_image(before["gates"])),
                    (dcol[layer - 1], per_image(dcol[layer - 1])),
                    (back[0], whole(back[0])),
                    (back[1], whole(back[1])),
                ] + routing + weights,
                [
                    images_out(count, length, width, F32),
                    images_out(count, length, width, BF16),
                    images_out(count, length, width, BF16),
                ] + outputs,
                flops=dense_flops,
            )
            rows, *picked = done[:3]
            done = done[3:]
            before["picked"] = picked
        middle, queries, keys, values, context, sums, gates = done[:7]
        arrived = [exchange(item) for item in done[7:]]
        produced = [expert_forward(arrived[j], experts[layer], j) for j in range(local)]
        back = [exchange(item) for item in produced]
        slopes = [expert_slopes(arrived[j], experts[layer], j) for j in range(local)]
        back, slopes = lax.optimization_barrier((back, slopes))
        saved.append({
            "rows": rows, "middle": middle, "attend": (queries, keys, values, context, sums), "gates": gates,
            "arrived": arrived, "slopes": slopes,
        })

    last = saved[-1]
    result, dz, *sent = call(
        turn_kernel, (count,),
        [(last["middle"], per_image(last["middle"])), (last["gates"], per_image(last["gates"]))]
        + [(dcol[-1], per_image(dcol[-1])), (back[0], whole(back[0])), (back[1], whole(back[1]))]
        + [(cotangent, per_image(cotangent)), (routes[-1], per_image(routes[-1])), (drow[-1], per_image(drow[-1]))],
        [images_out(count, length, width, F32), images_out(count, length, MISC, BF16)] + slots_out(half, width),
        flops=dense_flops,
    )
    upstream = cotangent
    dense_grads = [None] * LAYERS
    finished = []
    waiting = []
    for layer in reversed(range(LAYERS)):
        kept = saved[layer]
        dys = [exchange(item) for item in sent]
        dxs, grads, came, reduced = [], [], [], []
        for j in range(local):
            dys[j], done = lax.optimization_barrier((dys[j], waiting[j : j + 1]))
            finished += done
            du, dx = expert_backward(dys[j], kept["slopes"][j][1], experts[layer], j)
            dxs.append(dx)
            grad = expert_weight_grads(kept["arrived"][j], kept["slopes"][j][0], du, dys[j], parts)
            grads.append(grad)
            reduced.append(lax.psum_scatter(grad[0], "dp", scatter_dimension=0, tiled=False))
            if j + 1 < local:
                dys[j + 1], grad = lax.optimization_barrier((dys[j + 1], grad))
                grads[j] = grad
        came = [exchange(item) for item in dxs]
        waiting = reduced
        own = [
            jnp.concatenate([g[1].reshape(width, ff // width), g[2].reshape(width, 1)], axis=1) for g in grads
        ]
        first_column = lax.axis_index("expert") * (local * bias_columns)
        bias = lax.dynamic_update_slice(
            jnp.zeros((width, bias_room), F32), jnp.concatenate(own, axis=1), (0, first_column)
        ).astype(BF16)
        came, bias = lax.optimization_barrier((came, bias))
        weights = [(packed[layer], s) for s in packed_specs(packed[layer])]
        inputs = [upstream, kept["rows"], kept["middle"], *kept["attend"], dz, dcol[layer]]
        inputs = [(a, per_image(a)) for a in inputs] + [(a, whole(a)) for a in came] + weights
        inputs += [(bias, whole(bias))]
        outputs = [
            images_out(count, length, width, F32),
            (
                (width, 4 * width + MISC + bias_room), BF16,
                pl.BlockSpec((width, 4 * width + MISC + bias_room), lambda i: (0, 0)),
            ),
        ]
        if layer > 0:
            below = saved[layer - 1]
            extra = [*below["picked"], below["gates"], routes[layer - 1], drow[layer - 1]]
            inputs += [(a, per_image(a)) for a in extra]
            outputs += [images_out(count, length, MISC, BF16)] + slots_out(half, width)
        done = call(
            back_kernel, (count,), inputs, outputs,
            [pltpu.VMEM((width, 4 * width + MISC), F32), pltpu.VMEM((MISC, width), F32)], flops=3 * dense_flops,
        )
        upstream, wgrad = done[:2]
        if layer > 0:
            dz, *sent = done[2:]
        mine = lax.psum_scatter(wgrad, "dp", scatter_dimension=0, tiled=True)
        dense_grads[layer] = lax.psum(mine, "expert")
    expert_grads = [waiting, finished]

    both = jnp.stack(dense_grads).astype(F32)
    square_grads = [both[:, :, n * width : (n + 1) * width] for n in range(4)]
    tail = both[:, :, 4 * width : 4 * width + MISC]
    own = lax.dynamic_slice_in_dim(
        both[:, :, 4 * width + MISC :], lax.axis_index("expert") * (local * bias_columns), local * bias_columns, 2
    )
    own = jnp.transpose(own.reshape(LAYERS, share, local, bias_columns), (0, 2, 1, 3))
    pieces = jnp.stack([jnp.stack(g) for g in expert_grads])
    inner_grad = pieces[:, :, : ff // parts].reshape(LAYERS, local, ff // FF_BLOCK, share, FF_BLOCK)
    inner_grad = jnp.transpose(inner_grad, (0, 1, 3, 2, 4)).reshape(inner_weight.shape)
    return (
        result,
        upstream,
        *square_grads,
        tail[:, :, :experts_all],
        *[tail[:, :, VEC_AT + n] for n in range(7)],
        inner_grad.astype(F32),
        own[..., :-1].reshape(LAYERS, local, ff // parts),
        pieces[:, :, ff // parts :].astype(F32),
        own[..., -1],
    )


def solution(mesh):
    both = P(("dp", "expert"), None, None)
    square = P(None, "dp", None)
    vector = P(None, "dp")
    matrix = P(None, "expert", "dp", None)
    bias = P(None, "expert", "dp")
    grads = (square,) * 5 + (vector,) * 7 + (matrix, bias, matrix, bias)
    return jax.shard_map(
        shards,
        mesh=mesh,
        in_specs=(both, both, P(None, ("dp", "expert"), None, None)) + grads,
        out_specs=(both, both) + grads,
        check_vma=False,
    )
```

```python
import functools

import jax
import jax.numpy as jnp
from jax import lax
from jax.experimental import pallas as pl
from jax.experimental.pallas import tpu as pltpu
from jax.sharding import PartitionSpec as P

HEADS = 8
HEAD_DIM = 64
LAYERS = 2
EPSILON = 1e-06
FACTOR = HEAD_DIM**-0.5
VEC_AT = 64
BIAS_AT = 72
MISC = 128
FF_BLOCK = 512
VMEM = 56 * 1024 * 1024

F32 = jnp.float32
BF16 = jnp.bfloat16


def dot(a, b):
    return jnp.dot(a, b, preferred_element_type=F32)


def dot_nt(a, b):
    return lax.dot_general(a, b, (((1,), (1,)), ((), ())), preferred_element_type=F32)


def dot_tn(a, b):
    return lax.dot_general(a, b, (((0,), (0,)), ((), ())), preferred_element_type=F32)


def standardize(rows):
    mean_value = jnp.mean(rows, axis=-1, keepdims=True)
    centered = rows - mean_value
    variance = jnp.mean(centered * centered, axis=-1, keepdims=True)
    scale = lax.rsqrt(variance + EPSILON)
    return centered * scale, scale


def standardize_back(upstream, unit, scale, gain):
    along = upstream * gain
    inner = (
        along
        - jnp.mean(along, axis=-1, keepdims=True)
        - unit * jnp.mean(along * unit, axis=-1, keepdims=True)
    )
    return inner * scale


def vectors_of(misc_ref):
    turned = misc_ref[...].astype(F32).T
    return [turned[VEC_AT + n : VEC_AT + n + 1, :] for n in range(7)]


def pick(dest, buffers):
    total = None
    for number, buffer in enumerate(buffers):
        count = buffer.shape[0]
        lanes = lax.broadcasted_iota(jnp.int32, (dest.shape[0], count), 1)
        chosen = (dest - number * count == lanes).astype(F32).astype(BF16)
        part = dot(chosen, buffer[...])
        total = part if total is None else total + part
    return total


def spread(dest_rows, sources, outs, first):
    half = outs[0].shape[0]
    step = 256
    length = dest_rows[0].shape[1]
    for number, out in enumerate(outs):
        for start in range(0, half, step):
            slots = lax.broadcasted_iota(jnp.int32, (step, length), 0) + (number * half + start)
            if len(sources) == 1:
                hit = (slots == dest_rows[0]) | (slots == dest_rows[1])
                block = dot(hit.astype(F32).astype(BF16), sources[0])
            else:
                block = dot((slots == dest_rows[0]).astype(F32).astype(BF16), sources[0])
                block = block + dot((slots == dest_rows[1]).astype(F32).astype(BF16), sources[1])
            block = block.astype(BF16)

            @pl.when(first)
            def _(out=out, start=start, block=block):
                out[start : start + step, :] = block

            @pl.when(jnp.logical_not(first))
            def _(out=out, start=start, block=block):
                out[start : start + step, :] += block


def lane_masks(length):
    lanes = lax.broadcasted_iota(jnp.int32, (length, 2 * HEAD_DIM), 1)
    return (lanes < HEAD_DIM).astype(F32).astype(BF16), (lanes >= HEAD_DIM).astype(F32).astype(BF16)


def attend_body(
    rows, routes_ref, drow_ref, wq, wk, wv, wo, misc,
    t_ref, q_ref, k_ref, v_ref, o_ref, lse_ref, gates_ref, outs,
):
    length = rows.shape[0]
    qb, vb, ob, again, ashift, egain, eshift = vectors_of(misc)
    unit, _ = standardize(rows)
    low = (unit * again + ashift).astype(BF16)
    queries = (dot(low, wq[...]) + qb).astype(BF16)
    keys = dot(low, wk[...]).astype(BF16)
    values = (dot(low, wv[...]) + vb).astype(BF16)
    q_ref[0] = queries
    k_ref[0] = keys
    v_ref[0] = values
    masks = lane_masks(length)
    lanes = lax.broadcasted_iota(jnp.int32, (length, MISC), 1)
    first_half = lax.broadcasted_iota(jnp.int32, (length, 2 * HEAD_DIM), 1) < HEAD_DIM
    sums = jnp.zeros((length, MISC), F32)
    for pair in range(HEADS // 2):
        cols = slice(pair * 2 * HEAD_DIM, (pair + 1) * 2 * HEAD_DIM)
        mixed = []
        for side in range(2):
            scores = dot_nt(queries[:, cols] * (masks[side] * FACTOR), keys[:, cols])
            highest = jnp.max(scores, axis=-1, keepdims=True)
            expo = jnp.exp(scores - highest)
            total = jnp.sum(expo, axis=-1, keepdims=True)
            attention = (expo * (1.0 / total)).astype(BF16)
            sums = jnp.where(lanes == 2 * pair + side, highest + jnp.log(total), sums)
            mixed.append(dot(attention, values[:, cols]))
        o_ref[0, :, cols] = jnp.where(first_half, mixed[0], mixed[1]).astype(BF16)
    lse_ref[0] = sums
    middle = rows + (dot(o_ref[0], wo[...]) + ob)
    t_ref[0] = middle
    unit_two, _ = standardize(middle)
    hidden = (unit_two * egain + eshift).astype(BF16)
    logits = dot(hidden, misc[...])
    pair_experts = routes_ref[0]
    zero = jnp.sum(jnp.where(lanes == pair_experts[:, 0:1], logits, 0.0), axis=-1, keepdims=True)
    one = jnp.sum(jnp.where(lanes == pair_experts[:, 1:2], logits, 0.0), axis=-1, keepdims=True)
    gate_zero = 1.0 / (1.0 + jnp.exp(one - zero))
    gate_one = 1.0 / (1.0 + jnp.exp(zero - one))
    gates_ref[0, :, 0:1] = gate_zero
    gates_ref[0, :, 1:2] = gate_one
    drow = drow_ref[0]
    spread([drow[0:1, :], drow[1:2, :]], [hidden], outs, pl.program_id(0) == 0)


def combine_body(middle, gates_ref, dcol_ref, back, yzero_ref, yone_ref):
    dest = dcol_ref[0]
    gates = gates_ref[0]
    zero = pick(dest[:, 0:1], back)
    one = pick(dest[:, 1:2], back)
    if yzero_ref is not None:
        yzero_ref[0] = zero.astype(BF16)
        yone_ref[0] = one.astype(BF16)
    return middle + (gates[:, 0:1] * zero + gates[:, 1:2] * one), zero, one


def grads_body(upstream, zero, one, gates_ref, routes_ref, drow_ref, dz_ref, outs):
    length = upstream.shape[0]
    gates = gates_ref[0]
    gate_zero, gate_one = gates[:, 0:1], gates[:, 1:2]
    grad_zero = jnp.sum(zero * upstream, axis=-1, keepdims=True)
    grad_one = jnp.sum(one * upstream, axis=-1, keepdims=True)
    along = gate_zero * grad_zero + gate_one * grad_one
    lanes = lax.broadcasted_iota(jnp.int32, (length, MISC), 1)
    pair_experts = routes_ref[0]
    dz = jnp.where(lanes == pair_experts[:, 0:1], gate_zero * (grad_zero - along), 0.0)
    dz = dz + jnp.where(lanes == pair_experts[:, 1:2], gate_one * (grad_one - along), 0.0)
    dz_ref[0] = dz.astype(BF16)
    drow = drow_ref[0]
    spread(
        [drow[0:1, :], drow[1:2, :]],
        [(gate_zero * upstream).astype(BF16), (gate_one * upstream).astype(BF16)],
        outs,
        pl.program_id(0) == 0,
    )


def first_kernel(rows, routes, drow, wq, wk, wv, wo, misc, *outs):
    attend_body(rows[0], routes, drow, wq, wk, wv, wo, misc, *outs[:7], outs[7:])


def next_kernel(
    middle, gates, dcol, back, routes, drow, wq, wk, wv, wo, misc, rows_ref, yzero, yone, *outs
):
    rows, _, _ = combine_body(middle[0], gates, dcol, (back,), yzero, yone)
    rows_ref[0] = rows
    attend_body(rows, routes, drow, wq, wk, wv, wo, misc, *outs[:7], outs[7:])


def turn_kernel(middle, gates, dcol, back, cotangent, routes, drow, result, dz, out):
    rows, zero, one = combine_body(middle[0], gates, dcol, (back,), None, None)
    result[0] = rows
    grads_body(cotangent[0], zero, one, gates, routes, drow, dz, (out,))


def back_kernel(
    upstream, rows, middle, q_ref, k_ref, v_ref, o_ref, lse_ref, dz_ref, dcol, came,
    wq, wk, wv, wo, misc, *rest,
):
    bias, *rest = rest
    if len(rest) > 4:
        yzero, yone, gates_below, routes_below, drow_below, grad_ref, sent, dz_below, out, wgrad, vgrad = rest
    else:
        grad_ref, sent, wgrad, vgrad = rest
    first = pl.program_id(0) == 0
    length = rows.shape[1]
    width = rows.shape[2]
    qb, vb, ob, again, ashift, egain, eshift = vectors_of(misc)

    @pl.when(first)
    def _():
        wgrad[...] = jnp.zeros_like(wgrad)
        vgrad[...] = jnp.zeros_like(vgrad)

    def add_vector(number, value):
        vgrad[VEC_AT + number : VEC_AT + number + 1, :] += jnp.sum(value, axis=0, keepdims=True)

    unit_two, scale_two = standardize(middle[0])
    hidden = (unit_two * egain + eshift).astype(BF16)
    dz = dz_ref[0]
    dest = dcol[0]
    dhidden = dot_nt(dz, misc[...])
    lanes = lax.broadcasted_iota(jnp.int32, (length, came.shape[0]), 1)
    hit = (dest[:, 0:1] == lanes) | (dest[:, 1:2] == lanes)
    dhidden = dhidden + dot(hit.astype(F32).astype(BF16), came[...])
    wgrad[:, 4 * width :] += dot_tn(hidden, dz)
    add_vector(5, dhidden * unit_two)
    add_vector(6, dhidden)
    dmiddle = upstream[0] + standardize_back(dhidden, unit_two, scale_two, egain)
    dbranch = dmiddle.astype(BF16)
    wgrad[:, 3 * width : 4 * width] += dot_tn(o_ref[0], dbranch)
    add_vector(2, dbranch.astype(F32))
    dcontext = dot_nt(dbranch, wo[...]).astype(BF16)
    masks = lane_masks(length)
    first_half = lax.broadcasted_iota(jnp.int32, (length, 2 * HEAD_DIM), 1) < HEAD_DIM
    dqs, dks, dvs = [], [], []
    for pair in range(HEADS // 2):
        cols = slice(pair * 2 * HEAD_DIM, (pair + 1) * 2 * HEAD_DIM)
        keys = k_ref[0, :, cols]
        values = v_ref[0, :, cols]
        queries = q_ref[0, :, cols]
        dvalues, dqueries, dkeys = None, [], None
        for side in range(2):
            own_queries = queries * (masks[side] * FACTOR)
            own_context = dcontext[:, cols] * masks[side]
            scores = dot_nt(own_queries, keys)
            number = 2 * pair + side
            attention = jnp.exp(scores - lse_ref[0, :, number : number + 1])
            prob = dot_nt(own_context, values)
            weighed = attention * prob
            delta = jnp.sum(weighed, axis=-1, keepdims=True)
            dscores = (weighed - attention * delta).astype(BF16)
            dvalue = dot_tn(attention.astype(BF16), own_context)
            dkey = dot_tn(dscores, own_queries)
            dvalues = dvalue if dvalues is None else dvalues + dvalue
            dkeys = dkey if dkeys is None else dkeys + dkey
            dqueries.append(dot(dscores, keys))
        dqs.append((jnp.where(first_half, dqueries[0], dqueries[1]) * FACTOR).astype(BF16))
        dks.append(dkeys.astype(BF16))
        dvs.append(dvalues.astype(BF16))
    dq = jnp.concatenate(dqs, axis=1)
    dk = jnp.concatenate(dks, axis=1)
    dv = jnp.concatenate(dvs, axis=1)
    unit, scale = standardize(rows[0])
    low = (unit * again + ashift).astype(BF16)
    wgrad[:, 0:width] += dot_tn(low, dq)
    wgrad[:, width : 2 * width] += dot_tn(low, dk)
    wgrad[:, 2 * width : 3 * width] += dot_tn(low, dv)
    add_vector(0, dq.astype(F32))
    add_vector(1, dv.astype(F32))
    dlow = dot_nt(dq, wq[...]) + dot_nt(dk, wk[...]) + dot_nt(dv, wv[...])
    add_vector(3, dlow * unit)
    add_vector(4, dlow)
    grad = dmiddle + standardize_back(dlow, unit, scale, again)
    grad_ref[0] = grad
    if len(rest) > 4:
        grads_body(
            grad, yzero[0].astype(F32), yone[0].astype(F32), gates_below, routes_below, drow_below, dz_below,
            (out,),
        )

    @pl.when(pl.program_id(0) == pl.num_programs(0) - 1)
    def _():
        wgrad[:, 4 * width :] += vgrad[...].T
        sent[:, : 4 * width + MISC] = wgrad[...].astype(BF16)
        sent[:, 4 * width + MISC :] = bias[...]


def per_image(array):
    return pl.BlockSpec((1,) + array.shape[1:], lambda i: (i,) + (0,) * (len(array.shape) - 1))


def whole(array):
    return pl.BlockSpec(array.shape, lambda i: (0,) * len(array.shape))


def packed_specs(packed):
    width = packed.shape[0]
    specs = [pl.BlockSpec((width, width), lambda i, n=n: (0, n)) for n in range(4)]
    return specs + [pl.BlockSpec((width, MISC), lambda i: (0, 4 * width // MISC))]


def call(body, grid, inputs, outputs, scratch=(), flops=0, aliases=None):
    moved = sum(a.size * a.dtype.itemsize for a, _ in inputs)
    shapes = [jax.ShapeDtypeStruct(s, t) for s, t, _ in outputs]
    moved += sum(s.size * s.dtype.itemsize for s in shapes)
    return pl.pallas_call(
        body,
        grid=grid,
        in_specs=[s for _, s in inputs],
        out_specs=[s for _, _, s in outputs],
        out_shape=shapes,
        scratch_shapes=list(scratch),
        compiler_params=pltpu.CompilerParams(vmem_limit_bytes=VMEM),
        cost_estimate=pl.CostEstimate(flops=flops, bytes_accessed=moved, transcendentals=0),
    )(*[a for a, _ in inputs])


def images_out(images, length, columns, kind):
    shape = (images, length, columns)
    return (shape, kind, pl.BlockSpec((1, length, columns), lambda i: (i, 0, 0)))


def slots_out(slots, width):
    return [((slots, width), BF16, pl.BlockSpec((slots, width), lambda i: (0, 0)))]


def attend_outputs(images, length, width, slots):
    return [
        images_out(images, length, width, F32),
        images_out(images, length, width, BF16),
        images_out(images, length, width, BF16),
        images_out(images, length, width, BF16),
        images_out(images, length, width, BF16),
        images_out(images, length, MISC, F32),
        images_out(images, length, 2, F32),
    ] + slots_out(slots, width)


ROOT_HALF = 0.7071067811865476
ROOT_TWO_PI_INVERSE = 0.3989422804014327
MESH = pl.DeviceIdType.MESH


def order_of(count):
    return sorted(range(1, count), key=lambda k: -min(k, count - k))


class Swap:
    def __init__(self, sent, arrived, made, back, sems):
        self.sent, self.arrived, self.made, self.back = sent, arrived, made, back
        self.out_send, self.out_recv, self.home_send, self.home_recv, self.own = sems
        self.local, self.count = arrived.shape[0], arrived.shape[1]
        self.me = lax.axis_index("expert")

    def greet(self):
        barrier = pltpu.get_barrier_semaphore()
        for k in range(1, self.count):
            peer = lax.rem(self.me + k, self.count)
            pl.semaphore_signal(barrier, inc=1, device_id={"expert": peer}, device_id_type=MESH)
        pl.semaphore_wait(barrier, self.count - 1)

    def outward(self, j, k, peer):
        return pltpu.make_async_remote_copy(
            src_ref=self.sent.at[j, peer], dst_ref=self.arrived.at[j, self.me],
            send_sem=self.out_send.at[j, k], recv_sem=self.out_recv.at[j, k],
            device_id={"expert": peer}, device_id_type=MESH,
        )

    def homeward(self, j, k, peer):
        return pltpu.make_async_remote_copy(
            src_ref=self.made.at[j, peer], dst_ref=self.back.at[j, self.me],
            send_sem=self.home_send.at[j, k], recv_sem=self.home_recv.at[j, k],
            device_id={"expert": peer}, device_id_type=MESH,
        )

    def own_out(self, j):
        return pltpu.make_async_copy(self.sent.at[j, self.me], self.arrived.at[j, self.me], self.own.at[j])

    def own_home(self, j):
        return pltpu.make_async_copy(self.made.at[j, self.me], self.back.at[j, self.me], self.own.at[self.local + j])

    def send_all(self):
        for j in range(self.local):
            for k in order_of(self.count):
                self.outward(j, k, lax.rem(self.me + k, self.count)).start()
            self.own_out(j).start()

    def chip(self, turn):
        chips = self.count // 2
        return lax.rem(self.me // 2 - turn + chips, chips)

    def wait_chip(self, j, chip):
        for core in range(2):
            source = 2 * chip + core
            k = lax.rem(self.me - source + self.count, self.count)

            @pl.when(source != self.me)
            def _(k=k, source=source):
                pltpu.make_async_remote_copy(
                    src_ref=self.arrived.at[j, source], dst_ref=self.arrived.at[j, source],
                    send_sem=self.out_send.at[j, k], recv_sem=self.out_recv.at[j, k],
                    device_id={"expert": source}, device_id_type=MESH,
                ).wait_recv()

            @pl.when(source == self.me)
            def _():
                self.own_out(j).wait()

    def send_home(self, j, chip):
        for core in range(2):
            peer = 2 * chip + core
            k = lax.rem(peer - self.me + self.count, self.count)

            @pl.when(peer != self.me)
            def _(k=k, peer=peer):
                self.homeward(j, k, peer).start()

            @pl.when(peer == self.me)
            def _():
                self.own_home(j).start()

    def finish(self):
        for j in range(self.local):
            self.own_home(j).wait()
            for k in range(1, self.count):
                peer = lax.rem(self.me + k, self.count)
                self.outward(j, k, peer).wait_send()
                self.homeward(j, k, peer).wait()


def weight_blocks(weights, j, f):
    _, parts, rows, width = weights.shape
    share, take = width // parts, rows // 2
    each = FF_BLOCK // take
    first = weights[j, :, f * share : (f + 1) * share, :].reshape(width, width)
    second = weights[j, f * each : (f + 1) * each, take:, :].reshape(FF_BLOCK, width)
    return first, second


def expert_kernel(
    sent, packed, b1, b2, back, arrived_out, g_out, s_out,
    arrived, made, weights, g_stage, s_stage, out_send, out_recv, home_send, home_recv, own, load, stores, last,
):
    swap = Swap(sent, arrived, made, back, (out_send, out_recv, home_send, home_recv, own))
    local, count, capacity, width = arrived.shape
    chips = count // 2
    rows = 2 * capacity
    ff = g_out.shape[2]
    loads = [pltpu.make_async_copy(packed.at[:, j], weights.at[j], load.at[j]) for j in range(local)]
    for copy in loads:
        copy.start()
    swap.greet()
    swap.send_all()

    def kept(j, slot, chip):
        place = pl.ds(pl.multiple_of(chip * rows, rows), rows)
        return (
            pltpu.make_async_copy(g_stage.at[slot], g_out.at[j, place, :], stores.at[0, slot]),
            pltpu.make_async_copy(s_stage.at[slot], s_out.at[j, place, :], stores.at[1, slot]),
        )

    for j in range(local):
        loads[j].wait()

        def chip_step(turn, carry, j=j):
            chip = swap.chip(turn)
            slot = lax.rem(turn, 2)
            swap.wait_chip(j, chip)

            @pl.when(j * chips + turn >= 2)
            def _():
                for copy in kept(j, slot, chip):
                    copy.wait()

            x = arrived[j, pl.ds(2 * chip, 2)].reshape(rows, width)
            total = jnp.broadcast_to(b2[j], (rows, width))
            for f in range(ff // FF_BLOCK):
                cols = slice(f * FF_BLOCK, (f + 1) * FF_BLOCK)
                first, second = weight_blocks(weights, j, f)
                inner = dot(x, first) + b1[j, :, cols]
                normal = 0.5 * (1.0 + lax.erf(inner * ROOT_HALF))
                g = (inner * normal).astype(BF16)
                density = jnp.exp(-0.5 * inner * inner) * ROOT_TWO_PI_INVERSE
                g_stage[slot, :, cols] = g
                s_stage[slot, :, cols] = (normal + inner * density).astype(BF16)
                total = total + dot(g, second)
            made[j, pl.ds(2 * chip, 2)] = total.astype(BF16).reshape(2, capacity, width)
            swap.send_home(j, chip)
            for copy in kept(j, slot, chip):
                copy.start()
            return carry

        lax.fori_loop(0, chips, chip_step, 0)
    final = pltpu.make_async_copy(arrived, arrived_out, last)
    final.start()
    for slot in range(2):
        for copy in kept(0, slot, 0):
            copy.wait()
    swap.finish()
    final.wait()


def expert_back_kernel(
    sent, packed, arrived_x, g_in, s_in, back, out, db1, db2,
    arrived, made, weights, x, du, s_stage, g_stage, first_stage, second_stage,
    out_send, out_recv, home_send, home_recv, own, load, fetch, stores,
):
    swap = Swap(sent, arrived, made, back, (out_send, out_recv, home_send, home_recv, own))
    local, count, capacity, width = arrived.shape
    chips = count // 2
    rows = 2 * capacity
    ff = g_in.shape[2]
    blocks = ff // FF_BLOCK
    _, parts, all_rows, _ = weights.shape
    share, take = width // parts, all_rows // 2
    each = FF_BLOCK // take
    loads = [pltpu.make_async_copy(packed.at[:, j], weights.at[j], load.at[j]) for j in range(local)]
    loads.append(pltpu.make_async_copy(arrived_x, x, load.at[local]))
    for copy in loads:
        copy.start()

    def slopes(j, turn):
        slot = lax.rem(turn, 2)
        place = pl.ds(pl.multiple_of(swap.chip(turn) * rows, rows), rows)
        return pltpu.make_async_copy(s_in.at[j, place, :], s_stage.at[slot], fetch.at[0, slot])

    def activations(j, f):
        return pltpu.make_async_copy(
            g_in.at[j, :, f * FF_BLOCK : (f + 1) * FF_BLOCK], g_stage.at[f % 2], fetch.at[1, f % 2]
        )

    def results(j, f):
        return (
            pltpu.make_async_copy(
                first_stage.at[f % 2], out.at[:, j, f * share : (f + 1) * share, :], stores.at[0, f % 2]
            ),
            pltpu.make_async_copy(
                second_stage.at[f % 2], out.at[f * each : (f + 1) * each, j, take:, :], stores.at[1, f % 2]
            ),
        )

    slopes(0, 0).start()
    swap.greet()
    swap.send_all()
    for j in range(local):
        loads[j].wait()
        activations(j, 0).start()

        def chip_step(turn, carry, j=j):
            chip = swap.chip(turn)
            slot = lax.rem(turn, 2)

            @pl.when(turn + 1 < chips)
            def _():
                slopes(j, turn + 1).start()

            swap.wait_chip(j, chip)
            slopes(j, turn).wait()
            dy = arrived[j, pl.ds(2 * chip, 2)].reshape(rows, width)
            place = pl.ds(pl.multiple_of(chip * rows, rows), rows)
            total = jnp.zeros((rows, width), F32)
            for f in range(blocks):
                cols = slice(f * FF_BLOCK, (f + 1) * FF_BLOCK)
                first, second = weight_blocks(weights, j, f)
                part = (dot_nt(dy, second) * s_stage[slot, :, cols].astype(F32)).astype(BF16)
                du[place, cols] = part
                total = total + dot_nt(part, first)
            made[j, pl.ds(2 * chip, 2)] = total.astype(BF16).reshape(2, capacity, width)
            swap.send_home(j, chip)
            return carry

        lax.fori_loop(0, chips, chip_step, 0)
        if j + 1 < local:
            slopes(j + 1, 0).start()
        if j == 0:
            loads[local].wait()
        dy = arrived[j].reshape(count * capacity, width)
        db2[j] = jnp.sum(dy.astype(F32), axis=0, keepdims=True)
        for f in range(blocks):
            cols = slice(f * FF_BLOCK, (f + 1) * FF_BLOCK)
            if f + 1 < blocks:
                activations(j, f + 1).start()
            if j > 0 or f > 1:
                for copy in results(j, f):
                    copy.wait()
            part = du[:, cols]
            grad = dot_tn(x[j].reshape(count * capacity, width), part).astype(BF16)
            first_stage[f % 2] = grad.reshape(parts, share, width)
            db1[j, :, cols] = jnp.sum(part.astype(F32), axis=0, keepdims=True)
            activations(j, f).wait()
            grad = dot_tn(g_stage[f % 2], dy).astype(BF16)
            second_stage[f % 2] = grad.reshape(each, take, width)
            for copy in results(j, f):
                copy.start()
    for f in range(2):
        for copy in results(0, f):
            copy.wait()
    swap.finish()


def swap_sems(local, count):
    pairs = [pltpu.SemaphoreType.DMA((local, count))] * 4
    return pairs + [pltpu.SemaphoreType.DMA((2 * local,))]


def expert_call(body, inputs, outputs, scratch, number, flops):
    def spec(held):
        return pl.BlockSpec(memory_space=pltpu.VMEM if held else pl.ANY)

    shapes = [jax.ShapeDtypeStruct(s, t) for s, t, _ in outputs]
    moved = sum(a.size * a.dtype.itemsize for a, _ in inputs) + sum(s.size * s.dtype.itemsize for s in shapes)
    return pl.pallas_call(
        body,
        in_specs=[spec(held) for _, held in inputs],
        out_specs=[spec(held) for _, _, held in outputs],
        out_shape=shapes,
        scratch_shapes=scratch,
        compiler_params=pltpu.CompilerParams(
            collective_id=number, has_side_effects=True, vmem_limit_bytes=VMEM
        ),
        cost_estimate=pl.CostEstimate(flops=flops, bytes_accessed=moved, transcendentals=0),
    )(*[a for a, _ in inputs])


def expert_forward(sent, expert, number):
    packed, b1, b2 = expert
    local, count, capacity, width = sent.shape
    ff = b1.shape[2]
    rows = 2 * capacity
    slots = (local, count * capacity, ff)
    return expert_call(
        expert_kernel,
        [(sent, False), (packed, False), (b1, True), (b2, True)],
        [(sent.shape, BF16, False), (sent.shape, BF16, False), (slots, BF16, False), (slots, BF16, False)],
        [
            pltpu.VMEM(sent.shape, BF16), pltpu.VMEM(sent.shape, BF16),
            pltpu.VMEM((local, packed.shape[0], *packed.shape[2:]), BF16),
            pltpu.VMEM((2, rows, ff), BF16), pltpu.VMEM((2, rows, ff), BF16),
        ] + swap_sems(local, count) + [
            pltpu.SemaphoreType.DMA((local,)), pltpu.SemaphoreType.DMA((2, 2)), pltpu.SemaphoreType.DMA,
        ],
        number,
        4 * local * count * capacity * width * ff,
    )


def expert_backward(sent, expert, arrived, g, s, number):
    packed, b1, b2 = expert
    local, count, capacity, width = sent.shape
    ff = b1.shape[2]
    rows = 2 * capacity
    parts, _, all_rows, _ = packed.shape
    share, take = width // parts, all_rows // 2
    return expert_call(
        expert_back_kernel,
        [(sent, False), (packed, False), (arrived, False), (g, False), (s, False)],
        [
            (sent.shape, BF16, False), (packed.shape, BF16, False),
            (b1.shape, F32, True), (b2.shape, F32, True),
        ],
        [
            pltpu.VMEM(sent.shape, BF16), pltpu.VMEM(sent.shape, BF16),
            pltpu.VMEM((local, parts, all_rows, width), BF16), pltpu.VMEM(sent.shape, BF16),
            pltpu.VMEM((count * capacity, ff), BF16), pltpu.VMEM((2, rows, ff), BF16),
            pltpu.VMEM((2, count * capacity, FF_BLOCK), BF16), pltpu.VMEM((2, parts, share, width), BF16),
            pltpu.VMEM((2, FF_BLOCK // take, take, width), BF16),
        ] + swap_sems(local, count) + [
            pltpu.SemaphoreType.DMA((local + 1,)), pltpu.SemaphoreType.DMA((2, 2)), pltpu.SemaphoreType.DMA((2, 2)),
        ],
        number,
        8 * local * count * capacity * width * ff,
    )


def destinations(routes, experts_all, owners):
    layers, images, length, _ = routes.shape
    tokens = images * length
    pairs = routes.reshape(layers, tokens, 2)
    hot = (pairs[..., None] == jnp.arange(experts_all, dtype=jnp.int32)).astype(F32)
    counts = (hot[:, :, 0] + hot[:, :, 1]).astype(BF16)
    earlier = (jnp.arange(tokens)[:, None] > jnp.arange(tokens)[None, :]).astype(BF16)
    before = jnp.einsum("ts,lse->lte", earlier, counts, preferred_element_type=F32)
    slot = jnp.sum(before[:, :, None, :] * hot, axis=-1).astype(jnp.int32)
    capacity = (10 * tokens // (4 * experts_all) + 7) // 8 * 8
    local = experts_all // owners
    row = ((pairs % local) * owners + pairs // local) * capacity + slot
    dest = jnp.where(slot < capacity, row, -1)
    return dest.reshape(layers, images, length, 2), capacity


def shards(
    images, cotangent, routes, query_weight, key_weight, value_weight, output_weight, router_weight, query_bias,
    value_bias, output_bias, attend_gain, attend_shift, expert_gain, expert_shift, inner_weight, inner_bias,
    outer_weight, outer_bias,
):
    count, length, width = images.shape
    parts = lax.axis_size("dp")
    owners = lax.axis_size("expert")
    experts_all = router_weight.shape[2]
    local = inner_weight.shape[1]
    ff = inner_weight.shape[3]
    share = width // parts
    tokens = count * length
    squares = (query_weight, key_weight, value_weight, output_weight)
    vectors = (query_bias, value_bias, output_bias, attend_gain, attend_shift, expert_gain, expert_shift)
    bias_columns = ff // width + 1
    bias_room = -(-experts_all * bias_columns // MISC) * MISC

    biases = jnp.concatenate(
        [inner_bias.reshape(LAYERS, local, share, ff // width), outer_bias.reshape(LAYERS, local, share, 1)], axis=3
    )
    biases = jnp.transpose(biases, (2, 0, 1, 3)).reshape(share, LAYERS * local * bias_columns)

    packed = []
    experts = []
    for layer in range(LAYERS):
        misc = [router_weight[layer], jnp.zeros((share, VEC_AT - experts_all), F32)]
        misc += [jnp.stack([v[layer] for v in vectors], axis=1), jnp.zeros((share, BIAS_AT - VEC_AT - 7), F32)]
        if layer == 0:
            misc += [biases, jnp.zeros((share, MISC - BIAS_AT - biases.shape[1]), F32)]
        else:
            misc += [jnp.zeros((share, MISC - BIAS_AT), F32)]
        mine = jnp.concatenate([s[layer] for s in squares] + misc, axis=1).astype(BF16)
        packed.append(lax.all_gather(mine, "dp", axis=0, tiled=True))
        mine = jnp.transpose(inner_weight[layer].reshape(local, share, ff // FF_BLOCK, FF_BLOCK), (0, 2, 1, 3))
        mine = jnp.concatenate([mine.reshape(local, ff // parts, width), outer_weight[layer]], axis=1).astype(BF16)
        experts.append(lax.all_gather(mine, "dp", axis=0, tiled=False))
    spare = packed[0][:, 4 * width + BIAS_AT : 4 * width + BIAS_AT + biases.shape[1]].astype(F32)
    spare = jnp.transpose(spare.reshape(width, LAYERS, local, bias_columns), (1, 2, 0, 3))
    inner_biases = spare[..., :-1].reshape(LAYERS, local, 1, ff)
    outer_biases = spare[..., -1].reshape(LAYERS, local, 1, width)
    experts = [(experts[n], inner_biases[n], outer_biases[n]) for n in range(LAYERS)]

    dcol, capacity = destinations(routes, experts_all, owners)
    drow = jnp.transpose(dcol, (0, 1, 3, 2))
    slots = experts_all * capacity
    dense_flops = 8 * tokens * width * width + 4 * tokens * slots * width

    saved = []
    back = None
    rows = images
    for layer in range(LAYERS):
        weights = [(packed[layer], s) for s in packed_specs(packed[layer])]
        routing = [(routes[layer], per_image(routes[layer])), (drow[layer], per_image(drow[layer]))]
        outputs = attend_outputs(count, length, width, slots)
        if layer == 0:
            done = call(
                first_kernel, (count,), [(rows, per_image(rows))] + routing + weights, outputs, flops=dense_flops
            )
            picked = None
        else:
            before = saved[-1]
            done = call(
                next_kernel, (count,),
                [
                    (before["middle"], per_image(before["middle"])),
                    (before["gates"], per_image(before["gates"])),
                    (dcol[layer - 1], per_image(dcol[layer - 1])),
                    (back, whole(back)),
                ] + routing + weights,
                [
                    images_out(count, length, width, F32),
                    images_out(count, length, width, BF16),
                    images_out(count, length, width, BF16),
                ] + outputs,
                flops=dense_flops,
            )
            rows, *picked = done[:3]
            done = done[3:]
            before["picked"] = picked
        middle, queries, keys, values, context, sums, gates = done[:7]
        sent = done[7].reshape(local, owners, capacity, width)
        back, arrived, g, s = expert_forward(sent, experts[layer], layer)
        back = back.reshape(slots, width)
        saved.append({
            "rows": rows, "middle": middle, "attend": (queries, keys, values, context, sums), "gates": gates,
            "experts": (arrived, g, s),
        })

    last = saved[-1]
    result, dz, sent = call(
        turn_kernel, (count,),
        [(last["middle"], per_image(last["middle"])), (last["gates"], per_image(last["gates"]))]
        + [(dcol[-1], per_image(dcol[-1])), (back, whole(back))]
        + [(cotangent, per_image(cotangent)), (routes[-1], per_image(routes[-1])), (drow[-1], per_image(drow[-1]))],
        [images_out(count, length, width, F32), images_out(count, length, MISC, BF16)] + slots_out(slots, width),
        flops=dense_flops,
    )
    upstream = cotangent
    dense_grads = [None] * LAYERS
    finished = []
    waiting = []
    for layer in reversed(range(LAYERS)):
        kept = saved[layer]
        sent = sent.reshape(local, owners, capacity, width)
        came, grads, db1, db2 = expert_backward(sent, experts[layer], *kept["experts"], LAYERS + layer)
        came = came.reshape(slots, width)
        came, waiting = lax.optimization_barrier((came, waiting))
        finished += waiting
        waiting = [lax.psum_scatter(grads, "dp", scatter_dimension=0, tiled=False)]
        own = [
            jnp.concatenate([db1[j].reshape(width, ff // width), db2[j].reshape(width, 1)], axis=1)
            for j in range(local)
        ]
        first_column = lax.axis_index("expert") * (local * bias_columns)
        bias = lax.dynamic_update_slice(
            jnp.zeros((width, bias_room), F32), jnp.concatenate(own, axis=1), (0, first_column)
        ).astype(BF16)
        weights = [(packed[layer], s) for s in packed_specs(packed[layer])]
        inputs = [upstream, kept["rows"], kept["middle"], *kept["attend"], dz, dcol[layer]]
        inputs = [(a, per_image(a)) for a in inputs] + [(came, whole(came))] + weights
        inputs += [(bias, whole(bias))]
        outputs = [
            images_out(count, length, width, F32),
            (
                (width, 4 * width + MISC + bias_room), BF16,
                pl.BlockSpec((width, 4 * width + MISC + bias_room), lambda i: (0, 0)),
            ),
        ]
        if layer > 0:
            below = saved[layer - 1]
            extra = [*below["picked"], below["gates"], routes[layer - 1], drow[layer - 1]]
            inputs += [(a, per_image(a)) for a in extra]
            outputs += [images_out(count, length, MISC, BF16)] + slots_out(slots, width)
        done = call(
            back_kernel, (count,), inputs, outputs,
            [pltpu.VMEM((width, 4 * width + MISC), F32), pltpu.VMEM((MISC, width), F32)], flops=3 * dense_flops,
        )
        upstream, wgrad = done[:2]
        if layer > 0:
            dz, sent = done[2:]
        mine = lax.psum_scatter(wgrad, "dp", scatter_dimension=0, tiled=True)
        dense_grads[layer] = lax.psum(mine, "expert")
    expert_grads = waiting + finished

    both = jnp.stack(dense_grads).astype(F32)
    square_grads = [both[:, :, n * width : (n + 1) * width] for n in range(4)]
    tail = both[:, :, 4 * width : 4 * width + MISC]
    own = lax.dynamic_slice_in_dim(
        both[:, :, 4 * width + MISC :], lax.axis_index("expert") * (local * bias_columns), local * bias_columns, 2
    )
    own = jnp.transpose(own.reshape(LAYERS, share, local, bias_columns), (0, 2, 1, 3))
    pieces = jnp.stack(expert_grads)
    inner_grad = pieces[:, :, : ff // parts].reshape(LAYERS, local, ff // FF_BLOCK, share, FF_BLOCK)
    inner_grad = jnp.transpose(inner_grad, (0, 1, 3, 2, 4)).reshape(inner_weight.shape)
    return (
        result,
        upstream,
        *square_grads,
        tail[:, :, :experts_all],
        *[tail[:, :, VEC_AT + n] for n in range(7)],
        inner_grad.astype(F32),
        own[..., :-1].reshape(LAYERS, local, ff // parts),
        pieces[:, :, ff // parts :].astype(F32),
        own[..., -1],
    )


def solution(mesh):
    both = P(("dp", "expert"), None, None)
    square = P(None, "dp", None)
    vector = P(None, "dp")
    matrix = P(None, "expert", "dp", None)
    bias = P(None, "expert", "dp")
    grads = (square,) * 5 + (vector,) * 7 + (matrix, bias, matrix, bias)
    return jax.shard_map(
        shards,
        mesh=mesh,
        in_specs=(both, both, P(None, ("dp", "expert"), None, None)) + grads,
        out_specs=(both, both) + grads,
        check_vma=False,
    )
```

```python
import functools

import jax
import jax.numpy as jnp
from jax import lax
from jax.experimental import pallas as pl
from jax.experimental.pallas import tpu as pltpu
from jax.sharding import PartitionSpec as P

HEADS = 8
HEAD_DIM = 64
LAYERS = 2
EPSILON = 1e-06
FACTOR = HEAD_DIM**-0.5
VEC_AT = 64
MISC = 128
FF_BLOCK = 512
COST = 1024
VMEM = 56 * 1024 * 1024

F32 = jnp.float32
BF16 = jnp.bfloat16


def dot(a, b):
    return jnp.dot(a, b, preferred_element_type=F32)


def dot_nt(a, b):
    return lax.dot_general(a, b, (((1,), (1,)), ((), ())), preferred_element_type=F32)


def dot_tn(a, b):
    return lax.dot_general(a, b, (((0,), (0,)), ((), ())), preferred_element_type=F32)


def standardize(rows):
    mean_value = jnp.mean(rows, axis=-1, keepdims=True)
    centered = rows - mean_value
    variance = jnp.mean(centered * centered, axis=-1, keepdims=True)
    scale = lax.rsqrt(variance + EPSILON)
    return centered * scale, scale


def standardize_back(upstream, unit, scale, gain):
    along = upstream * gain
    inner = (
        along
        - jnp.mean(along, axis=-1, keepdims=True)
        - unit * jnp.mean(along * unit, axis=-1, keepdims=True)
    )
    return inner * scale


def vectors_of(misc_ref):
    turned = misc_ref[...].astype(F32).T
    return [turned[VEC_AT + n : VEC_AT + n + 1, :] for n in range(7)]


def pick(dest, buffers):
    total = None
    for number, buffer in enumerate(buffers):
        count = buffer.shape[0]
        lanes = lax.broadcasted_iota(jnp.int32, (dest.shape[0], count), 1)
        chosen = (dest - number * count == lanes).astype(F32).astype(BF16)
        part = dot(chosen, buffer[...])
        total = part if total is None else total + part
    return total


def spread(dest_rows, sources, outs, first):
    half = outs[0].shape[0]
    step = 256
    length = dest_rows[0].shape[1]
    for number, out in enumerate(outs):
        for start in range(0, half, step):
            slots = lax.broadcasted_iota(jnp.int32, (step, length), 0) + (number * half + start)
            if len(sources) == 1:
                hit = (slots == dest_rows[0]) | (slots == dest_rows[1])
                block = dot(hit.astype(F32).astype(BF16), sources[0])
            else:
                block = dot((slots == dest_rows[0]).astype(F32).astype(BF16), sources[0])
                block = block + dot((slots == dest_rows[1]).astype(F32).astype(BF16), sources[1])
            block = block.astype(BF16)

            @pl.when(first)
            def _(out=out, start=start, block=block):
                out[start : start + step, :] = block

            @pl.when(jnp.logical_not(first))
            def _(out=out, start=start, block=block):
                out[start : start + step, :] += block


def lane_masks(length):
    lanes = lax.broadcasted_iota(jnp.int32, (length, 2 * HEAD_DIM), 1)
    return (lanes < HEAD_DIM).astype(F32).astype(BF16), (lanes >= HEAD_DIM).astype(F32).astype(BF16)


def attend_body(
    rows, routes_ref, drow_ref, wq, wk, wv, wo, misc,
    t_ref, q_ref, k_ref, v_ref, o_ref, lse_ref, gates_ref, outs,
):
    length = rows.shape[0]
    qb, vb, ob, again, ashift, egain, eshift = vectors_of(misc)
    unit, _ = standardize(rows)
    low = (unit * again + ashift).astype(BF16)
    queries = (dot(low, wq[...]) + qb).astype(BF16)
    keys = dot(low, wk[...]).astype(BF16)
    values = (dot(low, wv[...]) + vb).astype(BF16)
    q_ref[0] = queries
    k_ref[0] = keys
    v_ref[0] = values
    masks = lane_masks(length)
    lanes = lax.broadcasted_iota(jnp.int32, (length, MISC), 1)
    first_half = lax.broadcasted_iota(jnp.int32, (length, 2 * HEAD_DIM), 1) < HEAD_DIM
    sums = jnp.zeros((length, MISC), F32)
    for pair in range(HEADS // 2):
        cols = slice(pair * 2 * HEAD_DIM, (pair + 1) * 2 * HEAD_DIM)
        mixed = []
        for side in range(2):
            scores = dot_nt(queries[:, cols] * (masks[side] * FACTOR), keys[:, cols])
            highest = jnp.max(scores, axis=-1, keepdims=True)
            expo = jnp.exp(scores - highest)
            total = jnp.sum(expo, axis=-1, keepdims=True)
            attention = (expo * (1.0 / total)).astype(BF16)
            sums = jnp.where(lanes == 2 * pair + side, highest + jnp.log(total), sums)
            mixed.append(dot(attention, values[:, cols]))
        o_ref[0, :, cols] = jnp.where(first_half, mixed[0], mixed[1]).astype(BF16)
    lse_ref[0] = sums
    middle = rows + (dot(o_ref[0], wo[...]) + ob)
    t_ref[0] = middle
    unit_two, _ = standardize(middle)
    hidden = (unit_two * egain + eshift).astype(BF16)
    logits = dot(hidden, misc[...])
    pair_experts = routes_ref[0]
    zero = jnp.sum(jnp.where(lanes == pair_experts[:, 0:1], logits, 0.0), axis=-1, keepdims=True)
    one = jnp.sum(jnp.where(lanes == pair_experts[:, 1:2], logits, 0.0), axis=-1, keepdims=True)
    gate_zero = 1.0 / (1.0 + jnp.exp(one - zero))
    gate_one = 1.0 / (1.0 + jnp.exp(zero - one))
    gates_ref[0, :, 0:1] = gate_zero
    gates_ref[0, :, 1:2] = gate_one
    drow = drow_ref[0]
    spread([drow[0:1, :], drow[1:2, :]], [hidden], outs, pl.program_id(0) == 0)


def combine_body(middle, gates_ref, dcol_ref, back, yzero_ref, yone_ref):
    dest = dcol_ref[0]
    gates = gates_ref[0]
    zero = pick(dest[:, 0:1], back)
    one = pick(dest[:, 1:2], back)
    if yzero_ref is not None:
        yzero_ref[0] = zero.astype(BF16)
        yone_ref[0] = one.astype(BF16)
    return middle + (gates[:, 0:1] * zero + gates[:, 1:2] * one), zero, one


def grads_body(upstream, zero, one, gates_ref, routes_ref, drow_ref, dz_ref, outs):
    length = upstream.shape[0]
    gates = gates_ref[0]
    gate_zero, gate_one = gates[:, 0:1], gates[:, 1:2]
    grad_zero = jnp.sum(zero * upstream, axis=-1, keepdims=True)
    grad_one = jnp.sum(one * upstream, axis=-1, keepdims=True)
    along = gate_zero * grad_zero + gate_one * grad_one
    lanes = lax.broadcasted_iota(jnp.int32, (length, MISC), 1)
    pair_experts = routes_ref[0]
    dz = jnp.where(lanes == pair_experts[:, 0:1], gate_zero * (grad_zero - along), 0.0)
    dz = dz + jnp.where(lanes == pair_experts[:, 1:2], gate_one * (grad_one - along), 0.0)
    dz_ref[0] = dz.astype(BF16)
    drow = drow_ref[0]
    spread(
        [drow[0:1, :], drow[1:2, :]],
        [(gate_zero * upstream).astype(BF16), (gate_one * upstream).astype(BF16)],
        outs,
        pl.program_id(0) == 0,
    )


def first_kernel(rows, routes, drow, wq, wk, wv, wo, misc, *outs):
    attend_body(rows[0], routes, drow, wq, wk, wv, wo, misc, *outs[:7], outs[7:])


def next_kernel(
    middle, gates, dcol, back, routes, drow, wq, wk, wv, wo, misc, rows_ref, yzero, yone, *outs
):
    rows, _, _ = combine_body(middle[0], gates, dcol, (back,), yzero, yone)
    rows_ref[0] = rows
    attend_body(rows, routes, drow, wq, wk, wv, wo, misc, *outs[:7], outs[7:])


def turn_kernel(middle, gates, dcol, back, cotangent, routes, drow, result, dz, out):
    rows, zero, one = combine_body(middle[0], gates, dcol, (back,), None, None)
    result[0] = rows
    grads_body(cotangent[0], zero, one, gates, routes, drow, dz, (out,))


def back_kernel(
    upstream, rows, middle, q_ref, k_ref, v_ref, o_ref, lse_ref, dz_ref, dcol, came,
    wq, wk, wv, wo, misc, *rest,
):
    bias, *rest = rest
    if len(rest) > 4:
        yzero, yone, gates_below, routes_below, drow_below, grad_ref, sent, dz_below, out, wgrad, vgrad = rest
    else:
        grad_ref, sent, wgrad, vgrad = rest
    first = pl.program_id(0) == 0
    length = rows.shape[1]
    width = rows.shape[2]
    qb, vb, ob, again, ashift, egain, eshift = vectors_of(misc)

    @pl.when(first)
    def _():
        wgrad[...] = jnp.zeros_like(wgrad)
        vgrad[...] = jnp.zeros_like(vgrad)

    def add_vector(number, value):
        vgrad[VEC_AT + number : VEC_AT + number + 1, :] += jnp.sum(value, axis=0, keepdims=True)

    unit_two, scale_two = standardize(middle[0])
    hidden = (unit_two * egain + eshift).astype(BF16)
    dz = dz_ref[0]
    dest = dcol[0]
    dhidden = dot_nt(dz, misc[...])
    lanes = lax.broadcasted_iota(jnp.int32, (length, came.shape[0]), 1)
    hit = (dest[:, 0:1] == lanes) | (dest[:, 1:2] == lanes)
    dhidden = dhidden + dot(hit.astype(F32).astype(BF16), came[...])
    wgrad[:, 4 * width :] += dot_tn(hidden, dz)
    add_vector(5, dhidden * unit_two)
    add_vector(6, dhidden)
    dmiddle = upstream[0] + standardize_back(dhidden, unit_two, scale_two, egain)
    dbranch = dmiddle.astype(BF16)
    wgrad[:, 3 * width : 4 * width] += dot_tn(o_ref[0], dbranch)
    add_vector(2, dbranch.astype(F32))
    dcontext = dot_nt(dbranch, wo[...]).astype(BF16)
    masks = lane_masks(length)
    first_half = lax.broadcasted_iota(jnp.int32, (length, 2 * HEAD_DIM), 1) < HEAD_DIM
    dqs, dks, dvs = [], [], []
    for pair in range(HEADS // 2):
        cols = slice(pair * 2 * HEAD_DIM, (pair + 1) * 2 * HEAD_DIM)
        keys = k_ref[0, :, cols]
        values = v_ref[0, :, cols]
        queries = q_ref[0, :, cols]
        dvalues, dqueries, dkeys = None, [], None
        for side in range(2):
            own_queries = queries * (masks[side] * FACTOR)
            own_context = dcontext[:, cols] * masks[side]
            scores = dot_nt(own_queries, keys)
            number = 2 * pair + side
            attention = jnp.exp(scores - lse_ref[0, :, number : number + 1])
            prob = dot_nt(own_context, values)
            weighed = attention * prob
            delta = jnp.sum(weighed, axis=-1, keepdims=True)
            dscores = (weighed - attention * delta).astype(BF16)
            dvalue = dot_tn(attention.astype(BF16), own_context)
            dkey = dot_tn(dscores, own_queries)
            dvalues = dvalue if dvalues is None else dvalues + dvalue
            dkeys = dkey if dkeys is None else dkeys + dkey
            dqueries.append(dot(dscores, keys))
        dqs.append((jnp.where(first_half, dqueries[0], dqueries[1]) * FACTOR).astype(BF16))
        dks.append(dkeys.astype(BF16))
        dvs.append(dvalues.astype(BF16))
    dq = jnp.concatenate(dqs, axis=1)
    dk = jnp.concatenate(dks, axis=1)
    dv = jnp.concatenate(dvs, axis=1)
    unit, scale = standardize(rows[0])
    low = (unit * again + ashift).astype(BF16)
    wgrad[:, 0:width] += dot_tn(low, dq)
    wgrad[:, width : 2 * width] += dot_tn(low, dk)
    wgrad[:, 2 * width : 3 * width] += dot_tn(low, dv)
    add_vector(0, dq.astype(F32))
    add_vector(1, dv.astype(F32))
    dlow = dot_nt(dq, wq[...]) + dot_nt(dk, wk[...]) + dot_nt(dv, wv[...])
    add_vector(3, dlow * unit)
    add_vector(4, dlow)
    grad = dmiddle + standardize_back(dlow, unit, scale, again)
    grad_ref[0] = grad
    if len(rest) > 4:
        grads_body(
            grad, yzero[0].astype(F32), yone[0].astype(F32), gates_below, routes_below, drow_below, dz_below,
            (out,),
        )

    @pl.when(pl.program_id(0) == pl.num_programs(0) - 1)
    def _():
        wgrad[:, 4 * width :] += vgrad[...].T
        sent[:, : 4 * width + MISC] = wgrad[...].astype(BF16)
        sent[:, 4 * width + MISC :] = bias[...]


def per_image(array):
    return pl.BlockSpec((1,) + array.shape[1:], lambda i: (i,) + (0,) * (len(array.shape) - 1))


def per_layer(array, layer):
    shape = (None, 1) + array.shape[2:]
    return pl.BlockSpec(shape, lambda i: (layer, i) + (0,) * (len(shape) - 2))


def whole(array):
    return pl.BlockSpec(array.shape, lambda i: (0,) * len(array.shape))


def packed_specs(packed):
    width = packed.shape[0]
    specs = [pl.BlockSpec((width, width), lambda i, n=n: (0, n)) for n in range(4)]
    return specs + [pl.BlockSpec((width, MISC), lambda i: (0, 4 * width // MISC))]


def call(body, grid, inputs, outputs, scratch=(), flops=0, aliases=None):
    shapes = [jax.ShapeDtypeStruct(s, t) for s, t, _ in outputs]
    return pl.pallas_call(
        body,
        grid=grid,
        in_specs=[s for _, s in inputs],
        out_specs=[s for _, _, s in outputs],
        out_shape=shapes,
        scratch_shapes=list(scratch),
        compiler_params=pltpu.CompilerParams(vmem_limit_bytes=VMEM),
        cost_estimate=pl.CostEstimate(flops=COST, bytes_accessed=COST, transcendentals=0),
    )(*[a for a, _ in inputs])


def images_out(images, length, columns, kind):
    shape = (images, length, columns)
    return (shape, kind, pl.BlockSpec((1, length, columns), lambda i: (i, 0, 0)))


def slots_out(slots, width):
    return [((slots, width), BF16, pl.BlockSpec((slots, width), lambda i: (0, 0)))]


def attend_outputs(images, length, width, slots):
    return [
        images_out(images, length, width, F32),
        images_out(images, length, width, BF16),
        images_out(images, length, width, BF16),
        images_out(images, length, width, BF16),
        images_out(images, length, width, BF16),
        images_out(images, length, MISC, F32),
        images_out(images, length, 2, F32),
    ] + slots_out(slots, width)


ROOT_HALF = 0.7071067811865476
ROOT_TWO_PI_INVERSE = 0.3989422804014327
MESH = pl.DeviceIdType.MESH


def order_of(count):
    return sorted(range(1, count), key=lambda k: -min(k, count - k))


def greet_all(peers):
    barrier = pltpu.get_barrier_semaphore()
    for peer in peers:
        pl.semaphore_signal(barrier, inc=1, device_id=peer, device_id_type=MESH)
    pl.semaphore_wait(barrier, len(peers))


class Swap:
    def __init__(self, sent, arrived, made, back, sems):
        self.sent, self.arrived, self.made, self.back = sent, arrived, made, back
        self.out_send, self.out_recv, self.home_send, self.home_recv, self.own = sems
        self.local, self.count = arrived.shape[0], arrived.shape[1]
        self.me = lax.axis_index("expert")

    def greet(self, others=()):
        greet_all([{"expert": lax.rem(self.me + k, self.count)} for k in range(1, self.count)] + list(others))

    def outward(self, j, k, peer):
        return pltpu.make_async_remote_copy(
            src_ref=self.sent.at[j, peer], dst_ref=self.arrived.at[j, self.me],
            send_sem=self.out_send.at[j, k], recv_sem=self.out_recv.at[j, k],
            device_id={"expert": peer}, device_id_type=MESH,
        )

    def homeward(self, j, k, peer):
        return pltpu.make_async_remote_copy(
            src_ref=self.made.at[j, peer], dst_ref=self.back.at[j, self.me],
            send_sem=self.home_send.at[j, k], recv_sem=self.home_recv.at[j, k],
            device_id={"expert": peer}, device_id_type=MESH,
        )

    def own_out(self, j):
        return pltpu.make_async_copy(self.sent.at[j, self.me], self.arrived.at[j, self.me], self.own.at[j])

    def own_home(self, j):
        return pltpu.make_async_copy(self.made.at[j, self.me], self.back.at[j, self.me], self.own.at[self.local + j])

    def send_all(self):
        for j in range(self.local):
            for k in order_of(self.count):
                self.outward(j, k, lax.rem(self.me + k, self.count)).start()
            self.own_out(j).start()

    def chip(self, turn):
        chips = self.count // 2
        return lax.rem(self.me // 2 - turn + chips, chips)

    def wait_chip(self, j, chip):
        for core in range(2):
            source = 2 * chip + core
            k = lax.rem(self.me - source + self.count, self.count)

            @pl.when(source != self.me)
            def _(k=k, source=source):
                pltpu.make_async_remote_copy(
                    src_ref=self.arrived.at[j, source], dst_ref=self.arrived.at[j, source],
                    send_sem=self.out_send.at[j, k], recv_sem=self.out_recv.at[j, k],
                    device_id={"expert": source}, device_id_type=MESH,
                ).wait_recv()

            @pl.when(source == self.me)
            def _():
                self.own_out(j).wait()

    def send_home(self, j, chip):
        for core in range(2):
            peer = 2 * chip + core
            k = lax.rem(peer - self.me + self.count, self.count)

            @pl.when(peer != self.me)
            def _(k=k, peer=peer):
                self.homeward(j, k, peer).start()

            @pl.when(peer == self.me)
            def _():
                self.own_home(j).start()

    def finish(self):
        for j in range(self.local):
            self.own_home(j).wait()
            for k in range(1, self.count):
                peer = lax.rem(self.me + k, self.count)
                self.outward(j, k, peer).wait_send()
                self.homeward(j, k, peer).wait()


def weight_blocks(weights, j, f):
    _, parts, rows, width = weights.shape
    share, take = width // parts, rows // 2
    each = FF_BLOCK // take
    first = weights[j, :, f * share : (f + 1) * share, :].reshape(width, width)
    second = weights[j, f * each : (f + 1) * each, take:, :].reshape(FF_BLOCK, width)
    return first, second


def expert_kernel(
    layer, sent, packed, mine, b1, b2, back, arrived_out, g_out, s_out, packed_out,
    arrived, made, weights, g_stage, s_stage, out_send, out_recv, home_send, home_recv, own, load, stores, last,
    share_send, share_recv,
):
    row = lax.axis_index("dp")
    parts = weights.shape[1]
    swap = Swap(sent, arrived, made, back, (out_send, out_recv, home_send, home_recv, own))
    local, count, capacity, width = arrived.shape
    chips = count // 2
    rows = 2 * capacity
    ff = g_out.shape[2]
    loads = [
        pltpu.make_async_copy(packed, weights.at[0], load.at[0]),
        pltpu.make_async_copy(mine, weights.at[1, row], load.at[1]),
    ]
    for copy in loads:
        copy.start()
    shares = [
        pltpu.make_async_remote_copy(
            src_ref=mine, dst_ref=weights.at[1, row], send_sem=share_send.at[k - 1], recv_sem=share_recv.at[k - 1],
            device_id={"dp": lax.rem(row + k, parts)}, device_id_type=MESH,
        )
        for k in range(1, parts)
    ]
    swap.greet([{"dp": lax.rem(row + k, parts)} for k in range(1, parts)])
    swap.send_all()
    for copy in shares:
        copy.start()
    packed_copy = pltpu.make_async_copy(weights.at[1], packed_out, last.at[1])

    def kept(j, slot, chip):
        place = pl.ds(pl.multiple_of(chip * rows, rows), rows)
        return (
            pltpu.make_async_copy(g_stage.at[slot], g_out.at[j, place, :], stores.at[0, slot]),
            pltpu.make_async_copy(s_stage.at[slot], s_out.at[j, place, :], stores.at[1, slot]),
        )

    for j in range(local):
        loads[j].wait()
        if j == 1:
            for copy in shares:
                copy.wait_recv()
            packed_copy.start()
        number = layer * local + j

        def chip_step(turn, carry, j=j, number=number):
            chip = swap.chip(turn)
            slot = lax.rem(turn, 2)
            swap.wait_chip(j, chip)

            @pl.when(j * chips + turn >= 2)
            def _():
                for copy in kept(j, slot, chip):
                    copy.wait()

            x = arrived[j, pl.ds(2 * chip, 2)].reshape(rows, width)
            total = jnp.broadcast_to(b2[number : number + 1, :], (rows, width))
            for f in range(ff // FF_BLOCK):
                cols = slice(f * FF_BLOCK, (f + 1) * FF_BLOCK)
                first, second = weight_blocks(weights, j, f)
                inner = dot(x, first) + b1[number : number + 1, cols]
                normal = 0.5 * (1.0 + lax.erf(inner * ROOT_HALF))
                g = (inner * normal).astype(BF16)
                density = jnp.exp(-0.5 * inner * inner) * ROOT_TWO_PI_INVERSE
                g_stage[slot, :, cols] = g
                s_stage[slot, :, cols] = (normal + inner * density).astype(BF16)
                total = total + dot(g, second)
            made[j, pl.ds(2 * chip, 2)] = total.astype(BF16).reshape(2, capacity, width)
            swap.send_home(j, chip)
            for copy in kept(j, slot, chip):
                copy.start()
            return carry

        lax.fori_loop(0, chips, chip_step, 0)
    final = pltpu.make_async_copy(arrived, arrived_out, last.at[0])
    final.start()
    for slot in range(2):
        for copy in kept(0, slot, 0):
            copy.wait()
    swap.finish()
    for copy in shares:
        copy.wait_send()
    packed_copy.wait()
    final.wait()


def expert_back_kernel(with_above, *refs):
    if with_above:
        *refs, above_in, above_own, above_send, above_recv, above_load = refs
        refs = list(refs)
        above, above_sum = refs.pop(6), refs.pop(11)
    (
        sent, packed_first, packed_second, arrived_x, g_in, s_in, back, summed, out, db1, db2,
        arrived, made, weights, x, du, s_stage, g_stage, first_stage, second_stage, share_out, share_in,
        out_send, out_recv, home_send, home_recv, own, load, fetch, stores, share_send, share_recv,
    ) = refs
    swap = Swap(sent, arrived, made, back, (out_send, out_recv, home_send, home_recv, own))
    row = lax.axis_index("dp")
    local, count, capacity, width = arrived.shape
    chips = count // 2
    rows = 2 * capacity
    ff = g_in.shape[2]
    blocks = ff // FF_BLOCK
    _, parts, all_rows, _ = weights.shape
    share, take = width // parts, all_rows // 2
    each = FF_BLOCK // take
    loads = [
        pltpu.make_async_copy(packed, weights.at[j], load.at[j]) for j, packed in enumerate((packed_first, packed_second))
    ]
    loads.append(pltpu.make_async_copy(arrived_x, x, load.at[local]))
    for copy in loads:
        copy.start()

    def slopes(j, turn):
        slot = lax.rem(turn, 2)
        place = pl.ds(pl.multiple_of(swap.chip(turn) * rows, rows), rows)
        return pltpu.make_async_copy(s_in.at[j, place, :], s_stage.at[slot], fetch.at[0, slot])

    def activations(j, f):
        return pltpu.make_async_copy(
            g_in.at[j, :, f * FF_BLOCK : (f + 1) * FF_BLOCK], g_stage.at[f % 2], fetch.at[1, f % 2]
        )

    def results(j, f):
        return (
            pltpu.make_async_copy(
                first_stage.at[f % 2], out.at[:, j - 1, f * share : (f + 1) * share, :], stores.at[0, f % 2]
            ),
            pltpu.make_async_copy(
                second_stage.at[f % 2], out.at[f * each : (f + 1) * each, j - 1, take:, :], stores.at[1, f % 2]
            ),
        )

    def share_copy(k):
        peer = lax.rem(row + k, parts)
        return pltpu.make_async_remote_copy(
            src_ref=share_out.at[peer], dst_ref=share_in.at[k - 1],
            send_sem=share_send.at[k - 1], recv_sem=share_recv.at[k - 1],
            device_id={"dp": peer}, device_id_type=MESH,
        )

    slopes(0, 0).start()
    peers = [{"dp": lax.rem(row + k, parts)} for k in range(1, parts)]
    swap.greet(peers)
    swap.send_all()
    if with_above:
        above_copies = [
            pltpu.make_async_remote_copy(
                src_ref=above.at[lax.rem(row + k, parts)], dst_ref=above_in.at[k - 1],
                send_sem=above_send.at[k - 1], recv_sem=above_recv.at[k - 1],
                device_id=peers[k - 1], device_id_type=MESH,
            )
            for k in range(1, parts)
        ]
        above_copies.append(pltpu.make_async_copy(above.at[row], above_own, above_load))
        for copy in above_copies:
            copy.start()
    for j in range(local):
        loads[j].wait()
        activations(j, 0).start()

        def chip_step(turn, carry, j=j):
            chip = swap.chip(turn)
            slot = lax.rem(turn, 2)

            @pl.when(turn + 1 < chips)
            def _():
                slopes(j, turn + 1).start()

            swap.wait_chip(j, chip)
            slopes(j, turn).wait()
            dy = arrived[j, pl.ds(2 * chip, 2)].reshape(rows, width)
            place = pl.ds(pl.multiple_of(chip * rows, rows), rows)
            total = jnp.zeros((rows, width), F32)
            for f in range(blocks):
                cols = slice(f * FF_BLOCK, (f + 1) * FF_BLOCK)
                first, second = weight_blocks(weights, j, f)
                part = (dot_nt(dy, second) * s_stage[slot, :, cols].astype(F32)).astype(BF16)
                du[place, cols] = part
                total = total + dot_nt(part, first)
            made[j, pl.ds(2 * chip, 2)] = total.astype(BF16).reshape(2, capacity, width)
            swap.send_home(j, chip)
            return carry

        lax.fori_loop(0, chips, chip_step, 0)
        if j + 1 < local:
            slopes(j + 1, 0).start()
        if j == 0:
            loads[local].wait()
        dy = arrived[j].reshape(count * capacity, width)
        db2[j] = jnp.sum(dy.astype(F32), axis=0, keepdims=True)
        for f in range(blocks):
            cols = slice(f * FF_BLOCK, (f + 1) * FF_BLOCK)
            if f + 1 < blocks:
                activations(j, f + 1).start()
            if j > 1 or (j == 1 and f > 1):
                for copy in results(j, f):
                    copy.wait()
            part = du[:, cols]
            grad = dot_tn(x[j].reshape(count * capacity, width), part).astype(BF16)
            if j == 0:
                share_out[:, f * share : (f + 1) * share, :] = grad.reshape(parts, share, width)
            else:
                first_stage[f % 2] = grad.reshape(parts, share, width)
            db1[j, :, cols] = jnp.sum(part.astype(F32), axis=0, keepdims=True)
            activations(j, f).wait()
            grad = dot_tn(g_stage[f % 2], dy).astype(BF16).reshape(each, take, width)
            if j == 0:
                share_out[f * each : (f + 1) * each, take:, :] = grad
            else:
                second_stage[f % 2] = grad
                for copy in results(j, f):
                    copy.start()
        if j == 0:
            for k in range(1, parts):
                share_copy(k).start()
    if with_above:
        for copy in above_copies:
            copy.wait()
        total = above_own[...].astype(F32)
        for k in range(1, parts):
            total = total + above_in[k - 1].astype(F32)
        above_sum[...] = total.astype(BF16)
    for k in range(1, parts):
        share_copy(k).wait_recv()
    step = 64

    def add_up(turn, carry):
        place = pl.ds(pl.multiple_of(turn * step, step), step)
        total = share_out[row, place, :].astype(F32)
        for k in range(1, parts):
            total = total + share_in[k - 1, place, :].astype(F32)
        summed[place, :] = total
        return carry

    lax.fori_loop(0, all_rows // step, add_up, 0)
    for k in range(1, parts):
        share_copy(k).wait_send()
    for f in range(2):
        for copy in results(1, f):
            copy.wait()
    swap.finish()


def swap_sems(local, count):
    pairs = [pltpu.SemaphoreType.DMA((local, count))] * 4
    return pairs + [pltpu.SemaphoreType.DMA((2 * local,))]


def expert_call(body, inputs, outputs, scratch, number):
    def spec(held):
        return pl.BlockSpec(memory_space=pltpu.VMEM if held else pl.ANY)

    shapes = [jax.ShapeDtypeStruct(s, t) for s, t, _ in outputs]
    return pl.pallas_call(
        body,
        in_specs=[spec(held) for _, held in inputs],
        out_specs=[spec(held) for _, _, held in outputs],
        out_shape=shapes,
        scratch_shapes=scratch,
        compiler_params=pltpu.CompilerParams(
            collective_id=number, has_side_effects=True, vmem_limit_bytes=VMEM
        ),
        cost_estimate=pl.CostEstimate(flops=COST, bytes_accessed=COST, transcendentals=0),
    )(*[a for a, _ in inputs])


def expert_forward(sent, packed, mine, biases, layer):
    b1, b2 = biases
    local, count, capacity, width = sent.shape
    ff = b1.shape[1]
    rows = 2 * capacity
    parts = packed.shape[0]
    slots = (local, count * capacity, ff)
    return expert_call(
        functools.partial(expert_kernel, layer),
        [(sent, False), (packed, False), (mine, False), (b1, True), (b2, True)],
        [
            (sent.shape, BF16, False), (sent.shape, BF16, False), (slots, BF16, False), (slots, BF16, False),
            (packed.shape, BF16, False),
        ],
        [
            pltpu.VMEM(sent.shape, BF16), pltpu.VMEM(sent.shape, BF16), pltpu.VMEM((local, *packed.shape), BF16),
            pltpu.VMEM((2, rows, ff), BF16), pltpu.VMEM((2, rows, ff), BF16),
        ] + swap_sems(local, count) + [
            pltpu.SemaphoreType.DMA((local,)), pltpu.SemaphoreType.DMA((2, 2)), pltpu.SemaphoreType.DMA((2,)),
            pltpu.SemaphoreType.DMA((parts - 1,)), pltpu.SemaphoreType.DMA((parts - 1,)),
        ],
        layer,
    )


def expert_backward(sent, weights, arrived, g, s, above, layer):
    local, count, capacity, width = sent.shape
    ff = g.shape[2]
    rows = 2 * capacity
    parts, all_rows, _ = weights[0].shape
    share, take = width // parts, all_rows // 2
    inputs = [(a, False) for a in (sent, *weights, arrived, g, s)]
    outputs = [
        (sent.shape, BF16, False), ((all_rows, width), F32, True), ((parts, local - 1, all_rows, width), BF16, False),
        ((local, 1, ff), F32, True), ((local, 1, width), F32, True),
    ]
    scratch = [
        pltpu.VMEM(sent.shape, BF16), pltpu.VMEM(sent.shape, BF16),
        pltpu.VMEM((local, parts, all_rows, width), BF16), pltpu.VMEM(sent.shape, BF16),
        pltpu.VMEM((count * capacity, ff), BF16), pltpu.VMEM((2, rows, ff), BF16),
        pltpu.VMEM((2, count * capacity, FF_BLOCK), BF16), pltpu.VMEM((2, parts, share, width), BF16),
        pltpu.VMEM((2, FF_BLOCK // take, take, width), BF16),
        pltpu.VMEM((parts, all_rows, width), BF16), pltpu.VMEM((parts - 1, all_rows, width), BF16),
    ] + swap_sems(local, count) + [
        pltpu.SemaphoreType.DMA((local + 1,)), pltpu.SemaphoreType.DMA((2, 2)), pltpu.SemaphoreType.DMA((2, 2)),
        pltpu.SemaphoreType.DMA((parts - 1,)), pltpu.SemaphoreType.DMA((parts - 1,)),
    ]
    if above is not None:
        inputs.append((above, False))
        outputs.append((above.shape[1:], BF16, True))
        scratch += [
            pltpu.VMEM((parts - 1, *above.shape[1:]), BF16), pltpu.VMEM(above.shape[1:], BF16),
            pltpu.SemaphoreType.DMA((parts - 1,)), pltpu.SemaphoreType.DMA((parts - 1,)), pltpu.SemaphoreType.DMA,
        ]
    return expert_call(
        functools.partial(expert_back_kernel, above is not None), inputs, outputs, scratch, LAYERS + layer
    )


def prepare_kernel(capacity, owners, *refs):
    squares, (router, *vectors), (inner_bias, outer_bias, routes) = refs[:4], refs[4:12], refs[12:15]
    out, above, b1, b2, dcol, drow = refs[15:21]
    mine, turned, inner_low, outer_low = refs[21:25]
    send, recv, pass_send, pass_recv, b1_send, b1_recv, b2_send, b2_recv, own = refs[25:]
    parts, share, _ = out.shape
    width = squares[0].shape[2]
    experts_all = router.shape[2]
    local, part_ff = inner_bias.shape[1:]
    half = share // 2
    row, me = lax.axis_index("dp"), lax.axis_index("expert")
    core = lax.rem(me, 2)
    sibling = {"expert": me + 1 - 2 * core}
    rows = pl.ds(pl.multiple_of(core * half, half), half)
    peers = [{"dp": lax.rem(row + k, parts)} for k in range(1, parts)]

    def pack(target, layer):
        for n in range(4):
            target[:, n * width : (n + 1) * width] = squares[n][layer].astype(BF16)
        turned[...] = jnp.zeros_like(turned)
        for n in range(7):
            turned[VEC_AT + n : VEC_AT + n + 1, :] = vectors[n][layer : layer + 1, :]
        target[:, 4 * width :] = turned[...].T.astype(BF16)
        target[:, 4 * width : 4 * width + experts_all] = router[layer].astype(BF16)

    def remote(source, target, send_sem, recv_sem, device):
        return pltpu.make_async_remote_copy(
            src_ref=source, dst_ref=target, send_sem=send_sem, recv_sem=recv_sem, device_id=device, device_id_type=MESH
        )

    def hand(k):
        place = out.at[lax.rem(row - k + parts, parts), rows]
        return remote(place, place, pass_send.at[k - 1], pass_recv.at[k - 1], sibling)

    pack(mine, 0)
    for layer in range(LAYERS):
        for j in range(local):
            n = layer * local + j
            inner_low[n : n + 1, :] = inner_bias[layer, j : j + 1, :].astype(BF16).astype(F32)
            outer_low[n : n + 1, :] = outer_bias[layer, j : j + 1, :].astype(BF16).astype(F32)
    greet_all([sibling] + peers)
    place = pl.ds(pl.multiple_of(row * part_ff, part_ff), part_ff)
    fetches = [
        remote(mine.at[rows], out.at[row, rows], send.at[k], recv.at[k], peers[k]) for k in range(parts - 1)
    ]
    singles = [
        remote(inner_low, b1.at[:, place], b1_send.at[k], b1_recv.at[k], peers[k]) for k in range(parts - 1)
    ] + [remote(outer_low, b2.at[row], b2_send.at[k], b2_recv.at[k], peers[k]) for k in range(parts - 1)]
    keeps = [
        pltpu.make_async_copy(mine, out.at[row], own.at[0]),
        pltpu.make_async_copy(inner_low, b1.at[:, place], own.at[1]),
        pltpu.make_async_copy(outer_low, b2.at[row], own.at[2]),
    ]
    for copy in fetches + singles + keeps:
        copy.start()
    pack(above, 1)

    length = routes.shape[2]
    lanes = lax.broadcasted_iota(jnp.int32, (length, MISC), 1)
    earlier = (
        lax.broadcasted_iota(jnp.int32, (length, length), 0) > lax.broadcasted_iota(jnp.int32, (length, length), 1)
    ).astype(F32).astype(BF16)
    for layer in range(LAYERS):
        seen = jnp.zeros((1, MISC), F32)
        for image in range(routes.shape[1]):
            hots, dests = [], []
            for k in range(2):
                hots.append((lanes == routes[layer, image, :, k : k + 1]).astype(F32))
            counts = hots[0] + hots[1]
            before = dot(earlier, counts.astype(BF16)) + seen
            seen = seen + jnp.sum(counts, axis=0, keepdims=True)
            for k in range(2):
                slot = jnp.sum(hots[k] * before, axis=-1, keepdims=True)
                expert = routes[layer, image, :, k : k + 1].astype(F32)
                owner = jnp.floor(expert * (1.0 / local))
                place = ((expert - owner * local) * owners + owner) * capacity + slot
                dests.append(jnp.where(slot < capacity, place, -1.0))
                dcol[layer, image, :, k : k + 1] = dests[k].astype(jnp.int32)
            both = jnp.where(lanes == 0, dests[0], jnp.where(lanes == 1, dests[1], 0.0))
            drow[layer, image] = both.T[0:2, :].astype(jnp.int32)

    for k in range(1, parts):
        fetches[k - 1].wait_recv()
        hand(k).start()
    for k in range(1, parts):
        fetches[k - 1].wait_send()
        hand(k).wait()
    for copy in singles + keeps:
        copy.wait()


def prepare(squares, router, vectors, inner_bias, outer_bias, routes, parts, owners, number):
    layers, share, width = squares[0].shape
    experts_all = router.shape[2]
    local, part_ff = inner_bias.shape[1:]
    _, images, length, _ = routes.shape
    capacity = (10 * images * length // (4 * experts_all) + 7) // 8 * 8
    columns = 4 * width + MISC
    count = layers * local
    sems = [pltpu.SemaphoreType.DMA((parts - 1,))] * 8 + [pltpu.SemaphoreType.DMA((3,))]
    inputs = [*squares, router, *vectors, inner_bias, outer_bias, routes]
    out, above, b1, b2, dcol, drow = expert_call(
        functools.partial(prepare_kernel, capacity, owners), [(a, True) for a in inputs],
        [
            ((parts, share, columns), BF16, False), ((share, columns), BF16, True),
            ((count, part_ff * parts), F32, False), ((parts, count, share), F32, False),
            ((layers, images, length, 2), jnp.int32, True), ((layers, images, 2, length), jnp.int32, True),
        ],
        [
            pltpu.VMEM((share, columns), BF16), pltpu.VMEM((MISC, share), F32),
            pltpu.VMEM((count, part_ff), F32), pltpu.VMEM((count, share), F32),
        ] + sems,
        number,
    )
    b2 = jnp.transpose(b2, (1, 0, 2)).reshape(count, width)
    return out.reshape(width, columns), above, (b1, b2), dcol, drow, capacity


def settle_kernel(
    grads, above, final, own, paired, own_above, paired_above, scattered, total, chips_in,
    pair_send, pair_recv, local, dp_send, dp_recv, out_send, out_recv, back_send, back_recv, pass_send, pass_recv,
):
    parts, share, columns = grads.shape
    half = share // 2
    row, me = lax.axis_index("dp"), lax.axis_index("expert")
    core, chip = lax.rem(me, 2), me // 2
    chips = chips_in.shape[0] + 1
    block = columns // chips
    sibling = {"expert": me + 1 - 2 * core}
    mine = pl.ds(pl.multiple_of(core * half, half), half)
    other = pl.ds(pl.multiple_of((1 - core) * half, half), half)

    def remote(source, target, send, recv, device):
        return pltpu.make_async_remote_copy(
            src_ref=source, dst_ref=target, send_sem=send, recv_sem=recv, device_id=device, device_id_type=MESH
        )

    def cols(number):
        return pl.ds(pl.multiple_of(number * block, block), block)

    def chip_at(k):
        return lax.rem(chip + k + chips, chips)

    dp_peers = [{"dp": lax.rem(row + k, parts)} for k in range(1, parts)]
    chip_peers = [{"expert": 2 * chip_at(k) + core} for k in range(1, chips)]
    greet_all([sibling] + dp_peers + chip_peers)

    pairs, locals_ = [], []
    for i in range(parts):
        part = lax.rem(row + 1 + i, parts)
        pairs.append(remote(grads.at[part, other], paired.at[part], pair_send.at[i], pair_recv.at[i], sibling))
        locals_.append(pltpu.make_async_copy(grads.at[part, mine], own.at[part], local.at[i]))
    pairs.append(remote(above.at[other], paired_above, pair_send.at[parts], pair_recv.at[parts], sibling))
    locals_.append(pltpu.make_async_copy(above.at[mine], own_above, local.at[parts]))
    for pair, keep in zip(pairs, locals_):
        pair.start()
        keep.start()
    scatters = []
    for i in range(parts):
        part = lax.rem(row + 1 + i, parts)
        pairs[i].wait_recv()
        locals_[i].wait()
        own[part] = (own[part].astype(F32) + paired[part].astype(F32)).astype(BF16)
        if i + 1 < parts:
            scatters.append(remote(own.at[part], scattered.at[i], dp_send.at[i], dp_recv.at[i], dp_peers[i]))
            scatters[i].start()
    pairs[parts].wait_recv()
    locals_[parts].wait()
    total[1] = (own_above[...].astype(F32) + paired_above[...].astype(F32)).astype(BF16)
    value = own[row].astype(F32)
    for i in range(parts - 1):
        scatters[i].wait_recv()
        value = value + scattered[i].astype(F32)
    total[0] = value.astype(BF16)
    outs = []
    for k in range(1, chips):
        outs.append(remote(
            total.at[:, :, cols(chip_at(k))], chips_in.at[k - 1], out_send.at[k - 1], out_recv.at[k - 1],
            chip_peers[k - 1],
        ))
        outs[-1].start()
    value = total[:, :, cols(chip)].astype(F32)
    for k in range(1, chips):
        outs[k - 1].wait_recv()
        value = value + chips_in[k - 1].astype(F32)
    final[:, mine, cols(chip)] = value.astype(BF16)
    backs, hands = [], []
    place = final.at[:, mine, cols(chip)]
    for k in range(1, chips):
        backs.append(remote(place, place, back_send.at[k - 1], back_recv.at[k - 1], chip_peers[k - 1]))
        backs[-1].start()
    hands.append(remote(place, place, pass_send.at[0], pass_recv.at[0], sibling))
    hands[0].start()
    for k in range(1, chips):
        backs[k - 1].wait_recv()
        place = final.at[:, mine, cols(chip_at(-k))]
        hands.append(remote(place, place, pass_send.at[k], pass_recv.at[k], sibling))
        hands[k].start()
    for copy in pairs + scatters + outs + backs:
        copy.wait_send()
    for copy in hands:
        copy.wait()


def settle_dense(grads, above, chips, number):
    parts, share, columns = grads.shape
    half = share // 2
    quarter = pltpu.VMEM((half, columns), BF16)
    sems = [parts + 1] * 3 + [parts - 1] * 2 + [chips - 1] * 4 + [chips] * 2
    return expert_call(
        settle_kernel, [(grads, False), (above, False)], [((2, share, columns), BF16, True)],
        [
            pltpu.VMEM((parts, half, columns), BF16), pltpu.VMEM((parts, half, columns), BF16), quarter, quarter,
            pltpu.VMEM((parts - 1, half, columns), BF16), pltpu.VMEM((2, half, columns), BF16),
            pltpu.VMEM((chips - 1, 2, half, columns // chips), BF16),
        ] + [pltpu.SemaphoreType.DMA((n,)) for n in sems],
        number,
    )[0]


def unpack_kernel(*refs):
    count = 2 * LAYERS
    pieces, both = refs[:count], refs[count]
    squares, router, vectors, biases, inner, outer = refs[count + 1 : count + 5], *refs[count + 5 :]
    layer = pl.program_id(0)
    share = both.shape[1]
    width = squares[0].shape[2]
    for n in range(4):
        squares[n][0] = both[0, :, n * width : (n + 1) * width].astype(F32)
    misc = both[0, :, 4 * width : 4 * width + MISC].astype(F32)
    router[0] = misc[:, : router.shape[2]]
    turned = misc.T
    vectors[0] = turned[VEC_AT : VEC_AT + 8, :]
    biases[0] = both[0, :, 4 * width + MISC :].astype(F32)
    blocks = inner.shape[3] // FF_BLOCK

    for number in range(LAYERS):

        @pl.when(layer == number)
        def _(number=number):
            for j in range(2):
                piece = pieces[2 * number + j]
                for f in range(blocks):
                    inner[0, j, :, f * FF_BLOCK : (f + 1) * FF_BLOCK] = piece[
                        f * share : (f + 1) * share, :
                    ].astype(F32)
                outer[0, j] = piece[blocks * share :, :].astype(F32)


def unpack(pieces, both, local, ff, experts_all):
    layers, share, columns = both.shape
    rows, width = pieces[0].shape
    take = rows // 2
    by_layer = lambda *shape: ((layers, *shape), F32, pl.BlockSpec((1, *shape), lambda i: (i,) + (0,) * len(shape)))
    return call(
        unpack_kernel, (layers,),
        [(p, whole(p)) for p in pieces] + [(both, pl.BlockSpec((1, share, columns), lambda i: (i, 0, 0)))],
        [by_layer(share, width)] * 4 + [
            by_layer(share, experts_all), by_layer(8, share), by_layer(share, columns - 4 * width - MISC),
            by_layer(local, share, ff), by_layer(local, take, width),
        ],
    )


def shards(
    images, cotangent, routes, query_weight, key_weight, value_weight, output_weight, router_weight, query_bias,
    value_bias, output_bias, attend_gain, attend_shift, expert_gain, expert_shift, inner_weight, inner_bias,
    outer_weight, outer_bias,
):
    count, length, width = images.shape
    parts = lax.axis_size("dp")
    owners = lax.axis_size("expert")
    experts_all = router_weight.shape[2]
    local = inner_weight.shape[1]
    ff = inner_weight.shape[3]
    share = width // parts
    tokens = count * length
    squares = (query_weight, key_weight, value_weight, output_weight)
    vectors = (query_bias, value_bias, output_bias, attend_gain, attend_shift, expert_gain, expert_shift)
    bias_columns = ff // width + 1
    columns = 4 * width + MISC + experts_all * bias_columns
    columns = -(-columns // (MISC * (owners // 2))) * MISC * (owners // 2)
    bias_room = columns - 4 * width - MISC

    mine = []
    for layer in range(LAYERS):
        for j in range(local):
            first = inner_weight[layer, j].reshape(share, ff // FF_BLOCK, FF_BLOCK)
            first = jnp.transpose(first, (1, 0, 2)).reshape(ff // parts, width)
            mine.append(jnp.concatenate([first, outer_weight[layer, j]], axis=0).astype(BF16))
    dense, above, expert_biases, dcol, drow, capacity = prepare(
        squares, router_weight, vectors, inner_bias, outer_bias, routes, parts, owners, 2 * LAYERS
    )
    packed = [dense, lax.all_gather(above, "dp", axis=0, tiled=True)]
    firsts = [lax.all_gather(mine[layer * local], "dp", axis=0, tiled=False) for layer in range(LAYERS)]
    slots = experts_all * capacity
    dense_flops = 8 * tokens * width * width + 4 * tokens * slots * width

    saved = []
    back = None
    rows = images
    for layer in range(LAYERS):
        weights = [(packed[layer], s) for s in packed_specs(packed[layer])]
        routing = [(routes, per_layer(routes, layer)), (drow, per_layer(drow, layer))]
        outputs = attend_outputs(count, length, width, slots)
        if layer == 0:
            done = call(
                first_kernel, (count,), [(rows, per_image(rows))] + routing + weights, outputs, flops=dense_flops
            )
            picked = None
        else:
            before = saved[-1]
            done = call(
                next_kernel, (count,),
                [
                    (before["middle"], per_image(before["middle"])),
                    (before["gates"], per_image(before["gates"])),
                    (dcol, per_layer(dcol, layer - 1)),
                    (back, whole(back)),
                ] + routing + weights,
                [
                    images_out(count, length, width, F32),
                    images_out(count, length, width, BF16),
                    images_out(count, length, width, BF16),
                ] + outputs,
                flops=dense_flops,
            )
            rows, *picked = done[:3]
            done = done[3:]
            before["picked"] = picked
        middle, queries, keys, values, context, sums, gates = done[:7]
        sent = done[7].reshape(local, owners, capacity, width)
        back, arrived, g, s, second = expert_forward(
            sent, firsts[layer], mine[layer * local + 1], expert_biases, layer
        )
        back = back.reshape(slots, width)
        saved.append({
            "rows": rows, "middle": middle, "attend": (queries, keys, values, context, sums), "gates": gates,
            "experts": (arrived, g, s), "weights": (firsts[layer], second),
        })

    last = saved[-1]
    result, dz, sent = call(
        turn_kernel, (count,),
        [(last["middle"], per_image(last["middle"])), (last["gates"], per_image(last["gates"]))]
        + [(dcol, per_layer(dcol, LAYERS - 1)), (back, whole(back))]
        + [(cotangent, per_image(cotangent)), (routes, per_layer(routes, LAYERS - 1)), (drow, per_layer(drow, LAYERS - 1))],
        [images_out(count, length, width, F32), images_out(count, length, MISC, BF16)] + slots_out(slots, width),
        flops=dense_flops,
    )
    upstream = cotangent
    finished = []
    waiting = []
    wgrad = None
    for layer in reversed(range(LAYERS)):
        kept = saved[layer]
        sent = sent.reshape(local, owners, capacity, width)
        came, shares, grads, db1, db2, *above = expert_backward(
            sent, kept["weights"], *kept["experts"], wgrad, layer
        )
        came = came.reshape(slots, width)
        came, waiting = lax.optimization_barrier((came, waiting))
        finished += waiting
        waiting = [shares, lax.psum_scatter(grads, "dp", scatter_dimension=0, tiled=False)]
        own = [
            jnp.concatenate([db1[j].reshape(width, ff // width), db2[j].reshape(width, 1)], axis=1)
            for j in range(local)
        ]
        first_column = lax.axis_index("expert") * (local * bias_columns)
        bias = lax.dynamic_update_slice(
            jnp.zeros((width, bias_room), F32), jnp.concatenate(own, axis=1), (0, first_column)
        ).astype(BF16)
        weights = [(packed[layer], s) for s in packed_specs(packed[layer])]
        inputs = [upstream, kept["rows"], kept["middle"], *kept["attend"], dz]
        inputs = [(a, per_image(a)) for a in inputs]
        inputs += [(dcol, per_layer(dcol, layer)), (came, whole(came))] + weights
        inputs += [(bias, whole(bias))]
        outputs = [
            images_out(count, length, width, F32),
            (
                (width, 4 * width + MISC + bias_room), BF16,
                pl.BlockSpec((width, 4 * width + MISC + bias_room), lambda i: (0, 0)),
            ),
        ]
        if layer > 0:
            below = saved[layer - 1]
            inputs += [(a, per_image(a)) for a in (*below["picked"], below["gates"])]
            inputs += [(a, per_layer(a, layer - 1)) for a in (routes, drow)]
            outputs += [images_out(count, length, MISC, BF16)] + slots_out(slots, width)
        done = call(
            back_kernel, (count,), inputs, outputs,
            [pltpu.VMEM((width, 4 * width + MISC), F32), pltpu.VMEM((MISC, width), F32)], flops=3 * dense_flops,
        )
        upstream, wgrad = done[:2]
        if layer > 0:
            dz, sent = done[2:]
        wgrad = wgrad.reshape(parts, share, columns)
    both = settle_dense(wgrad, above[0], owners // 2, 2 * LAYERS + 1)
    pieces = [waiting[0], waiting[1][0], finished[0], finished[1][0]]
    *squares, router, vectors, biases, inner, outer = unpack(pieces, both, local, ff, experts_all)
    own = lax.dynamic_slice_in_dim(biases, lax.axis_index("expert") * (local * bias_columns), local * bias_columns, 2)
    own = jnp.transpose(own.reshape(LAYERS, share, local, bias_columns), (0, 2, 1, 3))
    return (
        result,
        upstream,
        *squares,
        router,
        *[vectors[:, n] for n in range(7)],
        inner,
        own[..., :-1].reshape(LAYERS, local, ff // parts),
        outer,
        own[..., -1],
    )


def solution(mesh):
    both = P(("dp", "expert"), None, None)
    square = P(None, "dp", None)
    vector = P(None, "dp")
    matrix = P(None, "expert", "dp", None)
    bias = P(None, "expert", "dp")
    grads = (square,) * 5 + (vector,) * 7 + (matrix, bias, matrix, bias)
    return jax.shard_map(
        shards,
        mesh=mesh,
        in_specs=(both, both, P(None, ("dp", "expert"), None, None)) + grads,
        out_specs=(both, both) + grads,
        check_vma=False,
    )
```

```python
import functools

import jax
import jax.numpy as jnp
from jax import lax
from jax.experimental import pallas as pl
from jax.experimental.pallas import tpu as pltpu
from jax.sharding import PartitionSpec as P

HEADS = 8
HEAD_DIM = 64
LAYERS = 2
EPSILON = 1e-06
FACTOR = HEAD_DIM**-0.5
VEC_AT = 64
MISC = 128
FF_BLOCK = 512
COST = 1024
VMEM = 56 * 1024 * 1024

MESH = pl.DeviceIdType.MESH
F32 = jnp.float32
BF16 = jnp.bfloat16


def dot(a, b):
    return jnp.dot(a, b, preferred_element_type=F32)


def dot_nt(a, b):
    return lax.dot_general(a, b, (((1,), (1,)), ((), ())), preferred_element_type=F32)


def dot_tn(a, b):
    return lax.dot_general(a, b, (((0,), (0,)), ((), ())), preferred_element_type=F32)


def standardize(rows):
    mean_value = jnp.mean(rows, axis=-1, keepdims=True)
    centered = rows - mean_value
    variance = jnp.mean(centered * centered, axis=-1, keepdims=True)
    scale = lax.rsqrt(variance + EPSILON)
    return centered * scale, scale


def standardize_back(upstream, unit, scale, gain):
    along = upstream * gain
    inner = (
        along
        - jnp.mean(along, axis=-1, keepdims=True)
        - unit * jnp.mean(along * unit, axis=-1, keepdims=True)
    )
    return inner * scale


def vectors_of(misc_ref):
    turned = misc_ref[...].astype(F32).T
    return [turned[VEC_AT + n : VEC_AT + n + 1, :] for n in range(7)]


def pick(dest, buffers):
    total = None
    for number, buffer in enumerate(buffers):
        count = buffer.shape[0]
        lanes = lax.broadcasted_iota(jnp.int32, (dest.shape[0], count), 1)
        chosen = (dest - number * count == lanes).astype(F32).astype(BF16)
        part = dot(chosen, buffer[...])
        total = part if total is None else total + part
    return total


def lane_masks(length):
    lanes = lax.broadcasted_iota(jnp.int32, (length, 2 * HEAD_DIM), 1)
    return (lanes < HEAD_DIM).astype(F32).astype(BF16), (lanes >= HEAD_DIM).astype(F32).astype(BF16)


def attend_body(
    rows, routes_ref, wq, wk, wv, wo, misc,
    t_ref, q_ref, k_ref, v_ref, o_ref, lse_ref, gates_ref, hidden_ref,
):
    length = rows.shape[0]
    qb, vb, ob, again, ashift, egain, eshift = vectors_of(misc)
    unit, _ = standardize(rows)
    low = (unit * again + ashift).astype(BF16)
    queries = (dot(low, wq[...]) + qb).astype(BF16)
    keys = dot(low, wk[...]).astype(BF16)
    values = (dot(low, wv[...]) + vb).astype(BF16)
    q_ref[0] = queries
    k_ref[0] = keys
    v_ref[0] = values
    masks = lane_masks(length)
    lanes = lax.broadcasted_iota(jnp.int32, (length, MISC), 1)
    first_half = lax.broadcasted_iota(jnp.int32, (length, 2 * HEAD_DIM), 1) < HEAD_DIM
    sums = jnp.zeros((length, MISC), F32)
    for pair in range(HEADS // 2):
        cols = slice(pair * 2 * HEAD_DIM, (pair + 1) * 2 * HEAD_DIM)
        mixed = []
        for side in range(2):
            scores = dot_nt(queries[:, cols] * (masks[side] * FACTOR), keys[:, cols])
            highest = jnp.max(scores, axis=-1, keepdims=True)
            expo = jnp.exp(scores - highest)
            total = jnp.sum(expo, axis=-1, keepdims=True)
            attention = (expo * (1.0 / total)).astype(BF16)
            sums = jnp.where(lanes == 2 * pair + side, highest + jnp.log(total), sums)
            mixed.append(dot(attention, values[:, cols]))
        o_ref[0, :, cols] = jnp.where(first_half, mixed[0], mixed[1]).astype(BF16)
    lse_ref[0] = sums
    middle = rows + (dot(o_ref[0], wo[...]) + ob)
    t_ref[0] = middle
    unit_two, _ = standardize(middle)
    hidden = (unit_two * egain + eshift).astype(BF16)
    logits = dot(hidden, misc[...])
    pair_experts = routes_ref[0]
    zero = jnp.sum(jnp.where(lanes == pair_experts[:, 0:1], logits, 0.0), axis=-1, keepdims=True)
    one = jnp.sum(jnp.where(lanes == pair_experts[:, 1:2], logits, 0.0), axis=-1, keepdims=True)
    gate_zero = 1.0 / (1.0 + jnp.exp(one - zero))
    gate_one = 1.0 / (1.0 + jnp.exp(zero - one))
    gates_ref[0, :, 0:1] = gate_zero
    gates_ref[0, :, 1:2] = gate_one
    hidden_ref[0] = hidden


def combine_body(middle, gates_ref, dcol_ref, back, yzero_ref, yone_ref):
    dest = dcol_ref[0]
    gates = gates_ref[0]
    zero = pick(dest[:, 0:1], back)
    one = pick(dest[:, 1:2], back)
    if yzero_ref is not None:
        yzero_ref[0] = zero.astype(BF16)
        yone_ref[0] = one.astype(BF16)
    return middle + (gates[:, 0:1] * zero + gates[:, 1:2] * one), zero, one


def grads_body(upstream, zero, one, gates_ref, routes_ref, dz_ref, zero_ref, one_ref):
    length = upstream.shape[0]
    gates = gates_ref[0]
    gate_zero, gate_one = gates[:, 0:1], gates[:, 1:2]
    grad_zero = jnp.sum(zero * upstream, axis=-1, keepdims=True)
    grad_one = jnp.sum(one * upstream, axis=-1, keepdims=True)
    along = gate_zero * grad_zero + gate_one * grad_one
    lanes = lax.broadcasted_iota(jnp.int32, (length, MISC), 1)
    pair_experts = routes_ref[0]
    dz = jnp.where(lanes == pair_experts[:, 0:1], gate_zero * (grad_zero - along), 0.0)
    dz = dz + jnp.where(lanes == pair_experts[:, 1:2], gate_one * (grad_one - along), 0.0)
    dz_ref[0] = dz.astype(BF16)
    zero_ref[0] = (gate_zero * upstream).astype(BF16)
    one_ref[0] = (gate_one * upstream).astype(BF16)


def first_kernel(rows, routes, wq, wk, wv, wo, misc, *outs):
    attend_body(rows[0], routes, wq, wk, wv, wo, misc, *outs)


def next_kernel(
    middle, gates, dcol, back, routes, wq, wk, wv, wo, misc, rows_ref, yzero, yone, *outs
):
    rows, _, _ = combine_body(middle[0], gates, dcol, (back,), yzero, yone)
    rows_ref[0] = rows
    attend_body(rows, routes, wq, wk, wv, wo, misc, *outs)


def turn_kernel(middle, gates, dcol, back, cotangent, routes, result, dz, zero_ref, one_ref):
    rows, zero, one = combine_body(middle[0], gates, dcol, (back,), None, None)
    result[0] = rows
    grads_body(cotangent[0], zero, one, gates, routes, dz, zero_ref, one_ref)


def back_kernel(
    upstream, rows, middle, q_ref, k_ref, v_ref, o_ref, lse_ref, dz_ref, dcol, came,
    wq, wk, wv, wo, misc, *rest,
):
    if len(rest) > 4:
        yzero, yone, gates_below, routes_below, grad_ref, sent, dz_below, zero_ref, one_ref, wgrad, vgrad = rest
    else:
        grad_ref, sent, wgrad, vgrad = rest
    first = pl.program_id(0) == 0
    length = rows.shape[1]
    width = rows.shape[2]
    qb, vb, ob, again, ashift, egain, eshift = vectors_of(misc)

    @pl.when(first)
    def _():
        wgrad[...] = jnp.zeros_like(wgrad)
        vgrad[...] = jnp.zeros_like(vgrad)

    def add_vector(number, value):
        vgrad[VEC_AT + number : VEC_AT + number + 1, :] += jnp.sum(value, axis=0, keepdims=True)

    unit_two, scale_two = standardize(middle[0])
    hidden = (unit_two * egain + eshift).astype(BF16)
    dz = dz_ref[0]
    dest = dcol[0]
    dhidden = dot_nt(dz, misc[...])
    lanes = lax.broadcasted_iota(jnp.int32, (length, came.shape[0]), 1)
    hit = (dest[:, 0:1] == lanes) | (dest[:, 1:2] == lanes)
    dhidden = dhidden + dot(hit.astype(F32).astype(BF16), came[...])
    wgrad[:, 4 * width :] += dot_tn(hidden, dz)
    add_vector(5, dhidden * unit_two)
    add_vector(6, dhidden)
    dmiddle = upstream[0] + standardize_back(dhidden, unit_two, scale_two, egain)
    dbranch = dmiddle.astype(BF16)
    wgrad[:, 3 * width : 4 * width] += dot_tn(o_ref[0], dbranch)
    add_vector(2, dbranch.astype(F32))
    dcontext = dot_nt(dbranch, wo[...]).astype(BF16)
    masks = lane_masks(length)
    first_half = lax.broadcasted_iota(jnp.int32, (length, 2 * HEAD_DIM), 1) < HEAD_DIM
    dqs, dks, dvs = [], [], []
    for pair in range(HEADS // 2):
        cols = slice(pair * 2 * HEAD_DIM, (pair + 1) * 2 * HEAD_DIM)
        keys = k_ref[0, :, cols]
        values = v_ref[0, :, cols]
        queries = q_ref[0, :, cols]
        dvalues, dqueries, dkeys = None, [], None
        for side in range(2):
            own_queries = queries * (masks[side] * FACTOR)
            own_context = dcontext[:, cols] * masks[side]
            scores = dot_nt(own_queries, keys)
            number = 2 * pair + side
            attention = jnp.exp(scores - lse_ref[0, :, number : number + 1])
            prob = dot_nt(own_context, values)
            weighed = attention * prob
            delta = jnp.sum(weighed, axis=-1, keepdims=True)
            dscores = (weighed - attention * delta).astype(BF16)
            dvalue = dot_tn(attention.astype(BF16), own_context)
            dkey = dot_tn(dscores, own_queries)
            dvalues = dvalue if dvalues is None else dvalues + dvalue
            dkeys = dkey if dkeys is None else dkeys + dkey
            dqueries.append(dot(dscores, keys))
        dqs.append((jnp.where(first_half, dqueries[0], dqueries[1]) * FACTOR).astype(BF16))
        dks.append(dkeys.astype(BF16))
        dvs.append(dvalues.astype(BF16))
    dq = jnp.concatenate(dqs, axis=1)
    dk = jnp.concatenate(dks, axis=1)
    dv = jnp.concatenate(dvs, axis=1)
    unit, scale = standardize(rows[0])
    low = (unit * again + ashift).astype(BF16)
    wgrad[:, 0:width] += dot_tn(low, dq)
    wgrad[:, width : 2 * width] += dot_tn(low, dk)
    wgrad[:, 2 * width : 3 * width] += dot_tn(low, dv)
    add_vector(0, dq.astype(F32))
    add_vector(1, dv.astype(F32))
    dlow = dot_nt(dq, wq[...]) + dot_nt(dk, wk[...]) + dot_nt(dv, wv[...])
    add_vector(3, dlow * unit)
    add_vector(4, dlow)
    grad = dmiddle + standardize_back(dlow, unit, scale, again)
    grad_ref[0] = grad
    if len(rest) > 4:
        grads_body(
            grad, yzero[0].astype(F32), yone[0].astype(F32), gates_below, routes_below, dz_below,
            zero_ref, one_ref,
        )

    @pl.when(pl.program_id(0) == pl.num_programs(0) - 1)
    def _():
        wgrad[:, 4 * width :] += vgrad[...].T
        sent[:, : 4 * width + MISC] = wgrad[...].astype(BF16)
        sent[:, 4 * width + MISC :] = jnp.zeros((width, sent.shape[1] - 4 * width - MISC), BF16)


def per_image(array):
    return pl.BlockSpec((1,) + array.shape[1:], lambda i: (i,) + (0,) * (len(array.shape) - 1))


def per_layer(array, layer):
    shape = (None, 1) + array.shape[2:]
    return pl.BlockSpec(shape, lambda i: (layer, i) + (0,) * (len(shape) - 2))


def whole(array):
    return pl.BlockSpec(array.shape, lambda i: (0,) * len(array.shape))


def packed_specs(packed):
    width = packed.shape[0]
    specs = [pl.BlockSpec((width, width), lambda i, n=n: (0, n)) for n in range(4)]
    return specs + [pl.BlockSpec((width, MISC), lambda i: (0, 4 * width // MISC))]


def call(body, grid, inputs, outputs, scratch=(), flops=0, aliases=None):
    shapes = [jax.ShapeDtypeStruct(s, t) for s, t, _ in outputs]
    return pl.pallas_call(
        body,
        grid=grid,
        in_specs=[s for _, s in inputs],
        out_specs=[s for _, _, s in outputs],
        out_shape=shapes,
        scratch_shapes=list(scratch),
        compiler_params=pltpu.CompilerParams(vmem_limit_bytes=VMEM),
        cost_estimate=pl.CostEstimate(flops=COST, bytes_accessed=COST, transcendentals=0),
    )(*[a for a, _ in inputs])


def images_out(images, length, columns, kind):
    shape = (images, length, columns)
    return (shape, kind, pl.BlockSpec((1, length, columns), lambda i: (i, 0, 0)))


def attend_outputs(images, length, width):
    return [
        images_out(images, length, width, F32),
        images_out(images, length, width, BF16),
        images_out(images, length, width, BF16),
        images_out(images, length, width, BF16),
        images_out(images, length, width, BF16),
        images_out(images, length, MISC, F32),
        images_out(images, length, 2, F32),
        images_out(images, length, width, BF16),
    ]


def greet_all(peers):
    barrier = pltpu.get_barrier_semaphore()
    for peer in peers:
        pl.semaphore_signal(barrier, inc=1, device_id=peer, device_id_type=MESH)
    pl.semaphore_wait(barrier, len(peers))


def remote(source, target, send, recv, device):
    return pltpu.make_async_remote_copy(
        src_ref=source, dst_ref=target, send_sem=send, recv_sem=recv, device_id=device, device_id_type=MESH
    )


class SharedGather:
    def __init__(self, mine, out, sems):
        send, recv, pass_send, pass_recv, own = sems
        parts, share, _ = out.shape
        half = share // 2
        row, me = lax.axis_index("dp"), lax.axis_index("expert")
        core = lax.rem(me, 2)
        sibling = {"expert": me + 1 - 2 * core}
        rows = pl.ds(pl.multiple_of(core * half, half), half)
        self.fetches, self.hands = [], []
        for k in range(1, parts):
            peer = {"dp": lax.rem(row + k, parts)}
            self.fetches.append(remote(mine.at[rows], out.at[row, rows], send.at[k - 1], recv.at[k - 1], peer))
            place = out.at[lax.rem(row - k + parts, parts), rows]
            self.hands.append(remote(place, place, pass_send.at[k - 1], pass_recv.at[k - 1], sibling))
        self.keep = pltpu.make_async_copy(mine, out.at[row], own)

    def start(self):
        for copy in self.fetches:
            copy.start()
        self.keep.start()

    def finish(self):
        for fetch, hand in zip(self.fetches, self.hands):
            fetch.wait_recv()
            hand.start()
        for fetch, hand in zip(self.fetches, self.hands):
            fetch.wait_send()
            hand.wait()
        self.keep.wait()


class Gather:
    def __init__(self, parts, mine, place, sems):
        send, recv, own = sems
        row = lax.axis_index("dp")
        self.first, self.second = [], []
        self.keep = pltpu.make_async_copy(mine, place(row), own)

        def add(group, source, target, peer):
            n = len(self.first) + len(self.second)
            group.append(remote(source, target, send.at[n], recv.at[n], {"dp": peer}))

        if parts != 4:
            for k in range(1, parts):
                add(self.first, mine, place(row), lax.rem(row + k, parts))
            return
        near, far = row + 1 - 2 * lax.rem(row, 2), lax.rem(row + 2, 4)
        quarter = mine.shape[0] // 4
        halves = [[slice(n * quarter, (n + 1) * quarter) for n in pair] for pair in ((0, 1), (2, 3))]
        for rows, peer in ((halves[0], near), (halves[1], far)):
            for part in rows:
                add(self.first, mine.at[part], place(row).at[part], peer)
        for rows, peer, other in ((halves[0], far, near), (halves[1], near, far)):
            for part in rows:
                add(self.second, mine.at[part], place(row).at[part], peer)
            for part in rows:
                add(self.second, place(other).at[part], place(other).at[part], peer)

    def start(self):
        for copy in self.first:
            copy.start()
        self.keep.start()

    def forward(self):
        for copy in self.first:
            copy.wait_recv()
        for copy in self.second:
            copy.start()

    def finish(self):
        for copy in self.second:
            copy.wait_recv()
        self.keep.wait()

    def drain(self):
        for copy in self.first + self.second:
            copy.wait_send()


def gather_sems(parts):
    count = 12 if parts == 4 else parts - 1
    return [pltpu.SemaphoreType.DMA((count,)), pltpu.SemaphoreType.DMA((count,)), pltpu.SemaphoreType.DMA]


def shared_sems(parts):
    return [pltpu.SemaphoreType.DMA((parts - 1,))] * 4 + [pltpu.SemaphoreType.DMA]


ROOT_HALF = 0.7071067811865476
ROOT_TWO_PI_INVERSE = 0.3989422804014327

class Swap:
    def __init__(self, sent, arrived, made, back, sems):
        self.sent, self.arrived, self.made, self.back = sent, arrived, made, back
        self.out_send, self.out_recv, self.home_send, self.home_recv, self.own = sems
        self.local, self.count = arrived.shape[0], arrived.shape[1]
        self.me = lax.axis_index("expert")

    def greet(self, others=()):
        greet_all([{"expert": lax.rem(self.me + k, self.count)} for k in range(1, self.count)] + list(others))

    def outward(self, j, k, peer):
        return pltpu.make_async_remote_copy(
            src_ref=self.sent.at[j, peer], dst_ref=self.arrived.at[j, self.me],
            send_sem=self.out_send.at[j, k], recv_sem=self.out_recv.at[j, k],
            device_id={"expert": peer}, device_id_type=MESH,
        )

    def homeward(self, j, k, peer):
        return pltpu.make_async_remote_copy(
            src_ref=self.made.at[j, peer], dst_ref=self.back.at[j, self.me],
            send_sem=self.home_send.at[j, k], recv_sem=self.home_recv.at[j, k],
            device_id={"expert": peer}, device_id_type=MESH,
        )

    def own_out(self, j):
        return pltpu.make_async_copy(self.sent.at[j, self.me], self.arrived.at[j, self.me], self.own.at[j])

    def own_home(self, j):
        return pltpu.make_async_copy(self.made.at[j, self.me], self.back.at[j, self.me], self.own.at[self.local + j])

    def send_all(self, sources, drow, layer):
        chips = self.count // 2
        capacity, width = self.sent.shape[2:]
        images, length, _ = sources[0].shape

        for j in range(self.local):

            def fill(turn, carry, j=j):
                sign = 2 * lax.rem(turn, 2) - 1
                chip = lax.rem(self.me // 2 + chips // 2 + sign * ((turn + 1) // 2) + chips, chips)
                first = (j * self.count + 2 * chip) * capacity
                slots = lax.broadcasted_iota(jnp.int32, (2 * capacity, length), 0) + first
                total = jnp.zeros((2 * capacity, width), F32)
                for image in range(images):
                    dest = drow[layer, image]
                    hits = [slots == dest[0:1, :], slots == dest[1:2, :]]
                    if len(sources) == 1:
                        hits = [hits[0] | hits[1]]
                    for hit, source in zip(hits, sources):
                        total = total + dot(hit.astype(F32).astype(BF16), source[image])
                self.sent[j, pl.ds(2 * chip, 2)] = total.astype(BF16).reshape(2, capacity, width)
                for core in range(2):
                    peer = 2 * chip + core
                    k = lax.rem(peer - self.me + self.count, self.count)

                    @pl.when(peer != self.me)
                    def _(k=k, peer=peer):
                        self.outward(j, k, peer).start()

                    @pl.when(peer == self.me)
                    def _():
                        self.own_out(j).start()

                return carry

            lax.fori_loop(0, chips, fill, 0)

    def chip(self, turn):
        chips = self.count // 2
        return lax.rem(self.me // 2 - turn + chips, chips)

    def wait_chip(self, j, chip):
        for core in range(2):
            source = 2 * chip + core
            k = lax.rem(self.me - source + self.count, self.count)

            @pl.when(source != self.me)
            def _(k=k, source=source):
                pltpu.make_async_remote_copy(
                    src_ref=self.arrived.at[j, source], dst_ref=self.arrived.at[j, source],
                    send_sem=self.out_send.at[j, k], recv_sem=self.out_recv.at[j, k],
                    device_id={"expert": source}, device_id_type=MESH,
                ).wait_recv()

            @pl.when(source == self.me)
            def _():
                self.own_out(j).wait()

    def send_home(self, j, chip):
        for core in range(2):
            peer = 2 * chip + core
            k = lax.rem(peer - self.me + self.count, self.count)

            @pl.when(peer != self.me)
            def _(k=k, peer=peer):
                self.homeward(j, k, peer).start()

            @pl.when(peer == self.me)
            def _():
                self.own_home(j).start()

    def finish(self):
        for j in range(self.local):
            self.own_home(j).wait()
            for k in range(1, self.count):
                peer = lax.rem(self.me + k, self.count)
                self.outward(j, k, peer).wait_send()
                self.homeward(j, k, peer).wait()


def weight_blocks(weights, j, f):
    _, parts, rows, width = weights.shape
    share, take = width // parts, rows // 2
    each = FF_BLOCK // take
    first = weights[j, :, f * share : (f + 1) * share, :].reshape(width, width)
    second = weights[j, f * each : (f + 1) * each, take:, :].reshape(FF_BLOCK, width)
    return first, second


def expert_kernel(layer, with_dense, *refs):
    if with_dense:
        *refs, n1, n2, n3, n4, n5 = refs
        refs = list(refs)
        dense = SharedGather(refs.pop(7), refs.pop(13), (n1, n2, n3, n4, n5))
    (
        hidden, drow, inner_first, outer_mine, mine, b1, b2, back, arrived_out, g_out, s_out, outer_out, packed_out,
        sent, arrived, made, weights, g_stage, s_stage, out_send, out_recv, home_send, home_recv, own, load, stores, last,
        *gather_refs,
    ) = refs
    row = lax.axis_index("dp")
    parts = weights.shape[1]
    take = outer_mine.shape[0]
    gathers = [
        Gather(parts, outer_mine, lambda p: weights.at[0, p, take:], gather_refs[:3]),
        Gather(parts, mine, lambda p: weights.at[1, p], gather_refs[3:]),
    ]
    swap = Swap(sent, arrived, made, back, (out_send, out_recv, home_send, home_recv, own))
    local, count, capacity, width = arrived.shape
    chips = count // 2
    rows = 2 * capacity
    ff = g_out.shape[2]
    first_load = pltpu.make_async_copy(inner_first, weights.at[0, :, :take], load)
    first_load.start()
    swap.greet([{"dp": lax.rem(row + k, parts)} for k in range(1, parts)])
    gathers[0].start()
    swap.send_all([hidden], drow, layer)
    gathers[0].forward()
    gathers[1].start()
    gathered = [
        pltpu.make_async_copy(weights.at[0, :, take:], outer_out, last.at[1]),
        pltpu.make_async_copy(weights.at[1], packed_out, last.at[2]),
    ]

    def kept(j, slot, chip):
        place = pl.ds(pl.multiple_of(chip * rows, rows), rows)
        return (
            pltpu.make_async_copy(g_stage.at[slot], g_out.at[j, place, :], stores.at[0, slot]),
            pltpu.make_async_copy(s_stage.at[slot], s_out.at[j, place, :], stores.at[1, slot]),
        )

    for j in range(local):
        if j == 0:
            first_load.wait()
        gathers[j].finish()
        gathered[j].start()
        number = layer * local + j

        def chip_step(turn, carry, j=j, number=number):
            chip = swap.chip(turn)
            slot = lax.rem(turn, 2)
            swap.wait_chip(j, chip)
            if j == 0:

                @pl.when(turn == 1)
                def _():
                    gathers[1].forward()
                    if with_dense:
                        dense.start()

            @pl.when(j * chips + turn >= 2)
            def _():
                for copy in kept(j, slot, chip):
                    copy.wait()

            x = arrived[j, pl.ds(2 * chip, 2)].reshape(rows, width)
            total = jnp.broadcast_to(b2[number : number + 1, :], (rows, width))
            for f in range(ff // FF_BLOCK):
                cols = slice(f * FF_BLOCK, (f + 1) * FF_BLOCK)
                first, second = weight_blocks(weights, j, f)
                inner = dot(x, first) + b1[number : number + 1, cols]
                normal = 0.5 * (1.0 + lax.erf(inner * ROOT_HALF))
                g = (inner * normal).astype(BF16)
                density = jnp.exp(-0.5 * inner * inner) * ROOT_TWO_PI_INVERSE
                g_stage[slot, :, cols] = g
                s_stage[slot, :, cols] = (normal + inner * density).astype(BF16)
                total = total + dot(g, second)
            made[j, pl.ds(2 * chip, 2)] = total.astype(BF16).reshape(2, capacity, width)
            swap.send_home(j, chip)
            for copy in kept(j, slot, chip):
                copy.start()
            return carry

        lax.fori_loop(0, chips, chip_step, 0)
    final = pltpu.make_async_copy(arrived, arrived_out, last.at[0])
    final.start()
    if with_dense:
        dense.finish()
    for slot in range(2):
        for copy in kept(0, slot, 0):
            copy.wait()
    swap.finish()
    for gather, copy in zip(gathers, gathered):
        gather.drain()
        copy.wait()
    final.wait()


def expert_back_kernel(layer, with_above, *refs):
    if with_above:
        *refs, above_in, above_own, above_send, above_recv, above_load = refs
        refs = list(refs)
        above, above_sum = refs.pop(9), refs.pop(14)
    (
        zero, one, drow, inner_first, outer_first, packed_second, arrived_x, g_in, s_in, back, summed, out, bias1, bias2,
        sent, arrived, made, weights, x, du, s_stage, g_stage, first_stage, second_stage, share_out, share_in,
        db1, db2, db1_in, db2_in,
        out_send, out_recv, home_send, home_recv, own, load, fetch, stores, share_send, share_recv,
        bias_send, bias_recv,
    ) = refs
    swap = Swap(sent, arrived, made, back, (out_send, out_recv, home_send, home_recv, own))
    row = lax.axis_index("dp")
    local, count, capacity, width = arrived.shape
    chips = count // 2
    rows = 2 * capacity
    ff = g_in.shape[2]
    blocks = ff // FF_BLOCK
    _, parts, all_rows, _ = weights.shape
    share, take = width // parts, all_rows // 2
    each = FF_BLOCK // take
    loads = [
        pltpu.make_async_copy(inner_first, weights.at[0, :, :take], load.at[0]),
        pltpu.make_async_copy(packed_second, weights.at[1], load.at[1]),
        pltpu.make_async_copy(arrived_x, x, load.at[local]),
        pltpu.make_async_copy(outer_first, weights.at[0, :, take:], load.at[local + 1]),
    ]
    for copy in loads:
        copy.start()

    def slopes(j, turn):
        slot = lax.rem(turn, 2)
        place = pl.ds(pl.multiple_of(swap.chip(turn) * rows, rows), rows)
        return pltpu.make_async_copy(s_in.at[j, place, :], s_stage.at[slot], fetch.at[0, slot])

    def activations(j, f):
        return pltpu.make_async_copy(
            g_in.at[j, :, f * FF_BLOCK : (f + 1) * FF_BLOCK], g_stage.at[f % 2], fetch.at[1, f % 2]
        )

    def results(j, f):
        return (
            pltpu.make_async_copy(
                first_stage.at[f % 2], out.at[:, j - 1, f * share : (f + 1) * share, :], stores.at[0, f % 2]
            ),
            pltpu.make_async_copy(
                second_stage.at[f % 2], out.at[f * each : (f + 1) * each, j - 1, take:, :], stores.at[1, f % 2]
            ),
        )

    def share_copy(k):
        peer = lax.rem(row + k, parts)
        return pltpu.make_async_remote_copy(
            src_ref=share_out.at[peer], dst_ref=share_in.at[k - 1],
            send_sem=share_send.at[k - 1], recv_sem=share_recv.at[k - 1],
            device_id={"dp": peer}, device_id_type=MESH,
        )

    slopes(0, 0).start()
    peers = [{"dp": lax.rem(row + k, parts)} for k in range(1, parts)]
    swap.greet(peers)
    if with_above:
        above_copies = [
            pltpu.make_async_remote_copy(
                src_ref=above.at[lax.rem(row + k, parts)], dst_ref=above_in.at[k - 1],
                send_sem=above_send.at[k - 1], recv_sem=above_recv.at[k - 1],
                device_id=peers[k - 1], device_id_type=MESH,
            )
            for k in range(1, parts)
        ]
        above_copies.append(pltpu.make_async_copy(above.at[row], above_own, above_load))
        for copy in above_copies:
            copy.start()
    swap.send_all([zero, one], drow, layer)
    loads[local + 1].wait()
    for j in range(local):
        loads[j].wait()
        activations(j, 0).start()

        def chip_step(turn, carry, j=j):
            chip = swap.chip(turn)
            slot = lax.rem(turn, 2)

            @pl.when(turn + 1 < chips)
            def _():
                slopes(j, turn + 1).start()

            swap.wait_chip(j, chip)
            slopes(j, turn).wait()
            dy = arrived[j, pl.ds(2 * chip, 2)].reshape(rows, width)
            place = pl.ds(pl.multiple_of(chip * rows, rows), rows)
            total = jnp.zeros((rows, width), F32)
            for f in range(blocks):
                cols = slice(f * FF_BLOCK, (f + 1) * FF_BLOCK)
                first, second = weight_blocks(weights, j, f)
                part = (dot_nt(dy, second) * s_stage[slot, :, cols].astype(F32)).astype(BF16)
                du[place, cols] = part
                total = total + dot_nt(part, first)
            made[j, pl.ds(2 * chip, 2)] = total.astype(BF16).reshape(2, capacity, width)
            swap.send_home(j, chip)
            return carry

        lax.fori_loop(0, chips, chip_step, 0)
        if j + 1 < local:
            slopes(j + 1, 0).start()
        if j == 0:
            loads[local].wait()
        dy = arrived[j].reshape(count * capacity, width)
        db2[j : j + 1, :] = jnp.sum(dy.astype(F32), axis=0, keepdims=True)
        for f in range(blocks):
            cols = slice(f * FF_BLOCK, (f + 1) * FF_BLOCK)
            if f + 1 < blocks:
                activations(j, f + 1).start()
            if j > 1 or (j == 1 and f > 1):
                for copy in results(j, f):
                    copy.wait()
            part = du[:, cols]
            grad = dot_tn(x[j].reshape(count * capacity, width), part).astype(BF16)
            if j == 0:
                share_out[:, f * share : (f + 1) * share, :] = grad.reshape(parts, share, width)
            else:
                first_stage[f % 2] = grad.reshape(parts, share, width)
            db1[j : j + 1, cols] = jnp.sum(part.astype(F32), axis=0, keepdims=True)
            activations(j, f).wait()
            grad = dot_tn(g_stage[f % 2], dy).astype(BF16).reshape(each, take, width)
            if j == 0:
                share_out[f * each : (f + 1) * each, take:, :] = grad
            else:
                second_stage[f % 2] = grad
                for copy in results(j, f):
                    copy.start()
        if j == 0:
            for k in range(1, parts):
                share_copy(k).start()
    part_ff = ff // parts
    bias_copies = []
    for k in range(1, parts):
        place = pl.ds(pl.multiple_of(lax.rem(row + k, parts) * part_ff, part_ff), part_ff)
        for n, (source, target) in enumerate(((db1.at[:, place], db1_in.at[k - 1]), (db2, db2_in.at[k - 1]))):
            bias_copies.append(pltpu.make_async_remote_copy(
                src_ref=source, dst_ref=target, send_sem=bias_send.at[n, k - 1], recv_sem=bias_recv.at[n, k - 1],
                device_id=peers[k - 1], device_id_type=MESH,
            ))
            bias_copies[-1].start()
    if with_above:
        for copy in above_copies:
            copy.wait()
        total = above_own[...].astype(F32)
        for k in range(1, parts):
            total = total + above_in[k - 1].astype(F32)
        above_sum[...] = total.astype(BF16)
    for k in range(1, parts):
        share_copy(k).wait_recv()
    step = 64

    def add_up(turn, carry):
        place = pl.ds(pl.multiple_of(turn * step, step), step)
        total = share_out[row, place, :].astype(F32)
        for k in range(1, parts):
            total = total + share_in[k - 1, place, :].astype(F32)
        summed[place, :] = total
        return carry

    lax.fori_loop(0, all_rows // step, add_up, 0)
    for copy in bias_copies:
        copy.wait_recv()
    total1, total2 = db1[:, pl.ds(pl.multiple_of(row * part_ff, part_ff), part_ff)], db2[...]
    for k in range(1, parts):
        total1, total2 = total1 + db1_in[k - 1], total2 + db2_in[k - 1]
    bias1[...], bias2[...] = total1, total2
    for copy in bias_copies:
        copy.wait_send()
    for k in range(1, parts):
        share_copy(k).wait_send()
    for f in range(2):
        for copy in results(1, f):
            copy.wait()
    swap.finish()


def swap_sems(local, count):
    pairs = [pltpu.SemaphoreType.DMA((local, count))] * 4
    return pairs + [pltpu.SemaphoreType.DMA((2 * local,))]


def expert_call(body, inputs, outputs, scratch, number):
    def spec(held):
        return pl.BlockSpec(memory_space=pltpu.VMEM if held else pl.ANY)

    shapes = [jax.ShapeDtypeStruct(s, t) for s, t, _ in outputs]
    return pl.pallas_call(
        body,
        in_specs=[spec(held) for _, held in inputs],
        out_specs=[spec(held) for _, _, held in outputs],
        out_shape=shapes,
        scratch_shapes=scratch,
        compiler_params=pltpu.CompilerParams(
            collective_id=number, has_side_effects=True, vmem_limit_bytes=VMEM
        ),
        cost_estimate=pl.CostEstimate(flops=COST, bytes_accessed=COST, transcendentals=0),
    )(*[a for a, _ in inputs])


def expert_forward(hidden, drow, shape, inner, outer_mine, mine, biases, dense, layer):
    b1, b2 = biases
    local, count, capacity, width = shape
    ff = b1.shape[1]
    rows = 2 * capacity
    parts = inner.shape[0]
    packed = (parts, *mine.shape)
    slots = (local, count * capacity, ff)
    inputs = [(hidden, True), (drow, True), (inner, False), (outer_mine, False), (mine, False), (b1, True), (b2, True)]
    outputs = [
        (shape, BF16, False), (shape, BF16, False), (slots, BF16, False), (slots, BF16, False),
        ((parts, *outer_mine.shape), BF16, False), (packed, BF16, False),
    ]
    scratch = [
        pltpu.VMEM(shape, BF16), pltpu.VMEM(shape, BF16), pltpu.VMEM(shape, BF16),
        pltpu.VMEM((local, *packed), BF16),
        pltpu.VMEM((2, rows, ff), BF16), pltpu.VMEM((2, rows, ff), BF16),
    ] + swap_sems(local, count) + [
        pltpu.SemaphoreType.DMA, pltpu.SemaphoreType.DMA((2, 2)), pltpu.SemaphoreType.DMA((3,)),
    ] + gather_sems(parts) * 2
    if dense is not None:
        inputs.append((dense, False))
        outputs.append(((parts, *dense.shape), BF16, False))
        scratch += shared_sems(parts)
    return expert_call(functools.partial(expert_kernel, layer, dense is not None), inputs, outputs, scratch, layer)


def expert_backward(sources, drow, weights, arrived, g, s, above, layer):
    shape = arrived.shape
    local, count, capacity, width = shape
    ff = g.shape[2]
    rows = 2 * capacity
    parts, all_rows, _ = weights[2].shape
    share, take = width // parts, all_rows // 2
    inputs = [(a, True) for a in (*sources, drow)] + [(a, False) for a in (*weights, arrived, g, s)]
    outputs = [
        (shape, BF16, False), ((all_rows, width), F32, True), ((parts, local - 1, all_rows, width), BF16, False),
        ((local, ff // parts), F32, True), ((local, width), F32, True),
    ]
    scratch = [
        pltpu.VMEM(shape, BF16), pltpu.VMEM(shape, BF16), pltpu.VMEM(shape, BF16),
        pltpu.VMEM((local, parts, all_rows, width), BF16), pltpu.VMEM(shape, BF16),
        pltpu.VMEM((count * capacity, ff), BF16), pltpu.VMEM((2, rows, ff), BF16),
        pltpu.VMEM((2, count * capacity, FF_BLOCK), BF16), pltpu.VMEM((2, parts, share, width), BF16),
        pltpu.VMEM((2, FF_BLOCK // take, take, width), BF16),
        pltpu.VMEM((parts, all_rows, width), BF16), pltpu.VMEM((parts - 1, all_rows, width), BF16),
        pltpu.VMEM((local, ff), F32), pltpu.VMEM((local, width), F32),
        pltpu.VMEM((parts - 1, local, ff // parts), F32), pltpu.VMEM((parts - 1, local, width), F32),
    ] + swap_sems(local, count) + [
        pltpu.SemaphoreType.DMA((local + 2,)), pltpu.SemaphoreType.DMA((2, 2)), pltpu.SemaphoreType.DMA((2, 2)),
        pltpu.SemaphoreType.DMA((parts - 1,)), pltpu.SemaphoreType.DMA((parts - 1,)),
        pltpu.SemaphoreType.DMA((2, parts - 1)), pltpu.SemaphoreType.DMA((2, parts - 1)),
    ]
    if above is not None:
        inputs.append((above, False))
        outputs.append((above.shape[1:], BF16, True))
        scratch += [
            pltpu.VMEM((parts - 1, *above.shape[1:]), BF16), pltpu.VMEM(above.shape[1:], BF16),
            pltpu.SemaphoreType.DMA((parts - 1,)), pltpu.SemaphoreType.DMA((parts - 1,)), pltpu.SemaphoreType.DMA,
        ]
    done = expert_call(
        functools.partial(expert_back_kernel, layer, above is not None), inputs, outputs, scratch, LAYERS + layer
    )
    return done if above is not None else [*done, None]


def prepare_kernel(capacity, owners, *refs):
    squares, (router, *vectors), (inner_bias, outer_bias, routes) = refs[:4], refs[4:12], refs[12:15]
    tokens_in, (out, above, b1, b2, dcol, drow), tokens_out = refs[15:17], refs[17:23], refs[23:25]
    mine, turned, inner_low, outer_low, token_ins, token_outs = refs[25:31]
    sems, (b1_send, b1_recv, b2_send, b2_recv, own, token_load, token_store) = refs[31:36], refs[36:]
    parts, share, _ = out.shape
    loads = [pltpu.make_async_copy(tokens_in[n], token_ins.at[n], token_load.at[n]) for n in range(2)]
    stores = [pltpu.make_async_copy(token_outs.at[n], tokens_out[n], token_store.at[n]) for n in range(2)]
    width = squares[0].shape[2]
    experts_all = router.shape[2]
    local, part_ff = inner_bias.shape[1:]
    row, me = lax.axis_index("dp"), lax.axis_index("expert")
    sibling = {"expert": me + 1 - 2 * lax.rem(me, 2)}
    peers = [{"dp": lax.rem(row + k, parts)} for k in range(1, parts)]
    gather = SharedGather(mine, out, sems)

    def pack(target, layer):
        for n in range(4):
            target[:, n * width : (n + 1) * width] = squares[n][layer].astype(BF16)
        turned[...] = jnp.zeros_like(turned)
        for n in range(7):
            turned[VEC_AT + n : VEC_AT + n + 1, :] = vectors[n][layer : layer + 1, :]
        target[:, 4 * width :] = turned[...].T.astype(BF16)
        target[:, 4 * width : 4 * width + experts_all] = router[layer].astype(BF16)

    pack(mine, 0)
    for layer in range(LAYERS):
        for j in range(local):
            n = layer * local + j
            inner_low[n : n + 1, :] = inner_bias[layer, j : j + 1, :].astype(BF16).astype(F32)
            outer_low[n : n + 1, :] = outer_bias[layer, j : j + 1, :].astype(BF16).astype(F32)
    greet_all([sibling] + peers)
    place = pl.ds(pl.multiple_of(row * part_ff, part_ff), part_ff)
    singles = [
        remote(inner_low, b1.at[:, place], b1_send.at[k], b1_recv.at[k], peers[k]) for k in range(parts - 1)
    ] + [remote(outer_low, b2.at[row], b2_send.at[k], b2_recv.at[k], peers[k]) for k in range(parts - 1)]
    keeps = [
        pltpu.make_async_copy(inner_low, b1.at[:, place], own.at[0]),
        pltpu.make_async_copy(outer_low, b2.at[row], own.at[1]),
    ]
    gather.start()
    for copy in singles + keeps + loads:
        copy.start()
    pack(above, 1)
    for n in range(2):
        loads[n].wait()
        for image in range(routes.shape[1]):
            token_outs[n, image] = token_ins[n, :, image, :]
        stores[n].start()

    length = routes.shape[2]
    lanes = lax.broadcasted_iota(jnp.int32, (length, MISC), 1)
    earlier = (
        lax.broadcasted_iota(jnp.int32, (length, length), 0) > lax.broadcasted_iota(jnp.int32, (length, length), 1)
    ).astype(F32).astype(BF16)
    for layer in range(LAYERS):
        seen = jnp.zeros((1, MISC), F32)
        for image in range(routes.shape[1]):
            hots, dests = [], []
            for k in range(2):
                hots.append((lanes == routes[layer, image, :, k : k + 1]).astype(F32))
            counts = hots[0] + hots[1]
            before = dot(earlier, counts.astype(BF16)) + seen
            seen = seen + jnp.sum(counts, axis=0, keepdims=True)
            for k in range(2):
                slot = jnp.sum(hots[k] * before, axis=-1, keepdims=True)
                expert = routes[layer, image, :, k : k + 1].astype(F32)
                owner = jnp.floor(expert * (1.0 / local))
                place = ((expert - owner * local) * owners + owner) * capacity + slot
                dests.append(jnp.where(slot < capacity, place, -1.0))
                dcol[layer, image, :, k : k + 1] = dests[k].astype(jnp.int32)
            both = jnp.where(lanes == 0, dests[0], jnp.where(lanes == 1, dests[1], 0.0))
            drow[layer, image] = both.T[0:2, :].astype(jnp.int32)

    gather.finish()
    for copy in singles + keeps + stores:
        copy.wait()


def prepare(squares, router, vectors, inner_bias, outer_bias, routes, tokens, parts, owners, number):
    layers, share, width = squares[0].shape
    experts_all = router.shape[2]
    local, part_ff = inner_bias.shape[1:]
    _, images, length, _ = routes.shape
    capacity = (10 * images * length // (4 * experts_all) + 7) // 8 * 8
    columns = 4 * width + MISC
    count = layers * local
    sems = shared_sems(parts) + [pltpu.SemaphoreType.DMA((parts - 1,))] * 4 + [pltpu.SemaphoreType.DMA((2,))] * 3
    inputs = [*squares, router, *vectors, inner_bias, outer_bias, routes]
    turned = [jnp.transpose(item, (1, 0, 2)) for item in tokens]
    out, above, b1, b2, dcol, drow, *tokens = expert_call(
        functools.partial(prepare_kernel, capacity, owners), [(a, True) for a in inputs] + [(a, False) for a in turned],
        [
            ((parts, share, columns), BF16, False), ((share, columns), BF16, True),
            ((count, part_ff * parts), F32, False), ((parts, count, share), F32, False),
            ((layers, images, length, 2), jnp.int32, True), ((layers, images, 2, length), jnp.int32, True),
            ((images, length, width), F32, False), ((images, length, width), F32, False),
        ],
        [
            pltpu.VMEM((share, columns), BF16), pltpu.VMEM((MISC, share), F32),
            pltpu.VMEM((count, part_ff), F32), pltpu.VMEM((count, share), F32),
            pltpu.VMEM((2, length, images, width), F32), pltpu.VMEM((2, images, length, width), F32),
        ] + sems,
        number,
    )
    b2 = jnp.transpose(b2, (1, 0, 2)).reshape(count, width)
    return out.reshape(width, columns), above, (b1, b2), dcol, drow, capacity, tokens


def settle_widths(columns, chips):
    blocks = columns // (MISC * chips)
    wide = (blocks + 1) // 2 * MISC
    return wide, columns // chips - wide


def settle_kernel(
    grads, above, final, own, paired, total, chips_in, dp_in, total_b, chips_in_b, dp_in_b,
    pair_send, pair_recv, local, out_send, out_recv, dp_send, dp_recv, out_send_b, out_recv_b, dp_send_b, dp_recv_b,
    back_send, back_recv, pass_send, pass_recv,
):
    parts, share, columns = grads.shape
    half = share // 2
    row, me = lax.axis_index("dp"), lax.axis_index("expert")
    core, chip = lax.rem(me, 2), me // 2
    chips = chips_in.shape[0] + 1
    wide, narrow = settle_widths(columns, chips)
    split = chips * wide
    sibling = {"expert": me + 1 - 2 * core}
    mine = pl.ds(pl.multiple_of(core * half, half), half)
    other = pl.ds(pl.multiple_of((1 - core) * half, half), half)

    def cols(number):
        return pl.ds(pl.multiple_of(number * wide, MISC), wide)

    def cols_b(number, start):
        return pl.ds(pl.multiple_of(start + number * narrow, MISC), narrow)

    def chip_at(k):
        return lax.rem(chip + k + chips, chips)

    dp_peers = [{"dp": lax.rem(row + k, parts)} for k in range(1, parts)]
    chip_peers = [{"expert": 2 * chip_at(k) + core} for k in range(1, chips)]
    greet_all([sibling] + dp_peers + chip_peers)

    order = [lax.rem(row + 1 + i, parts) for i in range(parts)]
    pairs, keeps = [], []
    for i in range(parts + 1):
        source = grads.at[order[i]] if i < parts else above
        pairs.append(remote(source.at[other], paired.at[i], pair_send.at[i], pair_recv.at[i], sibling))
        keeps.append(pltpu.make_async_copy(source.at[mine], own.at[i], local.at[i]))
        pairs[i].start()
        keeps[i].start()
    outs, scatters_b = [], []
    for i in range(parts + 1):
        pairs[i].wait_recv()
        keeps[i].wait()
        own[i] = (own[i].astype(F32) + paired[i].astype(F32)).astype(BF16)
        if i < parts - 1:
            scatters_b.append(
                remote(own.at[i, :, split:], dp_in_b.at[i], dp_send_b.at[i], dp_recv_b.at[i], dp_peers[i])
            )
            scatters_b[i].start()
        outs.append([
            remote(
                own.at[i, :, cols(chip_at(k))], chips_in.at[k - 1, i], out_send.at[k - 1, i], out_recv.at[k - 1, i],
                chip_peers[k - 1],
            )
            for k in range(1, chips)
        ])
        for copy in outs[i]:
            copy.start()
    value = own[parts - 1, :, split:].astype(F32)
    for i in range(parts - 1):
        scatters_b[i].wait_recv()
        value = value + dp_in_b[i].astype(F32)
    total_b[0] = value.astype(BF16)
    total_b[1] = own[parts, :, split:]
    outs_b = [
        remote(
            total_b.at[:, :, cols_b(chip_at(k), 0)], chips_in_b.at[k - 1], out_send_b.at[k - 1], out_recv_b.at[k - 1],
            chip_peers[k - 1],
        )
        for k in range(1, chips)
    ]
    for copy in outs_b:
        copy.start()
    scatters = []
    for i in range(parts + 1):
        value = own[i, :, cols(chip)].astype(F32)
        for k in range(1, chips):
            outs[i][k - 1].wait_recv()
            value = value + chips_in[k - 1, i].astype(F32)
        if i < parts - 1:
            total[i] = value.astype(BF16)
            scatters.append(remote(total.at[i], dp_in.at[i], dp_send.at[i], dp_recv.at[i], dp_peers[i]))
            scatters[i].start()
        elif i == parts - 1:
            kept = value
        else:
            final[1, mine, cols(chip)] = value.astype(BF16)
    value = total_b[:, :, cols_b(chip, 0)].astype(F32)
    for k in range(1, chips):
        outs_b[k - 1].wait_recv()
        value = value + chips_in_b[k - 1].astype(F32)
    final[:, mine, cols_b(chip, split)] = value.astype(BF16)
    for i in range(parts - 1):
        scatters[i].wait_recv()
        kept = kept + dp_in[i].astype(F32)
    final[0, mine, cols(chip)] = kept.astype(BF16)

    def places(number):
        return [final.at[:, mine, cols(number)], final.at[:, mine, cols_b(number, split)]]

    backs, hands = [], []
    for n, place in enumerate(places(chip)):
        for k in range(1, chips):
            backs.append(remote(place, place, back_send.at[n, k - 1], back_recv.at[n, k - 1], chip_peers[k - 1]))
            backs[-1].start()
        hands.append(remote(place, place, pass_send.at[n, 0], pass_recv.at[n, 0], sibling))
        hands[-1].start()
    for k in range(1, chips):
        for n, place in enumerate(places(chip_at(-k))):
            backs[n * (chips - 1) + k - 1].wait_recv()
            hands.append(remote(place, place, pass_send.at[n, k], pass_recv.at[n, k], sibling))
            hands[-1].start()
    for copy in pairs + [copy for group in outs for copy in group] + outs_b + scatters + scatters_b + backs:
        copy.wait_send()
    for copy in hands:
        copy.wait()


def settle_dense(grads, above, chips, number):
    parts, share, columns = grads.shape
    half = share // 2
    halves = pltpu.VMEM((parts + 1, half, columns), BF16)
    wide, narrow = settle_widths(columns, chips)
    dp_in = pltpu.VMEM((parts - 1, half, wide), BF16)
    rest = chips * narrow
    sems = [(parts + 1,)] * 3 + [(chips - 1, parts + 1)] * 2 + [(parts - 1,)] * 2
    sems += [(chips - 1,)] * 2 + [(parts - 1,)] * 2 + [(2, chips - 1)] * 2 + [(2, chips)] * 2
    return expert_call(
        settle_kernel, [(grads, False), (above, False)], [((2, share, columns), BF16, True)],
        [
            halves, halves, dp_in, pltpu.VMEM((chips - 1, parts + 1, half, wide), BF16), dp_in,
            pltpu.VMEM((2, half, rest), BF16), pltpu.VMEM((chips - 1, 2, half, narrow), BF16),
            pltpu.VMEM((parts - 1, half, rest), BF16),
        ] + [pltpu.SemaphoreType.DMA(n) for n in sems],
        number,
    )[0]


def unpack_kernel(*refs):
    count = 2 * LAYERS
    pieces, both = refs[:count], refs[count]
    squares, router, vectors, inner, outer = refs[count + 1 : count + 5], *refs[count + 5 :]
    layer = pl.program_id(0)
    share = both.shape[1]
    width = squares[0].shape[2]
    for n in range(4):
        squares[n][0] = both[0, :, n * width : (n + 1) * width].astype(F32)
    misc = both[0, :, 4 * width : 4 * width + MISC].astype(F32)
    router[0] = misc[:, : router.shape[2]]
    turned = misc.T
    vectors[0] = turned[VEC_AT : VEC_AT + 8, :]
    blocks = inner.shape[3] // FF_BLOCK

    for number in range(LAYERS):

        @pl.when(layer == number)
        def _(number=number):
            for j in range(2):
                piece = pieces[2 * number + j]
                for f in range(blocks):
                    inner[0, j, :, f * FF_BLOCK : (f + 1) * FF_BLOCK] = piece[
                        f * share : (f + 1) * share, :
                    ].astype(F32)
                outer[0, j] = piece[blocks * share :, :].astype(F32)


def unpack(pieces, both, local, ff, experts_all):
    layers, share, columns = both.shape
    rows, width = pieces[0].shape
    take = rows // 2
    by_layer = lambda *shape: ((layers, *shape), F32, pl.BlockSpec((1, *shape), lambda i: (i,) + (0,) * len(shape)))
    return call(
        unpack_kernel, (layers,),
        [(p, whole(p)) for p in pieces] + [(both, pl.BlockSpec((1, share, columns), lambda i: (i, 0, 0)))],
        [by_layer(share, width)] * 4 + [
            by_layer(share, experts_all), by_layer(8, share),
            by_layer(local, share, ff), by_layer(local, take, width),
        ],
    )


def shards(
    images, cotangent, routes, query_weight, key_weight, value_weight, output_weight, router_weight, query_bias,
    value_bias, output_bias, attend_gain, attend_shift, expert_gain, expert_shift, inner_weight, inner_bias,
    outer_weight, outer_bias,
):
    count, length, width = images.shape
    parts = lax.axis_size("dp")
    owners = lax.axis_size("expert")
    experts_all = router_weight.shape[2]
    local = inner_weight.shape[1]
    ff = inner_weight.shape[3]
    share = width // parts
    tokens = count * length
    squares = (query_weight, key_weight, value_weight, output_weight)
    vectors = (query_bias, value_bias, output_bias, attend_gain, attend_shift, expert_gain, expert_shift)
    columns = -(-(4 * width + MISC) // (MISC * (owners // 2))) * MISC * (owners // 2)

    inner_mine, outer_mine, mine = [], [], []
    for layer in range(LAYERS):
        first = inner_weight[layer].reshape(local, share, ff // FF_BLOCK, FF_BLOCK)
        first = jnp.transpose(first, (0, 2, 1, 3)).reshape(local, ff // parts, width).astype(BF16)
        second = outer_weight[layer].astype(BF16)
        inner_mine.append(first[0])
        outer_mine.append(second[0])
        mine.append(jnp.concatenate([first[1], second[1]], axis=0))
    dense, above, expert_biases, dcol, drow, capacity, (images, cotangent) = prepare(
        squares, router_weight, vectors, inner_bias, outer_bias, routes, (images, cotangent), parts, owners, 2 * LAYERS
    )
    packed = [dense]
    firsts = [lax.all_gather(item, "dp", axis=0, tiled=False) for item in inner_mine]
    slots = experts_all * capacity
    dense_flops = 8 * tokens * width * width + 4 * tokens * slots * width

    saved = []
    back = None
    rows = images
    for layer in range(LAYERS):
        weights = [(packed[layer], s) for s in packed_specs(packed[layer])]
        routing = [(routes, per_layer(routes, layer))]
        outputs = attend_outputs(count, length, width)
        if layer == 0:
            done = call(
                first_kernel, (count,), [(rows, per_image(rows))] + routing + weights, outputs, flops=dense_flops
            )
            picked = None
        else:
            before = saved[-1]
            done = call(
                next_kernel, (count,),
                [
                    (before["middle"], per_image(before["middle"])),
                    (before["gates"], per_image(before["gates"])),
                    (dcol, per_layer(dcol, layer - 1)),
                    (back, whole(back)),
                ] + routing + weights,
                [
                    images_out(count, length, width, F32),
                    images_out(count, length, width, BF16),
                    images_out(count, length, width, BF16),
                ] + outputs,
                flops=dense_flops,
            )
            rows, *picked = done[:3]
            done = done[3:]
            before["picked"] = picked
        middle, queries, keys, values, context, sums, gates = done[:7]
        back, arrived, g, s, outer, second, *dense = expert_forward(
            done[7], drow, (local, owners, capacity, width), firsts[layer], outer_mine[layer], mine[layer], expert_biases,
            above if layer == 0 else None, layer,
        )
        packed += [item.reshape(width, item.shape[2]) for item in dense]
        back = back.reshape(slots, width)
        saved.append({
            "rows": rows, "middle": middle, "attend": (queries, keys, values, context, sums), "gates": gates,
            "experts": (arrived, g, s), "weights": (firsts[layer], outer, second),
        })

    last = saved[-1]
    result, dz, *sources = call(
        turn_kernel, (count,),
        [(last["middle"], per_image(last["middle"])), (last["gates"], per_image(last["gates"]))]
        + [(dcol, per_layer(dcol, LAYERS - 1)), (back, whole(back))]
        + [(cotangent, per_image(cotangent)), (routes, per_layer(routes, LAYERS - 1))],
        [images_out(count, length, width, F32), images_out(count, length, MISC, BF16)]
        + [images_out(count, length, width, BF16)] * 2,
        flops=dense_flops,
    )
    upstream = cotangent
    bias_grads = [None] * LAYERS
    finished = []
    waiting = []
    wgrad = None
    for layer in reversed(range(LAYERS)):
        kept = saved[layer]
        came, shares, grads, *biases, above = expert_backward(
            sources, drow, kept["weights"], *kept["experts"], wgrad, layer
        )
        came = came.reshape(slots, width)
        came, waiting = lax.optimization_barrier((came, waiting))
        finished += waiting
        waiting = [shares, lax.psum_scatter(grads, "dp", scatter_dimension=0, tiled=False)]
        bias_grads[layer] = biases
        weights = [(packed[layer], s) for s in packed_specs(packed[layer])]
        inputs = [upstream, kept["rows"], kept["middle"], *kept["attend"], dz]
        inputs = [(a, per_image(a)) for a in inputs]
        inputs += [(dcol, per_layer(dcol, layer)), (came, whole(came))] + weights
        outputs = [
            images_out(count, length, width, F32),
            (
                (width, columns), BF16,
                pl.BlockSpec((width, columns), lambda i: (0, 0)),
            ),
        ]
        if layer > 0:
            below = saved[layer - 1]
            inputs += [(a, per_image(a)) for a in (*below["picked"], below["gates"])]
            inputs.append((routes, per_layer(routes, layer - 1)))
            outputs += [images_out(count, length, MISC, BF16)] + [images_out(count, length, width, BF16)] * 2
        done = call(
            back_kernel, (count,), inputs, outputs,
            [pltpu.VMEM((width, 4 * width + MISC), F32), pltpu.VMEM((MISC, width), F32)], flops=3 * dense_flops,
        )
        upstream, wgrad = done[:2]
        if layer > 0:
            dz, *sources = done[2:]
        wgrad = wgrad.reshape(parts, share, columns)
    both = settle_dense(wgrad, above, owners // 2, 2 * LAYERS + 1)
    pieces = [waiting[0], waiting[1][0], finished[0], finished[1][0]]
    *squares, router, vectors, inner, outer = unpack(pieces, both, local, ff, experts_all)
    outer_bias_grad = jnp.stack([b[1] for b in bias_grads])
    return (
        result,
        upstream,
        *squares,
        router,
        *[vectors[:, n] for n in range(7)],
        inner,
        jnp.stack([b[0] for b in bias_grads]),
        outer,
        lax.dynamic_slice_in_dim(outer_bias_grad, lax.axis_index("dp") * share, share, 2),
    )


def solution(mesh):
    both = P(("dp", "expert"), None, None)
    square = P(None, "dp", None)
    vector = P(None, "dp")
    matrix = P(None, "expert", "dp", None)
    bias = P(None, "expert", "dp")
    grads = (square,) * 5 + (vector,) * 7 + (matrix, bias, matrix, bias)
    return jax.shard_map(
        shards,
        mesh=mesh,
        in_specs=(both, both, P(None, ("dp", "expert"), None, None)) + grads,
        out_specs=(both, both) + grads,
        check_vma=False,
    )
```

```python
import functools

import jax
import jax.numpy as jnp
from jax import lax
from jax.experimental import pallas as pl
from jax.experimental.pallas import tpu as pltpu
from jax.sharding import PartitionSpec as P

HEADS = 8
HEAD_DIM = 64
LAYERS = 2
EPSILON = 1e-06
FACTOR = HEAD_DIM**-0.5
VEC_AT = 64
MISC = 128
FF_BLOCK = 512
COST = 1024
VMEM = 56 * 1024 * 1024

MESH = pl.DeviceIdType.MESH
F32 = jnp.float32
BF16 = jnp.bfloat16


def dot(a, b):
    return jnp.dot(a, b, preferred_element_type=F32)


def dot_nt(a, b):
    return lax.dot_general(a, b, (((1,), (1,)), ((), ())), preferred_element_type=F32)


def dot_tn(a, b):
    return lax.dot_general(a, b, (((0,), (0,)), ((), ())), preferred_element_type=F32)


def standardize(rows):
    mean_value = jnp.mean(rows, axis=-1, keepdims=True)
    centered = rows - mean_value
    variance = jnp.mean(centered * centered, axis=-1, keepdims=True)
    scale = lax.rsqrt(variance + EPSILON)
    return centered * scale, scale


def standardize_back(upstream, unit, scale, gain):
    along = upstream * gain
    inner = (
        along
        - jnp.mean(along, axis=-1, keepdims=True)
        - unit * jnp.mean(along * unit, axis=-1, keepdims=True)
    )
    return inner * scale


def vectors_of(misc_ref):
    turned = misc_ref[...].astype(F32).T
    return [turned[VEC_AT + n : VEC_AT + n + 1, :] for n in range(7)]


def lane_masks(length):
    lanes = lax.broadcasted_iota(jnp.int32, (length, 2 * HEAD_DIM), 1)
    return (lanes < HEAD_DIM).astype(F32).astype(BF16), (lanes >= HEAD_DIM).astype(F32).astype(BF16)


def attend_body(
    rows, routes_ref, wq, wk, wv, wo, misc,
    t_ref, q_ref, k_ref, v_ref, o_ref, lse_ref, gates_ref, hidden_ref,
):
    length = rows.shape[0]
    qb, vb, ob, again, ashift, egain, eshift = vectors_of(misc)
    unit, _ = standardize(rows)
    low = (unit * again + ashift).astype(BF16)
    queries = (dot(low, wq[...]) + qb).astype(BF16)
    keys = dot(low, wk[...]).astype(BF16)
    values = (dot(low, wv[...]) + vb).astype(BF16)
    q_ref[0] = queries
    k_ref[0] = keys
    v_ref[0] = values
    masks = lane_masks(length)
    lanes = lax.broadcasted_iota(jnp.int32, (length, MISC), 1)
    first_half = lax.broadcasted_iota(jnp.int32, (length, 2 * HEAD_DIM), 1) < HEAD_DIM
    sums = jnp.zeros((length, MISC), F32)
    for pair in range(HEADS // 2):
        cols = slice(pair * 2 * HEAD_DIM, (pair + 1) * 2 * HEAD_DIM)
        mixed = []
        for side in range(2):
            scores = dot_nt(queries[:, cols] * (masks[side] * FACTOR), keys[:, cols])
            highest = jnp.max(scores, axis=-1, keepdims=True)
            expo = jnp.exp(scores - highest)
            total = jnp.sum(expo, axis=-1, keepdims=True)
            attention = (expo * (1.0 / total)).astype(BF16)
            sums = jnp.where(lanes == 2 * pair + side, highest + jnp.log(total), sums)
            mixed.append(dot(attention, values[:, cols]))
        o_ref[0, :, cols] = jnp.where(first_half, mixed[0], mixed[1]).astype(BF16)
    lse_ref[0] = sums
    middle = rows + (dot(o_ref[0], wo[...]) + ob)
    t_ref[0] = middle
    unit_two, _ = standardize(middle)
    hidden = (unit_two * egain + eshift).astype(BF16)
    logits = dot(hidden, misc[...])
    pair_experts = routes_ref[0]
    zero = jnp.sum(jnp.where(lanes == pair_experts[:, 0:1], logits, 0.0), axis=-1, keepdims=True)
    one = jnp.sum(jnp.where(lanes == pair_experts[:, 1:2], logits, 0.0), axis=-1, keepdims=True)
    gate_zero = 1.0 / (1.0 + jnp.exp(one - zero))
    gate_one = 1.0 / (1.0 + jnp.exp(zero - one))
    gates_ref[0, :, 0:1] = gate_zero
    gates_ref[0, :, 1:2] = gate_one
    hidden_ref[0] = hidden


def combine(middle, gates_ref, zero_ref, one_ref):
    gates = gates_ref[0]
    zero, one = zero_ref[0].astype(F32), one_ref[0].astype(F32)
    return middle + (gates[:, 0:1] * zero + gates[:, 1:2] * one), zero, one


def grads_body(upstream, zero, one, gates_ref, routes_ref, dz_ref, zero_ref, one_ref):
    length = upstream.shape[0]
    gates = gates_ref[0]
    gate_zero, gate_one = gates[:, 0:1], gates[:, 1:2]
    grad_zero = jnp.sum(zero * upstream, axis=-1, keepdims=True)
    grad_one = jnp.sum(one * upstream, axis=-1, keepdims=True)
    along = gate_zero * grad_zero + gate_one * grad_one
    lanes = lax.broadcasted_iota(jnp.int32, (length, MISC), 1)
    pair_experts = routes_ref[0]
    dz = jnp.where(lanes == pair_experts[:, 0:1], gate_zero * (grad_zero - along), 0.0)
    dz = dz + jnp.where(lanes == pair_experts[:, 1:2], gate_one * (grad_one - along), 0.0)
    dz_ref[0] = dz.astype(BF16)
    zero_ref[0] = (gate_zero * upstream).astype(BF16)
    one_ref[0] = (gate_one * upstream).astype(BF16)


def first_kernel(rows, routes, wq, wk, wv, wo, misc, *outs):
    attend_body(rows[0], routes, wq, wk, wv, wo, misc, *outs)


def next_kernel(
    middle, gates, yzero, yone, routes, wq, wk, wv, wo, misc, rows_ref, *outs
):
    rows, _, _ = combine(middle[0], gates, yzero, yone)
    rows_ref[0] = rows
    attend_body(rows, routes, wq, wk, wv, wo, misc, *outs)


def turn_kernel(middle, gates, yzero, yone, cotangent, routes, result, dz, zero_ref, one_ref):
    rows, zero, one = combine(middle[0], gates, yzero, yone)
    result[0] = rows
    grads_body(cotangent[0], zero, one, gates, routes, dz, zero_ref, one_ref)


class Spread:
    def __init__(self, above, refs):
        self.own, self.paired, self.chips_in, self.final, *sems = refs
        pair_send, pair_recv, local, out_send, out_recv, back_send, back_recv, pass_send, pass_recv = sems
        half, columns = self.own.shape
        me = lax.axis_index("expert")
        core, chip = lax.rem(me, 2), me // 2
        self.chips = chips = self.chips_in.shape[0] + 1
        block = columns // chips
        sibling = {"expert": me + 1 - 2 * core}
        mine = pl.ds(pl.multiple_of(core * half, half), half)
        other = pl.ds(pl.multiple_of((1 - core) * half, half), half)

        def chip_at(k):
            return lax.rem(chip + k + chips, chips)

        def cols(number):
            return pl.ds(pl.multiple_of(number * block, block), block)

        peers = [{"expert": 2 * chip_at(k) + core} for k in range(1, chips)]
        self.peers = [sibling] + peers
        self.pair = remote(above.at[other], self.paired, pair_send, pair_recv, sibling)
        self.keep = pltpu.make_async_copy(above.at[mine], self.own, local)
        self.outs = [
            remote(
                self.own.at[:, cols(chip_at(k))], self.chips_in.at[k - 1], out_send.at[k - 1], out_recv.at[k - 1],
                peers[k - 1],
            )
            for k in range(1, chips)
        ]
        self.place = (mine, cols(chip))
        place = self.final.at[mine, cols(chip)]
        self.backs = [
            remote(place, place, back_send.at[k - 1], back_recv.at[k - 1], peers[k - 1]) for k in range(1, chips)
        ]
        self.hands = []
        for k in range(chips):
            place = self.final.at[mine, cols(chip_at(-k))]
            self.hands.append(remote(place, place, pass_send.at[k], pass_recv.at[k], sibling))

    def stage(self, number):
        if number == 0:
            greet_all(self.peers)
            self.pair.start()
            self.keep.start()
        elif number == 1:
            self.pair.wait_recv()
            self.keep.wait()
            self.own[...] = (self.own[...].astype(F32) + self.paired[...].astype(F32)).astype(BF16)
            for copy in self.outs:
                copy.start()
        elif number == 2:
            value = self.own[:, self.place[1]].astype(F32)
            for n, copy in enumerate(self.outs):
                copy.wait_recv()
                value = value + self.chips_in[n].astype(F32)
            self.final[self.place[0], self.place[1]] = value.astype(BF16)
            for copy in self.backs:
                copy.start()
        else:
            for copy in self.backs:
                copy.wait_recv()
            for copy in self.hands:
                copy.start()

    def finish(self, result):
        for copy in self.hands:
            copy.wait()
        for copy in [self.pair] + self.outs + self.backs:
            copy.wait_send()
        result[...] = self.final[...]


def spread_scratch(share, columns, chips):
    half = share // 2
    half_rows = pltpu.VMEM((half, columns), BF16)
    sems = [()] * 3 + [(chips - 1,)] * 4 + [(chips,)] * 2
    return [
        half_rows, half_rows, pltpu.VMEM((chips - 1, half, columns // chips), BF16), pltpu.VMEM((share, columns), BF16),
    ] + [pltpu.SemaphoreType.DMA(n) for n in sems]


def back_kernel(
    lowest, upstream, rows, middle, q_ref, k_ref, v_ref, o_ref, lse_ref, dz_ref, came,
    wq, wk, wv, wo, misc, *rest,
):
    if not lowest:
        yzero, yone, gates_below, routes_below, grad_ref, sent, dz_below, zero_ref, one_ref, wgrad, vgrad = rest
    else:
        above, grad_ref, sent, above_out, wgrad, vgrad, *spread_refs = rest
        spread = Spread(above, spread_refs)
        for number in range(4):

            @pl.when(pl.program_id(0) == number)
            def _(number=number):
                spread.stage(number)

    first = pl.program_id(0) == 0
    length = rows.shape[1]
    width = rows.shape[2]
    qb, vb, ob, again, ashift, egain, eshift = vectors_of(misc)

    @pl.when(first)
    def _():
        wgrad[...] = jnp.zeros_like(wgrad)
        vgrad[...] = jnp.zeros_like(vgrad)

    def add_vector(number, value):
        vgrad[VEC_AT + number : VEC_AT + number + 1, :] += jnp.sum(value, axis=0, keepdims=True)

    unit_two, scale_two = standardize(middle[0])
    hidden = (unit_two * egain + eshift).astype(BF16)
    dz = dz_ref[0]
    dhidden = dot_nt(dz, misc[...]) + came[0]
    wgrad[:, 4 * width :] += dot_tn(hidden, dz)
    add_vector(5, dhidden * unit_two)
    add_vector(6, dhidden)
    dmiddle = upstream[0] + standardize_back(dhidden, unit_two, scale_two, egain)
    dbranch = dmiddle.astype(BF16)
    wgrad[:, 3 * width : 4 * width] += dot_tn(o_ref[0], dbranch)
    add_vector(2, dbranch.astype(F32))
    dcontext = dot_nt(dbranch, wo[...]).astype(BF16)
    masks = lane_masks(length)
    first_half = lax.broadcasted_iota(jnp.int32, (length, 2 * HEAD_DIM), 1) < HEAD_DIM
    dqs, dks, dvs = [], [], []
    sums = lse_ref[0].T
    for pair in range(HEADS // 2):
        cols = slice(pair * 2 * HEAD_DIM, (pair + 1) * 2 * HEAD_DIM)
        keys = k_ref[0, :, cols]
        values = v_ref[0, :, cols]
        queries = q_ref[0, :, cols]
        dvalues, dqueries, dkeys = None, [], None
        for side in range(2):
            own_queries = queries * (masks[side] * FACTOR)
            own_context = dcontext[:, cols] * masks[side]
            scores = dot_nt(keys, own_queries)
            number = 2 * pair + side
            attention = jnp.exp(scores - sums[number : number + 1, :])
            prob = dot_nt(values, own_context)
            weighed = attention * prob
            delta = jnp.sum(weighed, axis=0, keepdims=True)
            dscores = (weighed - attention * delta).astype(BF16)
            dvalue = dot(attention.astype(BF16), own_context)
            dkey = dot(dscores, own_queries)
            dvalues = dvalue if dvalues is None else dvalues + dvalue
            dkeys = dkey if dkeys is None else dkeys + dkey
            dqueries.append(dot_tn(dscores, keys))
        dqs.append((jnp.where(first_half, dqueries[0], dqueries[1]) * FACTOR).astype(BF16))
        dks.append(dkeys.astype(BF16))
        dvs.append(dvalues.astype(BF16))
    dq = jnp.concatenate(dqs, axis=1)
    dk = jnp.concatenate(dks, axis=1)
    dv = jnp.concatenate(dvs, axis=1)
    unit, scale = standardize(rows[0])
    low = (unit * again + ashift).astype(BF16)
    wgrad[:, 0 : 3 * width] += dot_tn(low, jnp.concatenate([dq, dk, dv], axis=1))
    add_vector(0, dq.astype(F32))
    add_vector(1, dv.astype(F32))
    dlow = dot_nt(dq, wq[...]) + dot_nt(dk, wk[...]) + dot_nt(dv, wv[...])
    add_vector(3, dlow * unit)
    add_vector(4, dlow)
    grad = dmiddle + standardize_back(dlow, unit, scale, again)
    grad_ref[0] = grad
    if not lowest:
        grads_body(
            grad, yzero[0].astype(F32), yone[0].astype(F32), gates_below, routes_below, dz_below,
            zero_ref, one_ref,
        )

    @pl.when(pl.program_id(0) == pl.num_programs(0) - 1)
    def _():
        wgrad[:, 4 * width :] += vgrad[...].T
        sent[:, : 4 * width + MISC] = wgrad[...].astype(BF16)
        sent[:, 4 * width + MISC :] = jnp.zeros((width, sent.shape[1] - 4 * width - MISC), BF16)
        if lowest:
            spread.finish(above_out)


def per_image(array):
    return pl.BlockSpec((1,) + array.shape[1:], lambda i: (i,) + (0,) * (len(array.shape) - 1))


def per_layer(array, layer):
    shape = (None, 1) + array.shape[2:]
    return pl.BlockSpec(shape, lambda i: (layer, i) + (0,) * (len(shape) - 2))


def whole(array):
    return pl.BlockSpec(array.shape, lambda i: (0,) * len(array.shape))


def packed_specs(packed):
    width = packed.shape[0]
    specs = [pl.BlockSpec((width, width), lambda i, n=n: (0, n)) for n in range(4)]
    return specs + [pl.BlockSpec((width, MISC), lambda i: (0, 4 * width // MISC))]


def call(body, grid, inputs, outputs, scratch=(), number=None):
    shapes = [jax.ShapeDtypeStruct(s, t) for s, t, _ in outputs]
    return pl.pallas_call(
        body,
        grid=grid,
        in_specs=[s for _, s in inputs],
        out_specs=[s for _, _, s in outputs],
        out_shape=shapes,
        scratch_shapes=list(scratch),
        compiler_params=pltpu.CompilerParams(
            vmem_limit_bytes=VMEM, collective_id=number, has_side_effects=number is not None
        ),
        cost_estimate=pl.CostEstimate(flops=COST, bytes_accessed=COST, transcendentals=0),
    )(*[a for a, _ in inputs])


def images_out(images, length, columns, kind):
    shape = (images, length, columns)
    return (shape, kind, pl.BlockSpec((1, length, columns), lambda i: (i, 0, 0)))


def attend_outputs(images, length, width):
    return [
        images_out(images, length, width, F32),
        images_out(images, length, width, BF16),
        images_out(images, length, width, BF16),
        images_out(images, length, width, BF16),
        images_out(images, length, width, BF16),
        images_out(images, length, MISC, F32),
        images_out(images, length, 2, F32),
        images_out(images, length, width, BF16),
    ]


def greet_all(peers):
    barrier = pltpu.get_barrier_semaphore()
    for peer in peers:
        pl.semaphore_signal(barrier, inc=1, device_id=peer, device_id_type=MESH)
    pl.semaphore_wait(barrier, len(peers))


def remote(source, target, send, recv, device):
    return pltpu.make_async_remote_copy(
        src_ref=source, dst_ref=target, send_sem=send, recv_sem=recv, device_id=device, device_id_type=MESH
    )


class SharedGather:
    def __init__(self, mine, out, sems):
        send, recv, pass_send, pass_recv, own = sems
        parts, share, _ = out.shape
        half = share // 2
        row, me = lax.axis_index("dp"), lax.axis_index("expert")
        core = lax.rem(me, 2)
        sibling = {"expert": me + 1 - 2 * core}
        rows = pl.ds(pl.multiple_of(core * half, half), half)
        self.fetches, self.hands = [], []
        for k in range(1, parts):
            peer = {"dp": lax.rem(row + k, parts)}
            self.fetches.append(remote(mine.at[rows], out.at[row, rows], send.at[k - 1], recv.at[k - 1], peer))
            place = out.at[lax.rem(row - k + parts, parts), rows]
            self.hands.append(remote(place, place, pass_send.at[k - 1], pass_recv.at[k - 1], sibling))
        self.keep = pltpu.make_async_copy(mine, out.at[row], own)

    def start(self):
        for copy in self.fetches:
            copy.start()
        self.keep.start()

    def finish(self):
        for fetch, hand in zip(self.fetches, self.hands):
            fetch.wait_recv()
            hand.start()
        for fetch, hand in zip(self.fetches, self.hands):
            fetch.wait_send()
            hand.wait()
        self.keep.wait()


class Gather:
    def __init__(self, parts, mine, place, sems):
        send, recv, own = sems
        row = lax.axis_index("dp")
        self.first, self.second = [], []
        self.keep = pltpu.make_async_copy(mine, place(row), own)

        def add(group, source, target, peer):
            n = len(self.first) + len(self.second)
            group.append(remote(source, target, send.at[n], recv.at[n], {"dp": peer}))

        if parts != 4:
            for k in range(1, parts):
                add(self.first, mine, place(row), lax.rem(row + k, parts))
            return
        near, far = row + 1 - 2 * lax.rem(row, 2), lax.rem(row + 2, 4)
        quarter = mine.shape[0] // 4
        halves = [[slice(n * quarter, (n + 1) * quarter) for n in pair] for pair in ((0, 1), (2, 3))]
        for rows, peer in ((halves[0], near), (halves[1], far)):
            for part in rows:
                add(self.first, mine.at[part], place(row).at[part], peer)
        for rows, peer, other in ((halves[0], far, near), (halves[1], near, far)):
            for part in rows:
                add(self.second, mine.at[part], place(row).at[part], peer)
            for part in rows:
                add(self.second, place(other).at[part], place(other).at[part], peer)

    def start(self):
        for copy in self.first:
            copy.start()
        self.keep.start()

    def forward(self):
        for copy in self.first:
            copy.wait_recv()
        for copy in self.second:
            copy.start()

    def finish(self):
        for copy in self.second:
            copy.wait_recv()
        self.keep.wait()

    def drain(self):
        for copy in self.first + self.second:
            copy.wait_send()


def gather_sems(parts):
    count = 12 if parts == 4 else parts - 1
    return [pltpu.SemaphoreType.DMA((count,)), pltpu.SemaphoreType.DMA((count,)), pltpu.SemaphoreType.DMA]


def shared_sems(parts):
    return [pltpu.SemaphoreType.DMA((parts - 1,))] * 4 + [pltpu.SemaphoreType.DMA]


ROOT_HALF = 0.7071067811865476
ROOT_TWO_PI_INVERSE = 0.3989422804014327

class Swap:
    def __init__(self, sent, arrived, made, back, sems):
        self.sent, self.arrived, self.made, self.back = sent, arrived, made, back
        self.out_send, self.out_recv, self.home_send, self.home_recv, self.own = sems
        self.local, self.count = arrived.shape[0], arrived.shape[1]
        self.me = lax.axis_index("expert")

    def greet(self, others=()):
        greet_all([{"expert": lax.rem(self.me + k, self.count)} for k in range(1, self.count)] + list(others))

    def outward(self, j, k, peer):
        return pltpu.make_async_remote_copy(
            src_ref=self.sent.at[j, peer], dst_ref=self.arrived.at[j, self.me],
            send_sem=self.out_send.at[j, k], recv_sem=self.out_recv.at[j, k],
            device_id={"expert": peer}, device_id_type=MESH,
        )

    def homeward(self, j, k, peer):
        return pltpu.make_async_remote_copy(
            src_ref=self.made.at[j, peer], dst_ref=self.back.at[j, self.me],
            send_sem=self.home_send.at[j, k], recv_sem=self.home_recv.at[j, k],
            device_id={"expert": peer}, device_id_type=MESH,
        )

    def own_out(self, j):
        return pltpu.make_async_copy(self.sent.at[j, self.me], self.arrived.at[j, self.me], self.own.at[j])

    def own_home(self, j):
        return pltpu.make_async_copy(self.made.at[j, self.me], self.back.at[j, self.me], self.own.at[self.local + j])

    def send_all(self, sources, drow, layer):
        chips = self.count // 2
        capacity, width = self.sent.shape[2:]
        images, length, _ = sources[0].shape

        for j in range(self.local):

            def fill(turn, carry, j=j):
                sign = 2 * lax.rem(turn, 2) - 1
                chip = lax.rem(self.me // 2 + chips // 2 + sign * ((turn + 1) // 2) + chips, chips)
                first = (j * self.count + 2 * chip) * capacity
                slots = lax.broadcasted_iota(jnp.int32, (2 * capacity, length), 0) + first
                total = jnp.zeros((2 * capacity, width), F32)
                for image in range(images):
                    dest = drow[layer, image]
                    hits = [slots == dest[0:1, :], slots == dest[1:2, :]]
                    if len(sources) == 1:
                        hits = [hits[0] | hits[1]]
                    for hit, source in zip(hits, sources):
                        total = total + dot(hit.astype(F32).astype(BF16), source[image])
                self.sent[j, pl.ds(2 * chip, 2)] = total.astype(BF16).reshape(2, capacity, width)
                for core in range(2):
                    peer = 2 * chip + core
                    k = lax.rem(peer - self.me + self.count, self.count)

                    @pl.when(peer != self.me)
                    def _(k=k, peer=peer):
                        self.outward(j, k, peer).start()

                    @pl.when(peer == self.me)
                    def _():
                        self.own_out(j).start()

                return carry

            lax.fori_loop(0, chips, fill, 0)

    def chip(self, turn):
        chips = self.count // 2
        return lax.rem(self.me // 2 - turn + chips, chips)

    def wait_chip(self, j, chip):
        for core in range(2):
            source = 2 * chip + core
            k = lax.rem(self.me - source + self.count, self.count)

            @pl.when(source != self.me)
            def _(k=k, source=source):
                pltpu.make_async_remote_copy(
                    src_ref=self.arrived.at[j, source], dst_ref=self.arrived.at[j, source],
                    send_sem=self.out_send.at[j, k], recv_sem=self.out_recv.at[j, k],
                    device_id={"expert": source}, device_id_type=MESH,
                ).wait_recv()

            @pl.when(source == self.me)
            def _():
                self.own_out(j).wait()

    def send_home(self, j, chip):
        for core in range(2):
            peer = 2 * chip + core
            k = lax.rem(peer - self.me + self.count, self.count)

            @pl.when(peer != self.me)
            def _(k=k, peer=peer):
                self.homeward(j, k, peer).start()

            @pl.when(peer == self.me)
            def _():
                self.own_home(j).start()

    def wait_home(self, j, chip):
        for core in range(2):
            source = 2 * chip + core
            k = lax.rem(self.me - source + self.count, self.count)

            @pl.when(source != self.me)
            def _(k=k, source=source):
                place = self.back.at[j, source]
                remote(place, place, self.home_send.at[j, k], self.home_recv.at[j, k], {"expert": source}).wait_recv()

            @pl.when(source == self.me)
            def _():
                self.own_home(j).wait()

    def take_home(self, dcol, layer, total):
        count, images, length, width = total.shape
        capacity = self.back.shape[2]
        total[...] = jnp.zeros_like(total)
        for j in range(self.local):

            def step(turn, carry, j=j):
                chip = self.chip(turn)
                self.wait_home(j, chip)
                rows = self.back[j, pl.ds(2 * chip, 2)].reshape(2 * capacity, width)
                first = (j * self.count + 2 * chip) * capacity
                lanes = lax.broadcasted_iota(jnp.int32, (length, 2 * capacity), 1) + first
                for image in range(images):
                    dest = dcol[layer, image]
                    hits = [dest[:, 0:1] == lanes, dest[:, 1:2] == lanes]
                    if count == 1:
                        hits = [hits[0] | hits[1]]
                    for k, hit in enumerate(hits):
                        total[k, image] += dot(hit.astype(F32).astype(BF16), rows).astype(total.dtype)
                return carry

            lax.fori_loop(0, self.count // 2, step, 0)

    def finish(self):
        for j in range(self.local):
            for k in range(1, self.count):
                peer = lax.rem(self.me + k, self.count)
                self.outward(j, k, peer).wait_send()
                self.homeward(j, k, peer).wait_send()


def weight_blocks(weights, j, f):
    _, parts, rows, width = weights.shape
    share, take = width // parts, rows // 2
    each = FF_BLOCK // take
    first = weights[j, :, f * share : (f + 1) * share, :].reshape(width, width)
    second = weights[j, f * each : (f + 1) * each, take:, :].reshape(FF_BLOCK, width)
    return first, second


def expert_kernel(layer, with_dense, *refs):
    if with_dense:
        *refs, n1, n2, n3, n4, n5, m1, m2, m3 = refs
        refs = list(refs)
        dense_in, next_in, dense_out, next_out = refs.pop(8), refs.pop(8), refs.pop(14), refs.pop(14)
        dense = SharedGather(dense_in, dense_out, (n1, n2, n3, n4, n5))
        following = Gather(dense_out.shape[0], next_in, lambda p: next_out.at[p], (m1, m2, m3))
    (
        hidden, drow, dcol, inner_first, outer_mine, mine, b1, b2, picked, arrived_out, g_out, s_out, outer_out, packed_out,
        back, sent, arrived, made, weights, g_stage, s_stage, out_send, out_recv, home_send, home_recv, own, load, stores, last,
        *gather_refs,
    ) = refs
    row = lax.axis_index("dp")
    parts = weights.shape[1]
    take = outer_mine.shape[0]
    gathers = [
        Gather(parts, outer_mine, lambda p: weights.at[0, p, take:], gather_refs[:3]),
        Gather(parts, mine, lambda p: weights.at[1, p], gather_refs[3:]),
    ]
    swap = Swap(sent, arrived, made, back, (out_send, out_recv, home_send, home_recv, own))
    local, count, capacity, width = arrived.shape
    chips = count // 2
    rows = 2 * capacity
    ff = g_out.shape[2]
    first_load = pltpu.make_async_copy(inner_first, weights.at[0, :, :take], load)
    first_load.start()
    swap.greet([{"dp": lax.rem(row + k, parts)} for k in range(1, parts)])
    gathers[0].start()
    swap.send_all([hidden], drow, layer)
    gathers[0].forward()
    gathers[1].start()
    gathered = [
        pltpu.make_async_copy(weights.at[0, :, take:], outer_out, last.at[1]),
        pltpu.make_async_copy(weights.at[1], packed_out, last.at[2]),
    ]

    def kept(j, slot, chip):
        place = pl.ds(pl.multiple_of(chip * rows, rows), rows)
        return (
            pltpu.make_async_copy(g_stage.at[slot], g_out.at[j, place, :], stores.at[0, slot]),
            pltpu.make_async_copy(s_stage.at[slot], s_out.at[j, place, :], stores.at[1, slot]),
        )

    for j in range(local):
        if j == 0:
            first_load.wait()
        gathers[j].finish()
        gathered[j].start()
        if j == 1 and with_dense:
            following.start()
        number = layer * local + j

        def chip_step(turn, carry, j=j, number=number):
            chip = swap.chip(turn)
            slot = lax.rem(turn, 2)
            swap.wait_chip(j, chip)
            if j == 0:

                @pl.when(turn == 1)
                def _():
                    gathers[1].forward()
                    if with_dense:
                        dense.start()

            if j == 1 and with_dense:

                @pl.when(turn == 2)
                def _():
                    following.forward()

            @pl.when(j * chips + turn >= 2)
            def _():
                for copy in kept(j, slot, chip):
                    copy.wait()

            x = arrived[j, pl.ds(2 * chip, 2)].reshape(rows, width)
            total = jnp.broadcast_to(b2[number : number + 1, :], (rows, width))
            for f in range(ff // FF_BLOCK):
                cols = slice(f * FF_BLOCK, (f + 1) * FF_BLOCK)
                first, second = weight_blocks(weights, j, f)
                inner = dot(x, first) + b1[number : number + 1, cols]
                normal = 0.5 * (1.0 + lax.erf(inner * ROOT_HALF))
                g = (inner * normal).astype(BF16)
                density = jnp.exp(-0.5 * inner * inner) * ROOT_TWO_PI_INVERSE
                g_stage[slot, :, cols] = g
                s_stage[slot, :, cols] = (normal + inner * density).astype(BF16)
                total = total + dot(g, second)
            made[j, pl.ds(2 * chip, 2)] = total.astype(BF16).reshape(2, capacity, width)
            swap.send_home(j, chip)
            for copy in kept(j, slot, chip):
                copy.start()
            return carry

        lax.fori_loop(0, chips, chip_step, 0)
    final = pltpu.make_async_copy(arrived, arrived_out, last.at[0])
    final.start()
    if with_dense:
        dense.finish()
        following.finish()
        following.drain()
    for slot in range(2):
        for copy in kept(0, slot, 0):
            copy.wait()
    swap.take_home(dcol, layer, picked)
    swap.finish()
    for gather, copy in zip(gathers, gathered):
        gather.drain()
        copy.wait()
    final.wait()


def expert_back_kernel(layer, with_above, *refs):
    if with_above:
        *refs, above_in, above_own, above_send, above_recv, above_load = refs
        refs = list(refs)
        above, above_sum = refs.pop(10), refs.pop(15)
    (
        zero, one, drow, dcol, inner_first, outer_first, packed_second, arrived_x, g_in, s_in,
        came, summed, out, bias1, bias2, back, sent, arrived, made, weights, x, du, s_stage, g_stage, first_stage, second_stage, share_out, share_in,
        db1, db2, db1_in, db2_in,
        out_send, out_recv, home_send, home_recv, own, load, fetch, stores, share_send, share_recv,
        bias_send, bias_recv,
    ) = refs
    swap = Swap(sent, arrived, made, back, (out_send, out_recv, home_send, home_recv, own))
    row = lax.axis_index("dp")
    local, count, capacity, width = arrived.shape
    chips = count // 2
    rows = 2 * capacity
    ff = g_in.shape[2]
    blocks = ff // FF_BLOCK
    _, parts, all_rows, _ = weights.shape
    share, take = width // parts, all_rows // 2
    each = FF_BLOCK // take
    loads = [
        pltpu.make_async_copy(inner_first, weights.at[0, :, :take], load.at[0]),
        pltpu.make_async_copy(packed_second, weights.at[1], load.at[1]),
        pltpu.make_async_copy(arrived_x, x, load.at[local]),
        pltpu.make_async_copy(outer_first, weights.at[0, :, take:], load.at[local + 1]),
    ]
    for copy in loads:
        copy.start()

    def slopes(j, turn):
        slot = lax.rem(turn, 2)
        place = pl.ds(pl.multiple_of(swap.chip(turn) * rows, rows), rows)
        return pltpu.make_async_copy(s_in.at[j, place, :], s_stage.at[slot], fetch.at[0, slot])

    def activations(j, f):
        return pltpu.make_async_copy(
            g_in.at[j, :, f * FF_BLOCK : (f + 1) * FF_BLOCK], g_stage.at[f % 2], fetch.at[1, f % 2]
        )

    def results(j, f):
        return (
            pltpu.make_async_copy(
                first_stage.at[f % 2], out.at[:, j - 1, f * share : (f + 1) * share, :], stores.at[0, f % 2]
            ),
            pltpu.make_async_copy(
                second_stage.at[f % 2], out.at[f * each : (f + 1) * each, j - 1, take:, :], stores.at[1, f % 2]
            ),
        )

    def share_copy(k):
        peer = lax.rem(row + k, parts)
        return pltpu.make_async_remote_copy(
            src_ref=share_out.at[peer], dst_ref=share_in.at[k - 1],
            send_sem=share_send.at[k - 1], recv_sem=share_recv.at[k - 1],
            device_id={"dp": peer}, device_id_type=MESH,
        )

    slopes(0, 0).start()
    peers = [{"dp": lax.rem(row + k, parts)} for k in range(1, parts)]
    swap.greet(peers)
    if with_above:
        above_copies = [
            pltpu.make_async_remote_copy(
                src_ref=above.at[lax.rem(row + k, parts)], dst_ref=above_in.at[k - 1],
                send_sem=above_send.at[k - 1], recv_sem=above_recv.at[k - 1],
                device_id=peers[k - 1], device_id_type=MESH,
            )
            for k in range(1, parts)
        ]
        above_copies.append(pltpu.make_async_copy(above.at[row], above_own, above_load))
        for copy in above_copies:
            copy.start()
    swap.send_all([zero, one], drow, layer)
    loads[local + 1].wait()
    for j in range(local):
        loads[j].wait()
        activations(j, 0).start()

        def chip_step(turn, carry, j=j):
            chip = swap.chip(turn)
            slot = lax.rem(turn, 2)

            @pl.when(turn + 1 < chips)
            def _():
                slopes(j, turn + 1).start()

            swap.wait_chip(j, chip)
            slopes(j, turn).wait()
            dy = arrived[j, pl.ds(2 * chip, 2)].reshape(rows, width)
            place = pl.ds(pl.multiple_of(chip * rows, rows), rows)
            total = jnp.zeros((rows, width), F32)
            for f in range(blocks):
                cols = slice(f * FF_BLOCK, (f + 1) * FF_BLOCK)
                first, second = weight_blocks(weights, j, f)
                part = (dot_nt(dy, second) * s_stage[slot, :, cols].astype(F32)).astype(BF16)
                du[place, cols] = part
                total = total + dot_nt(part, first)
            made[j, pl.ds(2 * chip, 2)] = total.astype(BF16).reshape(2, capacity, width)
            swap.send_home(j, chip)
            return carry

        lax.fori_loop(0, chips, chip_step, 0)
        if j + 1 < local:
            slopes(j + 1, 0).start()
        if j == 0:
            loads[local].wait()
        dy = arrived[j].reshape(count * capacity, width)
        db2[j : j + 1, :] = jnp.sum(dy.astype(F32), axis=0, keepdims=True)
        for f in range(blocks):
            cols = slice(f * FF_BLOCK, (f + 1) * FF_BLOCK)
            if f + 1 < blocks:
                activations(j, f + 1).start()
            if j > 1 or (j == 1 and f > 1):
                for copy in results(j, f):
                    copy.wait()
            part = du[:, cols]
            grad = dot_tn(x[j].reshape(count * capacity, width), part).astype(BF16)
            if j == 0:
                share_out[:, f * share : (f + 1) * share, :] = grad.reshape(parts, share, width)
            else:
                first_stage[f % 2] = grad.reshape(parts, share, width)
            db1[j : j + 1, cols] = jnp.sum(part.astype(F32), axis=0, keepdims=True)
            activations(j, f).wait()
            grad = dot_tn(g_stage[f % 2], dy).astype(BF16).reshape(each, take, width)
            if j == 0:
                share_out[f * each : (f + 1) * each, take:, :] = grad
            else:
                second_stage[f % 2] = grad
                for copy in results(j, f):
                    copy.start()
        if j == 0:
            for k in range(1, parts):
                share_copy(k).start()
    part_ff = ff // parts
    bias_copies = []
    for k in range(1, parts):
        place = pl.ds(pl.multiple_of(lax.rem(row + k, parts) * part_ff, part_ff), part_ff)
        for n, (source, target) in enumerate(((db1.at[:, place], db1_in.at[k - 1]), (db2, db2_in.at[k - 1]))):
            bias_copies.append(pltpu.make_async_remote_copy(
                src_ref=source, dst_ref=target, send_sem=bias_send.at[n, k - 1], recv_sem=bias_recv.at[n, k - 1],
                device_id=peers[k - 1], device_id_type=MESH,
            ))
            bias_copies[-1].start()
    if with_above:
        for copy in above_copies:
            copy.wait()
        total = above_own[...].astype(F32)
        for k in range(1, parts):
            total = total + above_in[k - 1].astype(F32)
        above_sum[...] = total.astype(BF16)
    for k in range(1, parts):
        share_copy(k).wait_recv()
    step = 64

    def add_up(turn, carry):
        place = pl.ds(pl.multiple_of(turn * step, step), step)
        total = share_out[row, place, :].astype(F32)
        for k in range(1, parts):
            total = total + share_in[k - 1, place, :].astype(F32)
        summed[place, :] = total
        return carry

    lax.fori_loop(0, all_rows // step, add_up, 0)
    for copy in bias_copies:
        copy.wait_recv()
    total1, total2 = db1[:, pl.ds(pl.multiple_of(row * part_ff, part_ff), part_ff)], db2[...]
    for k in range(1, parts):
        total1, total2 = total1 + db1_in[k - 1], total2 + db2_in[k - 1]
    bias1[...], bias2[...] = total1, total2
    swap.take_home(dcol, layer, came)
    for copy in bias_copies:
        copy.wait_send()
    for k in range(1, parts):
        share_copy(k).wait_send()
    for f in range(2):
        for copy in results(1, f):
            copy.wait()
    swap.finish()


def swap_sems(local, count):
    pairs = [pltpu.SemaphoreType.DMA((local, count))] * 4
    return pairs + [pltpu.SemaphoreType.DMA((2 * local,))]


def expert_call(body, inputs, outputs, scratch, number):
    def spec(held):
        return pl.BlockSpec(memory_space=pltpu.VMEM if held else pl.ANY)

    shapes = [jax.ShapeDtypeStruct(s, t) for s, t, _ in outputs]
    return pl.pallas_call(
        body,
        in_specs=[spec(held) for _, held in inputs],
        out_specs=[spec(held) for _, _, held in outputs],
        out_shape=shapes,
        scratch_shapes=scratch,
        compiler_params=pltpu.CompilerParams(
            collective_id=number, has_side_effects=True, vmem_limit_bytes=VMEM
        ),
        cost_estimate=pl.CostEstimate(flops=COST, bytes_accessed=COST, transcendentals=0),
    )(*[a for a, _ in inputs])


def expert_forward(hidden, drow, dcol, shape, inner, outer_mine, mine, biases, following, layer):
    b1, b2 = biases
    local, count, capacity, width = shape
    ff = b1.shape[1]
    rows = 2 * capacity
    parts = inner.shape[0]
    packed = (parts, *mine.shape)
    slots = (local, count * capacity, ff)
    inputs = [(hidden, True), (drow, True), (dcol, True), (inner, False), (outer_mine, False), (mine, False), (b1, True), (b2, True)]
    outputs = [
        ((2, *hidden.shape), BF16, True), (shape, BF16, False), (slots, BF16, False), (slots, BF16, False),
        ((parts, *outer_mine.shape), BF16, False), (packed, BF16, False),
    ]
    scratch = [
        pltpu.VMEM(shape, BF16), pltpu.VMEM(shape, BF16), pltpu.VMEM(shape, BF16), pltpu.VMEM(shape, BF16),
        pltpu.VMEM((local, *packed), BF16),
        pltpu.VMEM((2, rows, ff), BF16), pltpu.VMEM((2, rows, ff), BF16),
    ] + swap_sems(local, count) + [
        pltpu.SemaphoreType.DMA, pltpu.SemaphoreType.DMA((2, 2)), pltpu.SemaphoreType.DMA((3,)),
    ] + gather_sems(parts) * 2
    if following:
        inputs += [(item, False) for item in following]
        outputs += [((parts, *item.shape), BF16, False) for item in following]
        scratch += shared_sems(parts) + gather_sems(parts)
    return expert_call(functools.partial(expert_kernel, layer, bool(following)), inputs, outputs, scratch, layer)


def expert_backward(sources, drow, dcol, weights, arrived, g, s, above, layer):
    shape = arrived.shape
    local, count, capacity, width = shape
    ff = g.shape[2]
    rows = 2 * capacity
    parts, all_rows, _ = weights[2].shape
    share, take = width // parts, all_rows // 2
    inputs = [(a, True) for a in (*sources, drow, dcol)] + [(a, False) for a in (*weights, arrived, g, s)]
    outputs = [
        ((1, *sources[0].shape), F32, True), ((all_rows, width), F32, True), ((parts, local - 1, all_rows, width), BF16, False),
        ((local, ff // parts), F32, True), ((local, width), F32, True),
    ]
    scratch = [
        pltpu.VMEM(shape, BF16), pltpu.VMEM(shape, BF16), pltpu.VMEM(shape, BF16), pltpu.VMEM(shape, BF16),
        pltpu.VMEM((local, parts, all_rows, width), BF16), pltpu.VMEM(shape, BF16),
        pltpu.VMEM((count * capacity, ff), BF16), pltpu.VMEM((2, rows, ff), BF16),
        pltpu.VMEM((2, count * capacity, FF_BLOCK), BF16), pltpu.VMEM((2, parts, share, width), BF16),
        pltpu.VMEM((2, FF_BLOCK // take, take, width), BF16),
        pltpu.VMEM((parts, all_rows, width), BF16), pltpu.VMEM((parts - 1, all_rows, width), BF16),
        pltpu.VMEM((local, ff), F32), pltpu.VMEM((local, width), F32),
        pltpu.VMEM((parts - 1, local, ff // parts), F32), pltpu.VMEM((parts - 1, local, width), F32),
    ] + swap_sems(local, count) + [
        pltpu.SemaphoreType.DMA((local + 2,)), pltpu.SemaphoreType.DMA((2, 2)), pltpu.SemaphoreType.DMA((2, 2)),
        pltpu.SemaphoreType.DMA((parts - 1,)), pltpu.SemaphoreType.DMA((parts - 1,)),
        pltpu.SemaphoreType.DMA((2, parts - 1)), pltpu.SemaphoreType.DMA((2, parts - 1)),
    ]
    if above is not None:
        inputs.append((above, False))
        outputs.append((above.shape[1:], BF16, True))
        scratch += [
            pltpu.VMEM((parts - 1, *above.shape[1:]), BF16), pltpu.VMEM(above.shape[1:], BF16),
            pltpu.SemaphoreType.DMA((parts - 1,)), pltpu.SemaphoreType.DMA((parts - 1,)), pltpu.SemaphoreType.DMA,
        ]
    done = expert_call(
        functools.partial(expert_back_kernel, layer, above is not None), inputs, outputs, scratch, LAYERS + layer
    )
    return done if above is not None else [*done, None]


def prepare_kernel(capacity, owners, *refs):
    squares, (router, *vectors), (inner_bias, outer_bias, routes) = refs[:4], refs[4:12], refs[12:15]
    tokens_in, (out, above, b1, b2, dcol, drow), tokens_out = refs[15:17], refs[17:23], refs[23:25]
    mine, turned, inner_low, outer_low, token_ins, token_outs = refs[25:31]
    sems, (b1_send, b1_recv, b2_send, b2_recv, own, token_load, token_store) = refs[31:36], refs[36:]
    parts, share, _ = out.shape
    loads = [pltpu.make_async_copy(tokens_in[n], token_ins.at[n], token_load.at[n]) for n in range(2)]
    stores = [pltpu.make_async_copy(token_outs.at[n], tokens_out[n], token_store.at[n]) for n in range(2)]
    width = squares[0].shape[2]
    experts_all = router.shape[2]
    local, part_ff = inner_bias.shape[1:]
    row, me = lax.axis_index("dp"), lax.axis_index("expert")
    sibling = {"expert": me + 1 - 2 * lax.rem(me, 2)}
    peers = [{"dp": lax.rem(row + k, parts)} for k in range(1, parts)]
    gather = SharedGather(mine, out, sems)

    def pack(target, layer):
        for n in range(4):
            target[:, n * width : (n + 1) * width] = squares[n][layer].astype(BF16)
        turned[...] = jnp.zeros_like(turned)
        for n in range(7):
            turned[VEC_AT + n : VEC_AT + n + 1, :] = vectors[n][layer : layer + 1, :]
        target[:, 4 * width :] = turned[...].T.astype(BF16)
        target[:, 4 * width : 4 * width + experts_all] = router[layer].astype(BF16)

    pack(mine, 0)
    for layer in range(LAYERS):
        for j in range(local):
            n = layer * local + j
            inner_low[n : n + 1, :] = inner_bias[layer, j : j + 1, :].astype(BF16).astype(F32)
            outer_low[n : n + 1, :] = outer_bias[layer, j : j + 1, :].astype(BF16).astype(F32)
    greet_all([sibling] + peers)
    place = pl.ds(pl.multiple_of(row * part_ff, part_ff), part_ff)
    singles = [
        remote(inner_low, b1.at[:, place], b1_send.at[k], b1_recv.at[k], peers[k]) for k in range(parts - 1)
    ] + [remote(outer_low, b2.at[row], b2_send.at[k], b2_recv.at[k], peers[k]) for k in range(parts - 1)]
    keeps = [
        pltpu.make_async_copy(inner_low, b1.at[:, place], own.at[0]),
        pltpu.make_async_copy(outer_low, b2.at[row], own.at[1]),
    ]
    gather.start()
    for copy in singles + keeps + loads:
        copy.start()
    pack(above, 1)
    for n in range(2):
        loads[n].wait()
        for image in range(routes.shape[1]):
            token_outs[n, image] = token_ins[n, :, image, :]
        stores[n].start()

    length = routes.shape[2]
    lanes = lax.broadcasted_iota(jnp.int32, (length, MISC), 1)
    earlier = (
        lax.broadcasted_iota(jnp.int32, (length, length), 0) > lax.broadcasted_iota(jnp.int32, (length, length), 1)
    ).astype(F32).astype(BF16)
    for layer in range(LAYERS):
        seen = jnp.zeros((1, MISC), F32)
        for image in range(routes.shape[1]):
            hots, dests = [], []
            for k in range(2):
                hots.append((lanes == routes[layer, image, :, k : k + 1]).astype(F32))
            counts = hots[0] + hots[1]
            before = dot(earlier, counts.astype(BF16)) + seen
            seen = seen + jnp.sum(counts, axis=0, keepdims=True)
            for k in range(2):
                slot = jnp.sum(hots[k] * before, axis=-1, keepdims=True)
                expert = routes[layer, image, :, k : k + 1].astype(F32)
                owner = jnp.floor(expert * (1.0 / local))
                place = ((expert - owner * local) * owners + owner) * capacity + slot
                dests.append(jnp.where(slot < capacity, place, -1.0))
                dcol[layer, image, :, k : k + 1] = dests[k].astype(jnp.int32)
            both = jnp.where(lanes == 0, dests[0], jnp.where(lanes == 1, dests[1], 0.0))
            drow[layer, image] = both.T[0:2, :].astype(jnp.int32)

    gather.finish()
    for copy in singles + keeps + stores:
        copy.wait()


def prepare(squares, router, vectors, inner_bias, outer_bias, routes, tokens, parts, owners, number):
    layers, share, width = squares[0].shape
    experts_all = router.shape[2]
    local, part_ff = inner_bias.shape[1:]
    _, images, length, _ = routes.shape
    capacity = (10 * images * length // (4 * experts_all) + 7) // 8 * 8
    columns = 4 * width + MISC
    count = layers * local
    sems = shared_sems(parts) + [pltpu.SemaphoreType.DMA((parts - 1,))] * 4 + [pltpu.SemaphoreType.DMA((2,))] * 3
    inputs = [*squares, router, *vectors, inner_bias, outer_bias, routes]
    turned = [jnp.transpose(item, (1, 0, 2)) for item in tokens]
    out, above, b1, b2, dcol, drow, *tokens = expert_call(
        functools.partial(prepare_kernel, capacity, owners), [(a, True) for a in inputs] + [(a, False) for a in turned],
        [
            ((parts, share, columns), BF16, False), ((share, columns), BF16, True),
            ((count, part_ff * parts), F32, False), ((parts, count, share), F32, False),
            ((layers, images, length, 2), jnp.int32, True), ((layers, images, 2, length), jnp.int32, True),
            ((images, length, width), F32, False), ((images, length, width), F32, False),
        ],
        [
            pltpu.VMEM((share, columns), BF16), pltpu.VMEM((MISC, share), F32),
            pltpu.VMEM((count, part_ff), F32), pltpu.VMEM((count, share), F32),
            pltpu.VMEM((2, length, images, width), F32), pltpu.VMEM((2, images, length, width), F32),
        ] + sems,
        number,
    )
    b2 = jnp.transpose(b2, (1, 0, 2)).reshape(count, width)
    return out.reshape(width, columns), above, (b1, b2), dcol, drow, capacity, tokens


def settle_widths(columns, chips):
    blocks = columns // (MISC * chips)
    wide = (blocks + 1) // 2 * MISC
    return wide, columns // chips - wide


def settle_kernel(
    grads, tokens_a, tokens_b, final, tokens_out_a, tokens_out_b, own, paired, total, chips_in, dp_in, total_b, chips_in_b, dp_in_b,
    pair_send, pair_recv, local, out_send, out_recv, dp_send, dp_recv, out_send_b, out_recv_b, dp_send_b, dp_recv_b,
    back_send, back_recv, pass_send, pass_recv, token_ins, token_outs, token_load, token_store,
):
    parts, share, columns = grads.shape
    half = share // 2
    row, me = lax.axis_index("dp"), lax.axis_index("expert")
    core, chip = lax.rem(me, 2), me // 2
    chips = chips_in.shape[0] + 1
    wide, narrow = settle_widths(columns, chips)
    split = chips * wide
    sibling = {"expert": me + 1 - 2 * core}
    mine = pl.ds(pl.multiple_of(core * half, half), half)
    other = pl.ds(pl.multiple_of((1 - core) * half, half), half)

    def cols(number):
        return pl.ds(pl.multiple_of(number * wide, MISC), wide)

    def cols_b(number, start):
        return pl.ds(pl.multiple_of(start + number * narrow, MISC), narrow)

    def chip_at(k):
        return lax.rem(chip + k + chips, chips)

    dp_peers = [{"dp": lax.rem(row + k, parts)} for k in range(1, parts)]
    chip_peers = [{"expert": 2 * chip_at(k) + core} for k in range(1, chips)]
    greet_all([sibling] + dp_peers + chip_peers)

    order = [lax.rem(row + 1 + i, parts) for i in range(parts)]
    pairs, keeps = [], []
    for i in range(parts):
        source = grads.at[order[i]]
        pairs.append(remote(source.at[other], paired.at[i], pair_send.at[i], pair_recv.at[i], sibling))
        keeps.append(pltpu.make_async_copy(source.at[mine], own.at[i], local.at[i]))
        pairs[i].start()
        keeps[i].start()
    loads = [pltpu.make_async_copy(t, token_ins.at[n], token_load.at[n]) for n, t in enumerate((tokens_a, tokens_b))]
    stores = [
        pltpu.make_async_copy(token_outs.at[n], t, token_store.at[n]) for n, t in enumerate((tokens_out_a, tokens_out_b))
    ]
    for copy in loads:
        copy.start()
    outs, scatters_b = [], []
    for i in range(parts):
        pairs[i].wait_recv()
        keeps[i].wait()
        own[i] = (own[i].astype(F32) + paired[i].astype(F32)).astype(BF16)
        if i < parts - 1:
            scatters_b.append(
                remote(own.at[i, :, split:], dp_in_b.at[i], dp_send_b.at[i], dp_recv_b.at[i], dp_peers[i])
            )
            scatters_b[i].start()
        outs.append([
            remote(
                own.at[i, :, cols(chip_at(k))], chips_in.at[k - 1, i], out_send.at[k - 1, i], out_recv.at[k - 1, i],
                chip_peers[k - 1],
            )
            for k in range(1, chips)
        ])
        for copy in outs[i]:
            copy.start()
    for n in range(2):
        loads[n].wait()
        for image in range(token_ins.shape[1]):
            token_outs[n, :, image, :] = token_ins[n, image]
        stores[n].start()
    value = own[parts - 1, :, split:].astype(F32)
    for i in range(parts - 1):
        scatters_b[i].wait_recv()
        value = value + dp_in_b[i].astype(F32)
    total_b[...] = value.astype(BF16)
    outs_b = [
        remote(
            total_b.at[:, cols_b(chip_at(k), 0)], chips_in_b.at[k - 1], out_send_b.at[k - 1], out_recv_b.at[k - 1],
            chip_peers[k - 1],
        )
        for k in range(1, chips)
    ]
    for copy in outs_b:
        copy.start()
    scatters = []
    for i in range(parts):
        value = own[i, :, cols(chip)].astype(F32)
        for k in range(1, chips):
            outs[i][k - 1].wait_recv()
            value = value + chips_in[k - 1, i].astype(F32)
        if i < parts - 1:
            total[i] = value.astype(BF16)
            scatters.append(remote(total.at[i], dp_in.at[i], dp_send.at[i], dp_recv.at[i], dp_peers[i]))
            scatters[i].start()
        else:
            kept = value
    value = total_b[:, cols_b(chip, 0)].astype(F32)
    for k in range(1, chips):
        outs_b[k - 1].wait_recv()
        value = value + chips_in_b[k - 1].astype(F32)
    final[mine, cols_b(chip, split)] = value.astype(BF16)
    for i in range(parts - 1):
        scatters[i].wait_recv()
        kept = kept + dp_in[i].astype(F32)
    final[mine, cols(chip)] = kept.astype(BF16)

    def places(number):
        return [final.at[mine, cols(number)], final.at[mine, cols_b(number, split)]]

    backs, hands = [], []
    for n, place in enumerate(places(chip)):
        for k in range(1, chips):
            backs.append(remote(place, place, back_send.at[n, k - 1], back_recv.at[n, k - 1], chip_peers[k - 1]))
            backs[-1].start()
        hands.append(remote(place, place, pass_send.at[n, 0], pass_recv.at[n, 0], sibling))
        hands[-1].start()
    for k in range(1, chips):
        for n, place in enumerate(places(chip_at(-k))):
            backs[n * (chips - 1) + k - 1].wait_recv()
            hands.append(remote(place, place, pass_send.at[n, k], pass_recv.at[n, k], sibling))
            hands[-1].start()
    for copy in pairs + [copy for group in outs for copy in group] + outs_b + scatters + scatters_b + backs:
        copy.wait_send()
    for copy in hands + stores:
        copy.wait()


def settle(grads, tokens, chips, number):
    parts, share, columns = grads.shape
    half = share // 2
    images, length, width = tokens[0].shape
    halves = pltpu.VMEM((parts, half, columns), BF16)
    wide, narrow = settle_widths(columns, chips)
    dp_in = pltpu.VMEM((parts - 1, half, wide), BF16)
    rest = chips * narrow
    sems = [(parts,)] * 3 + [(chips - 1, parts)] * 2 + [(parts - 1,)] * 2
    sems += [(chips - 1,)] * 2 + [(parts - 1,)] * 2 + [(2, chips - 1)] * 2 + [(2, chips)] * 2
    turned = ((length, images, width), F32, False)
    return expert_call(
        settle_kernel, [(item, False) for item in (grads, *tokens)], [((share, columns), BF16, True), turned, turned],
        [
            halves, halves, dp_in, pltpu.VMEM((chips - 1, parts, half, wide), BF16), dp_in,
            pltpu.VMEM((half, rest), BF16), pltpu.VMEM((chips - 1, half, narrow), BF16),
            pltpu.VMEM((parts - 1, half, rest), BF16),
        ] + [pltpu.SemaphoreType.DMA(n) for n in sems] + [
            pltpu.VMEM((2, images, length, width), F32), pltpu.VMEM((2, length, images, width), F32),
            pltpu.SemaphoreType.DMA((2,)), pltpu.SemaphoreType.DMA((2,)),
        ],
        number,
    )


def unpack_kernel(*refs):
    count = 2 * LAYERS
    pieces, both, refs = refs[:count], refs[count : count + LAYERS], refs[count + LAYERS :]
    squares, router, vectors, (inner, outer) = refs[:4], refs[4], refs[5:12], refs[12:]
    layer = pl.program_id(0)
    share = both[0].shape[0]
    width = squares[0].shape[2]
    blocks = inner.shape[3] // FF_BLOCK

    for number in range(LAYERS):

        @pl.when(layer == number)
        def _(number=number):
            dense = both[number]
            for n in range(4):
                squares[n][0] = dense[:, n * width : (n + 1) * width].astype(F32)
            turned = dense[:, 4 * width : 4 * width + MISC].astype(F32).T
            router[0] = turned[: router.shape[1], :]
            for n in range(7):
                vectors[n][number : number + 1, :] = turned[VEC_AT + n : VEC_AT + n + 1, :]
            for j in range(2):
                piece = pieces[2 * number + j]
                for f in range(blocks):
                    inner[0, j, :, f * FF_BLOCK : (f + 1) * FF_BLOCK] = piece[
                        f * share : (f + 1) * share, :
                    ].astype(F32)
                outer[0, j] = piece[blocks * share :, :].astype(F32)


def unpack(pieces, both, local, ff, experts_all):
    layers, (share, columns) = len(both), both[0].shape
    rows, width = pieces[0].shape
    take = rows // 2
    by_layer = lambda *shape: ((layers, *shape), F32, pl.BlockSpec((1, *shape), lambda i: (i,) + (0,) * len(shape)))
    return call(
        unpack_kernel, (layers,),
        [(p, whole(p)) for p in (*pieces, *both)],
        [by_layer(share, width)] * 4 + [
            by_layer(experts_all, share),
        ] + [((layers, share), F32, pl.BlockSpec((layers, share), lambda i: (0, 0)))] * 7 + [
            by_layer(local, share, ff), by_layer(local, take, width),
        ],
    )


def shards(
    images, cotangent, routes, query_weight, key_weight, value_weight, output_weight, router_weight, query_bias,
    value_bias, output_bias, attend_gain, attend_shift, expert_gain, expert_shift, inner_weight, inner_bias,
    outer_weight, outer_bias,
):
    count, length, width = images.shape
    parts = lax.axis_size("dp")
    owners = lax.axis_size("expert")
    experts_all = router_weight.shape[2]
    local = inner_weight.shape[1]
    ff = inner_weight.shape[3]
    share = width // parts
    tokens = count * length
    squares = (query_weight, key_weight, value_weight, output_weight)
    vectors = (query_bias, value_bias, output_bias, attend_gain, attend_shift, expert_gain, expert_shift)
    columns = -(-(4 * width + MISC) // (MISC * (owners // 2))) * MISC * (owners // 2)

    inner_mine, outer_mine, mine = [], [], []
    for layer in range(LAYERS):
        first = inner_weight[layer].reshape(local, share, ff // FF_BLOCK, FF_BLOCK)
        first = jnp.transpose(first, (0, 2, 1, 3)).reshape(local, ff // parts, width).astype(BF16)
        second = outer_weight[layer].astype(BF16)
        inner_mine.append(first[0])
        outer_mine.append(second[0])
        mine.append(jnp.concatenate([first[1], second[1]], axis=0))
    dense, above, expert_biases, dcol, drow, capacity, (images, cotangent) = prepare(
        squares, router_weight, vectors, inner_bias, outer_bias, routes, (images, cotangent), parts, owners, 2 * LAYERS
    )
    packed = [dense]
    firsts = [lax.all_gather(inner_mine[0], "dp", axis=0, tiled=False)]
    slots = experts_all * capacity

    saved = []
    back = None
    rows = images
    for layer in range(LAYERS):
        weights = [(packed[layer], s) for s in packed_specs(packed[layer])]
        routing = [(routes, per_layer(routes, layer))]
        outputs = attend_outputs(count, length, width)
        if layer == 0:
            done = call(
                first_kernel, (count,), [(rows, per_image(rows))] + routing + weights, outputs
            )
        else:
            before = saved[-1]
            done = call(
                next_kernel, (count,),
                [
                    (before["middle"], per_image(before["middle"])),
                    (before["gates"], per_image(before["gates"])),
                    (picked, per_layer(picked, 0)),
                    (picked, per_layer(picked, 1)),
                ] + routing + weights,
                [
                    images_out(count, length, width, F32),
                ] + outputs
            )
            rows, *done = done
        middle, queries, keys, values, context, sums, gates = done[:7]
        picked, arrived, g, s, outer, second, *following = expert_forward(
            done[7], drow, dcol, (local, owners, capacity, width), firsts[layer], outer_mine[layer], mine[layer], expert_biases,
            (above, inner_mine[layer + 1]) if layer + 1 < LAYERS else (), layer,
        )
        if following:
            packed.append(following[0].reshape(width, following[0].shape[2]))
            firsts.append(following[1])
        saved.append({
            "rows": rows, "middle": middle, "attend": (queries, keys, values, context, sums), "gates": gates,
            "experts": (arrived, g, s), "weights": (firsts[layer], outer, second), "picked": picked,
        })

    last = saved[-1]
    result, dz, *sources = call(
        turn_kernel, (count,),
        [(last["middle"], per_image(last["middle"])), (last["gates"], per_image(last["gates"]))]
        + [(picked, per_layer(picked, k)) for k in range(2)]
        + [(cotangent, per_image(cotangent)), (routes, per_layer(routes, LAYERS - 1))],
        [images_out(count, length, width, F32), images_out(count, length, MISC, BF16)]
        + [images_out(count, length, width, BF16)] * 2
    )
    upstream = cotangent
    bias_grads = [None] * LAYERS
    finished = []
    waiting = []
    wgrad = None
    for layer in reversed(range(LAYERS)):
        kept = saved[layer]
        came, shares, grads, *biases, above = expert_backward(
            sources, drow, dcol, kept["weights"], *kept["experts"], wgrad, layer
        )
        came = came[0]
        came, waiting = lax.optimization_barrier((came, waiting))
        finished += waiting
        waiting = [shares, lax.psum_scatter(grads, "dp", scatter_dimension=0, tiled=False)]
        bias_grads[layer] = biases
        weights = [(packed[layer], s) for s in packed_specs(packed[layer])]
        inputs = [upstream, kept["rows"], kept["middle"], *kept["attend"], dz]
        inputs = [(a, per_image(a)) for a in inputs]
        inputs += [(came, per_image(came))] + weights
        outputs = [
            images_out(count, length, width, F32),
            (
                (width, columns), BF16,
                pl.BlockSpec((width, columns), lambda i: (0, 0)),
            ),
        ]
        if layer > 0:
            below = saved[layer - 1]
            inputs += [(below["picked"], per_layer(below["picked"], k)) for k in range(2)]
            inputs.append((below["gates"], per_image(below["gates"])))
            inputs.append((routes, per_layer(routes, layer - 1)))
            outputs += [images_out(count, length, MISC, BF16)] + [images_out(count, length, width, BF16)] * 2
        scratch = [pltpu.VMEM((width, 4 * width + MISC), F32), pltpu.VMEM((MISC, width), F32)]
        number = None
        if layer == 0:
            inputs.append((above, pl.BlockSpec(memory_space=pl.ANY)))
            outputs.append((above.shape, BF16, pl.BlockSpec(above.shape, lambda i: (0, 0))))
            scratch += spread_scratch(share, columns, owners // 2)
            number = 2 * LAYERS + 2
        done = call(functools.partial(back_kernel, layer == 0), (count,), inputs, outputs, scratch, number)
        upstream, wgrad = done[:2]
        if layer > 0:
            dz, *sources = done[2:]
        wgrad = wgrad.reshape(parts, share, columns)
    lowest, result, upstream = settle(wgrad, (result, upstream), owners // 2, 2 * LAYERS + 1)
    both = (lowest, done[2])
    pieces = [waiting[0], waiting[1][0], finished[0], finished[1][0]]
    *squares, router, v0, v1, v2, v3, v4, v5, v6, inner, outer = unpack(pieces, both, local, ff, experts_all)
    outer_bias_grad = jnp.stack([b[1] for b in bias_grads])
    return (
        jnp.transpose(result, (1, 0, 2)),
        jnp.transpose(upstream, (1, 0, 2)),
        *squares,
        jnp.transpose(router, (0, 2, 1)),
        v0, v1, v2, v3, v4, v5, v6,
        inner,
        jnp.stack([b[0] for b in bias_grads]),
        outer,
        lax.dynamic_slice_in_dim(outer_bias_grad, lax.axis_index("dp") * share, share, 2),
    )


def solution(mesh):
    both = P(("dp", "expert"), None, None)
    square = P(None, "dp", None)
    vector = P(None, "dp")
    matrix = P(None, "expert", "dp", None)
    bias = P(None, "expert", "dp")
    grads = (square,) * 5 + (vector,) * 7 + (matrix, bias, matrix, bias)
    return jax.shard_map(
        shards,
        mesh=mesh,
        in_specs=(both, both, P(None, ("dp", "expert"), None, None)) + grads,
        out_specs=(both, both) + grads,
        check_vma=False,
    )
```

```python
import functools

import jax
import jax.numpy as jnp
from jax import lax
from jax.experimental import pallas as pl
from jax.experimental.pallas import tpu as pltpu
from jax.sharding import PartitionSpec as P

HEADS = 8
HEAD_DIM = 64
LAYERS = 2
EPSILON = 1e-06
FACTOR = HEAD_DIM**-0.5
VEC_AT = 64
MISC = 128
FF_BLOCK = 512
COST = 1024
VMEM = 56 * 1024 * 1024

MESH = pl.DeviceIdType.MESH
F32 = jnp.float32
BF16 = jnp.bfloat16


def dot(a, b):
    return jnp.dot(a, b, preferred_element_type=F32)


def dot_nt(a, b):
    return lax.dot_general(a, b, (((1,), (1,)), ((), ())), preferred_element_type=F32)


def dot_tn(a, b):
    return lax.dot_general(a, b, (((0,), (0,)), ((), ())), preferred_element_type=F32)


def standardize(rows):
    mean_value = jnp.mean(rows, axis=-1, keepdims=True)
    centered = rows - mean_value
    variance = jnp.mean(centered * centered, axis=-1, keepdims=True)
    scale = lax.rsqrt(variance + EPSILON)
    return centered * scale, scale


def standardize_back(upstream, unit, scale, gain):
    along = upstream * gain
    inner = (
        along
        - jnp.mean(along, axis=-1, keepdims=True)
        - unit * jnp.mean(along * unit, axis=-1, keepdims=True)
    )
    return inner * scale


def vectors_of(misc_ref):
    turned = misc_ref[...].astype(F32).T
    return [turned[VEC_AT + n : VEC_AT + n + 1, :] for n in range(7)]


def lane_masks(length):
    lanes = lax.broadcasted_iota(jnp.int32, (length, 2 * HEAD_DIM), 1)
    return (lanes < HEAD_DIM).astype(F32).astype(BF16), (lanes >= HEAD_DIM).astype(F32).astype(BF16)


def attend_body(
    rows, routes_ref, wq, wk, wv, wo, misc,
    t_ref, q_ref, k_ref, v_ref, o_ref, lse_ref, gates_ref, hidden_ref,
):
    length = rows.shape[0]
    qb, vb, ob, again, ashift, egain, eshift = vectors_of(misc)
    unit, _ = standardize(rows)
    low = (unit * again + ashift).astype(BF16)
    queries = (dot(low, wq[...]) + qb).astype(BF16)
    keys = dot(low, wk[...]).astype(BF16)
    values = (dot(low, wv[...]) + vb).astype(BF16)
    q_ref[0] = queries
    k_ref[0] = keys
    v_ref[0] = values
    masks = lane_masks(length)
    lanes = lax.broadcasted_iota(jnp.int32, (length, MISC), 1)
    first_half = lax.broadcasted_iota(jnp.int32, (length, 2 * HEAD_DIM), 1) < HEAD_DIM
    sums = jnp.zeros((length, MISC), F32)
    for pair in range(HEADS // 2):
        cols = slice(pair * 2 * HEAD_DIM, (pair + 1) * 2 * HEAD_DIM)
        mixed = []
        for side in range(2):
            scores = dot_nt(queries[:, cols] * (masks[side] * FACTOR), keys[:, cols])
            highest = jnp.max(scores, axis=-1, keepdims=True)
            expo = jnp.exp(scores - highest)
            total = jnp.sum(expo, axis=-1, keepdims=True)
            attention = (expo * (1.0 / total)).astype(BF16)
            sums = jnp.where(lanes == 2 * pair + side, highest + jnp.log(total), sums)
            mixed.append(dot(attention, values[:, cols]))
        o_ref[0, :, cols] = jnp.where(first_half, mixed[0], mixed[1]).astype(BF16)
    lse_ref[0] = sums
    middle = rows + (dot(o_ref[0], wo[...]) + ob)
    t_ref[0] = middle
    unit_two, _ = standardize(middle)
    hidden = (unit_two * egain + eshift).astype(BF16)
    logits = dot(hidden, misc[...])
    pair_experts = routes_ref[0]
    zero = jnp.sum(jnp.where(lanes == pair_experts[:, 0:1], logits, 0.0), axis=-1, keepdims=True)
    one = jnp.sum(jnp.where(lanes == pair_experts[:, 1:2], logits, 0.0), axis=-1, keepdims=True)
    gate_zero = 1.0 / (1.0 + jnp.exp(one - zero))
    gate_one = 1.0 / (1.0 + jnp.exp(zero - one))
    gates_ref[0, :, 0:1] = gate_zero
    gates_ref[0, :, 1:2] = gate_one
    hidden_ref[0] = hidden


def combine(middle, gates_ref, zero_ref, one_ref):
    gates = gates_ref[0]
    zero, one = zero_ref[0].astype(F32), one_ref[0].astype(F32)
    return middle + (gates[:, 0:1] * zero + gates[:, 1:2] * one), zero, one


def grads_body(upstream, zero, one, gates_ref, routes_ref, dz_ref, zero_ref, one_ref):
    length = upstream.shape[0]
    gates = gates_ref[0]
    gate_zero, gate_one = gates[:, 0:1], gates[:, 1:2]
    grad_zero = jnp.sum(zero * upstream, axis=-1, keepdims=True)
    grad_one = jnp.sum(one * upstream, axis=-1, keepdims=True)
    along = gate_zero * grad_zero + gate_one * grad_one
    lanes = lax.broadcasted_iota(jnp.int32, (length, MISC), 1)
    pair_experts = routes_ref[0]
    dz = jnp.where(lanes == pair_experts[:, 0:1], gate_zero * (grad_zero - along), 0.0)
    dz = dz + jnp.where(lanes == pair_experts[:, 1:2], gate_one * (grad_one - along), 0.0)
    dz_ref[0] = dz.astype(BF16)
    zero_ref[0] = (gate_zero * upstream).astype(BF16)
    one_ref[0] = (gate_one * upstream).astype(BF16)


def first_kernel(rows, routes, wq, wk, wv, wo, misc, *outs):
    attend_body(rows[0], routes, wq, wk, wv, wo, misc, *outs)


def next_kernel(
    middle, gates, yzero, yone, routes, wq, wk, wv, wo, misc, rows_ref, *outs
):
    rows, _, _ = combine(middle[0], gates, yzero, yone)
    rows_ref[0] = rows
    attend_body(rows, routes, wq, wk, wv, wo, misc, *outs)


def turn_kernel(middle, gates, yzero, yone, cotangent, routes, result, dz, zero_ref, one_ref):
    rows, zero, one = combine(middle[0], gates, yzero, yone)
    result[0] = rows
    grads_body(cotangent[0], zero, one, gates, routes, dz, zero_ref, one_ref)


class Spread:
    def __init__(self, above, refs):
        self.own, self.chips_in, self.final, *sems = refs
        local, out_send, out_recv, back_send, back_recv, pass_send, pass_recv = sems
        half, columns = self.own.shape
        me = lax.axis_index("expert")
        core, chip = lax.rem(me, 2), me // 2
        self.chips = chips = self.chips_in.shape[0] + 1
        block = columns // chips
        sibling = {"expert": me + 1 - 2 * core}
        mine = pl.ds(pl.multiple_of(core * half, half), half)

        def chip_at(k):
            return lax.rem(chip + k + chips, chips)

        def cols(number):
            return pl.ds(pl.multiple_of(number * block, block), block)

        peers = [{"expert": 2 * chip_at(k) + core} for k in range(1, chips)]
        self.peers = [sibling] + peers
        self.keep = pltpu.make_async_copy(above, self.own, local)
        self.outs = [
            remote(
                self.own.at[:, cols(chip_at(k))], self.chips_in.at[k - 1], out_send.at[k - 1], out_recv.at[k - 1],
                peers[k - 1],
            )
            for k in range(1, chips)
        ]
        self.place = (mine, cols(chip))
        place = self.final.at[mine, cols(chip)]
        self.backs = [
            remote(place, place, back_send.at[k - 1], back_recv.at[k - 1], peers[k - 1]) for k in range(1, chips)
        ]
        self.hands = []
        for k in range(chips):
            place = self.final.at[mine, cols(chip_at(-k))]
            self.hands.append(remote(place, place, pass_send.at[k], pass_recv.at[k], sibling))

    def stage(self, number):
        if number == 0:
            self.keep.start()
            greet_all(self.peers)
            self.keep.wait()
            for copy in self.outs:
                copy.start()
        elif number == 1:
            value = self.own[:, self.place[1]].astype(F32)
            for n, copy in enumerate(self.outs):
                copy.wait_recv()
                value = value + self.chips_in[n].astype(F32)
            self.final[self.place[0], self.place[1]] = value.astype(BF16)
            for copy in self.backs:
                copy.start()
        else:
            for copy in self.backs:
                copy.wait_recv()
            for copy in self.hands:
                copy.start()

    def finish(self, result):
        for copy in self.hands:
            copy.wait()
        for copy in self.outs + self.backs:
            copy.wait_send()
        result[...] = self.final[...]


def spread_scratch(share, columns, chips):
    half = share // 2
    half_rows = pltpu.VMEM((half, columns), BF16)
    sems = [()] + [(chips - 1,)] * 4 + [(chips,)] * 2
    return [
        half_rows, pltpu.VMEM((chips - 1, half, columns // chips), BF16), pltpu.VMEM((share, columns), BF16),
    ] + [pltpu.SemaphoreType.DMA(n) for n in sems]


def back_kernel(
    lowest, upstream, rows, middle, q_ref, k_ref, v_ref, o_ref, lse_ref, dz_ref, came,
    wq, wk, wv, wo, misc, *rest,
):
    if not lowest:
        yzero, yone, gates_below, routes_below, grad_ref, sent, dz_below, zero_ref, one_ref, wgrad, vgrad = rest
    else:
        above, grad_ref, sent, above_out, wgrad, vgrad, *spread_refs = rest
        spread = Spread(above, spread_refs)
        for number in range(3):

            @pl.when(pl.program_id(0) == number)
            def _(number=number):
                spread.stage(number)

    first = pl.program_id(0) == 0
    length = rows.shape[1]
    width = rows.shape[2]
    qb, vb, ob, again, ashift, egain, eshift = vectors_of(misc)

    @pl.when(first)
    def _():
        wgrad[...] = jnp.zeros_like(wgrad)
        vgrad[...] = jnp.zeros_like(vgrad)

    def add_vector(number, value):
        vgrad[VEC_AT + number : VEC_AT + number + 1, :] += jnp.sum(value, axis=0, keepdims=True)

    unit_two, scale_two = standardize(middle[0])
    hidden = (unit_two * egain + eshift).astype(BF16)
    dz = dz_ref[0]
    dhidden = dot_nt(dz, misc[...]) + came[0]
    wgrad[:, 4 * width :] += dot_tn(hidden, dz)
    add_vector(5, dhidden * unit_two)
    add_vector(6, dhidden)
    dmiddle = upstream[0] + standardize_back(dhidden, unit_two, scale_two, egain)
    dbranch = dmiddle.astype(BF16)
    wgrad[:, 3 * width : 4 * width] += dot_tn(o_ref[0], dbranch)
    add_vector(2, dbranch.astype(F32))
    dcontext = dot_nt(dbranch, wo[...]).astype(BF16)
    masks = lane_masks(length)
    first_half = lax.broadcasted_iota(jnp.int32, (length, 2 * HEAD_DIM), 1) < HEAD_DIM
    dqs, dks, dvs = [], [], []
    sums = lse_ref[0].T
    for pair in range(HEADS // 2):
        cols = slice(pair * 2 * HEAD_DIM, (pair + 1) * 2 * HEAD_DIM)
        keys = k_ref[0, :, cols]
        values = v_ref[0, :, cols]
        queries = q_ref[0, :, cols]
        dvalues, dqueries, dkeys = None, [], None
        for side in range(2):
            own_queries = queries * (masks[side] * FACTOR)
            own_context = dcontext[:, cols] * masks[side]
            scores = dot_nt(keys, own_queries)
            number = 2 * pair + side
            attention = jnp.exp(scores - sums[number : number + 1, :])
            prob = dot_nt(values, own_context)
            weighed = attention * prob
            delta = jnp.sum(weighed, axis=0, keepdims=True)
            dscores = (weighed - attention * delta).astype(BF16)
            dvalue = dot(attention.astype(BF16), own_context)
            dkey = dot(dscores, own_queries)
            dvalues = dvalue if dvalues is None else dvalues + dvalue
            dkeys = dkey if dkeys is None else dkeys + dkey
            dqueries.append(dot_tn(dscores, keys))
        dqs.append((jnp.where(first_half, dqueries[0], dqueries[1]) * FACTOR).astype(BF16))
        dks.append(dkeys.astype(BF16))
        dvs.append(dvalues.astype(BF16))
    dq = jnp.concatenate(dqs, axis=1)
    dk = jnp.concatenate(dks, axis=1)
    dv = jnp.concatenate(dvs, axis=1)
    unit, scale = standardize(rows[0])
    low = (unit * again + ashift).astype(BF16)
    wgrad[:, 0 : 3 * width] += dot_tn(low, jnp.concatenate([dq, dk, dv], axis=1))
    add_vector(0, dq.astype(F32))
    add_vector(1, dv.astype(F32))
    dlow = dot_nt(dq, wq[...]) + dot_nt(dk, wk[...]) + dot_nt(dv, wv[...])
    add_vector(3, dlow * unit)
    add_vector(4, dlow)
    grad = dmiddle + standardize_back(dlow, unit, scale, again)
    grad_ref[0] = grad
    if not lowest:
        grads_body(
            grad, yzero[0].astype(F32), yone[0].astype(F32), gates_below, routes_below, dz_below,
            zero_ref, one_ref,
        )

    @pl.when(pl.program_id(0) == pl.num_programs(0) - 1)
    def _():
        wgrad[:, 4 * width :] += vgrad[...].T
        sent[:, : 4 * width + MISC] = wgrad[...].astype(BF16)
        sent[:, 4 * width + MISC :] = jnp.zeros((width, sent.shape[1] - 4 * width - MISC), BF16)
        if lowest:
            spread.finish(above_out)


def per_image(array):
    return pl.BlockSpec((1,) + array.shape[1:], lambda i: (i,) + (0,) * (len(array.shape) - 1))


def per_layer(array, layer):
    shape = (None, 1) + array.shape[2:]
    return pl.BlockSpec(shape, lambda i: (layer, i) + (0,) * (len(shape) - 2))


def whole(array):
    return pl.BlockSpec(array.shape, lambda i: (0,) * len(array.shape))


def packed_specs(packed):
    width = packed.shape[0]
    specs = [pl.BlockSpec((width, width), lambda i, n=n: (0, n)) for n in range(4)]
    return specs + [pl.BlockSpec((width, MISC), lambda i: (0, 4 * width // MISC))]


def call(body, grid, inputs, outputs, scratch=(), number=None):
    shapes = [jax.ShapeDtypeStruct(s, t) for s, t, _ in outputs]
    return pl.pallas_call(
        body,
        grid=grid,
        in_specs=[s for _, s in inputs],
        out_specs=[s for _, _, s in outputs],
        out_shape=shapes,
        scratch_shapes=list(scratch),
        compiler_params=pltpu.CompilerParams(
            vmem_limit_bytes=VMEM, collective_id=number, has_side_effects=number is not None
        ),
        cost_estimate=pl.CostEstimate(flops=COST, bytes_accessed=COST, transcendentals=0),
    )(*[a for a, _ in inputs])


def images_out(images, length, columns, kind):
    shape = (images, length, columns)
    return (shape, kind, pl.BlockSpec((1, length, columns), lambda i: (i, 0, 0)))


def attend_outputs(images, length, width):
    return [
        images_out(images, length, width, F32),
        images_out(images, length, width, BF16),
        images_out(images, length, width, BF16),
        images_out(images, length, width, BF16),
        images_out(images, length, width, BF16),
        images_out(images, length, MISC, F32),
        images_out(images, length, 2, F32),
        images_out(images, length, width, BF16),
    ]


def greet_all(peers):
    barrier = pltpu.get_barrier_semaphore()
    for peer in peers:
        pl.semaphore_signal(barrier, inc=1, device_id=peer, device_id_type=MESH)
    pl.semaphore_wait(barrier, len(peers))


def remote(source, target, send, recv, device):
    return pltpu.make_async_remote_copy(
        src_ref=source, dst_ref=target, send_sem=send, recv_sem=recv, device_id=device, device_id_type=MESH
    )


class SharedGather:
    def __init__(self, mine, out, sems):
        send, recv, pass_send, pass_recv, own = sems
        parts, share, _ = out.shape
        half = share // 2
        row, me = lax.axis_index("dp"), lax.axis_index("expert")
        core = lax.rem(me, 2)
        sibling = {"expert": me + 1 - 2 * core}
        rows = pl.ds(pl.multiple_of(core * half, half), half)
        self.fetches, self.hands = [], []
        for k in range(1, parts):
            peer = {"dp": lax.rem(row + k, parts)}
            self.fetches.append(remote(mine.at[rows], out.at[row, rows], send.at[k - 1], recv.at[k - 1], peer))
            place = out.at[lax.rem(row - k + parts, parts), rows]
            self.hands.append(remote(place, place, pass_send.at[k - 1], pass_recv.at[k - 1], sibling))
        self.keep = pltpu.make_async_copy(mine, out.at[row], own)

    def start(self):
        for copy in self.fetches:
            copy.start()
        self.keep.start()

    def finish(self):
        for fetch, hand in zip(self.fetches, self.hands):
            fetch.wait_recv()
            hand.start()
        for fetch, hand in zip(self.fetches, self.hands):
            fetch.wait_send()
            hand.wait()
        self.keep.wait()


class Gather:
    def __init__(self, parts, mine, place, sems):
        send, recv, own = sems
        row = lax.axis_index("dp")
        self.first, self.second = [], []
        self.keep = pltpu.make_async_copy(mine, place(row), own)

        def add(group, source, target, peer):
            n = len(self.first) + len(self.second)
            group.append(remote(source, target, send.at[n], recv.at[n], {"dp": peer}))

        if parts != 4:
            for k in range(1, parts):
                add(self.first, mine, place(row), lax.rem(row + k, parts))
            return
        near, far = row + 1 - 2 * lax.rem(row, 2), lax.rem(row + 2, 4)
        quarter = mine.shape[0] // 4
        halves = [[slice(n * quarter, (n + 1) * quarter) for n in pair] for pair in ((0, 1), (2, 3))]
        for rows, peer in ((halves[0], near), (halves[1], far)):
            for part in rows:
                add(self.first, mine.at[part], place(row).at[part], peer)
        for rows, peer, other in ((halves[0], far, near), (halves[1], near, far)):
            for part in rows:
                add(self.second, mine.at[part], place(row).at[part], peer)
            for part in rows:
                add(self.second, place(other).at[part], place(other).at[part], peer)

    def start(self):
        for copy in self.first:
            copy.start()
        self.keep.start()

    def forward(self):
        for copy in self.first:
            copy.wait_recv()
        for copy in self.second:
            copy.start()

    def finish(self):
        for copy in self.second:
            copy.wait_recv()
        self.keep.wait()

    def drain(self):
        for copy in self.first + self.second:
            copy.wait_send()


def gather_sems(parts):
    count = 12 if parts == 4 else parts - 1
    return [pltpu.SemaphoreType.DMA((count,)), pltpu.SemaphoreType.DMA((count,)), pltpu.SemaphoreType.DMA]


def shared_sems(parts):
    return [pltpu.SemaphoreType.DMA((parts - 1,))] * 4 + [pltpu.SemaphoreType.DMA]


ROOT_HALF = 0.7071067811865476
ROOT_TWO_PI_INVERSE = 0.3989422804014327

class Swap:
    def __init__(self, sent, arrived, made, back, sems):
        self.sent, self.arrived, self.made, self.back = sent, arrived, made, back
        self.out_send, self.out_recv, self.home_send, self.home_recv, self.own = sems
        self.local, self.count = arrived.shape[0], arrived.shape[1]
        self.me = lax.axis_index("expert")

    def greet(self, others=()):
        greet_all([{"expert": lax.rem(self.me + k, self.count)} for k in range(1, self.count)] + list(others))

    def outward(self, j, k, peer):
        return pltpu.make_async_remote_copy(
            src_ref=self.sent.at[j, peer], dst_ref=self.arrived.at[j, self.me],
            send_sem=self.out_send.at[j, k], recv_sem=self.out_recv.at[j, k],
            device_id={"expert": peer}, device_id_type=MESH,
        )

    def homeward(self, j, k, peer):
        return pltpu.make_async_remote_copy(
            src_ref=self.made.at[j, peer], dst_ref=self.back.at[j, self.me],
            send_sem=self.home_send.at[j, k], recv_sem=self.home_recv.at[j, k],
            device_id={"expert": peer}, device_id_type=MESH,
        )

    def own_out(self, j):
        return pltpu.make_async_copy(self.sent.at[j, self.me], self.arrived.at[j, self.me], self.own.at[j])

    def own_home(self, j):
        return pltpu.make_async_copy(self.made.at[j, self.me], self.back.at[j, self.me], self.own.at[self.local + j])

    def send_all(self, sources, drow, layer):
        chips = self.count // 2
        capacity, width = self.sent.shape[2:]
        images, length, _ = sources[0].shape

        for j in range(self.local):

            def fill(turn, carry, j=j):
                sign = 2 * lax.rem(turn, 2) - 1
                chip = lax.rem(self.me // 2 + chips // 2 + sign * ((turn + 1) // 2) + chips, chips)
                first = (j * self.count + 2 * chip) * capacity
                slots = lax.broadcasted_iota(jnp.int32, (2 * capacity, length), 0) + first
                total = jnp.zeros((2 * capacity, width), F32)
                for image in range(images):
                    dest = drow[layer, image]
                    hits = [slots == dest[0:1, :], slots == dest[1:2, :]]
                    if len(sources) == 1:
                        hits = [hits[0] | hits[1]]
                    for hit, source in zip(hits, sources):
                        total = total + dot(hit.astype(F32).astype(BF16), source[image])
                self.sent[j, pl.ds(2 * chip, 2)] = total.astype(BF16).reshape(2, capacity, width)
                for core in range(2):
                    peer = 2 * chip + core
                    k = lax.rem(peer - self.me + self.count, self.count)

                    @pl.when(peer != self.me)
                    def _(k=k, peer=peer):
                        self.outward(j, k, peer).start()

                    @pl.when(peer == self.me)
                    def _():
                        self.own_out(j).start()

                return carry

            lax.fori_loop(0, chips, fill, 0)

    def chip(self, turn):
        chips = self.count // 2
        return lax.rem(self.me // 2 - turn + chips, chips)

    def wait_chip(self, j, chip):
        for core in range(2):
            source = 2 * chip + core
            k = lax.rem(self.me - source + self.count, self.count)

            @pl.when(source != self.me)
            def _(k=k, source=source):
                pltpu.make_async_remote_copy(
                    src_ref=self.arrived.at[j, source], dst_ref=self.arrived.at[j, source],
                    send_sem=self.out_send.at[j, k], recv_sem=self.out_recv.at[j, k],
                    device_id={"expert": source}, device_id_type=MESH,
                ).wait_recv()

            @pl.when(source == self.me)
            def _():
                self.own_out(j).wait()

    def send_home(self, j, chip):
        for core in range(2):
            peer = 2 * chip + core
            k = lax.rem(peer - self.me + self.count, self.count)

            @pl.when(peer != self.me)
            def _(k=k, peer=peer):
                self.homeward(j, k, peer).start()

            @pl.when(peer == self.me)
            def _():
                self.own_home(j).start()

    def wait_home(self, j, chip):
        for core in range(2):
            source = 2 * chip + core
            k = lax.rem(self.me - source + self.count, self.count)

            @pl.when(source != self.me)
            def _(k=k, source=source):
                place = self.back.at[j, source]
                remote(place, place, self.home_send.at[j, k], self.home_recv.at[j, k], {"expert": source}).wait_recv()

            @pl.when(source == self.me)
            def _():
                self.own_home(j).wait()

    def take_home(self, dcol, layer, total):
        count, images, length, width = total.shape
        capacity = self.back.shape[2]
        total[...] = jnp.zeros_like(total)
        for j in range(self.local):

            def step(turn, carry, j=j):
                chip = self.chip(turn)
                self.wait_home(j, chip)
                rows = self.back[j, pl.ds(2 * chip, 2)].reshape(2 * capacity, width)
                first = (j * self.count + 2 * chip) * capacity
                lanes = lax.broadcasted_iota(jnp.int32, (length, 2 * capacity), 1) + first
                for image in range(images):
                    dest = dcol[layer, image]
                    hits = [dest[:, 0:1] == lanes, dest[:, 1:2] == lanes]
                    if count == 1:
                        hits = [hits[0] | hits[1]]
                    for k, hit in enumerate(hits):
                        total[k, image] += dot(hit.astype(F32).astype(BF16), rows).astype(total.dtype)
                return carry

            lax.fori_loop(0, self.count // 2, step, 0)

    def finish(self):
        for j in range(self.local):
            for k in range(1, self.count):
                peer = lax.rem(self.me + k, self.count)
                self.outward(j, k, peer).wait_send()
                self.homeward(j, k, peer).wait_send()


def weight_blocks(weights, j, f):
    _, parts, rows, width = weights.shape
    share, take = width // parts, rows // 2
    each = FF_BLOCK // take
    first = weights[j, :, f * share : (f + 1) * share, :].reshape(width, width)
    second = weights[j, f * each : (f + 1) * each, take:, :].reshape(FF_BLOCK, width)
    return first, second


def expert_kernel(layer, with_dense, *refs):
    if with_dense:
        *refs, n1, n2, n3, n4, n5, m1, m2, m3 = refs
        refs = list(refs)
        dense_in, dense_out, next_out = refs.pop(7), refs.pop(13), refs.pop(13)
        dense = SharedGather(dense_in, dense_out, (n1, n2, n3, n4, n5))
        next_in = refs[4].at[layer + 1, 0, : next_out.shape[1]]
        following = Gather(dense_out.shape[0], next_in, lambda p: next_out.at[p], (m1, m2, m3))
    (
        hidden, drow, dcol, inner_first, shares, b1, b2, picked, arrived_out, g_out, s_out, outer_out, packed_out,
        back, sent, arrived, made, weights, g_stage, s_stage, out_send, out_recv, home_send, home_recv, own, load, stores, last,
        *gather_refs,
    ) = refs
    row = lax.axis_index("dp")
    parts = weights.shape[1]
    take = weights.shape[2] // 2
    mine = shares.at[layer, 1]
    gathers = [
        Gather(parts, shares.at[layer, 0, take:], lambda p: weights.at[0, p, take:], gather_refs[:3]),
        Gather(parts, mine, lambda p: weights.at[1, p], gather_refs[3:]),
    ]
    swap = Swap(sent, arrived, made, back, (out_send, out_recv, home_send, home_recv, own))
    local, count, capacity, width = arrived.shape
    chips = count // 2
    rows = 2 * capacity
    ff = g_out.shape[2]
    first_load = pltpu.make_async_copy(inner_first, weights.at[0, :, :take], load)
    first_load.start()
    swap.greet([{"dp": lax.rem(row + k, parts)} for k in range(1, parts)])
    gathers[0].start()
    swap.send_all([hidden], drow, layer)
    gathers[0].forward()
    gathers[1].start()
    gathered = [
        pltpu.make_async_copy(weights.at[0, :, take:], outer_out, last.at[1]),
        pltpu.make_async_copy(weights.at[1], packed_out, last.at[2]),
    ]

    def kept(j, slot, chip):
        place = pl.ds(pl.multiple_of(chip * rows, rows), rows)
        return (
            pltpu.make_async_copy(g_stage.at[slot], g_out.at[j, place, :], stores.at[0, slot]),
            pltpu.make_async_copy(s_stage.at[slot], s_out.at[j, place, :], stores.at[1, slot]),
        )

    for j in range(local):
        if j == 0:
            first_load.wait()
        gathers[j].finish()
        gathered[j].start()
        if j == 1 and with_dense:
            following.start()
        number = layer * local + j

        def chip_step(turn, carry, j=j, number=number):
            chip = swap.chip(turn)
            slot = lax.rem(turn, 2)
            swap.wait_chip(j, chip)
            if j == 0:

                @pl.when(turn == 1)
                def _():
                    gathers[1].forward()
                    if with_dense:
                        dense.start()

            if j == 1 and with_dense:

                @pl.when(turn == 2)
                def _():
                    following.forward()

            @pl.when(j * chips + turn >= 2)
            def _():
                for copy in kept(j, slot, chip):
                    copy.wait()

            x = arrived[j, pl.ds(2 * chip, 2)].reshape(rows, width)
            total = jnp.broadcast_to(b2[number : number + 1, :], (rows, width))
            for f in range(ff // FF_BLOCK):
                cols = slice(f * FF_BLOCK, (f + 1) * FF_BLOCK)
                first, second = weight_blocks(weights, j, f)
                inner = dot(x, first) + b1[number : number + 1, cols]
                normal = 0.5 * (1.0 + lax.erf(inner * ROOT_HALF))
                g = (inner * normal).astype(BF16)
                density = jnp.exp(-0.5 * inner * inner) * ROOT_TWO_PI_INVERSE
                g_stage[slot, :, cols] = g
                s_stage[slot, :, cols] = (normal + inner * density).astype(BF16)
                total = total + dot(g, second)
            made[j, pl.ds(2 * chip, 2)] = total.astype(BF16).reshape(2, capacity, width)
            swap.send_home(j, chip)
            for copy in kept(j, slot, chip):
                copy.start()
            return carry

        lax.fori_loop(0, chips, chip_step, 0)
    final = pltpu.make_async_copy(arrived, arrived_out, last.at[0])
    final.start()
    if with_dense:
        dense.finish()
        following.finish()
        following.drain()
    for slot in range(2):
        for copy in kept(0, slot, 0):
            copy.wait()
    swap.take_home(dcol, layer, picked)
    swap.finish()
    for gather, copy in zip(gathers, gathered):
        gather.drain()
        copy.wait()
    final.wait()


def expert_back_kernel(layer, with_above, *refs):
    if with_above:
        *refs, above_in, above_own, above_paired, above_send, above_recv, above_load, pair_send, pair_recv = refs
        refs = list(refs)
        above, above_sum = refs.pop(10), refs.pop(15)
    (
        zero, one, drow, dcol, inner_first, outer_first, packed_second, arrived_x, g_in, s_in,
        came, summed, out, bias1, bias2, back, sent, arrived, made, weights, x, du, s_stage, g_stage, first_stage, second_stage, share_out, share_in,
        db1, db2, db1_in, db2_in,
        out_send, out_recv, home_send, home_recv, own, load, fetch, stores, share_send, share_recv,
        bias_send, bias_recv,
    ) = refs
    swap = Swap(sent, arrived, made, back, (out_send, out_recv, home_send, home_recv, own))
    row = lax.axis_index("dp")
    local, count, capacity, width = arrived.shape
    chips = count // 2
    rows = 2 * capacity
    ff = g_in.shape[2]
    blocks = ff // FF_BLOCK
    _, parts, all_rows, _ = weights.shape
    share, take = width // parts, all_rows // 2
    each = FF_BLOCK // take
    loads = [
        pltpu.make_async_copy(inner_first, weights.at[0, :, :take], load.at[0]),
        pltpu.make_async_copy(packed_second, weights.at[1], load.at[1]),
        pltpu.make_async_copy(arrived_x, x, load.at[local]),
        pltpu.make_async_copy(outer_first, weights.at[0, :, take:], load.at[local + 1]),
    ]
    for copy in loads:
        copy.start()

    def slopes(j, turn):
        slot = lax.rem(turn, 2)
        place = pl.ds(pl.multiple_of(swap.chip(turn) * rows, rows), rows)
        return pltpu.make_async_copy(s_in.at[j, place, :], s_stage.at[slot], fetch.at[0, slot])

    def activations(j, f):
        return pltpu.make_async_copy(
            g_in.at[j, :, f * FF_BLOCK : (f + 1) * FF_BLOCK], g_stage.at[f % 2], fetch.at[1, f % 2]
        )

    def results(j, f):
        return (
            pltpu.make_async_copy(
                first_stage.at[f % 2], out.at[:, j - 1, f * share : (f + 1) * share, :], stores.at[0, f % 2]
            ),
            pltpu.make_async_copy(
                second_stage.at[f % 2], out.at[f * each : (f + 1) * each, j - 1, take:, :], stores.at[1, f % 2]
            ),
        )

    def share_copy(k):
        peer = lax.rem(row + k, parts)
        return pltpu.make_async_remote_copy(
            src_ref=share_out.at[peer], dst_ref=share_in.at[k - 1],
            send_sem=share_send.at[k - 1], recv_sem=share_recv.at[k - 1],
            device_id={"dp": peer}, device_id_type=MESH,
        )

    slopes(0, 0).start()
    peers = [{"dp": lax.rem(row + k, parts)} for k in range(1, parts)]
    swap.greet(peers)
    if with_above:
        core = lax.rem(swap.me, 2)
        half = above_own.shape[1]
        mine = pl.ds(pl.multiple_of(core * half, half), half)
        other = pl.ds(pl.multiple_of((1 - core) * half, half), half)
        pair = remote(above.at[:, other], above_paired, pair_send, pair_recv, {"expert": swap.me + 1 - 2 * core})
        keep = pltpu.make_async_copy(above.at[:, mine], above_own, above_load)
        pair.start()
        keep.start()
        above_copies = [
            remote(
                above_own.at[lax.rem(row + k, parts)], above_in.at[k - 1], above_send.at[k - 1], above_recv.at[k - 1],
                peers[k - 1],
            )
            for k in range(1, parts)
        ]
    swap.send_all([zero, one], drow, layer)
    if with_above:
        pair.wait_recv()
        keep.wait()
        for part in range(parts):
            above_own[part] = (above_own[part].astype(F32) + above_paired[part].astype(F32)).astype(BF16)
        for copy in above_copies:
            copy.start()
    loads[local + 1].wait()
    for j in range(local):
        loads[j].wait()
        activations(j, 0).start()

        def chip_step(turn, carry, j=j):
            chip = swap.chip(turn)
            slot = lax.rem(turn, 2)

            @pl.when(turn + 1 < chips)
            def _():
                slopes(j, turn + 1).start()

            swap.wait_chip(j, chip)
            slopes(j, turn).wait()
            dy = arrived[j, pl.ds(2 * chip, 2)].reshape(rows, width)
            place = pl.ds(pl.multiple_of(chip * rows, rows), rows)
            total = jnp.zeros((rows, width), F32)
            for f in range(blocks):
                cols = slice(f * FF_BLOCK, (f + 1) * FF_BLOCK)
                first, second = weight_blocks(weights, j, f)
                part = (dot_nt(dy, second) * s_stage[slot, :, cols].astype(F32)).astype(BF16)
                du[place, cols] = part
                total = total + dot_nt(part, first)
            made[j, pl.ds(2 * chip, 2)] = total.astype(BF16).reshape(2, capacity, width)
            swap.send_home(j, chip)
            return carry

        lax.fori_loop(0, chips, chip_step, 0)
        if j + 1 < local:
            slopes(j + 1, 0).start()
        if j == 0:
            loads[local].wait()
        dy = arrived[j].reshape(count * capacity, width)
        db2[j : j + 1, :] = jnp.sum(dy.astype(F32), axis=0, keepdims=True)
        for f in range(blocks):
            cols = slice(f * FF_BLOCK, (f + 1) * FF_BLOCK)
            if f + 1 < blocks:
                activations(j, f + 1).start()
            if j > 1 or (j == 1 and f > 1):
                for copy in results(j, f):
                    copy.wait()
            part = du[:, cols]
            grad = dot_tn(x[j].reshape(count * capacity, width), part).astype(BF16)
            if j == 0:
                share_out[:, f * share : (f + 1) * share, :] = grad.reshape(parts, share, width)
            else:
                first_stage[f % 2] = grad.reshape(parts, share, width)
            db1[j : j + 1, cols] = jnp.sum(part.astype(F32), axis=0, keepdims=True)
            activations(j, f).wait()
            grad = dot_tn(g_stage[f % 2], dy).astype(BF16).reshape(each, take, width)
            if j == 0:
                share_out[f * each : (f + 1) * each, take:, :] = grad
            else:
                second_stage[f % 2] = grad
                for copy in results(j, f):
                    copy.start()
        if j == 0:
            for k in range(1, parts):
                share_copy(k).start()
    part_ff = ff // parts
    bias_copies = []
    for k in range(1, parts):
        place = pl.ds(pl.multiple_of(lax.rem(row + k, parts) * part_ff, part_ff), part_ff)
        for n, (source, target) in enumerate(((db1.at[:, place], db1_in.at[k - 1]), (db2, db2_in.at[k - 1]))):
            bias_copies.append(pltpu.make_async_remote_copy(
                src_ref=source, dst_ref=target, send_sem=bias_send.at[n, k - 1], recv_sem=bias_recv.at[n, k - 1],
                device_id=peers[k - 1], device_id_type=MESH,
            ))
            bias_copies[-1].start()
    if with_above:
        for copy in above_copies:
            copy.wait_recv()
        total = above_own[row].astype(F32)
        for k in range(1, parts):
            total = total + above_in[k - 1].astype(F32)
        above_sum[...] = total.astype(BF16)
    for k in range(1, parts):
        share_copy(k).wait_recv()
    step = 64

    def add_up(turn, carry):
        place = pl.ds(pl.multiple_of(turn * step, step), step)
        total = share_out[row, place, :].astype(F32)
        for k in range(1, parts):
            total = total + share_in[k - 1, place, :].astype(F32)
        summed[place, :] = total
        return carry

    lax.fori_loop(0, all_rows // step, add_up, 0)
    for copy in bias_copies:
        copy.wait_recv()
    total1, total2 = db1[:, pl.ds(pl.multiple_of(row * part_ff, part_ff), part_ff)], db2[...]
    for k in range(1, parts):
        total1, total2 = total1 + db1_in[k - 1], total2 + db2_in[k - 1]
    bias1[...], bias2[...] = total1, total2
    swap.take_home(dcol, layer, came)
    if with_above:
        for copy in above_copies + [pair]:
            copy.wait_send()
    for copy in bias_copies:
        copy.wait_send()
    for k in range(1, parts):
        share_copy(k).wait_send()
    for f in range(2):
        for copy in results(1, f):
            copy.wait()
    swap.finish()


def swap_sems(local, count):
    pairs = [pltpu.SemaphoreType.DMA((local, count))] * 4
    return pairs + [pltpu.SemaphoreType.DMA((2 * local,))]


def expert_call(body, inputs, outputs, scratch, number):
    def spec(held):
        return pl.BlockSpec(memory_space=pltpu.VMEM if held else pl.ANY)

    shapes = [jax.ShapeDtypeStruct(s, t) for s, t, _ in outputs]
    return pl.pallas_call(
        body,
        in_specs=[spec(held) for _, held in inputs],
        out_specs=[spec(held) for _, _, held in outputs],
        out_shape=shapes,
        scratch_shapes=scratch,
        compiler_params=pltpu.CompilerParams(
            collective_id=number, has_side_effects=True, vmem_limit_bytes=VMEM
        ),
        cost_estimate=pl.CostEstimate(flops=COST, bytes_accessed=COST, transcendentals=0),
    )(*[a for a, _ in inputs])


def expert_forward(hidden, drow, dcol, shape, inner, shares, biases, following, layer):
    b1, b2 = biases
    local, count, capacity, width = shape
    ff = b1.shape[1]
    rows = 2 * capacity
    parts = inner.shape[0]
    packed = (parts, *shares.shape[2:])
    half = (parts, shares.shape[2] // 2, width)
    slots = (local, count * capacity, ff)
    inputs = [(hidden, True), (drow, True), (dcol, True), (inner, False), (shares, False), (b1, True), (b2, True)]
    outputs = [
        ((2, *hidden.shape), BF16, True), (shape, BF16, False), (slots, BF16, False), (slots, BF16, False),
        (half, BF16, False), (packed, BF16, False),
    ]
    scratch = [
        pltpu.VMEM(shape, BF16), pltpu.VMEM(shape, BF16), pltpu.VMEM(shape, BF16), pltpu.VMEM(shape, BF16),
        pltpu.VMEM((local, *packed), BF16),
        pltpu.VMEM((2, rows, ff), BF16), pltpu.VMEM((2, rows, ff), BF16),
    ] + swap_sems(local, count) + [
        pltpu.SemaphoreType.DMA, pltpu.SemaphoreType.DMA((2, 2)), pltpu.SemaphoreType.DMA((3,)),
    ] + gather_sems(parts) * 2
    if following is not None:
        inputs.append((following, False))
        outputs += [((parts, *following.shape), BF16, False), (half, BF16, False)]
        scratch += shared_sems(parts) + gather_sems(parts)
    return expert_call(functools.partial(expert_kernel, layer, following is not None), inputs, outputs, scratch, layer)


def expert_backward(sources, drow, dcol, weights, arrived, g, s, above, layer):
    shape = arrived.shape
    local, count, capacity, width = shape
    ff = g.shape[2]
    rows = 2 * capacity
    parts, all_rows, _ = weights[2].shape
    share, take = width // parts, all_rows // 2
    inputs = [(a, True) for a in (*sources, drow, dcol)] + [(a, False) for a in (*weights, arrived, g, s)]
    outputs = [
        ((1, *sources[0].shape), F32, True), ((all_rows, width), F32, True), ((parts, local - 1, all_rows, width), BF16, False),
        ((local, ff // parts), F32, True), ((local, width), F32, True),
    ]
    scratch = [
        pltpu.VMEM(shape, BF16), pltpu.VMEM(shape, BF16), pltpu.VMEM(shape, BF16), pltpu.VMEM(shape, BF16),
        pltpu.VMEM((local, parts, all_rows, width), BF16), pltpu.VMEM(shape, BF16),
        pltpu.VMEM((count * capacity, ff), BF16), pltpu.VMEM((2, rows, ff), BF16),
        pltpu.VMEM((2, count * capacity, FF_BLOCK), BF16), pltpu.VMEM((2, parts, share, width), BF16),
        pltpu.VMEM((2, FF_BLOCK // take, take, width), BF16),
        pltpu.VMEM((parts, all_rows, width), BF16), pltpu.VMEM((parts - 1, all_rows, width), BF16),
        pltpu.VMEM((local, ff), F32), pltpu.VMEM((local, width), F32),
        pltpu.VMEM((parts - 1, local, ff // parts), F32), pltpu.VMEM((parts - 1, local, width), F32),
    ] + swap_sems(local, count) + [
        pltpu.SemaphoreType.DMA((local + 2,)), pltpu.SemaphoreType.DMA((2, 2)), pltpu.SemaphoreType.DMA((2, 2)),
        pltpu.SemaphoreType.DMA((parts - 1,)), pltpu.SemaphoreType.DMA((parts - 1,)),
        pltpu.SemaphoreType.DMA((2, parts - 1)), pltpu.SemaphoreType.DMA((2, parts - 1)),
    ]
    if above is not None:
        inputs.append((above, False))
        halves = (share // 2, above.shape[2])
        outputs.append((halves, BF16, True))
        scratch += [
            pltpu.VMEM((parts - 1, *halves), BF16), pltpu.VMEM((parts, *halves), BF16), pltpu.VMEM((parts, *halves), BF16),
            pltpu.SemaphoreType.DMA((parts - 1,)), pltpu.SemaphoreType.DMA((parts - 1,)),
        ] + [pltpu.SemaphoreType.DMA] * 3
    done = expert_call(
        functools.partial(expert_back_kernel, layer, above is not None), inputs, outputs, scratch, LAYERS + layer
    )
    return done if above is not None else [*done, None]


def prepare_kernel(capacity, owners, *refs):
    squares, (router, *vectors), (inner_bias, outer_bias, routes) = refs[:4], refs[4:12], refs[12:15]
    tokens_in, matrices, refs = refs[15:17], refs[17:19], refs[19:]
    (out, above, b1, b2, dcol, drow), tokens_out, packed_out, refs = refs[:6], refs[6:8], refs[8], refs[9:]
    mine, turned, inner_low, outer_low, token_ins, token_outs, inner_in, outer_in, packs = refs[:9]
    sems, (b1_send, b1_recv, b2_send, b2_recv, own, token_load, token_store, weight_sems) = refs[9:14], refs[14:]
    weight_loads = [
        pltpu.make_async_copy(matrices[0], inner_in, weight_sems.at[0]),
        pltpu.make_async_copy(matrices[1], outer_in, weight_sems.at[1]),
    ]
    weight_store = pltpu.make_async_copy(packs, packed_out, weight_sems.at[2])
    parts, share, _ = out.shape
    loads = [pltpu.make_async_copy(tokens_in[n], token_ins.at[n], token_load.at[n]) for n in range(2)]
    stores = [pltpu.make_async_copy(token_outs.at[n], tokens_out[n], token_store.at[n]) for n in range(2)]
    width = squares[0].shape[2]
    experts_all = router.shape[2]
    local, part_ff = inner_bias.shape[1:]
    row, me = lax.axis_index("dp"), lax.axis_index("expert")
    sibling = {"expert": me + 1 - 2 * lax.rem(me, 2)}
    peers = [{"dp": lax.rem(row + k, parts)} for k in range(1, parts)]
    gather = SharedGather(mine, out, sems)

    def pack(target, layer):
        for n in range(4):
            target[:, n * width : (n + 1) * width] = squares[n][layer].astype(BF16)
        turned[...] = jnp.zeros_like(turned)
        for n in range(7):
            turned[VEC_AT + n : VEC_AT + n + 1, :] = vectors[n][layer : layer + 1, :]
        target[:, 4 * width :] = turned[...].T.astype(BF16)
        target[:, 4 * width : 4 * width + experts_all] = router[layer].astype(BF16)

    pack(mine, 0)
    for layer in range(LAYERS):
        for j in range(local):
            n = layer * local + j
            inner_low[n : n + 1, :] = inner_bias[layer, j : j + 1, :].astype(BF16).astype(F32)
            outer_low[n : n + 1, :] = outer_bias[layer, j : j + 1, :].astype(BF16).astype(F32)
    greet_all([sibling] + peers)
    place = pl.ds(pl.multiple_of(row * part_ff, part_ff), part_ff)
    singles = [
        remote(inner_low, b1.at[:, place], b1_send.at[k], b1_recv.at[k], peers[k]) for k in range(parts - 1)
    ] + [remote(outer_low, b2.at[row], b2_send.at[k], b2_recv.at[k], peers[k]) for k in range(parts - 1)]
    keeps = [
        pltpu.make_async_copy(inner_low, b1.at[:, place], own.at[0]),
        pltpu.make_async_copy(outer_low, b2.at[row], own.at[1]),
    ]
    gather.start()
    for copy in singles + keeps + loads + weight_loads:
        copy.start()
    pack(above, 1)
    for n in range(2):
        loads[n].wait()
        for image in range(routes.shape[1]):
            token_outs[n, image] = token_ins[n, :, image, :]
        stores[n].start()

    length = routes.shape[2]
    lanes = lax.broadcasted_iota(jnp.int32, (length, MISC), 1)
    earlier = (
        lax.broadcasted_iota(jnp.int32, (length, length), 0) > lax.broadcasted_iota(jnp.int32, (length, length), 1)
    ).astype(F32).astype(BF16)
    for layer in range(LAYERS):
        seen = jnp.zeros((1, MISC), F32)
        for image in range(routes.shape[1]):
            hots, dests = [], []
            for k in range(2):
                hots.append((lanes == routes[layer, image, :, k : k + 1]).astype(F32))
            counts = hots[0] + hots[1]
            before = dot(earlier, counts.astype(BF16)) + seen
            seen = seen + jnp.sum(counts, axis=0, keepdims=True)
            for k in range(2):
                slot = jnp.sum(hots[k] * before, axis=-1, keepdims=True)
                expert = routes[layer, image, :, k : k + 1].astype(F32)
                owner = jnp.floor(expert * (1.0 / local))
                place = ((expert - owner * local) * owners + owner) * capacity + slot
                dests.append(jnp.where(slot < capacity, place, -1.0))
                dcol[layer, image, :, k : k + 1] = dests[k].astype(jnp.int32)
            both = jnp.where(lanes == 0, dests[0], jnp.where(lanes == 1, dests[1], 0.0))
            drow[layer, image] = both.T[0:2, :].astype(jnp.int32)

    for copy in weight_loads:
        copy.wait()
    take = outer_in.shape[2]
    for layer in range(LAYERS):
        for j in range(local):
            for f in range(take // share):
                cols = slice(f * FF_BLOCK, (f + 1) * FF_BLOCK)
                packs[layer, j, f * share : (f + 1) * share, :] = inner_in[layer, j, :, cols].astype(BF16)
            packs[layer, j, take:, :] = outer_in[layer, j].astype(BF16)
    weight_store.start()
    gather.finish()
    for copy in singles + keeps + stores + [weight_store]:
        copy.wait()


def prepare(squares, router, vectors, inner_bias, outer_bias, routes, tokens, matrices, parts, owners, number):
    layers, share, width = squares[0].shape
    experts_all = router.shape[2]
    local, part_ff = inner_bias.shape[1:]
    _, images, length, _ = routes.shape
    capacity = (10 * images * length // (4 * experts_all) + 7) // 8 * 8
    columns = 4 * width + MISC
    count = layers * local
    sems = shared_sems(parts) + [pltpu.SemaphoreType.DMA((parts - 1,))] * 4 + [pltpu.SemaphoreType.DMA((2,))] * 3
    sems.append(pltpu.SemaphoreType.DMA((3,)))
    packs = (layers, local, 2 * matrices[1].shape[2], width)
    inputs = [*squares, router, *vectors, inner_bias, outer_bias, routes]
    turned = [jnp.transpose(item, (1, 0, 2)) for item in tokens]
    out, above, b1, b2, dcol, drow, *tokens, packs = expert_call(
        functools.partial(prepare_kernel, capacity, owners),
        [(a, True) for a in inputs] + [(a, False) for a in (*turned, *matrices)],
        [
            ((parts, share, columns), BF16, False), ((share, columns), BF16, True),
            ((count, part_ff * parts), F32, False), ((parts, count, share), F32, False),
            ((layers, images, length, 2), jnp.int32, True), ((layers, images, 2, length), jnp.int32, True),
            ((images, length, width), F32, False), ((images, length, width), F32, False), (packs, BF16, False),
        ],
        [
            pltpu.VMEM((share, columns), BF16), pltpu.VMEM((MISC, share), F32),
            pltpu.VMEM((count, part_ff), F32), pltpu.VMEM((count, share), F32),
            pltpu.VMEM((2, length, images, width), F32), pltpu.VMEM((2, images, length, width), F32),
            pltpu.VMEM(matrices[0].shape, F32), pltpu.VMEM(matrices[1].shape, F32), pltpu.VMEM(packs, BF16),
        ] + sems,
        number,
    )
    b2 = jnp.transpose(b2, (1, 0, 2)).reshape(count, width)
    return out.reshape(width, columns), above, (b1, b2), dcol, drow, capacity, tokens, packs


def settle_widths(columns, chips):
    blocks = columns // (MISC * chips)
    wide = (blocks + 1) // 2 * MISC
    return wide, columns // chips - wide


def settle_kernel(
    grads, tokens_a, tokens_b, final, tokens_out_a, tokens_out_b, own, paired, total, chips_in, dp_in, total_b, chips_in_b, dp_in_b,
    pair_send, pair_recv, local, out_send, out_recv, dp_send, dp_recv, out_send_b, out_recv_b, dp_send_b, dp_recv_b,
    back_send, back_recv, pass_send, pass_recv, token_ins, token_outs, token_load, token_store,
):
    parts, share, columns = grads.shape
    half = share // 2
    row, me = lax.axis_index("dp"), lax.axis_index("expert")
    core, chip = lax.rem(me, 2), me // 2
    chips = chips_in.shape[0] + 1
    wide, narrow = settle_widths(columns, chips)
    split = chips * wide
    sibling = {"expert": me + 1 - 2 * core}
    mine = pl.ds(pl.multiple_of(core * half, half), half)
    other = pl.ds(pl.multiple_of((1 - core) * half, half), half)

    def cols(number):
        return pl.ds(pl.multiple_of(number * wide, MISC), wide)

    def cols_b(number, start):
        return pl.ds(pl.multiple_of(start + number * narrow, MISC), narrow)

    def chip_at(k):
        return lax.rem(chip + k + chips, chips)

    dp_peers = [{"dp": lax.rem(row + k, parts)} for k in range(1, parts)]
    chip_peers = [{"expert": 2 * chip_at(k) + core} for k in range(1, chips)]
    greet_all([sibling] + dp_peers + chip_peers)

    order = [lax.rem(row + 1 + i, parts) for i in range(parts)]
    pairs, keeps = [], []
    for i in range(parts):
        source = grads.at[order[i]]
        pairs.append(remote(source.at[other], paired.at[i], pair_send.at[i], pair_recv.at[i], sibling))
        keeps.append(pltpu.make_async_copy(source.at[mine], own.at[i], local.at[i]))
        pairs[i].start()
        keeps[i].start()
    loads = [pltpu.make_async_copy(t, token_ins.at[n], token_load.at[n]) for n, t in enumerate((tokens_a, tokens_b))]
    stores = [
        pltpu.make_async_copy(token_outs.at[n], t, token_store.at[n]) for n, t in enumerate((tokens_out_a, tokens_out_b))
    ]
    for copy in loads:
        copy.start()
    outs, scatters_b = [], []
    for i in range(parts):
        pairs[i].wait_recv()
        keeps[i].wait()
        own[i] = (own[i].astype(F32) + paired[i].astype(F32)).astype(BF16)
        if i < parts - 1:
            scatters_b.append(
                remote(own.at[i, :, split:], dp_in_b.at[i], dp_send_b.at[i], dp_recv_b.at[i], dp_peers[i])
            )
            scatters_b[i].start()
        outs.append([
            remote(
                own.at[i, :, cols(chip_at(k))], chips_in.at[k - 1, i], out_send.at[k - 1, i], out_recv.at[k - 1, i],
                chip_peers[k - 1],
            )
            for k in range(1, chips)
        ])
        for copy in outs[i]:
            copy.start()
    for n in range(2):
        loads[n].wait()
        for image in range(token_ins.shape[1]):
            token_outs[n, :, image, :] = token_ins[n, image]
        stores[n].start()
    value = own[parts - 1, :, split:].astype(F32)
    for i in range(parts - 1):
        scatters_b[i].wait_recv()
        value = value + dp_in_b[i].astype(F32)
    total_b[...] = value.astype(BF16)
    outs_b = [
        remote(
            total_b.at[:, cols_b(chip_at(k), 0)], chips_in_b.at[k - 1], out_send_b.at[k - 1], out_recv_b.at[k - 1],
            chip_peers[k - 1],
        )
        for k in range(1, chips)
    ]
    for copy in outs_b:
        copy.start()
    scatters = []
    for i in range(parts):
        value = own[i, :, cols(chip)].astype(F32)
        for k in range(1, chips):
            outs[i][k - 1].wait_recv()
            value = value + chips_in[k - 1, i].astype(F32)
        if i < parts - 1:
            total[i] = value.astype(BF16)
            scatters.append(remote(total.at[i], dp_in.at[i], dp_send.at[i], dp_recv.at[i], dp_peers[i]))
            scatters[i].start()
        else:
            kept = value
    value = total_b[:, cols_b(chip, 0)].astype(F32)
    for k in range(1, chips):
        outs_b[k - 1].wait_recv()
        value = value + chips_in_b[k - 1].astype(F32)
    final[mine, cols_b(chip, split)] = value.astype(BF16)
    for i in range(parts - 1):
        scatters[i].wait_recv()
        kept = kept + dp_in[i].astype(F32)
    final[mine, cols(chip)] = kept.astype(BF16)

    def places(number):
        return [final.at[mine, cols(number)], final.at[mine, cols_b(number, split)]]

    backs, hands = [], []
    for n, place in enumerate(places(chip)):
        for k in range(1, chips):
            backs.append(remote(place, place, back_send.at[n, k - 1], back_recv.at[n, k - 1], chip_peers[k - 1]))
            backs[-1].start()
        hands.append(remote(place, place, pass_send.at[n, 0], pass_recv.at[n, 0], sibling))
        hands[-1].start()
    for k in range(1, chips):
        for n, place in enumerate(places(chip_at(-k))):
            backs[n * (chips - 1) + k - 1].wait_recv()
            hands.append(remote(place, place, pass_send.at[n, k], pass_recv.at[n, k], sibling))
            hands[-1].start()
    for copy in pairs + [copy for group in outs for copy in group] + outs_b + scatters + scatters_b + backs:
        copy.wait_send()
    for copy in hands + stores:
        copy.wait()


def settle(grads, tokens, chips, number):
    parts, share, columns = grads.shape
    half = share // 2
    images, length, width = tokens[0].shape
    halves = pltpu.VMEM((parts, half, columns), BF16)
    wide, narrow = settle_widths(columns, chips)
    dp_in = pltpu.VMEM((parts - 1, half, wide), BF16)
    rest = chips * narrow
    sems = [(parts,)] * 3 + [(chips - 1, parts)] * 2 + [(parts - 1,)] * 2
    sems += [(chips - 1,)] * 2 + [(parts - 1,)] * 2 + [(2, chips - 1)] * 2 + [(2, chips)] * 2
    turned = ((length, images, width), F32, False)
    return expert_call(
        settle_kernel, [(item, False) for item in (grads, *tokens)], [((share, columns), BF16, True), turned, turned],
        [
            halves, halves, dp_in, pltpu.VMEM((chips - 1, parts, half, wide), BF16), dp_in,
            pltpu.VMEM((half, rest), BF16), pltpu.VMEM((chips - 1, half, narrow), BF16),
            pltpu.VMEM((parts - 1, half, rest), BF16),
        ] + [pltpu.SemaphoreType.DMA(n) for n in sems] + [
            pltpu.VMEM((2, images, length, width), F32), pltpu.VMEM((2, length, images, width), F32),
            pltpu.SemaphoreType.DMA((2,)), pltpu.SemaphoreType.DMA((2,)),
        ],
        number,
    )


def unpack_kernel(*refs):
    count = 2 * LAYERS
    pieces, both, refs = refs[:count], refs[count : count + LAYERS], refs[count + LAYERS :]
    squares, router, vectors, (inner, outer) = refs[:4], refs[4], refs[5:12], refs[12:]
    layer = pl.program_id(0)
    share = both[0].shape[0]
    width = squares[0].shape[2]
    blocks = inner.shape[3] // FF_BLOCK

    for number in range(LAYERS):

        @pl.when(layer == number)
        def _(number=number):
            dense = both[number]
            for n in range(4):
                squares[n][0] = dense[:, n * width : (n + 1) * width].astype(F32)
            turned = dense[:, 4 * width : 4 * width + MISC].astype(F32).T
            router[0] = turned[: router.shape[1], :]
            for n in range(7):
                vectors[n][number : number + 1, :] = turned[VEC_AT + n : VEC_AT + n + 1, :]
            for j in range(2):
                piece = pieces[2 * number + j]
                for f in range(blocks):
                    inner[0, j, :, f * FF_BLOCK : (f + 1) * FF_BLOCK] = piece[
                        f * share : (f + 1) * share, :
                    ].astype(F32)
                outer[0, j] = piece[blocks * share :, :].astype(F32)


def unpack(pieces, both, local, ff, experts_all):
    layers, (share, columns) = len(both), both[0].shape
    rows, width = pieces[0].shape
    take = rows // 2
    by_layer = lambda *shape: ((layers, *shape), F32, pl.BlockSpec((1, *shape), lambda i: (i,) + (0,) * len(shape)))
    return call(
        unpack_kernel, (layers,),
        [(p, whole(p)) for p in (*pieces, *both)],
        [by_layer(share, width)] * 4 + [
            by_layer(experts_all, share),
        ] + [((layers, share), F32, pl.BlockSpec((layers, share), lambda i: (0, 0)))] * 7 + [
            by_layer(local, share, ff), by_layer(local, take, width),
        ],
    )


def shards(
    images, cotangent, routes, query_weight, key_weight, value_weight, output_weight, router_weight, query_bias,
    value_bias, output_bias, attend_gain, attend_shift, expert_gain, expert_shift, inner_weight, inner_bias,
    outer_weight, outer_bias,
):
    count, length, width = images.shape
    parts = lax.axis_size("dp")
    owners = lax.axis_size("expert")
    experts_all = router_weight.shape[2]
    local = inner_weight.shape[1]
    ff = inner_weight.shape[3]
    share = width // parts
    tokens = count * length
    squares = (query_weight, key_weight, value_weight, output_weight)
    vectors = (query_bias, value_bias, output_bias, attend_gain, attend_shift, expert_gain, expert_shift)
    columns = -(-(4 * width + MISC) // (MISC * (owners // 2))) * MISC * (owners // 2)

    first = inner_weight[0, 0].reshape(share, ff // FF_BLOCK, FF_BLOCK)
    first = jnp.transpose(first, (1, 0, 2)).reshape(ff // parts, width).astype(BF16)
    firsts = [lax.all_gather(first, "dp", axis=0, tiled=False)]
    dense, above, expert_biases, dcol, drow, capacity, (images, cotangent), mine = prepare(
        squares, router_weight, vectors, inner_bias, outer_bias, routes, (images, cotangent), (inner_weight, outer_weight),
        parts, owners, 2 * LAYERS,
    )
    packed = [dense]
    slots = experts_all * capacity

    saved = []
    back = None
    rows = images
    for layer in range(LAYERS):
        weights = [(packed[layer], s) for s in packed_specs(packed[layer])]
        routing = [(routes, per_layer(routes, layer))]
        outputs = attend_outputs(count, length, width)
        if layer == 0:
            done = call(
                first_kernel, (count,), [(rows, per_image(rows))] + routing + weights, outputs
            )
        else:
            before = saved[-1]
            done = call(
                next_kernel, (count,),
                [
                    (before["middle"], per_image(before["middle"])),
                    (before["gates"], per_image(before["gates"])),
                    (picked, per_layer(picked, 0)),
                    (picked, per_layer(picked, 1)),
                ] + routing + weights,
                [
                    images_out(count, length, width, F32),
                ] + outputs
            )
            rows, *done = done
        middle, queries, keys, values, context, sums, gates = done[:7]
        picked, arrived, g, s, outer, second, *following = expert_forward(
            done[7], drow, dcol, (local, owners, capacity, width), firsts[layer], mine, expert_biases,
            above if layer + 1 < LAYERS else None, layer,
        )
        if following:
            packed.append(following[0].reshape(width, following[0].shape[2]))
            firsts.append(following[1])
        saved.append({
            "rows": rows, "middle": middle, "attend": (queries, keys, values, context, sums), "gates": gates,
            "experts": (arrived, g, s), "weights": (firsts[layer], outer, second), "picked": picked,
        })

    last = saved[-1]
    result, dz, *sources = call(
        turn_kernel, (count,),
        [(last["middle"], per_image(last["middle"])), (last["gates"], per_image(last["gates"]))]
        + [(picked, per_layer(picked, k)) for k in range(2)]
        + [(cotangent, per_image(cotangent)), (routes, per_layer(routes, LAYERS - 1))],
        [images_out(count, length, width, F32), images_out(count, length, MISC, BF16)]
        + [images_out(count, length, width, BF16)] * 2
    )
    upstream = cotangent
    bias_grads = [None] * LAYERS
    finished = []
    waiting = []
    wgrad = None
    for layer in reversed(range(LAYERS)):
        kept = saved[layer]
        came, shares, grads, *biases, above = expert_backward(
            sources, drow, dcol, kept["weights"], *kept["experts"], wgrad, layer
        )
        came = came[0]
        came, waiting = lax.optimization_barrier((came, waiting))
        finished += waiting
        waiting = [shares, lax.psum_scatter(grads, "dp", scatter_dimension=0, tiled=False)]
        bias_grads[layer] = biases
        weights = [(packed[layer], s) for s in packed_specs(packed[layer])]
        inputs = [upstream, kept["rows"], kept["middle"], *kept["attend"], dz]
        inputs = [(a, per_image(a)) for a in inputs]
        inputs += [(came, per_image(came))] + weights
        outputs = [
            images_out(count, length, width, F32),
            (
                (width, columns), BF16,
                pl.BlockSpec((width, columns), lambda i: (0, 0)),
            ),
        ]
        if layer > 0:
            below = saved[layer - 1]
            inputs += [(below["picked"], per_layer(below["picked"], k)) for k in range(2)]
            inputs.append((below["gates"], per_image(below["gates"])))
            inputs.append((routes, per_layer(routes, layer - 1)))
            outputs += [images_out(count, length, MISC, BF16)] + [images_out(count, length, width, BF16)] * 2
        scratch = [pltpu.VMEM((width, 4 * width + MISC), F32), pltpu.VMEM((MISC, width), F32)]
        number = None
        if layer == 0:
            inputs.append((above, pl.BlockSpec(memory_space=pl.ANY)))
            outputs.append(((share, columns), BF16, pl.BlockSpec((share, columns), lambda i: (0, 0))))
            scratch += spread_scratch(share, columns, owners // 2)
            number = 2 * LAYERS + 2
        done = call(functools.partial(back_kernel, layer == 0), (count,), inputs, outputs, scratch, number)
        upstream, wgrad = done[:2]
        if layer > 0:
            dz, *sources = done[2:]
        wgrad = wgrad.reshape(parts, share, columns)
    lowest, result, upstream = settle(wgrad, (result, upstream), owners // 2, 2 * LAYERS + 1)
    both = (lowest, done[2])
    pieces = [waiting[0], waiting[1][0], finished[0], finished[1][0]]
    *squares, router, v0, v1, v2, v3, v4, v5, v6, inner, outer = unpack(pieces, both, local, ff, experts_all)
    outer_bias_grad = jnp.stack([b[1] for b in bias_grads])
    return (
        jnp.transpose(result, (1, 0, 2)),
        jnp.transpose(upstream, (1, 0, 2)),
        *squares,
        jnp.transpose(router, (0, 2, 1)),
        v0, v1, v2, v3, v4, v5, v6,
        inner,
        jnp.stack([b[0] for b in bias_grads]),
        outer,
        lax.dynamic_slice_in_dim(outer_bias_grad, lax.axis_index("dp") * share, share, 2),
    )


def solution(mesh):
    both = P(("dp", "expert"), None, None)
    square = P(None, "dp", None)
    vector = P(None, "dp")
    matrix = P(None, "expert", "dp", None)
    bias = P(None, "expert", "dp")
    grads = (square,) * 5 + (vector,) * 7 + (matrix, bias, matrix, bias)
    return jax.shard_map(
        shards,
        mesh=mesh,
        in_specs=(both, both, P(None, ("dp", "expert"), None, None)) + grads,
        out_specs=(both, both) + grads,
        check_vma=False,
    )
```

```python
import functools

import jax
import jax.numpy as jnp
from jax import lax
from jax.experimental import pallas as pl
from jax.experimental.pallas import tpu as pltpu
from jax.sharding import PartitionSpec as P

HEADS = 8
HEAD_DIM = 64
LAYERS = 2
EPSILON = 1e-06
FACTOR = HEAD_DIM**-0.5
VEC_AT = 64
MISC = 128
FF_BLOCK = 512
COST = 1024
VMEM = 56 * 1024 * 1024

MESH = pl.DeviceIdType.MESH
F32 = jnp.float32
BF16 = jnp.bfloat16


def dot(a, b):
    return jnp.dot(a, b, preferred_element_type=F32)


def dot_nt(a, b):
    return lax.dot_general(a, b, (((1,), (1,)), ((), ())), preferred_element_type=F32)


def dot_tn(a, b):
    return lax.dot_general(a, b, (((0,), (0,)), ((), ())), preferred_element_type=F32)


def standardize(rows):
    mean_value = jnp.mean(rows, axis=-1, keepdims=True)
    centered = rows - mean_value
    variance = jnp.mean(centered * centered, axis=-1, keepdims=True)
    scale = lax.rsqrt(variance + EPSILON)
    return centered * scale, scale


def standardize_back(upstream, unit, scale, gain):
    along = upstream * gain
    inner = (
        along
        - jnp.mean(along, axis=-1, keepdims=True)
        - unit * jnp.mean(along * unit, axis=-1, keepdims=True)
    )
    return inner * scale


def vectors_of(misc_ref):
    turned = misc_ref[...].astype(F32).T
    return [turned[VEC_AT + n : VEC_AT + n + 1, :] for n in range(7)]


def lane_masks(length):
    lanes = lax.broadcasted_iota(jnp.int32, (length, 2 * HEAD_DIM), 1)
    return (lanes < HEAD_DIM).astype(F32).astype(BF16), (lanes >= HEAD_DIM).astype(F32).astype(BF16)


def attend_body(
    rows, routes_ref, wq, wk, wv, wo, misc,
    t_ref, q_ref, k_ref, v_ref, o_ref, lse_ref, gates_ref, hidden_ref,
):
    length = rows.shape[0]
    qb, vb, ob, again, ashift, egain, eshift = vectors_of(misc)
    unit, _ = standardize(rows)
    low = (unit * again + ashift).astype(BF16)
    queries = (dot(low, wq[...]) + qb).astype(BF16)
    keys = dot(low, wk[...]).astype(BF16)
    values = (dot(low, wv[...]) + vb).astype(BF16)
    q_ref[0] = queries
    k_ref[0] = keys
    v_ref[0] = values
    masks = lane_masks(length)
    lanes = lax.broadcasted_iota(jnp.int32, (length, MISC), 1)
    first_half = lax.broadcasted_iota(jnp.int32, (length, 2 * HEAD_DIM), 1) < HEAD_DIM
    sums = jnp.zeros((length, MISC), F32)
    for pair in range(HEADS // 2):
        cols = slice(pair * 2 * HEAD_DIM, (pair + 1) * 2 * HEAD_DIM)
        mixed = []
        for side in range(2):
            scores = dot_nt(queries[:, cols] * (masks[side] * FACTOR), keys[:, cols])
            highest = jnp.max(scores, axis=-1, keepdims=True)
            expo = jnp.exp(scores - highest)
            total = jnp.sum(expo, axis=-1, keepdims=True)
            attention = (expo * (1.0 / total)).astype(BF16)
            sums = jnp.where(lanes == 2 * pair + side, highest + jnp.log(total), sums)
            mixed.append(dot(attention, values[:, cols]))
        o_ref[0, :, cols] = jnp.where(first_half, mixed[0], mixed[1]).astype(BF16)
    lse_ref[0] = sums
    middle = rows + (dot(o_ref[0], wo[...]) + ob)
    t_ref[0] = middle
    unit_two, _ = standardize(middle)
    hidden = (unit_two * egain + eshift).astype(BF16)
    logits = dot(hidden, misc[...])
    pair_experts = routes_ref[0]
    zero = jnp.sum(jnp.where(lanes == pair_experts[:, 0:1], logits, 0.0), axis=-1, keepdims=True)
    one = jnp.sum(jnp.where(lanes == pair_experts[:, 1:2], logits, 0.0), axis=-1, keepdims=True)
    gate_zero = 1.0 / (1.0 + jnp.exp(one - zero))
    gate_one = 1.0 / (1.0 + jnp.exp(zero - one))
    gates_ref[0, :, 0:1] = gate_zero
    gates_ref[0, :, 1:2] = gate_one
    hidden_ref[0] = hidden


def combine(middle, gates_ref, zero_ref, one_ref):
    gates = gates_ref[0]
    zero, one = zero_ref[0].astype(F32), one_ref[0].astype(F32)
    return middle + (gates[:, 0:1] * zero + gates[:, 1:2] * one), zero, one


def grads_body(upstream, zero, one, gates_ref, routes_ref, dz_ref, zero_ref, one_ref):
    length = upstream.shape[0]
    gates = gates_ref[0]
    gate_zero, gate_one = gates[:, 0:1], gates[:, 1:2]
    grad_zero = jnp.sum(zero * upstream, axis=-1, keepdims=True)
    grad_one = jnp.sum(one * upstream, axis=-1, keepdims=True)
    along = gate_zero * grad_zero + gate_one * grad_one
    lanes = lax.broadcasted_iota(jnp.int32, (length, MISC), 1)
    pair_experts = routes_ref[0]
    dz = jnp.where(lanes == pair_experts[:, 0:1], gate_zero * (grad_zero - along), 0.0)
    dz = dz + jnp.where(lanes == pair_experts[:, 1:2], gate_one * (grad_one - along), 0.0)
    dz_ref[0] = dz.astype(BF16)
    zero_ref[0] = (gate_zero * upstream).astype(BF16)
    one_ref[0] = (gate_one * upstream).astype(BF16)


def first_kernel(rows, routes, wq, wk, wv, wo, misc, *outs):
    attend_body(rows[0], routes, wq, wk, wv, wo, misc, *outs)


def next_kernel(
    middle, gates, yzero, yone, routes, wq, wk, wv, wo, misc, rows_ref, *outs
):
    rows, _, _ = combine(middle[0], gates, yzero, yone)
    rows_ref[0] = rows
    attend_body(rows, routes, wq, wk, wv, wo, misc, *outs)


def turn_kernel(middle, gates, yzero, yone, cotangent, routes, result, dz, zero_ref, one_ref):
    rows, zero, one = combine(middle[0], gates, yzero, yone)
    for image in range(result.shape[1]):

        @pl.when(pl.program_id(0) == image)
        def _(image=image):
            result[:, image, :] = rows

    grads_body(cotangent[0], zero, one, gates, routes, dz, zero_ref, one_ref)


class Spread:
    def __init__(self, above, refs):
        self.own, self.chips_in, self.final, *sems = refs
        local, out_send, out_recv, back_send, back_recv, pass_send, pass_recv = sems
        half, columns = self.own.shape
        me = lax.axis_index("expert")
        core, chip = lax.rem(me, 2), me // 2
        self.chips = chips = self.chips_in.shape[0] + 1
        block = columns // chips
        sibling = {"expert": me + 1 - 2 * core}
        mine = pl.ds(pl.multiple_of(core * half, half), half)

        def chip_at(k):
            return lax.rem(chip + k + chips, chips)

        def cols(number):
            return pl.ds(pl.multiple_of(number * block, block), block)

        peers = [{"expert": 2 * chip_at(k) + core} for k in range(1, chips)]
        self.peers = [sibling] + peers
        self.keep = pltpu.make_async_copy(above, self.own, local)
        self.outs = [
            remote(
                self.own.at[:, cols(chip_at(k))], self.chips_in.at[k - 1], out_send.at[k - 1], out_recv.at[k - 1],
                peers[k - 1],
            )
            for k in range(1, chips)
        ]
        self.place = (mine, cols(chip))
        place = self.final.at[mine, cols(chip)]
        self.backs = [
            remote(place, place, back_send.at[k - 1], back_recv.at[k - 1], peers[k - 1]) for k in range(1, chips)
        ]
        self.hands = []
        for k in range(chips):
            place = self.final.at[mine, cols(chip_at(-k))]
            self.hands.append(remote(place, place, pass_send.at[k], pass_recv.at[k], sibling))

    def stage(self, number):
        if number == 0:
            self.keep.start()
            greet_all(self.peers)
            self.keep.wait()
            for copy in self.outs:
                copy.start()
        elif number == 1:
            value = self.own[:, self.place[1]].astype(F32)
            for n, copy in enumerate(self.outs):
                copy.wait_recv()
                value = value + self.chips_in[n].astype(F32)
            self.final[self.place[0], self.place[1]] = value.astype(BF16)
            for copy in self.backs:
                copy.start()
        else:
            for copy in self.backs:
                copy.wait_recv()
            for copy in self.hands:
                copy.start()

    def finish(self, result):
        for copy in self.hands:
            copy.wait()
        for copy in self.outs + self.backs:
            copy.wait_send()
        result[...] = self.final[...]


def spread_scratch(share, columns, chips):
    half = share // 2
    half_rows = pltpu.VMEM((half, columns), BF16)
    sems = [()] + [(chips - 1,)] * 4 + [(chips,)] * 2
    return [
        half_rows, pltpu.VMEM((chips - 1, half, columns // chips), BF16), pltpu.VMEM((share, columns), BF16),
    ] + [pltpu.SemaphoreType.DMA(n) for n in sems]


def back_kernel(
    lowest, upstream, rows, middle, q_ref, k_ref, v_ref, o_ref, lse_ref, dz_ref, came,
    wq, wk, wv, wo, misc, *rest,
):
    if not lowest:
        yzero, yone, gates_below, routes_below, grad_ref, sent, dz_below, zero_ref, one_ref, wgrad, vgrad = rest
    else:
        above, grad_ref, sent, above_out, wgrad, vgrad, *spread_refs = rest
        spread = Spread(above, spread_refs)

        @pl.when(pl.program_id(0) == 0)
        def _():
            spread.stage(0)

    first = pl.program_id(0) == 0
    length = rows.shape[1]
    width = rows.shape[2]
    qb, vb, ob, again, ashift, egain, eshift = vectors_of(misc)

    @pl.when(first)
    def _():
        wgrad[...] = jnp.zeros_like(wgrad)
        vgrad[...] = jnp.zeros_like(vgrad)

    def add_vector(number, value):
        vgrad[VEC_AT + number : VEC_AT + number + 1, :] += jnp.sum(value, axis=0, keepdims=True)

    unit_two, scale_two = standardize(middle[0])
    hidden = (unit_two * egain + eshift).astype(BF16)
    dz = dz_ref[0]
    dhidden = dot_nt(dz, misc[...]) + came[0]
    wgrad[:, 4 * width :] += dot_tn(hidden, dz)
    add_vector(5, dhidden * unit_two)
    add_vector(6, dhidden)
    dmiddle = upstream[0] + standardize_back(dhidden, unit_two, scale_two, egain)
    dbranch = dmiddle.astype(BF16)
    wgrad[:, 3 * width : 4 * width] += dot_tn(o_ref[0], dbranch)
    add_vector(2, dbranch.astype(F32))
    dcontext = dot_nt(dbranch, wo[...]).astype(BF16)
    masks = lane_masks(length)
    first_half = lax.broadcasted_iota(jnp.int32, (length, 2 * HEAD_DIM), 1) < HEAD_DIM
    dqs, dks, dvs = [], [], []
    sums = lse_ref[0].T
    for pair in range(HEADS // 2):
        cols = slice(pair * 2 * HEAD_DIM, (pair + 1) * 2 * HEAD_DIM)
        keys = k_ref[0, :, cols]
        values = v_ref[0, :, cols]
        queries = q_ref[0, :, cols]
        dvalues, dqueries, dkeys = None, [], None
        for side in range(2):
            own_queries = queries * (masks[side] * FACTOR)
            own_context = dcontext[:, cols] * masks[side]
            scores = dot_nt(keys, own_queries)
            number = 2 * pair + side
            attention = jnp.exp(scores - sums[number : number + 1, :])
            prob = dot_nt(values, own_context)
            weighed = attention * prob
            delta = jnp.sum(weighed, axis=0, keepdims=True)
            dscores = (weighed - attention * delta).astype(BF16)
            dvalue = dot(attention.astype(BF16), own_context)
            dkey = dot(dscores, own_queries)
            dvalues = dvalue if dvalues is None else dvalues + dvalue
            dkeys = dkey if dkeys is None else dkeys + dkey
            dqueries.append(dot_tn(dscores, keys))
        dqs.append((jnp.where(first_half, dqueries[0], dqueries[1]) * FACTOR).astype(BF16))
        dks.append(dkeys.astype(BF16))
        dvs.append(dvalues.astype(BF16))
    dq = jnp.concatenate(dqs, axis=1)
    dk = jnp.concatenate(dks, axis=1)
    dv = jnp.concatenate(dvs, axis=1)
    unit, scale = standardize(rows[0])
    low = (unit * again + ashift).astype(BF16)
    wgrad[:, 0 : 3 * width] += dot_tn(low, jnp.concatenate([dq, dk, dv], axis=1))
    add_vector(0, dq.astype(F32))
    add_vector(1, dv.astype(F32))
    dlow = dot_nt(dq, wq[...]) + dot_nt(dk, wk[...]) + dot_nt(dv, wv[...])
    add_vector(3, dlow * unit)
    add_vector(4, dlow)
    grad = dmiddle + standardize_back(dlow, unit, scale, again)
    grad_ref[0] = grad
    if not lowest:
        grads_body(
            grad, yzero[0].astype(F32), yone[0].astype(F32), gates_below, routes_below, dz_below,
            zero_ref, one_ref,
        )

    if lowest:
        for number in range(1, 3):

            @pl.when(pl.program_id(0) == number)
            def _(number=number):
                spread.stage(number)

    @pl.when(pl.program_id(0) == pl.num_programs(0) - 1)
    def _():
        wgrad[:, 4 * width :] += vgrad[...].T
        sent[:, : 4 * width + MISC] = wgrad[...].astype(BF16)
        sent[:, 4 * width + MISC :] = jnp.zeros((width, sent.shape[1] - 4 * width - MISC), BF16)
        if lowest:
            spread.finish(above_out)


def per_image(array):
    return pl.BlockSpec((1,) + array.shape[1:], lambda i: (i,) + (0,) * (len(array.shape) - 1))


def per_layer(array, layer):
    shape = (None, 1) + array.shape[2:]
    return pl.BlockSpec(shape, lambda i: (layer, i) + (0,) * (len(shape) - 2))


def whole(array):
    return pl.BlockSpec(array.shape, lambda i: (0,) * len(array.shape))


def packed_specs(packed):
    width = packed.shape[0]
    specs = [pl.BlockSpec((width, width), lambda i, n=n: (0, n)) for n in range(4)]
    return specs + [pl.BlockSpec((width, MISC), lambda i: (0, 4 * width // MISC))]


def call(body, grid, inputs, outputs, scratch=(), number=None):
    shapes = [jax.ShapeDtypeStruct(s, t) for s, t, _ in outputs]
    return pl.pallas_call(
        body,
        grid=grid,
        in_specs=[s for _, s in inputs],
        out_specs=[s for _, _, s in outputs],
        out_shape=shapes,
        scratch_shapes=list(scratch),
        compiler_params=pltpu.CompilerParams(
            vmem_limit_bytes=VMEM, collective_id=number, has_side_effects=number is not None
        ),
        cost_estimate=pl.CostEstimate(flops=COST, bytes_accessed=COST, transcendentals=0),
    )(*[a for a, _ in inputs])


def images_out(images, length, columns, kind):
    shape = (images, length, columns)
    return (shape, kind, pl.BlockSpec((1, length, columns), lambda i: (i, 0, 0)))


def attend_outputs(images, length, width):
    return [
        images_out(images, length, width, F32),
        images_out(images, length, width, BF16),
        images_out(images, length, width, BF16),
        images_out(images, length, width, BF16),
        images_out(images, length, width, BF16),
        images_out(images, length, MISC, F32),
        images_out(images, length, 2, F32),
        images_out(images, length, width, BF16),
    ]


def greet_all(peers):
    barrier = pltpu.get_barrier_semaphore()
    for peer in peers:
        pl.semaphore_signal(barrier, inc=1, device_id=peer, device_id_type=MESH)
    pl.semaphore_wait(barrier, len(peers))


def remote(source, target, send, recv, device):
    return pltpu.make_async_remote_copy(
        src_ref=source, dst_ref=target, send_sem=send, recv_sem=recv, device_id=device, device_id_type=MESH
    )


class SharedGather:
    def __init__(self, mine, out, sems):
        send, recv, pass_send, pass_recv, own = sems
        parts, share, _ = out.shape
        half = share // 2
        row, me = lax.axis_index("dp"), lax.axis_index("expert")
        core = lax.rem(me, 2)
        sibling = {"expert": me + 1 - 2 * core}
        rows = pl.ds(pl.multiple_of(core * half, half), half)
        self.fetches, self.hands = [], []
        for k in range(1, parts):
            peer = {"dp": lax.rem(row + k, parts)}
            self.fetches.append(remote(mine.at[rows], out.at[row, rows], send.at[k - 1], recv.at[k - 1], peer))
            place = out.at[lax.rem(row - k + parts, parts), rows]
            self.hands.append(remote(place, place, pass_send.at[k - 1], pass_recv.at[k - 1], sibling))
        self.keep = pltpu.make_async_copy(mine, out.at[row], own)

    def start(self):
        for copy in self.fetches:
            copy.start()
        self.keep.start()

    def finish(self):
        for fetch, hand in zip(self.fetches, self.hands):
            fetch.wait_recv()
            hand.start()
        for fetch, hand in zip(self.fetches, self.hands):
            fetch.wait_send()
            hand.wait()
        self.keep.wait()


class Gather:
    def __init__(self, parts, mine, place, sems):
        send, recv, own = sems
        row = lax.axis_index("dp")
        self.first, self.second = [], []
        self.keep = pltpu.make_async_copy(mine, place(row), own)

        def add(group, source, target, peer):
            n = len(self.first) + len(self.second)
            group.append(remote(source, target, send.at[n], recv.at[n], {"dp": peer}))

        if parts != 4:
            for k in range(1, parts):
                add(self.first, mine, place(row), lax.rem(row + k, parts))
            return
        near, far = row + 1 - 2 * lax.rem(row, 2), lax.rem(row + 2, 4)
        quarter = mine.shape[0] // 4
        halves = [[slice(n * quarter, (n + 1) * quarter) for n in pair] for pair in ((0, 1), (2, 3))]
        for rows, peer in ((halves[0], near), (halves[1], far)):
            for part in rows:
                add(self.first, mine.at[part], place(row).at[part], peer)
        for rows, peer, other in ((halves[0], far, near), (halves[1], near, far)):
            for part in rows:
                add(self.second, mine.at[part], place(row).at[part], peer)
            for part in rows:
                add(self.second, place(other).at[part], place(other).at[part], peer)

    def start(self):
        for copy in self.first:
            copy.start()
        self.keep.start()

    def forward(self):
        for copy in self.first:
            copy.wait_recv()
        for copy in self.second:
            copy.start()

    def finish(self):
        for copy in self.second:
            copy.wait_recv()
        self.keep.wait()

    def drain(self):
        for copy in self.first + self.second:
            copy.wait_send()


def gather_sems(parts):
    count = 12 if parts == 4 else parts - 1
    return [pltpu.SemaphoreType.DMA((count,)), pltpu.SemaphoreType.DMA((count,)), pltpu.SemaphoreType.DMA]


def shared_sems(parts):
    return [pltpu.SemaphoreType.DMA((parts - 1,))] * 4 + [pltpu.SemaphoreType.DMA]


ROOT_HALF = 0.7071067811865476
ROOT_TWO_PI_INVERSE = 0.3989422804014327

class Swap:
    def __init__(self, sent, arrived, made, back, sems):
        self.sent, self.arrived, self.made, self.back = sent, arrived, made, back
        self.out_send, self.out_recv, self.home_send, self.home_recv, self.own = sems
        self.local, self.count = arrived.shape[0], arrived.shape[1]
        self.me = lax.axis_index("expert")

    def greet(self, others=()):
        greet_all([{"expert": lax.rem(self.me + k, self.count)} for k in range(1, self.count)] + list(others))

    def outward(self, j, k, peer):
        return pltpu.make_async_remote_copy(
            src_ref=self.sent.at[j, peer], dst_ref=self.arrived.at[j, self.me],
            send_sem=self.out_send.at[j, k], recv_sem=self.out_recv.at[j, k],
            device_id={"expert": peer}, device_id_type=MESH,
        )

    def homeward(self, j, k, peer):
        return pltpu.make_async_remote_copy(
            src_ref=self.made.at[j, peer], dst_ref=self.back.at[j, self.me],
            send_sem=self.home_send.at[j, k], recv_sem=self.home_recv.at[j, k],
            device_id={"expert": peer}, device_id_type=MESH,
        )

    def own_out(self, j):
        return pltpu.make_async_copy(self.sent.at[j, self.me], self.arrived.at[j, self.me], self.own.at[j])

    def own_home(self, j):
        return pltpu.make_async_copy(self.made.at[j, self.me], self.back.at[j, self.me], self.own.at[self.local + j])

    def send_all(self, sources, drow, layer):
        chips = self.count // 2
        capacity, width = self.sent.shape[2:]
        images, length, _ = sources[0].shape

        for j in range(self.local):

            def fill(turn, carry, j=j):
                sign = 2 * lax.rem(turn, 2) - 1
                chip = lax.rem(self.me // 2 + chips // 2 + sign * ((turn + 1) // 2) + chips, chips)
                first = (j * self.count + 2 * chip) * capacity
                slots = lax.broadcasted_iota(jnp.int32, (2 * capacity, length), 0) + first
                total = jnp.zeros((2 * capacity, width), F32)
                for image in range(images):
                    dest = drow[layer, image]
                    hits = [slots == dest[0:1, :], slots == dest[1:2, :]]
                    if len(sources) == 1:
                        hits = [hits[0] | hits[1]]
                    for hit, source in zip(hits, sources):
                        total = total + dot(hit.astype(F32).astype(BF16), source[image])
                self.sent[j, pl.ds(2 * chip, 2)] = total.astype(BF16).reshape(2, capacity, width)
                for core in range(2):
                    peer = 2 * chip + core
                    k = lax.rem(peer - self.me + self.count, self.count)

                    @pl.when(peer != self.me)
                    def _(k=k, peer=peer):
                        self.outward(j, k, peer).start()

                    @pl.when(peer == self.me)
                    def _():
                        self.own_out(j).start()

                return carry

            lax.fori_loop(0, chips, fill, 0)

    def chip(self, turn):
        chips = self.count // 2
        return lax.rem(self.me // 2 - turn + chips, chips)

    def wait_chip(self, j, chip):
        for core in range(2):
            source = 2 * chip + core
            k = lax.rem(self.me - source + self.count, self.count)

            @pl.when(source != self.me)
            def _(k=k, source=source):
                pltpu.make_async_remote_copy(
                    src_ref=self.arrived.at[j, source], dst_ref=self.arrived.at[j, source],
                    send_sem=self.out_send.at[j, k], recv_sem=self.out_recv.at[j, k],
                    device_id={"expert": source}, device_id_type=MESH,
                ).wait_recv()

            @pl.when(source == self.me)
            def _():
                self.own_out(j).wait()

    def send_home(self, j, chip):
        for core in range(2):
            peer = 2 * chip + core
            k = lax.rem(peer - self.me + self.count, self.count)

            @pl.when(peer != self.me)
            def _(k=k, peer=peer):
                self.homeward(j, k, peer).start()

            @pl.when(peer == self.me)
            def _():
                self.own_home(j).start()

    def wait_home(self, j, chip):
        for core in range(2):
            source = 2 * chip + core
            k = lax.rem(self.me - source + self.count, self.count)

            @pl.when(source != self.me)
            def _(k=k, source=source):
                place = self.back.at[j, source]
                remote(place, place, self.home_send.at[j, k], self.home_recv.at[j, k], {"expert": source}).wait_recv()

            @pl.when(source == self.me)
            def _():
                self.own_home(j).wait()

    def take_home(self, dcol, layer, total):
        count, images, length, width = total.shape
        capacity = self.back.shape[2]
        total[...] = jnp.zeros_like(total)
        for j in range(self.local):

            def step(turn, carry, j=j):
                chip = self.chip(turn)
                self.wait_home(j, chip)
                rows = self.back[j, pl.ds(2 * chip, 2)].reshape(2 * capacity, width)
                first = (j * self.count + 2 * chip) * capacity
                lanes = lax.broadcasted_iota(jnp.int32, (length, 2 * capacity), 1) + first
                for image in range(images):
                    dest = dcol[layer, image]
                    hits = [dest[:, 0:1] == lanes, dest[:, 1:2] == lanes]
                    if count == 1:
                        hits = [hits[0] | hits[1]]
                    for k, hit in enumerate(hits):
                        total[k, image] += dot(hit.astype(F32).astype(BF16), rows).astype(total.dtype)
                return carry

            lax.fori_loop(0, self.count // 2, step, 0)

    def finish(self):
        for j in range(self.local):
            for k in range(1, self.count):
                peer = lax.rem(self.me + k, self.count)
                self.outward(j, k, peer).wait_send()
                self.homeward(j, k, peer).wait_send()


def weight_blocks(weights, j, f):
    _, parts, rows, width = weights.shape
    share, take = width // parts, rows // 2
    each = FF_BLOCK // take
    first = weights[j, :, f * share : (f + 1) * share, :].reshape(width, width)
    second = weights[j, f * each : (f + 1) * each, take:, :].reshape(FF_BLOCK, width)
    return first, second


def expert_kernel(layer, with_dense, *refs):
    if with_dense:
        *refs, n1, n2, n3, n4, n5, m1, m2, m3 = refs
        refs = list(refs)
        dense_in, dense_out, next_out = refs.pop(7), refs.pop(13), refs.pop(13)
        dense = SharedGather(dense_in, dense_out, (n1, n2, n3, n4, n5))
        next_in = refs[4].at[layer + 1, 0, : next_out.shape[1]]
        following = Gather(dense_out.shape[0], next_in, lambda p: next_out.at[p], (m1, m2, m3))
    (
        hidden, drow, dcol, inner_first, shares, b1, b2, picked, arrived_out, g_out, s_out, outer_out, packed_out,
        back, sent, arrived, made, weights, g_stage, s_stage, out_send, out_recv, home_send, home_recv, own, load, stores, last,
        *gather_refs,
    ) = refs
    row = lax.axis_index("dp")
    parts = weights.shape[1]
    take = weights.shape[2] // 2
    mine = shares.at[layer, 1]
    gathers = [
        Gather(parts, shares.at[layer, 0, take:], lambda p: weights.at[0, p, take:], gather_refs[:3]),
        Gather(parts, mine, lambda p: weights.at[1, p], gather_refs[3:]),
    ]
    swap = Swap(sent, arrived, made, back, (out_send, out_recv, home_send, home_recv, own))
    local, count, capacity, width = arrived.shape
    chips = count // 2
    rows = 2 * capacity
    ff = g_out.shape[2]
    first_load = pltpu.make_async_copy(inner_first, weights.at[0, :, :take], load)
    first_load.start()
    swap.greet([{"dp": lax.rem(row + k, parts)} for k in range(1, parts)])
    gathers[0].start()
    swap.send_all([hidden], drow, layer)
    gathers[0].forward()
    gathers[1].start()
    gathered = [
        pltpu.make_async_copy(weights.at[0, :, take:], outer_out, last.at[1]),
        pltpu.make_async_copy(weights.at[1], packed_out, last.at[2]),
    ]

    def kept(j, slot, chip):
        place = pl.ds(pl.multiple_of(chip * rows, rows), rows)
        return (
            pltpu.make_async_copy(g_stage.at[slot], g_out.at[j, place, :], stores.at[0, slot]),
            pltpu.make_async_copy(s_stage.at[slot], s_out.at[j, place, :], stores.at[1, slot]),
        )

    for j in range(local):
        if j == 0:
            first_load.wait()
        gathers[j].finish()
        gathered[j].start()
        if j == 1 and with_dense:
            following.start()
        number = layer * local + j

        def chip_step(turn, carry, j=j, number=number):
            chip = swap.chip(turn)
            slot = lax.rem(turn, 2)
            swap.wait_chip(j, chip)
            if j == 0:

                @pl.when(turn == 1)
                def _():
                    gathers[1].forward()
                    if with_dense:
                        dense.start()

            if j == 1 and with_dense:

                @pl.when(turn == 2)
                def _():
                    following.forward()

            @pl.when(j * chips + turn >= 2)
            def _():
                for copy in kept(j, slot, chip):
                    copy.wait()

            x = arrived[j, pl.ds(2 * chip, 2)].reshape(rows, width)
            total = jnp.broadcast_to(b2[number : number + 1, :], (rows, width))
            for f in range(ff // FF_BLOCK):
                cols = slice(f * FF_BLOCK, (f + 1) * FF_BLOCK)
                first, second = weight_blocks(weights, j, f)
                inner = dot(x, first) + b1[number : number + 1, cols]
                normal = 0.5 * (1.0 + lax.erf(inner * ROOT_HALF))
                g = (inner * normal).astype(BF16)
                density = jnp.exp(-0.5 * inner * inner) * ROOT_TWO_PI_INVERSE
                g_stage[slot, :, cols] = g
                s_stage[slot, :, cols] = (normal + inner * density).astype(BF16)
                total = total + dot(g, second)
            made[j, pl.ds(2 * chip, 2)] = total.astype(BF16).reshape(2, capacity, width)
            swap.send_home(j, chip)
            for copy in kept(j, slot, chip):
                copy.start()
            return carry

        lax.fori_loop(0, chips, chip_step, 0)
    final = pltpu.make_async_copy(arrived, arrived_out, last.at[0])
    final.start()
    if with_dense:
        dense.finish()
        following.finish()
        following.drain()
    for slot in range(2):
        for copy in kept(0, slot, 0):
            copy.wait()
    swap.take_home(dcol, layer, picked)
    swap.finish()
    for gather, copy in zip(gathers, gathered):
        gather.drain()
        copy.wait()
    final.wait()


def expert_back_kernel(layer, with_above, *refs):
    if with_above:
        *refs, above_in, above_own, above_paired, above_send, above_recv, above_load, pair_send, pair_recv = refs
        refs = list(refs)
        above, above_sum = refs.pop(10), refs.pop(15)
    (
        zero, one, drow, dcol, inner_first, outer_first, packed_second, arrived_x, g_in, s_in,
        came, summed, out, bias1, bias2, back, sent, arrived, made, weights, x, du, s_stage, g_stage, first_stage, second_stage, share_out, share_in,
        db1, db2, db1_in, db2_in,
        out_send, out_recv, home_send, home_recv, own, load, fetch, stores, share_send, share_recv,
        bias_send, bias_recv,
    ) = refs
    swap = Swap(sent, arrived, made, back, (out_send, out_recv, home_send, home_recv, own))
    row = lax.axis_index("dp")
    local, count, capacity, width = arrived.shape
    chips = count // 2
    rows = 2 * capacity
    ff = g_in.shape[2]
    blocks = ff // FF_BLOCK
    _, parts, all_rows, _ = weights.shape
    share, take = width // parts, all_rows // 2
    each = FF_BLOCK // take
    loads = [
        pltpu.make_async_copy(inner_first, weights.at[0, :, :take], load.at[0]),
        pltpu.make_async_copy(packed_second, weights.at[1], load.at[1]),
        pltpu.make_async_copy(arrived_x, x, load.at[local]),
        pltpu.make_async_copy(outer_first, weights.at[0, :, take:], load.at[local + 1]),
    ]
    for copy in loads:
        copy.start()

    def slopes(j, turn):
        slot = lax.rem(turn, 2)
        place = pl.ds(pl.multiple_of(swap.chip(turn) * rows, rows), rows)
        return pltpu.make_async_copy(s_in.at[j, place, :], s_stage.at[slot], fetch.at[0, slot])

    def activations(j, f):
        return pltpu.make_async_copy(
            g_in.at[j, :, f * FF_BLOCK : (f + 1) * FF_BLOCK], g_stage.at[f % 2], fetch.at[1, f % 2]
        )

    def results(j, f):
        return (
            pltpu.make_async_copy(
                first_stage.at[f % 2], out.at[:, j - 1, f * share : (f + 1) * share, :], stores.at[0, f % 2]
            ),
            pltpu.make_async_copy(
                second_stage.at[f % 2], out.at[f * each : (f + 1) * each, j - 1, take:, :], stores.at[1, f % 2]
            ),
        )

    def share_copy(k):
        peer = lax.rem(row + k, parts)
        return pltpu.make_async_remote_copy(
            src_ref=share_out.at[peer], dst_ref=share_in.at[k - 1],
            send_sem=share_send.at[k - 1], recv_sem=share_recv.at[k - 1],
            device_id={"dp": peer}, device_id_type=MESH,
        )

    slopes(0, 0).start()
    peers = [{"dp": lax.rem(row + k, parts)} for k in range(1, parts)]
    swap.greet(peers)
    if with_above:
        core = lax.rem(swap.me, 2)
        half = above_own.shape[1]
        mine = pl.ds(pl.multiple_of(core * half, half), half)
        other = pl.ds(pl.multiple_of((1 - core) * half, half), half)
        pair = remote(above.at[:, other], above_paired, pair_send, pair_recv, {"expert": swap.me + 1 - 2 * core})
        keep = pltpu.make_async_copy(above.at[:, mine], above_own, above_load)
        pair.start()
        keep.start()
        above_copies = [
            remote(
                above_own.at[lax.rem(row + k, parts)], above_in.at[k - 1], above_send.at[k - 1], above_recv.at[k - 1],
                peers[k - 1],
            )
            for k in range(1, parts)
        ]
    swap.send_all([zero, one], drow, layer)
    if with_above:
        pair.wait_recv()
        keep.wait()
        for part in range(parts):
            above_own[part] = (above_own[part].astype(F32) + above_paired[part].astype(F32)).astype(BF16)
        for copy in above_copies:
            copy.start()
    loads[local + 1].wait()
    for j in range(local):
        loads[j].wait()
        activations(j, 0).start()

        def chip_step(turn, carry, j=j):
            chip = swap.chip(turn)
            slot = lax.rem(turn, 2)

            @pl.when(turn + 1 < chips)
            def _():
                slopes(j, turn + 1).start()

            swap.wait_chip(j, chip)
            slopes(j, turn).wait()
            dy = arrived[j, pl.ds(2 * chip, 2)].reshape(rows, width)
            place = pl.ds(pl.multiple_of(chip * rows, rows), rows)
            total = jnp.zeros((rows, width), F32)
            for f in range(blocks):
                cols = slice(f * FF_BLOCK, (f + 1) * FF_BLOCK)
                first, second = weight_blocks(weights, j, f)
                part = (dot_nt(dy, second) * s_stage[slot, :, cols].astype(F32)).astype(BF16)
                du[place, cols] = part
                total = total + dot_nt(part, first)
            made[j, pl.ds(2 * chip, 2)] = total.astype(BF16).reshape(2, capacity, width)
            swap.send_home(j, chip)
            return carry

        lax.fori_loop(0, chips, chip_step, 0)
        if j + 1 < local:
            slopes(j + 1, 0).start()
        if j == 0:
            loads[local].wait()
        dy = arrived[j].reshape(count * capacity, width)
        db2[j : j + 1, :] = jnp.sum(dy.astype(F32), axis=0, keepdims=True)
        for f in range(blocks):
            cols = slice(f * FF_BLOCK, (f + 1) * FF_BLOCK)
            if f + 1 < blocks:
                activations(j, f + 1).start()
            if j > 1 or (j == 1 and f > 1):
                for copy in results(j, f):
                    copy.wait()
            part = du[:, cols]
            grad = dot_tn(x[j].reshape(count * capacity, width), part).astype(BF16)
            if j == 0:
                share_out[:, f * share : (f + 1) * share, :] = grad.reshape(parts, share, width)
            else:
                first_stage[f % 2] = grad.reshape(parts, share, width)
            db1[j : j + 1, cols] = jnp.sum(part.astype(F32), axis=0, keepdims=True)
            activations(j, f).wait()
            grad = dot_tn(g_stage[f % 2], dy).astype(BF16).reshape(each, take, width)
            if j == 0:
                share_out[f * each : (f + 1) * each, take:, :] = grad
            else:
                second_stage[f % 2] = grad
                for copy in results(j, f):
                    copy.start()
        if j == 0:
            for k in range(1, parts):
                share_copy(k).start()
    part_ff = ff // parts
    bias_copies = []
    for k in range(1, parts):
        place = pl.ds(pl.multiple_of(lax.rem(row + k, parts) * part_ff, part_ff), part_ff)
        for n, (source, target) in enumerate(((db1.at[:, place], db1_in.at[k - 1]), (db2, db2_in.at[k - 1]))):
            bias_copies.append(pltpu.make_async_remote_copy(
                src_ref=source, dst_ref=target, send_sem=bias_send.at[n, k - 1], recv_sem=bias_recv.at[n, k - 1],
                device_id=peers[k - 1], device_id_type=MESH,
            ))
            bias_copies[-1].start()
    if with_above:
        for copy in above_copies:
            copy.wait_recv()
        total = above_own[row].astype(F32)
        for k in range(1, parts):
            total = total + above_in[k - 1].astype(F32)
        above_sum[...] = total.astype(BF16)
    for k in range(1, parts):
        share_copy(k).wait_recv()
    step = 64

    def add_up(turn, carry):
        place = pl.ds(pl.multiple_of(turn * step, step), step)
        total = share_out[row, place, :].astype(F32)
        for k in range(1, parts):
            total = total + share_in[k - 1, place, :].astype(F32)
        summed[place, :] = total.astype(BF16)
        return carry

    lax.fori_loop(0, all_rows // step, add_up, 0)
    for copy in bias_copies:
        copy.wait_recv()
    total1, total2 = db1[:, pl.ds(pl.multiple_of(row * part_ff, part_ff), part_ff)], db2[...]
    for k in range(1, parts):
        total1, total2 = total1 + db1_in[k - 1], total2 + db2_in[k - 1]
    bias1[...], bias2[...] = total1, total2
    swap.take_home(dcol, layer, came)
    if with_above:
        for copy in above_copies + [pair]:
            copy.wait_send()
    for copy in bias_copies:
        copy.wait_send()
    for k in range(1, parts):
        share_copy(k).wait_send()
    for f in range(2):
        for copy in results(1, f):
            copy.wait()
    swap.finish()


def swap_sems(local, count):
    pairs = [pltpu.SemaphoreType.DMA((local, count))] * 4
    return pairs + [pltpu.SemaphoreType.DMA((2 * local,))]


def expert_call(body, inputs, outputs, scratch, number):
    def spec(held):
        return pl.BlockSpec(memory_space=pltpu.VMEM if held else pl.ANY)

    shapes = [jax.ShapeDtypeStruct(s, t) for s, t, _ in outputs]
    return pl.pallas_call(
        body,
        in_specs=[spec(held) for _, held in inputs],
        out_specs=[spec(held) for _, _, held in outputs],
        out_shape=shapes,
        scratch_shapes=scratch,
        compiler_params=pltpu.CompilerParams(
            collective_id=number, has_side_effects=True, vmem_limit_bytes=VMEM
        ),
        cost_estimate=pl.CostEstimate(flops=COST, bytes_accessed=COST, transcendentals=0),
    )(*[a for a, _ in inputs])


def expert_forward(hidden, drow, dcol, shape, inner, shares, biases, following, layer):
    b1, b2 = biases
    local, count, capacity, width = shape
    ff = b1.shape[1]
    rows = 2 * capacity
    parts = inner.shape[0]
    packed = (parts, *shares.shape[2:])
    half = (parts, shares.shape[2] // 2, width)
    slots = (local, count * capacity, ff)
    inputs = [(hidden, True), (drow, True), (dcol, True), (inner, False), (shares, False), (b1, True), (b2, True)]
    outputs = [
        ((2, *hidden.shape), BF16, True), (shape, BF16, False), (slots, BF16, False), (slots, BF16, False),
        (half, BF16, False), (packed, BF16, False),
    ]
    scratch = [
        pltpu.VMEM(shape, BF16), pltpu.VMEM(shape, BF16), pltpu.VMEM(shape, BF16), pltpu.VMEM(shape, BF16),
        pltpu.VMEM((local, *packed), BF16),
        pltpu.VMEM((2, rows, ff), BF16), pltpu.VMEM((2, rows, ff), BF16),
    ] + swap_sems(local, count) + [
        pltpu.SemaphoreType.DMA, pltpu.SemaphoreType.DMA((2, 2)), pltpu.SemaphoreType.DMA((3,)),
    ] + gather_sems(parts) * 2
    if following is not None:
        inputs.append((following, False))
        outputs += [((parts, *following.shape), BF16, False), (half, BF16, False)]
        scratch += shared_sems(parts) + gather_sems(parts)
    return expert_call(functools.partial(expert_kernel, layer, following is not None), inputs, outputs, scratch, layer)


def expert_backward(sources, drow, dcol, weights, arrived, g, s, above, layer):
    shape = arrived.shape
    local, count, capacity, width = shape
    ff = g.shape[2]
    rows = 2 * capacity
    parts, all_rows, _ = weights[2].shape
    share, take = width // parts, all_rows // 2
    inputs = [(a, True) for a in (*sources, drow, dcol)] + [(a, False) for a in (*weights, arrived, g, s)]
    outputs = [
        ((1, *sources[0].shape), F32, True), ((all_rows, width), BF16, True), ((parts, local - 1, all_rows, width), BF16, False),
        ((local, ff // parts), F32, True), ((local, width), F32, True),
    ]
    scratch = [
        pltpu.VMEM(shape, BF16), pltpu.VMEM(shape, BF16), pltpu.VMEM(shape, BF16), pltpu.VMEM(shape, BF16),
        pltpu.VMEM((local, parts, all_rows, width), BF16), pltpu.VMEM(shape, BF16),
        pltpu.VMEM((count * capacity, ff), BF16), pltpu.VMEM((2, rows, ff), BF16),
        pltpu.VMEM((2, count * capacity, FF_BLOCK), BF16), pltpu.VMEM((2, parts, share, width), BF16),
        pltpu.VMEM((2, FF_BLOCK // take, take, width), BF16),
        pltpu.VMEM((parts, all_rows, width), BF16), pltpu.VMEM((parts - 1, all_rows, width), BF16),
        pltpu.VMEM((local, ff), F32), pltpu.VMEM((local, width), F32),
        pltpu.VMEM((parts - 1, local, ff // parts), F32), pltpu.VMEM((parts - 1, local, width), F32),
    ] + swap_sems(local, count) + [
        pltpu.SemaphoreType.DMA((local + 2,)), pltpu.SemaphoreType.DMA((2, 2)), pltpu.SemaphoreType.DMA((2, 2)),
        pltpu.SemaphoreType.DMA((parts - 1,)), pltpu.SemaphoreType.DMA((parts - 1,)),
        pltpu.SemaphoreType.DMA((2, parts - 1)), pltpu.SemaphoreType.DMA((2, parts - 1)),
    ]
    if above is not None:
        inputs.append((above, False))
        halves = (share // 2, above.shape[2])
        outputs.append((halves, BF16, True))
        scratch += [
            pltpu.VMEM((parts - 1, *halves), BF16), pltpu.VMEM((parts, *halves), BF16), pltpu.VMEM((parts, *halves), BF16),
            pltpu.SemaphoreType.DMA((parts - 1,)), pltpu.SemaphoreType.DMA((parts - 1,)),
        ] + [pltpu.SemaphoreType.DMA] * 3
    done = expert_call(
        functools.partial(expert_back_kernel, layer, above is not None), inputs, outputs, scratch, LAYERS + layer
    )
    return done if above is not None else [*done, None]


def prepare_kernel(capacity, owners, *refs):
    squares, (router, *vectors), (inner_bias, outer_bias, routes) = refs[:4], refs[4:12], refs[12:15]
    tokens_in, matrices, refs = refs[15:17], refs[17:19], refs[19:]
    (out, above, b1, b2, dcol, drow), tokens_out, packed_out, refs = refs[:6], refs[6:8], refs[8], refs[9:]
    mine, turned, inner_low, outer_low, token_ins, token_outs, inner_in, outer_in, packs = refs[:9]
    sems, (b1_send, b1_recv, b2_send, b2_recv, own, token_load, token_store, weight_sems) = refs[9:14], refs[14:]
    weight_loads = [
        pltpu.make_async_copy(matrices[0], inner_in, weight_sems.at[0]),
        pltpu.make_async_copy(matrices[1], outer_in, weight_sems.at[1]),
    ]
    weight_store = pltpu.make_async_copy(packs, packed_out, weight_sems.at[2])
    parts, share, _ = out.shape
    loads = [pltpu.make_async_copy(tokens_in[n], token_ins.at[n], token_load.at[n]) for n in range(2)]
    stores = [pltpu.make_async_copy(token_outs.at[n], tokens_out[n], token_store.at[n]) for n in range(2)]
    width = squares[0].shape[2]
    experts_all = router.shape[2]
    local, part_ff = inner_bias.shape[1:]
    row, me = lax.axis_index("dp"), lax.axis_index("expert")
    sibling = {"expert": me + 1 - 2 * lax.rem(me, 2)}
    peers = [{"dp": lax.rem(row + k, parts)} for k in range(1, parts)]
    gather = SharedGather(mine, out, sems)

    def pack(target, layer):
        for n in range(4):
            target[:, n * width : (n + 1) * width] = squares[n][layer].astype(BF16)
        turned[...] = jnp.zeros_like(turned)
        for n in range(7):
            turned[VEC_AT + n : VEC_AT + n + 1, :] = vectors[n][layer : layer + 1, :]
        target[:, 4 * width :] = turned[...].T.astype(BF16)
        target[:, 4 * width : 4 * width + experts_all] = router[layer].astype(BF16)

    pack(mine, 0)
    for layer in range(LAYERS):
        for j in range(local):
            n = layer * local + j
            inner_low[n : n + 1, :] = inner_bias[layer, j : j + 1, :].astype(BF16).astype(F32)
            outer_low[n : n + 1, :] = outer_bias[layer, j : j + 1, :].astype(BF16).astype(F32)
    greet_all([sibling] + peers)
    place = pl.ds(pl.multiple_of(row * part_ff, part_ff), part_ff)
    singles = [
        remote(inner_low, b1.at[:, place], b1_send.at[k], b1_recv.at[k], peers[k]) for k in range(parts - 1)
    ] + [remote(outer_low, b2.at[row], b2_send.at[k], b2_recv.at[k], peers[k]) for k in range(parts - 1)]
    keeps = [
        pltpu.make_async_copy(inner_low, b1.at[:, place], own.at[0]),
        pltpu.make_async_copy(outer_low, b2.at[row], own.at[1]),
    ]
    gather.start()
    for copy in singles + keeps + loads + weight_loads:
        copy.start()
    pack(above, 1)
    for n in range(2):
        loads[n].wait()
        for image in range(routes.shape[1]):
            token_outs[n, image] = token_ins[n, :, image, :]
        stores[n].start()

    length = routes.shape[2]
    lanes = lax.broadcasted_iota(jnp.int32, (length, MISC), 1)
    earlier = (
        lax.broadcasted_iota(jnp.int32, (length, length), 0) > lax.broadcasted_iota(jnp.int32, (length, length), 1)
    ).astype(F32).astype(BF16)
    for layer in range(LAYERS):
        seen = jnp.zeros((1, MISC), F32)
        for image in range(routes.shape[1]):
            hots, dests = [], []
            for k in range(2):
                hots.append((lanes == routes[layer, image, :, k : k + 1]).astype(F32))
            counts = hots[0] + hots[1]
            before = dot(earlier, counts.astype(BF16)) + seen
            seen = seen + jnp.sum(counts, axis=0, keepdims=True)
            for k in range(2):
                slot = jnp.sum(hots[k] * before, axis=-1, keepdims=True)
                expert = routes[layer, image, :, k : k + 1].astype(F32)
                owner = jnp.floor(expert * (1.0 / local))
                place = ((expert - owner * local) * owners + owner) * capacity + slot
                dests.append(jnp.where(slot < capacity, place, -1.0))
                dcol[layer, image, :, k : k + 1] = dests[k].astype(jnp.int32)
            both = jnp.where(lanes == 0, dests[0], jnp.where(lanes == 1, dests[1], 0.0))
            drow[layer, image] = both.T[0:2, :].astype(jnp.int32)

    for copy in weight_loads:
        copy.wait()
    take = outer_in.shape[2]
    for layer in range(LAYERS):
        for j in range(local):
            for f in range(take // share):
                cols = slice(f * FF_BLOCK, (f + 1) * FF_BLOCK)
                packs[layer, j, f * share : (f + 1) * share, :] = inner_in[layer, j, :, cols].astype(BF16)
            packs[layer, j, take:, :] = outer_in[layer, j].astype(BF16)
    weight_store.start()
    gather.finish()
    for copy in singles + keeps + stores + [weight_store]:
        copy.wait()


def prepare(squares, router, vectors, inner_bias, outer_bias, routes, tokens, matrices, parts, owners, number):
    layers, share, width = squares[0].shape
    experts_all = router.shape[2]
    local, part_ff = inner_bias.shape[1:]
    _, images, length, _ = routes.shape
    capacity = (10 * images * length // (4 * experts_all) + 7) // 8 * 8
    columns = 4 * width + MISC
    count = layers * local
    sems = shared_sems(parts) + [pltpu.SemaphoreType.DMA((parts - 1,))] * 4 + [pltpu.SemaphoreType.DMA((2,))] * 3
    sems.append(pltpu.SemaphoreType.DMA((3,)))
    packs = (layers, local, 2 * matrices[1].shape[2], width)
    inputs = [*squares, router, *vectors, inner_bias, outer_bias, routes]
    turned = [jnp.transpose(item, (1, 0, 2)) for item in tokens]
    out, above, b1, b2, dcol, drow, *tokens, packs = expert_call(
        functools.partial(prepare_kernel, capacity, owners),
        [(a, True) for a in inputs] + [(a, False) for a in (*turned, *matrices)],
        [
            ((parts, share, columns), BF16, False), ((share, columns), BF16, True),
            ((count, part_ff * parts), F32, False), ((parts, count, share), F32, False),
            ((layers, images, length, 2), jnp.int32, True), ((layers, images, 2, length), jnp.int32, True),
            ((images, length, width), F32, False), ((images, length, width), F32, False), (packs, BF16, False),
        ],
        [
            pltpu.VMEM((share, columns), BF16), pltpu.VMEM((MISC, share), F32),
            pltpu.VMEM((count, part_ff), F32), pltpu.VMEM((count, share), F32),
            pltpu.VMEM((2, length, images, width), F32), pltpu.VMEM((2, images, length, width), F32),
            pltpu.VMEM(matrices[0].shape, F32), pltpu.VMEM(matrices[1].shape, F32), pltpu.VMEM(packs, BF16),
        ] + sems,
        number,
    )
    b2 = jnp.transpose(b2, (1, 0, 2)).reshape(count, width)
    return out.reshape(width, columns), above, (b1, b2), dcol, drow, capacity, tokens, packs


def settle_widths(columns, chips):
    blocks = columns // (MISC * chips)
    wide = (blocks + 1) // 2 * MISC
    return wide, columns // chips - wide


def settle_kernel(
    grads, tokens, final, tokens_out, own, paired, total, chips_in, dp_in, total_b, chips_in_b, dp_in_b,
    pair_send, pair_recv, local, out_send, out_recv, dp_send, dp_recv, out_send_b, out_recv_b, dp_send_b, dp_recv_b,
    back_send, back_recv, pass_send, pass_recv, token_ins, token_outs, token_load, token_store,
):
    parts, share, columns = grads.shape
    half = share // 2
    row, me = lax.axis_index("dp"), lax.axis_index("expert")
    core, chip = lax.rem(me, 2), me // 2
    chips = chips_in.shape[0] + 1
    wide, narrow = settle_widths(columns, chips)
    split = chips * wide
    sibling = {"expert": me + 1 - 2 * core}
    mine = pl.ds(pl.multiple_of(core * half, half), half)
    other = pl.ds(pl.multiple_of((1 - core) * half, half), half)

    def cols(number):
        return pl.ds(pl.multiple_of(number * wide, MISC), wide)

    def cols_b(number, start):
        return pl.ds(pl.multiple_of(start + number * narrow, MISC), narrow)

    def chip_at(k):
        return lax.rem(chip + k + chips, chips)

    dp_peers = [{"dp": lax.rem(row + k, parts)} for k in range(1, parts)]
    chip_peers = [{"expert": 2 * chip_at(k) + core} for k in range(1, chips)]
    greet_all([sibling] + dp_peers + chip_peers)

    order = [lax.rem(row + 1 + i, parts) for i in range(parts)]
    pairs, keeps = [], []
    for i in range(parts):
        source = grads.at[order[i]]
        pairs.append(remote(source.at[other], paired.at[i], pair_send.at[i], pair_recv.at[i], sibling))
        keeps.append(pltpu.make_async_copy(source.at[mine], own.at[i], local.at[i]))
        pairs[i].start()
        keeps[i].start()
    tokens_load = pltpu.make_async_copy(tokens, token_ins, token_load)
    tokens_load.start()
    tokens_store = pltpu.make_async_copy(token_outs, tokens_out, token_store)
    outs, scatters_b = [], []
    for i in range(parts):
        pairs[i].wait_recv()
        keeps[i].wait()
        own[i] = (own[i].astype(F32) + paired[i].astype(F32)).astype(BF16)
        if i < parts - 1:
            scatters_b.append(
                remote(own.at[i, :, split:], dp_in_b.at[i], dp_send_b.at[i], dp_recv_b.at[i], dp_peers[i])
            )
            scatters_b[i].start()
        outs.append([
            remote(
                own.at[i, :, cols(chip_at(k))], chips_in.at[k - 1, i], out_send.at[k - 1, i], out_recv.at[k - 1, i],
                chip_peers[k - 1],
            )
            for k in range(1, chips)
        ])
        for copy in outs[i]:
            copy.start()
    tokens_load.wait()
    for image in range(token_ins.shape[0]):
        token_outs[:, image, :] = token_ins[image]
    tokens_store.start()
    value = own[parts - 1, :, split:].astype(F32)
    for i in range(parts - 1):
        scatters_b[i].wait_recv()
        value = value + dp_in_b[i].astype(F32)
    total_b[...] = value.astype(BF16)
    outs_b = [
        remote(
            total_b.at[:, cols_b(chip_at(k), 0)], chips_in_b.at[k - 1], out_send_b.at[k - 1], out_recv_b.at[k - 1],
            chip_peers[k - 1],
        )
        for k in range(1, chips)
    ]
    for copy in outs_b:
        copy.start()
    scatters = []
    for i in range(parts):
        value = own[i, :, cols(chip)].astype(F32)
        for k in range(1, chips):
            outs[i][k - 1].wait_recv()
            value = value + chips_in[k - 1, i].astype(F32)
        if i < parts - 1:
            total[i] = value.astype(BF16)
            scatters.append(remote(total.at[i], dp_in.at[i], dp_send.at[i], dp_recv.at[i], dp_peers[i]))
            scatters[i].start()
        else:
            kept = value
    value = total_b[:, cols_b(chip, 0)].astype(F32)
    for k in range(1, chips):
        outs_b[k - 1].wait_recv()
        value = value + chips_in_b[k - 1].astype(F32)
    final[mine, cols_b(chip, split)] = value.astype(BF16)
    for i in range(parts - 1):
        scatters[i].wait_recv()
        kept = kept + dp_in[i].astype(F32)
    final[mine, cols(chip)] = kept.astype(BF16)

    def places(number):
        return [final.at[mine, cols(number)], final.at[mine, cols_b(number, split)]]

    backs, hands = [], []
    for n, place in enumerate(places(chip)):
        for k in range(1, chips):
            backs.append(remote(place, place, back_send.at[n, k - 1], back_recv.at[n, k - 1], chip_peers[k - 1]))
            backs[-1].start()
        hands.append(remote(place, place, pass_send.at[n, 0], pass_recv.at[n, 0], sibling))
        hands[-1].start()
    for k in range(1, chips):
        for n, place in enumerate(places(chip_at(-k))):
            backs[n * (chips - 1) + k - 1].wait_recv()
            hands.append(remote(place, place, pass_send.at[n, k], pass_recv.at[n, k], sibling))
            hands[-1].start()
    for copy in pairs + [copy for group in outs for copy in group] + outs_b + scatters + scatters_b + backs:
        copy.wait_send()
    for copy in hands + [tokens_store]:
        copy.wait()


def settle(grads, tokens, chips, number):
    parts, share, columns = grads.shape
    half = share // 2
    images, length, width = tokens.shape
    halves = pltpu.VMEM((parts, half, columns), BF16)
    wide, narrow = settle_widths(columns, chips)
    dp_in = pltpu.VMEM((parts - 1, half, wide), BF16)
    rest = chips * narrow
    sems = [(parts,)] * 3 + [(chips - 1, parts)] * 2 + [(parts - 1,)] * 2
    sems += [(chips - 1,)] * 2 + [(parts - 1,)] * 2 + [(2, chips - 1)] * 2 + [(2, chips)] * 2
    return expert_call(
        settle_kernel, [(grads, False), (tokens, False)],
        [((share, columns), BF16, True), ((length, images, width), F32, False)],
        [
            halves, halves, dp_in, pltpu.VMEM((chips - 1, parts, half, wide), BF16), dp_in,
            pltpu.VMEM((half, rest), BF16), pltpu.VMEM((chips - 1, half, narrow), BF16),
            pltpu.VMEM((parts - 1, half, rest), BF16),
        ] + [pltpu.SemaphoreType.DMA(n) for n in sems] + [
            pltpu.VMEM((images, length, width), F32), pltpu.VMEM((length, images, width), F32),
            pltpu.SemaphoreType.DMA, pltpu.SemaphoreType.DMA,
        ],
        number,
    )


def unpack_kernel(*refs):
    count = 2 * LAYERS
    firsts, seconds, both, miscs = refs[:count], refs[count : 2 * count], refs[2 * count : 2 * count + 2], refs[2 * count + 2 : 2 * count + 4]
    refs = refs[2 * count + 4 :]
    squares, router, vectors, (inner, outer) = refs[:4], refs[4], refs[5:12], refs[12:]
    width = squares[0].shape[2]
    for layer in range(LAYERS):
        for n in range(4):
            squares[n][layer] = both[layer][:, n * width : (n + 1) * width].astype(F32)
        for j in range(2):
            first = firsts[2 * layer + j]
            for f in range(first.shape[0]):
                inner[layer, j, :, f * FF_BLOCK : (f + 1) * FF_BLOCK] = first[f].astype(F32)
            outer[layer, j] = seconds[2 * layer + j][...].astype(F32)

    @pl.when(pl.program_id(0) == 0)
    def _():
        for layer in range(LAYERS):
            turned = miscs[layer][...].astype(F32).T
            router[layer] = turned[: router.shape[1], :]
            for n in range(7):
                vectors[n][layer : layer + 1, :] = turned[VEC_AT + n : VEC_AT + n + 1, :]


def unpack(pieces, both, local, ff, experts_all):
    layers, (share, columns) = len(both), both[0].shape
    rows, width = pieces[0].shape
    take = rows // 2
    blocks = ff // FF_BLOCK
    steps = max(1, share // 32)
    part = share // steps
    firsts = pl.BlockSpec((None, blocks, part, width), lambda i: (0, 0, i, 0))
    seconds = pl.BlockSpec((None, take // steps, width), lambda i: (1, i, 0))
    some = lambda rows, *rest: ((layers, *rest[:-1], rows, rest[-1]), F32, pl.BlockSpec(
        (layers, *rest[:-1], rows // steps, rest[-1]), lambda i: (0,) * len(rest) + (i, 0)
    ))
    return call(
        unpack_kernel, (steps,),
        [(p.reshape(2, blocks, share, width), firsts) for p in pieces]
        + [(p.reshape(2, take, width), seconds) for p in pieces]
        + [(a, pl.BlockSpec((part, columns), lambda i: (i, 0))) for a in both]
        + [(a, pl.BlockSpec((share, MISC), lambda i: (0, 4 * width // MISC))) for a in both],
        [some(share, width)] * 4
        + [((layers, experts_all, share), F32, pl.BlockSpec((layers, experts_all, share), lambda i: (0, 0, 0)))]
        + [((layers, share), F32, pl.BlockSpec((layers, share), lambda i: (0, 0)))] * 7
        + [some(share, local, ff), some(take, local, width)],
    )


def shards(
    images, cotangent, routes, query_weight, key_weight, value_weight, output_weight, router_weight, query_bias,
    value_bias, output_bias, attend_gain, attend_shift, expert_gain, expert_shift, inner_weight, inner_bias,
    outer_weight, outer_bias,
):
    count, length, width = images.shape
    parts = lax.axis_size("dp")
    owners = lax.axis_size("expert")
    experts_all = router_weight.shape[2]
    local = inner_weight.shape[1]
    ff = inner_weight.shape[3]
    share = width // parts
    tokens = count * length
    squares = (query_weight, key_weight, value_weight, output_weight)
    vectors = (query_bias, value_bias, output_bias, attend_gain, attend_shift, expert_gain, expert_shift)
    columns = -(-(4 * width + MISC) // (MISC * (owners // 2))) * MISC * (owners // 2)

    first = inner_weight[0, 0].reshape(share, ff // FF_BLOCK, FF_BLOCK)
    first = jnp.transpose(first, (1, 0, 2)).reshape(ff // parts, width).astype(BF16)
    firsts = [lax.all_gather(first, "dp", axis=0, tiled=False)]
    dense, above, expert_biases, dcol, drow, capacity, (images, cotangent), mine = prepare(
        squares, router_weight, vectors, inner_bias, outer_bias, routes, (images, cotangent), (inner_weight, outer_weight),
        parts, owners, 2 * LAYERS,
    )
    packed = [dense]
    slots = experts_all * capacity

    saved = []
    back = None
    rows = images
    for layer in range(LAYERS):
        weights = [(packed[layer], s) for s in packed_specs(packed[layer])]
        routing = [(routes, per_layer(routes, layer))]
        outputs = attend_outputs(count, length, width)
        if layer == 0:
            done = call(
                first_kernel, (count,), [(rows, per_image(rows))] + routing + weights, outputs
            )
        else:
            before = saved[-1]
            done = call(
                next_kernel, (count,),
                [
                    (before["middle"], per_image(before["middle"])),
                    (before["gates"], per_image(before["gates"])),
                    (picked, per_layer(picked, 0)),
                    (picked, per_layer(picked, 1)),
                ] + routing + weights,
                [
                    images_out(count, length, width, F32),
                ] + outputs
            )
            rows, *done = done
        middle, queries, keys, values, context, sums, gates = done[:7]
        picked, arrived, g, s, outer, second, *following = expert_forward(
            done[7], drow, dcol, (local, owners, capacity, width), firsts[layer], mine, expert_biases,
            above if layer + 1 < LAYERS else None, layer,
        )
        if following:
            packed.append(following[0].reshape(width, following[0].shape[2]))
            firsts.append(following[1])
        saved.append({
            "rows": rows, "middle": middle, "attend": (queries, keys, values, context, sums), "gates": gates,
            "experts": (arrived, g, s), "weights": (firsts[layer], outer, second), "picked": picked,
        })

    last = saved[-1]
    result, dz, *sources = call(
        turn_kernel, (count,),
        [(last["middle"], per_image(last["middle"])), (last["gates"], per_image(last["gates"]))]
        + [(picked, per_layer(picked, k)) for k in range(2)]
        + [(cotangent, per_image(cotangent)), (routes, per_layer(routes, LAYERS - 1))],
        [((length, count, width), F32, pl.BlockSpec((length, count, width), lambda i: (0, 0, 0)))]
        + [images_out(count, length, MISC, BF16)]
        + [images_out(count, length, width, BF16)] * 2
    )
    upstream = cotangent
    bias_grads = [None] * LAYERS
    finished = []
    waiting = []
    wgrad = None
    for layer in reversed(range(LAYERS)):
        kept = saved[layer]
        came, shares, grads, *biases, above = expert_backward(
            sources, drow, dcol, kept["weights"], *kept["experts"], wgrad, layer
        )
        came = came[0]
        came, waiting = lax.optimization_barrier((came, waiting))
        finished += waiting
        waiting = [shares, lax.psum_scatter(grads, "dp", scatter_dimension=0, tiled=False)]
        bias_grads[layer] = biases
        weights = [(packed[layer], s) for s in packed_specs(packed[layer])]
        inputs = [upstream, kept["rows"], kept["middle"], *kept["attend"], dz]
        inputs = [(a, per_image(a)) for a in inputs]
        inputs += [(came, per_image(came))] + weights
        outputs = [
            images_out(count, length, width, F32),
            (
                (width, columns), BF16,
                pl.BlockSpec((width, columns), lambda i: (0, 0)),
            ),
        ]
        if layer > 0:
            below = saved[layer - 1]
            inputs += [(below["picked"], per_layer(below["picked"], k)) for k in range(2)]
            inputs.append((below["gates"], per_image(below["gates"])))
            inputs.append((routes, per_layer(routes, layer - 1)))
            outputs += [images_out(count, length, MISC, BF16)] + [images_out(count, length, width, BF16)] * 2
        scratch = [pltpu.VMEM((width, 4 * width + MISC), F32), pltpu.VMEM((MISC, width), F32)]
        number = None
        if layer == 0:
            inputs.append((above, pl.BlockSpec(memory_space=pl.ANY)))
            outputs.append(((share, columns), BF16, pl.BlockSpec((share, columns), lambda i: (0, 0))))
            scratch += spread_scratch(share, columns, owners // 2)
            number = 2 * LAYERS + 2
        done = call(functools.partial(back_kernel, layer == 0), (count,), inputs, outputs, scratch, number)
        upstream, wgrad = done[:2]
        if layer > 0:
            dz, *sources = done[2:]
        wgrad = wgrad.reshape(parts, share, columns)
    lowest, upstream = settle(wgrad, upstream, owners // 2, 2 * LAYERS + 1)
    both = (lowest, done[2])
    pieces = [waiting[0], waiting[1][0], finished[0], finished[1][0]]
    *squares, router, v0, v1, v2, v3, v4, v5, v6, inner, outer = unpack(pieces, both, local, ff, experts_all)
    outer_bias_grad = jnp.stack([b[1] for b in bias_grads])
    return (
        jnp.transpose(result, (1, 0, 2)),
        jnp.transpose(upstream, (1, 0, 2)),
        *squares,
        jnp.transpose(router, (0, 2, 1)),
        v0, v1, v2, v3, v4, v5, v6,
        inner,
        jnp.stack([b[0] for b in bias_grads]),
        outer,
        lax.dynamic_slice_in_dim(outer_bias_grad, lax.axis_index("dp") * share, share, 2),
    )


def solution(mesh):
    both = P(("dp", "expert"), None, None)
    square = P(None, "dp", None)
    vector = P(None, "dp")
    matrix = P(None, "expert", "dp", None)
    bias = P(None, "expert", "dp")
    grads = (square,) * 5 + (vector,) * 7 + (matrix, bias, matrix, bias)
    return jax.shard_map(
        shards,
        mesh=mesh,
        in_specs=(both, both, P(None, ("dp", "expert"), None, None)) + grads,
        out_specs=(both, both) + grads,
        check_vma=False,
    )
```

```python
import functools

import jax
import jax.numpy as jnp
from jax import lax
from jax.experimental import pallas as pl
from jax.experimental.pallas import tpu as pltpu
from jax.sharding import PartitionSpec as P

HEADS = 8
HEAD_DIM = 64
LAYERS = 2
EPSILON = 1e-06
FACTOR = HEAD_DIM**-0.5
VEC_AT = 64
MISC = 128
FF_BLOCK = 512
COST = 1024
VMEM = 56 * 1024 * 1024

MESH = pl.DeviceIdType.MESH
F32 = jnp.float32
BF16 = jnp.bfloat16


def dot(a, b):
    return jnp.dot(a, b, preferred_element_type=F32)


def dot_nt(a, b):
    return lax.dot_general(a, b, (((1,), (1,)), ((), ())), preferred_element_type=F32)


def dot_tn(a, b):
    return lax.dot_general(a, b, (((0,), (0,)), ((), ())), preferred_element_type=F32)


def standardize(rows):
    mean_value = jnp.mean(rows, axis=-1, keepdims=True)
    centered = rows - mean_value
    variance = jnp.mean(centered * centered, axis=-1, keepdims=True)
    scale = lax.rsqrt(variance + EPSILON)
    return centered * scale, scale


def standardize_back(upstream, unit, scale, gain):
    along = upstream * gain
    inner = (
        along
        - jnp.mean(along, axis=-1, keepdims=True)
        - unit * jnp.mean(along * unit, axis=-1, keepdims=True)
    )
    return inner * scale


def vectors_of(misc_ref):
    turned = misc_ref[...].astype(F32).T
    return [turned[VEC_AT + n : VEC_AT + n + 1, :] for n in range(7)]


def lane_masks(length):
    lanes = lax.broadcasted_iota(jnp.int32, (length, 2 * HEAD_DIM), 1)
    return (lanes < HEAD_DIM).astype(F32).astype(BF16), (lanes >= HEAD_DIM).astype(F32).astype(BF16)


def attend_body(
    rows, routes_ref, wq, wk, wv, wo, misc,
    t_ref, q_ref, k_ref, v_ref, o_ref, lse_ref, gates_ref, hidden_ref,
):
    length = rows.shape[0]
    qb, vb, ob, again, ashift, egain, eshift = vectors_of(misc)
    unit, _ = standardize(rows)
    low = (unit * again + ashift).astype(BF16)
    queries = (dot(low, wq[...]) + qb).astype(BF16)
    keys = dot(low, wk[...]).astype(BF16)
    values = (dot(low, wv[...]) + vb).astype(BF16)
    q_ref[0] = queries
    k_ref[0] = keys
    v_ref[0] = values
    masks = lane_masks(length)
    lanes = lax.broadcasted_iota(jnp.int32, (length, MISC), 1)
    first_half = lax.broadcasted_iota(jnp.int32, (length, 2 * HEAD_DIM), 1) < HEAD_DIM
    sums = jnp.zeros((length, MISC), F32)
    for pair in range(HEADS // 2):
        cols = slice(pair * 2 * HEAD_DIM, (pair + 1) * 2 * HEAD_DIM)
        mixed = []
        for side in range(2):
            scores = dot_nt(queries[:, cols] * (masks[side] * FACTOR), keys[:, cols])
            highest = jnp.max(scores, axis=-1, keepdims=True)
            expo = jnp.exp(scores - highest)
            total = jnp.sum(expo, axis=-1, keepdims=True)
            attention = (expo * (1.0 / total)).astype(BF16)
            sums = jnp.where(lanes == 2 * pair + side, highest + jnp.log(total), sums)
            mixed.append(dot(attention, values[:, cols]))
        o_ref[0, :, cols] = jnp.where(first_half, mixed[0], mixed[1]).astype(BF16)
    lse_ref[0] = sums
    middle = rows + (dot(o_ref[0], wo[...]) + ob)
    t_ref[0] = middle
    unit_two, _ = standardize(middle)
    hidden = (unit_two * egain + eshift).astype(BF16)
    logits = dot(hidden, misc[...])
    pair_experts = routes_ref[0]
    zero = jnp.sum(jnp.where(lanes == pair_experts[:, 0:1], logits, 0.0), axis=-1, keepdims=True)
    one = jnp.sum(jnp.where(lanes == pair_experts[:, 1:2], logits, 0.0), axis=-1, keepdims=True)
    gate_zero = 1.0 / (1.0 + jnp.exp(one - zero))
    gate_one = 1.0 / (1.0 + jnp.exp(zero - one))
    gates_ref[0, :, 0:1] = gate_zero
    gates_ref[0, :, 1:2] = gate_one
    hidden_ref[0] = hidden


def combine(middle, gates_ref, zero_ref, one_ref):
    gates = gates_ref[0]
    zero, one = zero_ref[0].astype(F32), one_ref[0].astype(F32)
    return middle + (gates[:, 0:1] * zero + gates[:, 1:2] * one), zero, one


def grads_body(upstream, zero, one, gates_ref, routes_ref, dz_ref, zero_ref, one_ref):
    length = upstream.shape[0]
    gates = gates_ref[0]
    gate_zero, gate_one = gates[:, 0:1], gates[:, 1:2]
    grad_zero = jnp.sum(zero * upstream, axis=-1, keepdims=True)
    grad_one = jnp.sum(one * upstream, axis=-1, keepdims=True)
    along = gate_zero * grad_zero + gate_one * grad_one
    lanes = lax.broadcasted_iota(jnp.int32, (length, MISC), 1)
    pair_experts = routes_ref[0]
    dz = jnp.where(lanes == pair_experts[:, 0:1], gate_zero * (grad_zero - along), 0.0)
    dz = dz + jnp.where(lanes == pair_experts[:, 1:2], gate_one * (grad_one - along), 0.0)
    dz_ref[0] = dz.astype(BF16)
    zero_ref[0] = (gate_zero * upstream).astype(BF16)
    one_ref[0] = (gate_one * upstream).astype(BF16)


def first_kernel(rows, routes, wq, wk, wv, wo, misc, *outs):
    attend_body(rows[0], routes, wq, wk, wv, wo, misc, *outs)


def next_kernel(
    middle, gates, yzero, yone, routes, wq, wk, wv, wo, misc, rows_ref, *outs
):
    rows, _, _ = combine(middle[0], gates, yzero, yone)
    rows_ref[0] = rows
    attend_body(rows, routes, wq, wk, wv, wo, misc, *outs)


def turn_kernel(middle, gates, yzero, yone, cotangent, routes, result, dz, zero_ref, one_ref):
    rows, zero, one = combine(middle[0], gates, yzero, yone)
    for image in range(result.shape[1]):

        @pl.when(pl.program_id(0) == image)
        def _(image=image):
            result[:, image, :] = rows

    grads_body(cotangent[0], zero, one, gates, routes, dz, zero_ref, one_ref)


class Spread:
    def __init__(self, above, refs):
        self.own, self.chips_in, self.final, *sems = refs
        local, out_send, out_recv, back_send, back_recv, pass_send, pass_recv = sems
        half, columns = self.own.shape
        me = lax.axis_index("expert")
        core, chip = lax.rem(me, 2), me // 2
        self.chips = chips = self.chips_in.shape[0] + 1
        block = columns // chips
        sibling = {"expert": me + 1 - 2 * core}
        mine = pl.ds(pl.multiple_of(core * half, half), half)

        def chip_at(k):
            return lax.rem(chip + k + chips, chips)

        def cols(number):
            return pl.ds(pl.multiple_of(number * block, block), block)

        peers = [{"expert": 2 * chip_at(k) + core} for k in range(1, chips)]
        self.peers = [sibling] + peers
        self.keep = pltpu.make_async_copy(above, self.own, local)
        self.outs = [
            remote(
                self.own.at[:, cols(chip_at(k))], self.chips_in.at[k - 1], out_send.at[k - 1], out_recv.at[k - 1],
                peers[k - 1],
            )
            for k in range(1, chips)
        ]
        self.place = (mine, cols(chip))
        place = self.final.at[mine, cols(chip)]
        self.backs = [
            remote(place, place, back_send.at[k - 1], back_recv.at[k - 1], peers[k - 1]) for k in range(1, chips)
        ]
        self.hands = []
        for k in range(chips):
            place = self.final.at[mine, cols(chip_at(-k))]
            self.hands.append(remote(place, place, pass_send.at[k], pass_recv.at[k], sibling))

    def stage(self, number):
        if number == 0:
            greet_all(self.peers)
            self.keep.wait()
            for copy in self.outs:
                copy.start()
        elif number == 1:
            value = self.own[:, self.place[1]].astype(F32)
            for n, copy in enumerate(self.outs):
                copy.wait_recv()
                value = value + self.chips_in[n].astype(F32)
            self.final[self.place[0], self.place[1]] = value.astype(BF16)
            for copy in self.backs:
                copy.start()
        else:
            for copy in self.backs:
                copy.wait_recv()
            for copy in self.hands:
                copy.start()

    def finish(self, result):
        for copy in self.hands:
            copy.wait()
        for copy in self.outs + self.backs:
            copy.wait_send()
        result[...] = self.final[...]


def spread_scratch(share, columns, chips):
    half = share // 2
    half_rows = pltpu.VMEM((half, columns), BF16)
    sems = [()] + [(chips - 1,)] * 4 + [(chips,)] * 2
    return [
        half_rows, pltpu.VMEM((chips - 1, half, columns // chips), BF16), pltpu.VMEM((share, columns), BF16),
    ] + [pltpu.SemaphoreType.DMA(n) for n in sems]


def back_kernel(
    lowest, upstream, rows, middle, q_ref, k_ref, v_ref, o_ref, lse_ref, dz_ref, came,
    wq, wk, wv, wo, misc, *rest,
):
    if not lowest:
        yzero, yone, gates_below, routes_below, grad_ref, sent, dz_below, zero_ref, one_ref, wgrad, vgrad = rest
    else:
        above, grad_ref, sent, above_out, wgrad, vgrad, *spread_refs = rest
        spread = Spread(above, spread_refs)

        @pl.when(pl.program_id(0) == 0)
        def _():
            spread.keep.start()

    first = pl.program_id(0) == 0
    length = rows.shape[1]
    width = rows.shape[2]
    qb, vb, ob, again, ashift, egain, eshift = vectors_of(misc)

    @pl.when(first)
    def _():
        wgrad[...] = jnp.zeros_like(wgrad)
        vgrad[...] = jnp.zeros_like(vgrad)

    def add_vector(number, value):
        vgrad[VEC_AT + number : VEC_AT + number + 1, :] += jnp.sum(value, axis=0, keepdims=True)

    unit_two, scale_two = standardize(middle[0])
    hidden = (unit_two * egain + eshift).astype(BF16)
    dz = dz_ref[0]
    dhidden = dot_nt(dz, misc[...]) + came[0]
    wgrad[:, 4 * width :] += dot_tn(hidden, dz)
    add_vector(5, dhidden * unit_two)
    add_vector(6, dhidden)
    dmiddle = upstream[0] + standardize_back(dhidden, unit_two, scale_two, egain)
    dbranch = dmiddle.astype(BF16)
    wgrad[:, 3 * width : 4 * width] += dot_tn(o_ref[0], dbranch)
    add_vector(2, dbranch.astype(F32))
    dcontext = dot_nt(dbranch, wo[...]).astype(BF16)
    masks = lane_masks(length)
    first_half = lax.broadcasted_iota(jnp.int32, (length, 2 * HEAD_DIM), 1) < HEAD_DIM
    dqs, dks, dvs = [], [], []
    sums = lse_ref[0].T
    for pair in range(HEADS // 2):
        cols = slice(pair * 2 * HEAD_DIM, (pair + 1) * 2 * HEAD_DIM)
        keys = k_ref[0, :, cols]
        values = v_ref[0, :, cols]
        queries = q_ref[0, :, cols]
        dvalues, dqueries, dkeys = None, [], None
        for side in range(2):
            own_queries = queries * (masks[side] * FACTOR)
            own_context = dcontext[:, cols] * masks[side]
            scores = dot_nt(keys, own_queries)
            number = 2 * pair + side
            attention = jnp.exp(scores - sums[number : number + 1, :])
            prob = dot_nt(values, own_context)
            weighed = attention * prob
            delta = jnp.sum(weighed, axis=0, keepdims=True)
            dscores = (weighed - attention * delta).astype(BF16)
            dvalue = dot(attention.astype(BF16), own_context)
            dkey = dot(dscores, own_queries)
            dvalues = dvalue if dvalues is None else dvalues + dvalue
            dkeys = dkey if dkeys is None else dkeys + dkey
            dqueries.append(dot_tn(dscores, keys))
        dqs.append((jnp.where(first_half, dqueries[0], dqueries[1]) * FACTOR).astype(BF16))
        dks.append(dkeys.astype(BF16))
        dvs.append(dvalues.astype(BF16))
    dq = jnp.concatenate(dqs, axis=1)
    dk = jnp.concatenate(dks, axis=1)
    dv = jnp.concatenate(dvs, axis=1)
    unit, scale = standardize(rows[0])
    low = (unit * again + ashift).astype(BF16)
    wgrad[:, 0 : 3 * width] += dot_tn(low, jnp.concatenate([dq, dk, dv], axis=1))
    add_vector(0, dq.astype(F32))
    add_vector(1, dv.astype(F32))
    dlow = dot_nt(dq, wq[...]) + dot_nt(dk, wk[...]) + dot_nt(dv, wv[...])
    add_vector(3, dlow * unit)
    add_vector(4, dlow)
    grad = dmiddle + standardize_back(dlow, unit, scale, again)
    grad_ref[0] = grad
    if not lowest:
        grads_body(
            grad, yzero[0].astype(F32), yone[0].astype(F32), gates_below, routes_below, dz_below,
            zero_ref, one_ref,
        )

    if lowest:
        for number in range(3):

            @pl.when(pl.program_id(0) == number)
            def _(number=number):
                spread.stage(number)

    @pl.when(pl.program_id(0) == pl.num_programs(0) - 1)
    def _():
        wgrad[:, 4 * width :] += vgrad[...].T
        sent[:, : 4 * width + MISC] = wgrad[...].astype(BF16)
        sent[:, 4 * width + MISC :] = jnp.zeros((width, sent.shape[1] - 4 * width - MISC), BF16)
        if lowest:
            spread.finish(above_out)


def per_image(array):
    return pl.BlockSpec((1,) + array.shape[1:], lambda i: (i,) + (0,) * (len(array.shape) - 1))


def per_layer(array, layer):
    shape = (None, 1) + array.shape[2:]
    return pl.BlockSpec(shape, lambda i: (layer, i) + (0,) * (len(shape) - 2))


def whole(array):
    return pl.BlockSpec(array.shape, lambda i: (0,) * len(array.shape))


def packed_specs(packed):
    width = packed.shape[0]
    specs = [pl.BlockSpec((width, width), lambda i, n=n: (0, n)) for n in range(4)]
    return specs + [pl.BlockSpec((width, MISC), lambda i: (0, 4 * width // MISC))]


def call(body, grid, inputs, outputs, scratch=(), number=None):
    shapes = [jax.ShapeDtypeStruct(s, t) for s, t, _ in outputs]
    return pl.pallas_call(
        body,
        grid=grid,
        in_specs=[s for _, s in inputs],
        out_specs=[s for _, _, s in outputs],
        out_shape=shapes,
        scratch_shapes=list(scratch),
        compiler_params=pltpu.CompilerParams(
            vmem_limit_bytes=VMEM, collective_id=number, has_side_effects=number is not None
        ),
        cost_estimate=pl.CostEstimate(flops=COST, bytes_accessed=COST, transcendentals=0),
    )(*[a for a, _ in inputs])


def images_out(images, length, columns, kind):
    shape = (images, length, columns)
    return (shape, kind, pl.BlockSpec((1, length, columns), lambda i: (i, 0, 0)))


def attend_outputs(images, length, width):
    return [
        images_out(images, length, width, F32),
        images_out(images, length, width, BF16),
        images_out(images, length, width, BF16),
        images_out(images, length, width, BF16),
        images_out(images, length, width, BF16),
        images_out(images, length, MISC, F32),
        images_out(images, length, 2, F32),
        images_out(images, length, width, BF16),
    ]


def greet_all(peers):
    barrier = pltpu.get_barrier_semaphore()
    for peer in peers:
        pl.semaphore_signal(barrier, inc=1, device_id=peer, device_id_type=MESH)
    pl.semaphore_wait(barrier, len(peers))


def remote(source, target, send, recv, device):
    return pltpu.make_async_remote_copy(
        src_ref=source, dst_ref=target, send_sem=send, recv_sem=recv, device_id=device, device_id_type=MESH
    )


class SharedGather:
    def __init__(self, mine, out, sems):
        send, recv, pass_send, pass_recv, own = sems
        parts, share, _ = out.shape
        half = share // 2
        row, me = lax.axis_index("dp"), lax.axis_index("expert")
        core = lax.rem(me, 2)
        sibling = {"expert": me + 1 - 2 * core}
        rows = pl.ds(pl.multiple_of(core * half, half), half)
        self.fetches, self.hands = [], []
        for k in range(1, parts):
            peer = {"dp": lax.rem(row + k, parts)}
            self.fetches.append(remote(mine.at[rows], out.at[row, rows], send.at[k - 1], recv.at[k - 1], peer))
            place = out.at[lax.rem(row - k + parts, parts), rows]
            self.hands.append(remote(place, place, pass_send.at[k - 1], pass_recv.at[k - 1], sibling))
        self.keep = pltpu.make_async_copy(mine, out.at[row], own)

    def start(self):
        for copy in self.fetches:
            copy.start()
        self.keep.start()

    def finish(self):
        for fetch, hand in zip(self.fetches, self.hands):
            fetch.wait_recv()
            hand.start()
        for fetch, hand in zip(self.fetches, self.hands):
            fetch.wait_send()
            hand.wait()
        self.keep.wait()


class Gather:
    def __init__(self, parts, mine, place, sems):
        send, recv, own = sems
        row = lax.axis_index("dp")
        self.first, self.second = [], []
        self.keep = pltpu.make_async_copy(mine, place(row), own)

        def add(group, source, target, peer):
            n = len(self.first) + len(self.second)
            group.append(remote(source, target, send.at[n], recv.at[n], {"dp": peer}))

        if parts != 4:
            for k in range(1, parts):
                add(self.first, mine, place(row), lax.rem(row + k, parts))
            return
        near, far = row + 1 - 2 * lax.rem(row, 2), lax.rem(row + 2, 4)
        quarter = mine.shape[0] // 4
        halves = [[slice(n * quarter, (n + 1) * quarter) for n in pair] for pair in ((0, 1), (2, 3))]
        for rows, peer in ((halves[0], near), (halves[1], far)):
            for part in rows:
                add(self.first, mine.at[part], place(row).at[part], peer)
        for rows, peer, other in ((halves[0], far, near), (halves[1], near, far)):
            for part in rows:
                add(self.second, mine.at[part], place(row).at[part], peer)
            for part in rows:
                add(self.second, place(other).at[part], place(other).at[part], peer)

    def start(self):
        for copy in self.first:
            copy.start()
        self.keep.start()

    def forward(self):
        for copy in self.first:
            copy.wait_recv()
        for copy in self.second:
            copy.start()

    def finish(self):
        for copy in self.second:
            copy.wait_recv()
        self.keep.wait()

    def drain(self):
        for copy in self.first + self.second:
            copy.wait_send()


def gather_sems(parts):
    count = 12 if parts == 4 else parts - 1
    return [pltpu.SemaphoreType.DMA((count,)), pltpu.SemaphoreType.DMA((count,)), pltpu.SemaphoreType.DMA]


def shared_sems(parts):
    return [pltpu.SemaphoreType.DMA((parts - 1,))] * 4 + [pltpu.SemaphoreType.DMA]


ROOT_HALF = 0.7071067811865476
ROOT_TWO_PI_INVERSE = 0.3989422804014327

class Swap:
    def __init__(self, sent, arrived, made, back, sems):
        self.sent, self.arrived, self.made, self.back = sent, arrived, made, back
        self.out_send, self.out_recv, self.home_send, self.home_recv, self.own = sems
        self.local, self.count = arrived.shape[0], arrived.shape[1]
        self.me = lax.axis_index("expert")

    def greet(self, others=()):
        greet_all([{"expert": lax.rem(self.me + k, self.count)} for k in range(1, self.count)] + list(others))

    def outward(self, j, k, peer):
        return pltpu.make_async_remote_copy(
            src_ref=self.sent.at[j, peer], dst_ref=self.arrived.at[j, self.me],
            send_sem=self.out_send.at[j, k], recv_sem=self.out_recv.at[j, k],
            device_id={"expert": peer}, device_id_type=MESH,
        )

    def homeward(self, j, k, peer):
        return pltpu.make_async_remote_copy(
            src_ref=self.made.at[j, peer], dst_ref=self.back.at[j, self.me],
            send_sem=self.home_send.at[j, k], recv_sem=self.home_recv.at[j, k],
            device_id={"expert": peer}, device_id_type=MESH,
        )

    def own_out(self, j):
        return pltpu.make_async_copy(self.sent.at[j, self.me], self.arrived.at[j, self.me], self.own.at[j])

    def own_home(self, j):
        return pltpu.make_async_copy(self.made.at[j, self.me], self.back.at[j, self.me], self.own.at[self.local + j])

    def send_all(self, sources, drow, layer):
        chips = self.count // 2
        capacity, width = self.sent.shape[2:]
        images, length, _ = sources[0].shape

        for j in range(self.local):

            def fill(turn, carry, j=j):
                sign = 2 * lax.rem(turn, 2) - 1
                chip = lax.rem(self.me // 2 + chips // 2 + sign * ((turn + 1) // 2) + chips, chips)
                first = (j * self.count + 2 * chip) * capacity
                slots = lax.broadcasted_iota(jnp.int32, (2 * capacity, length), 0) + first
                total = jnp.zeros((2 * capacity, width), F32)
                for image in range(images):
                    dest = drow[layer, image]
                    hits = [slots == dest[0:1, :], slots == dest[1:2, :]]
                    if len(sources) == 1:
                        hits = [hits[0] | hits[1]]
                    for hit, source in zip(hits, sources):
                        total = total + dot(hit.astype(F32).astype(BF16), source[image])
                self.sent[j, pl.ds(2 * chip, 2)] = total.astype(BF16).reshape(2, capacity, width)
                for core in range(2):
                    peer = 2 * chip + core
                    k = lax.rem(peer - self.me + self.count, self.count)

                    @pl.when(peer != self.me)
                    def _(k=k, peer=peer):
                        self.outward(j, k, peer).start()

                    @pl.when(peer == self.me)
                    def _():
                        self.own_out(j).start()

                return carry

            lax.fori_loop(0, chips, fill, 0)

    def chip(self, turn):
        chips = self.count // 2
        return lax.rem(self.me // 2 - turn + chips, chips)

    def wait_chip(self, j, chip):
        for core in range(2):
            source = 2 * chip + core
            k = lax.rem(self.me - source + self.count, self.count)

            @pl.when(source != self.me)
            def _(k=k, source=source):
                pltpu.make_async_remote_copy(
                    src_ref=self.arrived.at[j, source], dst_ref=self.arrived.at[j, source],
                    send_sem=self.out_send.at[j, k], recv_sem=self.out_recv.at[j, k],
                    device_id={"expert": source}, device_id_type=MESH,
                ).wait_recv()

            @pl.when(source == self.me)
            def _():
                self.own_out(j).wait()

    def send_home(self, j, chip):
        for core in range(2):
            peer = 2 * chip + core
            k = lax.rem(peer - self.me + self.count, self.count)

            @pl.when(peer != self.me)
            def _(k=k, peer=peer):
                self.homeward(j, k, peer).start()

            @pl.when(peer == self.me)
            def _():
                self.own_home(j).start()

    def wait_home(self, j, chip):
        for core in range(2):
            source = 2 * chip + core
            k = lax.rem(self.me - source + self.count, self.count)

            @pl.when(source != self.me)
            def _(k=k, source=source):
                place = self.back.at[j, source]
                remote(place, place, self.home_send.at[j, k], self.home_recv.at[j, k], {"expert": source}).wait_recv()

            @pl.when(source == self.me)
            def _():
                self.own_home(j).wait()

    def take_home(self, dcol, layer, total):
        count, images, length, width = total.shape
        capacity = self.back.shape[2]
        total[...] = jnp.zeros_like(total)
        for j in range(self.local):

            def step(turn, carry, j=j):
                chip = self.chip(turn)
                self.wait_home(j, chip)
                rows = self.back[j, pl.ds(2 * chip, 2)].reshape(2 * capacity, width)
                first = (j * self.count + 2 * chip) * capacity
                lanes = lax.broadcasted_iota(jnp.int32, (length, 2 * capacity), 1) + first
                for image in range(images):
                    dest = dcol[layer, image]
                    hits = [dest[:, 0:1] == lanes, dest[:, 1:2] == lanes]
                    if count == 1:
                        hits = [hits[0] | hits[1]]
                    for k, hit in enumerate(hits):
                        total[k, image] += dot(hit.astype(F32).astype(BF16), rows).astype(total.dtype)
                return carry

            lax.fori_loop(0, self.count // 2, step, 0)

    def finish(self):
        for j in range(self.local):
            for k in range(1, self.count):
                peer = lax.rem(self.me + k, self.count)
                self.outward(j, k, peer).wait_send()
                self.homeward(j, k, peer).wait_send()


def weight_blocks(weights, j, f):
    _, parts, rows, width = weights.shape
    share, take = width // parts, rows // 2
    each = FF_BLOCK // take
    first = weights[j, :, f * share : (f + 1) * share, :].reshape(width, width)
    second = weights[j, f * each : (f + 1) * each, take:, :].reshape(FF_BLOCK, width)
    return first, second


def expert_kernel(layer, with_dense, *refs):
    if with_dense:
        *refs, n1, n2, n3, n4, n5, m1, m2, m3 = refs
        refs = list(refs)
        dense_in, dense_out, next_out = refs.pop(7), refs.pop(13), refs.pop(13)
        dense = SharedGather(dense_in, dense_out, (n1, n2, n3, n4, n5))
        next_in = refs[4].at[layer + 1, 0, : next_out.shape[1]]
        following = Gather(dense_out.shape[0], next_in, lambda p: next_out.at[p], (m1, m2, m3))
    (
        hidden, drow, dcol, inner_first, shares, b1, b2, picked, arrived_out, g_out, s_out, outer_out, packed_out,
        back, sent, arrived, made, weights, g_stage, s_stage, out_send, out_recv, home_send, home_recv, own, load, stores, last,
        *gather_refs,
    ) = refs
    row = lax.axis_index("dp")
    parts = weights.shape[1]
    take = weights.shape[2] // 2
    mine = shares.at[layer, 1]
    gathers = [
        Gather(parts, shares.at[layer, 0, take:], lambda p: weights.at[0, p, take:], gather_refs[:3]),
        Gather(parts, mine, lambda p: weights.at[1, p], gather_refs[3:]),
    ]
    swap = Swap(sent, arrived, made, back, (out_send, out_recv, home_send, home_recv, own))
    local, count, capacity, width = arrived.shape
    chips = count // 2
    rows = 2 * capacity
    ff = g_out.shape[2]
    first_load = pltpu.make_async_copy(inner_first, weights.at[0, :, :take], load)
    first_load.start()
    swap.greet([{"dp": lax.rem(row + k, parts)} for k in range(1, parts)])
    gathers[0].start()
    swap.send_all([hidden], drow, layer)
    gathers[0].forward()
    gathers[1].start()
    gathered = [
        pltpu.make_async_copy(weights.at[0, :, take:], outer_out, last.at[1]),
        pltpu.make_async_copy(weights.at[1], packed_out, last.at[2]),
    ]

    def kept(j, slot, chip):
        place = pl.ds(pl.multiple_of(chip * rows, rows), rows)
        return (
            pltpu.make_async_copy(g_stage.at[slot], g_out.at[j, place, :], stores.at[0, slot]),
            pltpu.make_async_copy(s_stage.at[slot], s_out.at[j, place, :], stores.at[1, slot]),
        )

    for j in range(local):
        if j == 0:
            first_load.wait()
        gathers[j].finish()
        gathered[j].start()
        if j == 1 and with_dense:
            following.start()
        number = layer * local + j

        def chip_step(turn, carry, j=j, number=number):
            chip = swap.chip(turn)
            slot = lax.rem(turn, 2)
            swap.wait_chip(j, chip)
            if j == 0:

                @pl.when(turn == 1)
                def _():
                    gathers[1].forward()
                    if with_dense:
                        dense.start()

            if j == 1 and with_dense:

                @pl.when(turn == 2)
                def _():
                    following.forward()

            @pl.when(j * chips + turn >= 2)
            def _():
                for copy in kept(j, slot, chip):
                    copy.wait()

            x = arrived[j, pl.ds(2 * chip, 2)].reshape(rows, width)
            total = jnp.broadcast_to(b2[number : number + 1, :], (rows, width))
            for f in range(ff // FF_BLOCK):
                cols = slice(f * FF_BLOCK, (f + 1) * FF_BLOCK)
                first, second = weight_blocks(weights, j, f)
                inner = dot(x, first) + b1[number : number + 1, cols]
                normal = 0.5 * (1.0 + lax.erf(inner * ROOT_HALF))
                g = (inner * normal).astype(BF16)
                density = jnp.exp(-0.5 * inner * inner) * ROOT_TWO_PI_INVERSE
                g_stage[slot, :, cols] = g
                s_stage[slot, :, cols] = (normal + inner * density).astype(BF16)
                total = total + dot(g, second)
            made[j, pl.ds(2 * chip, 2)] = total.astype(BF16).reshape(2, capacity, width)
            swap.send_home(j, chip)
            for copy in kept(j, slot, chip):
                copy.start()
            return carry

        lax.fori_loop(0, chips, chip_step, 0)
    final = pltpu.make_async_copy(arrived, arrived_out, last.at[0])
    final.start()
    if with_dense:
        dense.finish()
        following.finish()
        following.drain()
    for slot in range(2):
        for copy in kept(0, slot, 0):
            copy.wait()
    swap.take_home(dcol, layer, picked)
    swap.finish()
    for gather, copy in zip(gathers, gathered):
        gather.drain()
        copy.wait()
    final.wait()


def expert_back_kernel(layer, with_above, *refs):
    if with_above:
        *refs, above_in, above_own, above_paired, above_send, above_recv, above_load, pair_send, pair_recv = refs
        refs = list(refs)
        above, above_sum = refs.pop(10), refs.pop(15)
    (
        zero, one, drow, dcol, inner_first, outer_first, packed_second, arrived_x, g_in, s_in,
        came, summed, out, bias1, bias2, back, sent, arrived, made, weights, x, du, s_stage, g_stage, first_stage, second_stage, share_out, share_in,
        db1, db2, db1_in, db2_in,
        out_send, out_recv, home_send, home_recv, own, load, fetch, stores, share_send, share_recv,
        bias_send, bias_recv,
    ) = refs
    swap = Swap(sent, arrived, made, back, (out_send, out_recv, home_send, home_recv, own))
    row = lax.axis_index("dp")
    local, count, capacity, width = arrived.shape
    chips = count // 2
    rows = 2 * capacity
    ff = g_in.shape[2]
    blocks = ff // FF_BLOCK
    _, parts, all_rows, _ = weights.shape
    share, take = width // parts, all_rows // 2
    each = FF_BLOCK // take
    loads = [
        pltpu.make_async_copy(inner_first, weights.at[0, :, :take], load.at[0]),
        pltpu.make_async_copy(packed_second, weights.at[1], load.at[1]),
        pltpu.make_async_copy(arrived_x, x, load.at[local]),
        pltpu.make_async_copy(outer_first, weights.at[0, :, take:], load.at[local + 1]),
    ]
    for copy in loads:
        copy.start()

    def slopes(j, turn):
        slot = lax.rem(turn, 2)
        place = pl.ds(pl.multiple_of(swap.chip(turn) * rows, rows), rows)
        return pltpu.make_async_copy(s_in.at[j, place, :], s_stage.at[slot], fetch.at[0, slot])

    def activations(j, f):
        return pltpu.make_async_copy(
            g_in.at[j, :, f * FF_BLOCK : (f + 1) * FF_BLOCK], g_stage.at[f % 2], fetch.at[1, f % 2]
        )

    def results(j, f):
        return (
            pltpu.make_async_copy(
                first_stage.at[f % 2], out.at[:, j - 1, f * share : (f + 1) * share, :], stores.at[0, f % 2]
            ),
            pltpu.make_async_copy(
                second_stage.at[f % 2], out.at[f * each : (f + 1) * each, j - 1, take:, :], stores.at[1, f % 2]
            ),
        )

    def share_copy(k):
        peer = lax.rem(row + k, parts)
        return pltpu.make_async_remote_copy(
            src_ref=share_out.at[peer], dst_ref=share_in.at[k - 1],
            send_sem=share_send.at[k - 1], recv_sem=share_recv.at[k - 1],
            device_id={"dp": peer}, device_id_type=MESH,
        )

    slopes(0, 0).start()
    peers = [{"dp": lax.rem(row + k, parts)} for k in range(1, parts)]
    swap.greet(peers)
    if with_above:
        core = lax.rem(swap.me, 2)
        half = above_own.shape[1]
        mine = pl.ds(pl.multiple_of(core * half, half), half)
        other = pl.ds(pl.multiple_of((1 - core) * half, half), half)
        pair = remote(above.at[:, other], above_paired, pair_send, pair_recv, {"expert": swap.me + 1 - 2 * core})
        keep = pltpu.make_async_copy(above.at[:, mine], above_own, above_load)
        pair.start()
        keep.start()
        above_copies = [
            remote(
                above_own.at[lax.rem(row + k, parts)], above_in.at[k - 1], above_send.at[k - 1], above_recv.at[k - 1],
                peers[k - 1],
            )
            for k in range(1, parts)
        ]
    swap.send_all([zero, one], drow, layer)
    if with_above:
        pair.wait_recv()
        keep.wait()
        for part in range(parts):
            above_own[part] = (above_own[part].astype(F32) + above_paired[part].astype(F32)).astype(BF16)
        for copy in above_copies:
            copy.start()
    loads[local + 1].wait()
    for j in range(local):
        loads[j].wait()
        activations(j, 0).start()

        def chip_step(turn, carry, j=j):
            chip = swap.chip(turn)
            slot = lax.rem(turn, 2)

            @pl.when(turn + 1 < chips)
            def _():
                slopes(j, turn + 1).start()

            swap.wait_chip(j, chip)
            slopes(j, turn).wait()
            dy = arrived[j, pl.ds(2 * chip, 2)].reshape(rows, width)
            place = pl.ds(pl.multiple_of(chip * rows, rows), rows)
            total = jnp.zeros((rows, width), F32)
            for f in range(blocks):
                cols = slice(f * FF_BLOCK, (f + 1) * FF_BLOCK)
                first, second = weight_blocks(weights, j, f)
                part = (dot_nt(dy, second) * s_stage[slot, :, cols].astype(F32)).astype(BF16)
                du[place, cols] = part
                total = total + dot_nt(part, first)
            made[j, pl.ds(2 * chip, 2)] = total.astype(BF16).reshape(2, capacity, width)
            swap.send_home(j, chip)
            return carry

        lax.fori_loop(0, chips, chip_step, 0)
        if j + 1 < local:
            slopes(j + 1, 0).start()
        if j == 0:
            loads[local].wait()
        dy = arrived[j].reshape(count * capacity, width)
        db2[j : j + 1, :] = jnp.sum(dy.astype(F32), axis=0, keepdims=True)
        for f in range(blocks):
            cols = slice(f * FF_BLOCK, (f + 1) * FF_BLOCK)
            if f + 1 < blocks:
                activations(j, f + 1).start()
            if j > 1 or (j == 1 and f > 1):
                for copy in results(j, f):
                    copy.wait()
            part = du[:, cols]
            grad = dot_tn(x[j].reshape(count * capacity, width), part).astype(BF16)
            if j == 0:
                share_out[:, f * share : (f + 1) * share, :] = grad.reshape(parts, share, width)
            else:
                first_stage[f % 2] = grad.reshape(parts, share, width)
            db1[j : j + 1, cols] = jnp.sum(part.astype(F32), axis=0, keepdims=True)
            activations(j, f).wait()
            grad = dot_tn(g_stage[f % 2], dy).astype(BF16).reshape(each, take, width)
            if j == 0:
                share_out[f * each : (f + 1) * each, take:, :] = grad
            else:
                second_stage[f % 2] = grad
                for copy in results(j, f):
                    copy.start()
        if j == 0:
            for k in range(1, parts):
                share_copy(k).start()
    part_ff = ff // parts
    bias_copies = []
    for k in range(1, parts):
        place = pl.ds(pl.multiple_of(lax.rem(row + k, parts) * part_ff, part_ff), part_ff)
        for n, (source, target) in enumerate(((db1.at[:, place], db1_in.at[k - 1]), (db2, db2_in.at[k - 1]))):
            bias_copies.append(pltpu.make_async_remote_copy(
                src_ref=source, dst_ref=target, send_sem=bias_send.at[n, k - 1], recv_sem=bias_recv.at[n, k - 1],
                device_id=peers[k - 1], device_id_type=MESH,
            ))
            bias_copies[-1].start()
    if with_above:
        for copy in above_copies:
            copy.wait_recv()
        total = above_own[row].astype(F32)
        for k in range(1, parts):
            total = total + above_in[k - 1].astype(F32)
        above_sum[...] = total.astype(BF16)
    for k in range(1, parts):
        share_copy(k).wait_recv()
    step = 64

    def add_up(turn, carry):
        place = pl.ds(pl.multiple_of(turn * step, step), step)
        total = share_out[row, place, :].astype(F32)
        for k in range(1, parts):
            total = total + share_in[k - 1, place, :].astype(F32)
        summed[place, :] = total.astype(BF16)
        return carry

    lax.fori_loop(0, all_rows // step, add_up, 0)
    for copy in bias_copies:
        copy.wait_recv()
    total1, total2 = db1[:, pl.ds(pl.multiple_of(row * part_ff, part_ff), part_ff)], db2[...]
    for k in range(1, parts):
        total1, total2 = total1 + db1_in[k - 1], total2 + db2_in[k - 1]
    bias1[...], bias2[...] = total1, total2
    swap.take_home(dcol, layer, came)
    if with_above:
        for copy in above_copies + [pair]:
            copy.wait_send()
    for copy in bias_copies:
        copy.wait_send()
    for k in range(1, parts):
        share_copy(k).wait_send()
    for f in range(2):
        for copy in results(1, f):
            copy.wait()
    swap.finish()


def swap_sems(local, count):
    pairs = [pltpu.SemaphoreType.DMA((local, count))] * 4
    return pairs + [pltpu.SemaphoreType.DMA((2 * local,))]


def expert_call(body, inputs, outputs, scratch, number):
    def spec(held):
        return pl.BlockSpec(memory_space=pltpu.VMEM if held else pl.ANY)

    shapes = [jax.ShapeDtypeStruct(s, t) for s, t, _ in outputs]
    return pl.pallas_call(
        body,
        in_specs=[spec(held) for _, held in inputs],
        out_specs=[spec(held) for _, _, held in outputs],
        out_shape=shapes,
        scratch_shapes=scratch,
        compiler_params=pltpu.CompilerParams(
            collective_id=number, has_side_effects=True, vmem_limit_bytes=VMEM
        ),
        cost_estimate=pl.CostEstimate(flops=COST, bytes_accessed=COST, transcendentals=0),
    )(*[a for a, _ in inputs])


def expert_forward(hidden, drow, dcol, shape, inner, shares, biases, following, layer):
    b1, b2 = biases
    local, count, capacity, width = shape
    ff = b1.shape[1]
    rows = 2 * capacity
    parts = inner.shape[0]
    packed = (parts, *shares.shape[2:])
    half = (parts, shares.shape[2] // 2, width)
    slots = (local, count * capacity, ff)
    inputs = [(hidden, True), (drow, True), (dcol, True), (inner, False), (shares, False), (b1, True), (b2, True)]
    outputs = [
        ((2, *hidden.shape), BF16, True), (shape, BF16, False), (slots, BF16, False), (slots, BF16, False),
        (half, BF16, False), (packed, BF16, False),
    ]
    scratch = [
        pltpu.VMEM(shape, BF16), pltpu.VMEM(shape, BF16), pltpu.VMEM(shape, BF16), pltpu.VMEM(shape, BF16),
        pltpu.VMEM((local, *packed), BF16),
        pltpu.VMEM((2, rows, ff), BF16), pltpu.VMEM((2, rows, ff), BF16),
    ] + swap_sems(local, count) + [
        pltpu.SemaphoreType.DMA, pltpu.SemaphoreType.DMA((2, 2)), pltpu.SemaphoreType.DMA((3,)),
    ] + gather_sems(parts) * 2
    if following is not None:
        inputs.append((following, False))
        outputs += [((parts, *following.shape), BF16, False), (half, BF16, False)]
        scratch += shared_sems(parts) + gather_sems(parts)
    return expert_call(functools.partial(expert_kernel, layer, following is not None), inputs, outputs, scratch, layer)


def expert_backward(sources, drow, dcol, weights, arrived, g, s, above, layer):
    shape = arrived.shape
    local, count, capacity, width = shape
    ff = g.shape[2]
    rows = 2 * capacity
    parts, all_rows, _ = weights[2].shape
    share, take = width // parts, all_rows // 2
    inputs = [(a, True) for a in (*sources, drow, dcol)] + [(a, False) for a in (*weights, arrived, g, s)]
    outputs = [
        ((1, *sources[0].shape), F32, True), ((all_rows, width), BF16, True), ((parts, local - 1, all_rows, width), BF16, False),
        ((local, ff // parts), F32, True), ((local, width), F32, True),
    ]
    scratch = [
        pltpu.VMEM(shape, BF16), pltpu.VMEM(shape, BF16), pltpu.VMEM(shape, BF16), pltpu.VMEM(shape, BF16),
        pltpu.VMEM((local, parts, all_rows, width), BF16), pltpu.VMEM(shape, BF16),
        pltpu.VMEM((count * capacity, ff), BF16), pltpu.VMEM((2, rows, ff), BF16),
        pltpu.VMEM((2, count * capacity, FF_BLOCK), BF16), pltpu.VMEM((2, parts, share, width), BF16),
        pltpu.VMEM((2, FF_BLOCK // take, take, width), BF16),
        pltpu.VMEM((parts, all_rows, width), BF16), pltpu.VMEM((parts - 1, all_rows, width), BF16),
        pltpu.VMEM((local, ff), F32), pltpu.VMEM((local, width), F32),
        pltpu.VMEM((parts - 1, local, ff // parts), F32), pltpu.VMEM((parts - 1, local, width), F32),
    ] + swap_sems(local, count) + [
        pltpu.SemaphoreType.DMA((local + 2,)), pltpu.SemaphoreType.DMA((2, 2)), pltpu.SemaphoreType.DMA((2, 2)),
        pltpu.SemaphoreType.DMA((parts - 1,)), pltpu.SemaphoreType.DMA((parts - 1,)),
        pltpu.SemaphoreType.DMA((2, parts - 1)), pltpu.SemaphoreType.DMA((2, parts - 1)),
    ]
    if above is not None:
        inputs.append((above, False))
        halves = (share // 2, above.shape[2])
        outputs.append((halves, BF16, True))
        scratch += [
            pltpu.VMEM((parts - 1, *halves), BF16), pltpu.VMEM((parts, *halves), BF16), pltpu.VMEM((parts, *halves), BF16),
            pltpu.SemaphoreType.DMA((parts - 1,)), pltpu.SemaphoreType.DMA((parts - 1,)),
        ] + [pltpu.SemaphoreType.DMA] * 3
    done = expert_call(
        functools.partial(expert_back_kernel, layer, above is not None), inputs, outputs, scratch, LAYERS + layer
    )
    return done if above is not None else [*done, None]


def prepare_kernel(capacity, owners, *refs):
    squares, (router, *vectors), (inner_bias, outer_bias, routes) = refs[:4], refs[4:12], refs[12:15]
    tokens_in, matrices, refs = refs[15:17], refs[17:19], refs[19:]
    (out, above, b1, b2, dcol, drow), tokens_out, packed_out, refs = refs[:6], refs[6:8], refs[8], refs[9:]
    mine, turned, inner_low, outer_low, token_ins, token_outs, inner_in, outer_in, packs = refs[:9]
    sems, (b1_send, b1_recv, b2_send, b2_recv, own, token_load, token_store, weight_sems) = refs[9:14], refs[14:]
    weight_loads = [
        pltpu.make_async_copy(matrices[0], inner_in, weight_sems.at[0]),
        pltpu.make_async_copy(matrices[1], outer_in, weight_sems.at[1]),
    ]
    weight_store = pltpu.make_async_copy(packs, packed_out, weight_sems.at[2])
    parts, share, _ = out.shape
    loads = [pltpu.make_async_copy(tokens_in[n], token_ins.at[n], token_load.at[n]) for n in range(2)]
    stores = [pltpu.make_async_copy(token_outs.at[n], tokens_out[n], token_store.at[n]) for n in range(2)]
    width = squares[0].shape[2]
    experts_all = router.shape[2]
    local, part_ff = inner_bias.shape[1:]
    row, me = lax.axis_index("dp"), lax.axis_index("expert")
    sibling = {"expert": me + 1 - 2 * lax.rem(me, 2)}
    peers = [{"dp": lax.rem(row + k, parts)} for k in range(1, parts)]
    gather = SharedGather(mine, out, sems)

    def pack(target, layer):
        for n in range(4):
            target[:, n * width : (n + 1) * width] = squares[n][layer].astype(BF16)
        turned[...] = jnp.zeros_like(turned)
        for n in range(7):
            turned[VEC_AT + n : VEC_AT + n + 1, :] = vectors[n][layer : layer + 1, :]
        target[:, 4 * width :] = turned[...].T.astype(BF16)
        target[:, 4 * width : 4 * width + experts_all] = router[layer].astype(BF16)

    pack(mine, 0)
    for layer in range(LAYERS):
        for j in range(local):
            n = layer * local + j
            inner_low[n : n + 1, :] = inner_bias[layer, j : j + 1, :].astype(BF16).astype(F32)
            outer_low[n : n + 1, :] = outer_bias[layer, j : j + 1, :].astype(BF16).astype(F32)
    greet_all([sibling] + peers)
    place = pl.ds(pl.multiple_of(row * part_ff, part_ff), part_ff)
    singles = [
        remote(inner_low, b1.at[:, place], b1_send.at[k], b1_recv.at[k], peers[k]) for k in range(parts - 1)
    ] + [remote(outer_low, b2.at[row], b2_send.at[k], b2_recv.at[k], peers[k]) for k in range(parts - 1)]
    keeps = [
        pltpu.make_async_copy(inner_low, b1.at[:, place], own.at[0]),
        pltpu.make_async_copy(outer_low, b2.at[row], own.at[1]),
    ]
    gather.start()
    for copy in singles + keeps + loads + weight_loads:
        copy.start()
    pack(above, 1)
    for n in range(2):
        loads[n].wait()
        for image in range(routes.shape[1]):
            token_outs[n, image] = token_ins[n, :, image, :]
        stores[n].start()

    length = routes.shape[2]
    lanes = lax.broadcasted_iota(jnp.int32, (length, MISC), 1)
    earlier = (
        lax.broadcasted_iota(jnp.int32, (length, length), 0) > lax.broadcasted_iota(jnp.int32, (length, length), 1)
    ).astype(F32).astype(BF16)
    for layer in range(LAYERS):
        seen = jnp.zeros((1, MISC), F32)
        for image in range(routes.shape[1]):
            hots, dests = [], []
            for k in range(2):
                hots.append((lanes == routes[layer, image, :, k : k + 1]).astype(F32))
            counts = hots[0] + hots[1]
            before = dot(earlier, counts.astype(BF16)) + seen
            seen = seen + jnp.sum(counts, axis=0, keepdims=True)
            for k in range(2):
                slot = jnp.sum(hots[k] * before, axis=-1, keepdims=True)
                expert = routes[layer, image, :, k : k + 1].astype(F32)
                owner = jnp.floor(expert * (1.0 / local))
                place = ((expert - owner * local) * owners + owner) * capacity + slot
                dests.append(jnp.where(slot < capacity, place, -1.0))
                dcol[layer, image, :, k : k + 1] = dests[k].astype(jnp.int32)
            both = jnp.where(lanes == 0, dests[0], jnp.where(lanes == 1, dests[1], 0.0))
            drow[layer, image] = both.T[0:2, :].astype(jnp.int32)

    for copy in weight_loads:
        copy.wait()
    take = outer_in.shape[2]
    for layer in range(LAYERS):
        for j in range(local):
            for f in range(take // share):
                cols = slice(f * FF_BLOCK, (f + 1) * FF_BLOCK)
                packs[layer, j, f * share : (f + 1) * share, :] = inner_in[layer, j, :, cols].astype(BF16)
            packs[layer, j, take:, :] = outer_in[layer, j].astype(BF16)
    weight_store.start()
    gather.finish()
    for copy in singles + keeps + stores + [weight_store]:
        copy.wait()


def prepare(squares, router, vectors, inner_bias, outer_bias, routes, tokens, matrices, parts, owners, number):
    layers, share, width = squares[0].shape
    experts_all = router.shape[2]
    local, part_ff = inner_bias.shape[1:]
    _, images, length, _ = routes.shape
    capacity = (10 * images * length // (4 * experts_all) + 7) // 8 * 8
    columns = 4 * width + MISC
    count = layers * local
    sems = shared_sems(parts) + [pltpu.SemaphoreType.DMA((parts - 1,))] * 4 + [pltpu.SemaphoreType.DMA((2,))] * 3
    sems.append(pltpu.SemaphoreType.DMA((3,)))
    packs = (layers, local, 2 * matrices[1].shape[2], width)
    inputs = [*squares, router, *vectors, inner_bias, outer_bias, routes]
    turned = [jnp.transpose(item, (1, 0, 2)) for item in tokens]
    out, above, b1, b2, dcol, drow, *tokens, packs = expert_call(
        functools.partial(prepare_kernel, capacity, owners),
        [(a, True) for a in inputs] + [(a, False) for a in (*turned, *matrices)],
        [
            ((parts, share, columns), BF16, False), ((share, columns), BF16, True),
            ((count, part_ff * parts), F32, False), ((parts, count, share), F32, False),
            ((layers, images, length, 2), jnp.int32, True), ((layers, images, 2, length), jnp.int32, True),
            ((images, length, width), F32, False), ((images, length, width), F32, False), (packs, BF16, False),
        ],
        [
            pltpu.VMEM((share, columns), BF16), pltpu.VMEM((MISC, share), F32),
            pltpu.VMEM((count, part_ff), F32), pltpu.VMEM((count, share), F32),
            pltpu.VMEM((2, length, images, width), F32), pltpu.VMEM((2, images, length, width), F32),
            pltpu.VMEM(matrices[0].shape, F32), pltpu.VMEM(matrices[1].shape, F32), pltpu.VMEM(packs, BF16),
        ] + sems,
        number,
    )
    b2 = jnp.transpose(b2, (1, 0, 2)).reshape(count, width)
    return out.reshape(width, columns), above, (b1, b2), dcol, drow, capacity, tokens, packs


def settle_widths(columns, chips):
    blocks = columns // (MISC * chips)
    wide = (blocks + 1) // 2 * MISC
    return wide, columns // chips - wide


def settle_kernel(
    grads, tokens, final, tokens_out, own, paired, total, chips_in, dp_in, total_b, chips_in_b, dp_in_b,
    pair_send, pair_recv, local, out_send, out_recv, dp_send, dp_recv, out_send_b, out_recv_b, dp_send_b, dp_recv_b,
    back_send, back_recv, pass_send, pass_recv, token_ins, token_outs, token_load, token_store,
):
    parts, share, columns = grads.shape
    half = share // 2
    row, me = lax.axis_index("dp"), lax.axis_index("expert")
    core, chip = lax.rem(me, 2), me // 2
    chips = chips_in.shape[0] + 1
    wide, narrow = settle_widths(columns, chips)
    split = chips * wide
    sibling = {"expert": me + 1 - 2 * core}
    mine = pl.ds(pl.multiple_of(core * half, half), half)
    other = pl.ds(pl.multiple_of((1 - core) * half, half), half)

    def cols(number):
        return pl.ds(pl.multiple_of(number * wide, MISC), wide)

    def cols_b(number, start):
        return pl.ds(pl.multiple_of(start + number * narrow, MISC), narrow)

    def chip_at(k):
        return lax.rem(chip + k + chips, chips)

    dp_peers = [{"dp": lax.rem(row + k, parts)} for k in range(1, parts)]
    chip_peers = [{"expert": 2 * chip_at(k) + core} for k in range(1, chips)]
    greet_all([sibling] + dp_peers + chip_peers)

    order = [lax.rem(row + 1 + i, parts) for i in range(parts)]
    pairs, keeps = [], []
    for i in range(parts):
        source = grads.at[order[i]]
        pairs.append(remote(source.at[other], paired.at[i], pair_send.at[i], pair_recv.at[i], sibling))
        keeps.append(pltpu.make_async_copy(source.at[mine], own.at[i], local.at[i]))
        pairs[i].start()
        keeps[i].start()
    tokens_load = pltpu.make_async_copy(tokens, token_ins, token_load)
    tokens_load.start()
    tokens_store = pltpu.make_async_copy(token_outs, tokens_out, token_store)
    outs, scatters_b = [], []
    for i in range(parts):
        pairs[i].wait_recv()
        keeps[i].wait()
        own[i] = (own[i].astype(F32) + paired[i].astype(F32)).astype(BF16)
        if i < parts - 1:
            scatters_b.append(
                remote(own.at[i, :, split:], dp_in_b.at[i], dp_send_b.at[i], dp_recv_b.at[i], dp_peers[i])
            )
            scatters_b[i].start()
        outs.append([
            remote(
                own.at[i, :, cols(chip_at(k))], chips_in.at[k - 1, i], out_send.at[k - 1, i], out_recv.at[k - 1, i],
                chip_peers[k - 1],
            )
            for k in range(1, chips)
        ])
        for copy in outs[i]:
            copy.start()
    tokens_load.wait()
    for image in range(token_ins.shape[0]):
        token_outs[:, image, :] = token_ins[image]
    tokens_store.start()
    value = own[parts - 1, :, split:].astype(F32)
    for i in range(parts - 1):
        scatters_b[i].wait_recv()
        value = value + dp_in_b[i].astype(F32)
    total_b[...] = value.astype(BF16)
    outs_b = [
        remote(
            total_b.at[:, cols_b(chip_at(k), 0)], chips_in_b.at[k - 1], out_send_b.at[k - 1], out_recv_b.at[k - 1],
            chip_peers[k - 1],
        )
        for k in range(1, chips)
    ]
    for copy in outs_b:
        copy.start()
    scatters = []
    for i in range(parts):
        value = own[i, :, cols(chip)].astype(F32)
        for k in range(1, chips):
            outs[i][k - 1].wait_recv()
            value = value + chips_in[k - 1, i].astype(F32)
        if i < parts - 1:
            total[i] = value.astype(BF16)
            scatters.append(remote(total.at[i], dp_in.at[i], dp_send.at[i], dp_recv.at[i], dp_peers[i]))
            scatters[i].start()
        else:
            kept = value
    value = total_b[:, cols_b(chip, 0)].astype(F32)
    for k in range(1, chips):
        outs_b[k - 1].wait_recv()
        value = value + chips_in_b[k - 1].astype(F32)
    final[mine, cols_b(chip, split)] = value.astype(BF16)
    for i in range(parts - 1):
        scatters[i].wait_recv()
        kept = kept + dp_in[i].astype(F32)
    final[mine, cols(chip)] = kept.astype(BF16)

    def places(number):
        return [final.at[mine, cols(number)], final.at[mine, cols_b(number, split)]]

    backs, hands = [], []
    for n, place in enumerate(places(chip)):
        for k in range(1, chips):
            backs.append(remote(place, place, back_send.at[n, k - 1], back_recv.at[n, k - 1], chip_peers[k - 1]))
            backs[-1].start()
        hands.append(remote(place, place, pass_send.at[n, 0], pass_recv.at[n, 0], sibling))
        hands[-1].start()
    for k in range(1, chips):
        for n, place in enumerate(places(chip_at(-k))):
            backs[n * (chips - 1) + k - 1].wait_recv()
            hands.append(remote(place, place, pass_send.at[n, k], pass_recv.at[n, k], sibling))
            hands[-1].start()
    for copy in pairs + [copy for group in outs for copy in group] + outs_b + scatters + scatters_b + backs:
        copy.wait_send()
    for copy in hands + [tokens_store]:
        copy.wait()


def settle(grads, tokens, chips, number):
    parts, share, columns = grads.shape
    half = share // 2
    images, length, width = tokens.shape
    halves = pltpu.VMEM((parts, half, columns), BF16)
    wide, narrow = settle_widths(columns, chips)
    dp_in = pltpu.VMEM((parts - 1, half, wide), BF16)
    rest = chips * narrow
    sems = [(parts,)] * 3 + [(chips - 1, parts)] * 2 + [(parts - 1,)] * 2
    sems += [(chips - 1,)] * 2 + [(parts - 1,)] * 2 + [(2, chips - 1)] * 2 + [(2, chips)] * 2
    return expert_call(
        settle_kernel, [(grads, False), (tokens, False)],
        [((share, columns), BF16, True), ((length, images, width), F32, False)],
        [
            halves, halves, dp_in, pltpu.VMEM((chips - 1, parts, half, wide), BF16), dp_in,
            pltpu.VMEM((half, rest), BF16), pltpu.VMEM((chips - 1, half, narrow), BF16),
            pltpu.VMEM((parts - 1, half, rest), BF16),
        ] + [pltpu.SemaphoreType.DMA(n) for n in sems] + [
            pltpu.VMEM((images, length, width), F32), pltpu.VMEM((length, images, width), F32),
            pltpu.SemaphoreType.DMA, pltpu.SemaphoreType.DMA,
        ],
        number,
    )


def unpack_kernel(*refs):
    count = 2 * LAYERS
    firsts, seconds, both, miscs = refs[:count], refs[count : 2 * count], refs[2 * count : 2 * count + 2], refs[2 * count + 2 : 2 * count + 4]
    refs = refs[2 * count + 4 :]
    squares, router, vectors, (inner, outer) = refs[:4], refs[4], refs[5:12], refs[12:]
    width = squares[0].shape[2]
    for layer in range(LAYERS):
        for n in range(4):
            squares[n][layer] = both[layer][:, n * width : (n + 1) * width].astype(F32)
        for j in range(2):
            first = firsts[2 * layer + j]
            for f in range(first.shape[0]):
                inner[layer, j, :, f * FF_BLOCK : (f + 1) * FF_BLOCK] = first[f].astype(F32)
            outer[layer, j] = seconds[2 * layer + j][...].astype(F32)

    @pl.when(pl.program_id(0) == 0)
    def _():
        for layer in range(LAYERS):
            turned = miscs[layer][...].astype(F32).T
            router[layer] = turned[: router.shape[1], :]
            for n in range(7):
                vectors[n][layer : layer + 1, :] = turned[VEC_AT + n : VEC_AT + n + 1, :]


def unpack(pieces, both, local, ff, experts_all):
    layers, (share, columns) = len(both), both[0].shape
    rows, width = pieces[0].shape
    take = rows // 2
    blocks = ff // FF_BLOCK
    steps = max(1, share // 32)
    part = share // steps
    firsts = pl.BlockSpec((None, blocks, part, width), lambda i: (0, 0, i, 0))
    seconds = pl.BlockSpec((None, take // steps, width), lambda i: (1, i, 0))
    some = lambda rows, *rest: ((layers, *rest[:-1], rows, rest[-1]), F32, pl.BlockSpec(
        (layers, *rest[:-1], rows // steps, rest[-1]), lambda i: (0,) * len(rest) + (i, 0)
    ))
    return call(
        unpack_kernel, (steps,),
        [(p.reshape(2, blocks, share, width), firsts) for p in pieces]
        + [(p.reshape(2, take, width), seconds) for p in pieces]
        + [(a, pl.BlockSpec((part, columns), lambda i: (i, 0))) for a in both]
        + [(a, pl.BlockSpec((share, MISC), lambda i: (0, 4 * width // MISC))) for a in both],
        [some(share, width)] * 4
        + [((layers, experts_all, share), F32, pl.BlockSpec((layers, experts_all, share), lambda i: (0, 0, 0)))]
        + [((layers, share), F32, pl.BlockSpec((layers, share), lambda i: (0, 0)))] * 7
        + [some(share, local, ff), some(take, local, width)],
    )


def shards(
    images, cotangent, routes, query_weight, key_weight, value_weight, output_weight, router_weight, query_bias,
    value_bias, output_bias, attend_gain, attend_shift, expert_gain, expert_shift, inner_weight, inner_bias,
    outer_weight, outer_bias,
):
    count, length, width = images.shape
    parts = lax.axis_size("dp")
    owners = lax.axis_size("expert")
    experts_all = router_weight.shape[2]
    local = inner_weight.shape[1]
    ff = inner_weight.shape[3]
    share = width // parts
    tokens = count * length
    squares = (query_weight, key_weight, value_weight, output_weight)
    vectors = (query_bias, value_bias, output_bias, attend_gain, attend_shift, expert_gain, expert_shift)
    columns = -(-(4 * width + MISC) // (MISC * (owners // 2))) * MISC * (owners // 2)

    first = inner_weight[0, 0].reshape(share, ff // FF_BLOCK, FF_BLOCK)
    first = jnp.transpose(first, (1, 0, 2)).reshape(ff // parts, width).astype(BF16)
    firsts = [lax.all_gather(first, "dp", axis=0, tiled=False)]
    dense, above, expert_biases, dcol, drow, capacity, (images, cotangent), mine = prepare(
        squares, router_weight, vectors, inner_bias, outer_bias, routes, (images, cotangent), (inner_weight, outer_weight),
        parts, owners, 2 * LAYERS,
    )
    packed = [dense]
    slots = experts_all * capacity

    saved = []
    back = None
    rows = images
    for layer in range(LAYERS):
        weights = [(packed[layer], s) for s in packed_specs(packed[layer])]
        routing = [(routes, per_layer(routes, layer))]
        outputs = attend_outputs(count, length, width)
        if layer == 0:
            done = call(
                first_kernel, (count,), [(rows, per_image(rows))] + routing + weights, outputs
            )
        else:
            before = saved[-1]
            done = call(
                next_kernel, (count,),
                [
                    (before["middle"], per_image(before["middle"])),
                    (before["gates"], per_image(before["gates"])),
                    (picked, per_layer(picked, 0)),
                    (picked, per_layer(picked, 1)),
                ] + routing + weights,
                [
                    images_out(count, length, width, F32),
                ] + outputs
            )
            rows, *done = done
        middle, queries, keys, values, context, sums, gates = done[:7]
        picked, arrived, g, s, outer, second, *following = expert_forward(
            done[7], drow, dcol, (local, owners, capacity, width), firsts[layer], mine, expert_biases,
            above if layer + 1 < LAYERS else None, layer,
        )
        if following:
            packed.append(following[0].reshape(width, following[0].shape[2]))
            firsts.append(following[1])
        saved.append({
            "rows": rows, "middle": middle, "attend": (queries, keys, values, context, sums), "gates": gates,
            "experts": (arrived, g, s), "weights": (firsts[layer], outer, second), "picked": picked,
        })

    last = saved[-1]
    result, dz, *sources = call(
        turn_kernel, (count,),
        [(last["middle"], per_image(last["middle"])), (last["gates"], per_image(last["gates"]))]
        + [(picked, per_layer(picked, k)) for k in range(2)]
        + [(cotangent, per_image(cotangent)), (routes, per_layer(routes, LAYERS - 1))],
        [((length, count, width), F32, pl.BlockSpec((length, count, width), lambda i: (0, 0, 0)))]
        + [images_out(count, length, MISC, BF16)]
        + [images_out(count, length, width, BF16)] * 2
    )
    upstream = cotangent
    bias_grads = [None] * LAYERS
    finished = []
    waiting = []
    wgrad = None
    for layer in reversed(range(LAYERS)):
        kept = saved[layer]
        came, shares, grads, *biases, above = expert_backward(
            sources, drow, dcol, kept["weights"], *kept["experts"], wgrad, layer
        )
        came = came[0]
        came, waiting = lax.optimization_barrier((came, waiting))
        finished += waiting
        waiting = [shares, lax.psum_scatter(grads, "dp", scatter_dimension=0, tiled=False)]
        bias_grads[layer] = biases
        weights = [(packed[layer], s) for s in packed_specs(packed[layer])]
        inputs = [upstream, kept["rows"], kept["middle"], *kept["attend"], dz]
        inputs = [(a, per_image(a)) for a in inputs]
        inputs += [(came, per_image(came))] + weights
        outputs = [
            images_out(count, length, width, F32),
            (
                (width, columns), BF16,
                pl.BlockSpec((width, columns), lambda i: (0, 0)),
            ),
        ]
        if layer > 0:
            below = saved[layer - 1]
            inputs += [(below["picked"], per_layer(below["picked"], k)) for k in range(2)]
            inputs.append((below["gates"], per_image(below["gates"])))
            inputs.append((routes, per_layer(routes, layer - 1)))
            outputs += [images_out(count, length, MISC, BF16)] + [images_out(count, length, width, BF16)] * 2
        scratch = [pltpu.VMEM((width, 4 * width + MISC), F32), pltpu.VMEM((MISC, width), F32)]
        number = None
        if layer == 0:
            inputs.append((above, pl.BlockSpec(memory_space=pl.ANY)))
            outputs.append(((share, columns), BF16, pl.BlockSpec((share, columns), lambda i: (0, 0))))
            scratch += spread_scratch(share, columns, owners // 2)
            number = 2 * LAYERS + 2
        done = call(functools.partial(back_kernel, layer == 0), (count,), inputs, outputs, scratch, number)
        upstream, wgrad = done[:2]
        if layer > 0:
            dz, *sources = done[2:]
        wgrad = wgrad.reshape(parts, share, columns)
    lowest, upstream = settle(wgrad, upstream, owners // 2, 2 * LAYERS + 1)
    both = (lowest, done[2])
    pieces = [waiting[0], waiting[1][0], finished[0], finished[1][0]]
    *squares, router, v0, v1, v2, v3, v4, v5, v6, inner, outer = unpack(pieces, both, local, ff, experts_all)
    outer_bias_grad = jnp.stack([b[1] for b in bias_grads])
    return (
        jnp.transpose(result, (1, 0, 2)),
        jnp.transpose(upstream, (1, 0, 2)),
        *squares,
        jnp.transpose(router, (0, 2, 1)),
        v0, v1, v2, v3, v4, v5, v6,
        inner,
        jnp.stack([b[0] for b in bias_grads]),
        outer,
        lax.dynamic_slice_in_dim(outer_bias_grad, lax.axis_index("dp") * share, share, 2),
    )


def solution(mesh):
    both = P(("dp", "expert"), None, None)
    square = P(None, "dp", None)
    vector = P(None, "dp")
    matrix = P(None, "expert", "dp", None)
    bias = P(None, "expert", "dp")
    grads = (square,) * 5 + (vector,) * 7 + (matrix, bias, matrix, bias)
    return jax.shard_map(
        shards,
        mesh=mesh,
        in_specs=(both, both, P(None, ("dp", "expert"), None, None)) + grads,
        out_specs=(both, both) + grads,
        check_vma=False,
    )
```
